32 devices in a mesh: ctx: 8 (over z, x), wsh: 4 (over y, core).
Axes of the slice: x: 2, y: 2, z: 4, core: 2. Of those that a mesh axis runs over, the one named last changes fastest.
Arguments:
- tokens: bfloat16 [4, 4096, 768], P('wsh', 'ctx'), may hold values from -6 to 6
- cotangent: bfloat16 [4, 4096, 768], P('wsh', 'ctx'), may hold values from -6 to 6
- doc_starts: int32 [4, 8], P('wsh'), may hold values from 0 to 4095, as said below
- query_weight: bfloat16 [768, 768], P('wsh'), may hold values from -0.21875 to 0.21875
- key_weight: bfloat16 [768, 768], P('wsh'), may hold values from -0.21875 to 0.21875
- value_weight: bfloat16 [768, 768], P('wsh'), may hold values from -0.21875 to 0.21875
- out_weight: bfloat16 [768, 768], P('wsh'), may hold values from -3.5 to 3.5
- up_weight: bfloat16 [768, 3072], P('wsh'), may hold values from -0.21875 to 0.21875
- down_weight: bfloat16 [3072, 768], P('wsh'), may hold values from -0.109375 to 0.109375
- query_bias: bfloat16 [768], P('wsh'), may hold values from -3 to 3
- value_bias: bfloat16 [768], P('wsh'), may hold values from -3 to 3
- out_bias: bfloat16 [768], P('wsh'), may hold values from -3 to 3
- attn_gain: bfloat16 [768], P('wsh'), may hold values from 0.5 to 1.5
- attn_shift: bfloat16 [768], P('wsh'), may hold values from -3 to 3
- up_bias: bfloat16 [3072], P('wsh'), may hold values from -3 to 3
- down_bias: bfloat16 [768], P('wsh'), may hold values from -3 to 3
- final_gain: bfloat16 [768], P('wsh'), may hold values from 0.5 to 1.5
- final_shift: bfloat16 [768], P('wsh'), may hold values from -3 to 3
Outputs:
- layer_out: bfloat16 [4, 4096, 768], P('wsh', 'ctx')
- tokens_grad: bfloat16 [4, 4096, 768], P('wsh', 'ctx')
- query_weight_grad: float32 [768, 768], P('wsh')
- key_weight_grad: float32 [768, 768], P('wsh')
- value_weight_grad: float32 [768, 768], P('wsh')
- out_weight_grad: float32 [768, 768], P('wsh')
- up_weight_grad: float32 [768, 3072], P('wsh')
- down_weight_grad: float32 [3072, 768], P('wsh')
- query_bias_grad: float32 [768], P('wsh')
- value_bias_grad: float32 [768], P('wsh')
- out_bias_grad: float32 [768], P('wsh')
- attn_gain_grad: float32 [768], P('wsh')
- attn_shift_grad: float32 [768], P('wsh')
- up_bias_grad: float32 [3072], P('wsh')
- down_bias_grad: float32 [768], P('wsh')
- final_gain_grad: float32 [768], P('wsh')
- final_shift_grad: float32 [768], P('wsh')
The draws below stay inside these ranges and needn't reach their ends.
Inputs may be any that keep to these rules, and one draw needn't show every extreme that they name: `doc_starts`: each row starts with 0 and rises strictly; each stream holds 8 documents, exactly one of them 2048 tokens long.
All inputs are finite; a program needn't handle non-finite values.
Results may differ from the reference program's by a relative error of at most 0.035.
Values may be sent and summed in bfloat16 or wider, within the bound.
A program may use at most 192 MiB of HBM per device.

```python
import math
import jax
import jax.numpy as jnp
from jax import lax

D = 768
HEADS = 12
HD = 64
FF = 3072
NDOC = 8
STREAM_LEN = 4096
LONGEST = 2048
STREAMS = 4


def draw_doc_starts(key, part):
    rest = STREAM_LEN - LONGEST

    def one_stream(index):
        stream_key = jax.random.fold_in(jax.random.fold_in(key, 7), index)
        cut_key, place_key = jax.random.split(stream_key)
        cuts = jnp.sort(jax.random.permutation(cut_key, rest - 1)[:NDOC - 2] + 1).astype(jnp.int32)
        edges = jnp.concatenate([jnp.zeros((1,), jnp.int32), cuts, jnp.full((1,), rest, jnp.int32)])
        short = edges[1:] - edges[:-1]
        where_long = jax.random.randint(place_key, (), 0, NDOC)
        slots = jnp.arange(NDOC, dtype=jnp.int32)
        before = jnp.concatenate([short, jnp.zeros((1,), jnp.int32)])
        after = jnp.concatenate([jnp.zeros((1,), jnp.int32), short])
        lengths = jnp.where(slots < where_long, before, jnp.where(slots == where_long, LONGEST, after))
        return (jnp.cumsum(lengths) - lengths).astype(jnp.int32)
    return jax.vmap(one_stream)(jnp.arange(STREAMS, dtype=jnp.int32))


def block_scale(key, extent, cuts, least, largest):
    factor_of, own = 1.0, jax.random.fold_in(key, 6)
    for position, parts in cuts:
        heights = jnp.exp(jax.random.uniform(jax.random.fold_in(own, position), (parts,), jnp.float32, least / len(cuts), largest / len(cuts)))
        factor_of = factor_of * jnp.repeat(heights, extent[position] // parts).reshape([-1 if axis == position else 1 for axis in range(len(extent))])
    return factor_of


def noise(rng, extent, spread, reach, shards=(), held_as=jnp.bfloat16):
    gain = block_scale(rng, extent, shards, -0.22, 0.18) if shards else 1.0
    array = jax.random.normal(rng, extent, jnp.float32) * spread * gain
    return jnp.minimum(jnp.maximum(array, -reach), reach).astype(held_as)


def setup_inputs(seed: int = 0) -> dict:
    key_list = jax.random.split(jax.random.key(seed), 19)
    tokens = noise(key_list[0], (STREAMS, STREAM_LEN, D), 1.0, 6.0, ((0, 4), (1, 8)))
    cotangent = noise(key_list[1], (STREAMS, STREAM_LEN, D), 1.0, 6.0, ((0, 4), (1, 8)))
    doc_starts = draw_doc_starts(jax.random.fold_in(key_list[18], 71), 0)
    query_weight = noise(key_list[3], (D, D), D ** -0.5, 0.21875, ((0, 4),))
    key_weight = noise(key_list[4], (D, D), D ** -0.5, 0.21875, ((0, 4),))
    value_weight = noise(key_list[5], (D, D), D ** -0.5, 0.21875, ((0, 4),))
    out_weight = noise(key_list[6], (D, D), (max(D // 256, 1)) ** -0.5, 3.5, ((0, 4),))
    up_weight = noise(key_list[7], (D, FF), D ** -0.5, 0.21875, ((0, 4),))
    down_weight = noise(key_list[8], (FF, D), FF ** -0.5, 0.109375, ((0, 4),))
    query_bias = noise(key_list[9], (D,), 0.5, 3.0, ((0, 4),))
    value_bias = noise(key_list[10], (D,), 0.5, 3.0, ((0, 4),))
    out_bias = noise(key_list[11], (D,), 0.5, 3.0, ((0, 4),))
    attn_gain = jnp.clip(1.0 + 0.1 * jax.random.normal(key_list[12], (D,), jnp.float32), 0.5, 1.5).astype(jnp.bfloat16)
    attn_shift = noise(key_list[13], (D,), 0.5, 3.0, ((0, 4),))
    up_bias = noise(key_list[14], (FF,), 0.5, 3.0, ((0, 4),))
    down_bias = noise(key_list[15], (D,), 0.5, 3.0, ((0, 4),))
    final_gain = jnp.clip(1.0 + 0.1 * jax.random.normal(key_list[16], (D,), jnp.float32), 0.5, 1.5).astype(jnp.bfloat16)
    final_shift = noise(key_list[17], (D,), 0.5, 3.0, ((0, 4),))
    return dict(tokens=tokens, cotangent=cotangent, doc_starts=doc_starts, query_weight=query_weight, key_weight=key_weight, value_weight=value_weight, out_weight=out_weight, up_weight=up_weight, down_weight=down_weight, query_bias=query_bias, value_bias=value_bias, out_bias=out_bias, attn_gain=attn_gain, attn_shift=attn_shift, up_bias=up_bias, down_bias=down_bias, final_gain=final_gain, final_shift=final_shift)


@jax.custom_vjp
def low(v):
    return lax.optimization_barrier(v.astype(jnp.bfloat16)).astype(jnp.float32)

@jax.custom_vjp
def low_back(v):
    return v

def low_keep(v):
    return (low(v), None)

def low_pass(kept, grad):
    return (grad,)

def back_keep(v):
    return (v, None)

def back_low(kept, grad):
    return (low(grad),)
low.defvjp(low_keep, low_pass)
low_back.defvjp(back_keep, back_low)
EPS = 1e-12
NEG = -1e+30
SCALE = 0.125
ROOT_HALF = 0.7071067811865476
HIGH = lax.Precision.HIGHEST

def matmul(left, right):
    return jnp.dot(left, right, precision=HIGH)

def layer_norm(values, gain_vec, shift_vec):
    average = lax.optimization_barrier(jnp.mean(values, axis=-1, keepdims=True))
    centred = values - average
    variance = lax.optimization_barrier(jnp.mean(centred * centred, axis=-1, keepdims=True))
    return centred * lax.rsqrt(variance + EPS) * gain_vec + shift_vec

def gelu_act(values):
    return 0.5 * values * (1.0 + lax.erf(values * ROOT_HALF))

def attend(queries, keys, values, segments):
    length = queries.shape[0]
    block_size = math.gcd(length, 512)
    query_blocks = queries.reshape(length // block_size, block_size, HEADS, HD)
    seg_blocks = segments.reshape(length // block_size, block_size)

    def one_block(items):
        query_part, seg_part = items
        scores = jnp.einsum('qhd,khd->hqk', query_part, keys, precision=HIGH) * SCALE
        scores = low_back(scores)
        allowed = (seg_part[:, None] == segments[None, :])[None]
        scores = jnp.where(allowed, scores, NEG)
        top = lax.optimization_barrier(jnp.max(scores, axis=2, keepdims=True))
        exp_terms = jnp.where(allowed, jnp.exp(scores - top), 0.0)
        weights_f = exp_terms / lax.optimization_barrier(jnp.sum(exp_terms, axis=2, keepdims=True))
        weights_f = low(weights_f)
        return jnp.einsum('hqk,khd->qhd', weights_f, values, precision=HIGH)
    result = lax.map(jax.checkpoint(one_block), (query_blocks, seg_blocks))
    return result.reshape(length, D)

def one_layer(inputs, doc_start, params):
    query_w, key_w, value_w, out_w, up_w, down_w, query_b, value_b, out_b, attn_g, attn_s, up_b, down_b, final_g, final_s = params
    length = inputs.shape[0]
    positions = jnp.arange(length, dtype=jnp.int32)
    segments = lax.optimization_barrier(jnp.sum((doc_start[None, :] <= positions[:, None]).astype(jnp.int32), axis=1)) - 1
    entered = low(inputs)
    queries = low_back(low(matmul(entered, query_w) + query_b)).reshape(length, HEADS, HD)
    keys = low_back(low(matmul(entered, key_w))).reshape(length, HEADS, HD)
    values = low_back(low(matmul(entered, value_w) + value_b)).reshape(length, HEADS, HD)
    attended = attend(queries, keys, values, segments)
    attended_b = low_back(low(attended))
    branch = low_back(matmul(attended_b, out_w) + out_b)
    first = layer_norm(inputs + branch, attn_g, attn_s)
    up_f = low_back(matmul(low(first), up_w) + up_b)
    act_f = gelu_act(up_f)
    down_f = low_back(matmul(low(act_f), down_w) + down_b)
    return layer_norm(first + down_f, final_g, final_s)

def reference(tokens, cotangent, doc_starts, query_weight, key_weight, value_weight, out_weight, up_weight, down_weight, query_bias, value_bias, out_bias, attn_gain, attn_shift, up_bias, down_bias, final_gain, final_shift):
    params = (query_weight.astype(jnp.float32), key_weight.astype(jnp.float32), value_weight.astype(jnp.float32), out_weight.astype(jnp.float32), up_weight.astype(jnp.float32), down_weight.astype(jnp.float32), query_bias.astype(jnp.float32), value_bias.astype(jnp.float32), out_bias.astype(jnp.float32), attn_gain.astype(jnp.float32), attn_shift.astype(jnp.float32), up_bias.astype(jnp.float32), down_bias.astype(jnp.float32), final_gain.astype(jnp.float32), final_shift.astype(jnp.float32))
    streams_f = tokens.astype(jnp.float32)

    def forward(stream_in, weights):

        def per_stream(pair):
            return one_layer(pair[0], pair[1], weights)
        return lax.map(per_stream, (stream_in, doc_starts))
    result, pullback = jax.vjp(forward, streams_f, params)
    grad_in, grads = pullback(cotangent.astype(jnp.float32))
    return (result.astype(jnp.bfloat16), grad_in.astype(jnp.bfloat16), grads[0], grads[1], grads[2], grads[3], grads[4], grads[5], grads[6], grads[7], grads[8], grads[9], grads[10], grads[11], grads[12], grads[13], grads[14])
```

```python
import functools

import jax
import jax.numpy as jnp
from jax import lax
from jax.experimental import pallas as pl
from jax.experimental.pallas import tpu as pltpu
from jax.sharding import PartitionSpec as P

D = 768
HEADS = 12
HD = 64
SCALE = 0.125
EPS = 1e-12
ROOT_HALF = 0.7071067811865476
BF = jnp.bfloat16
F32 = jnp.float32
NT = (((1,), (1,)), ((), ()))
NN = (((1,), (0,)), ((), ()))
TN = (((0,), (0,)), ((), ()))


def layer_norm(values, gain_vec, shift_vec):
    average = jnp.mean(values, axis=-1, keepdims=True)
    centred = values - average
    variance = jnp.mean(centred * centred, axis=-1, keepdims=True)
    return centred * lax.rsqrt(variance + EPS) * gain_vec + shift_vec


def gelu_act(values):
    return 0.5 * values * (1.0 + lax.erf(values * ROOT_HALF))


def key_range(doc_start, first_row, rows, stream_rows, tile):
    pos = jnp.arange(rows // tile, dtype=jnp.int32) * tile + first_row
    last = pos + tile - 1
    low = jnp.max(jnp.where(doc_start[None, :] <= pos[:, None], doc_start[None, :], 0), axis=1)
    high = jnp.min(
        jnp.where(doc_start[None, :] > last[:, None], doc_start[None, :], stream_rows), axis=1
    )
    first = low // 128 * 128
    count = (high - first + 255) // 256
    first = jnp.minimum(first, stream_rows - count * 256)
    return jnp.stack([first, count], axis=1).astype(jnp.int32)


def document_lanes(doc_start, first_row, rows, stream_rows):
    far = jnp.full((128 - doc_start.shape[0],), 2**30, jnp.int32)
    starts = jnp.concatenate([doc_start, far])
    ends = jnp.concatenate([doc_start[1:], jnp.full((1,), stream_rows, jnp.int32), far])
    query_pos = first_row + jnp.arange(rows, dtype=jnp.int32)[:, None]
    key_pos = jnp.arange(stream_rows, dtype=jnp.int32)[:, None]
    query_doc = ((query_pos >= starts) & (query_pos < ends)).astype(BF)
    key_doc = jnp.where((key_pos >= starts) & (key_pos < ends), 0.0, -1e30).astype(BF)
    return query_doc, key_doc


def stack_heads(x, extra=None):
    lane = lax.broadcasted_iota(jnp.int32, x.shape, 1)
    zero = jnp.zeros_like(x)
    lo = jnp.where(lane < 64, x, zero)
    hi = jnp.where(lane < 64, zero, x)
    if extra is not None:
        lo = jnp.concatenate([lo, extra], axis=1)
        hi = jnp.concatenate([hi, extra], axis=1)
    return jnp.concatenate([lo, hi], axis=0)

def pick_heads(x, tq):
    return jnp.concatenate([x[:64, :tq], x[64:, tq:]], axis=0)

def two_level(start, count, tk, body, init):
    big = tk // 256
    whole = count // big
    def large(t, c):
        return body(pl.multiple_of(t * tk, 256), pl.multiple_of(start + t * tk, 128), tk, c)
    def small(t, c):
        return body(pl.multiple_of(t * 256, 256), pl.multiple_of(start + t * 256, 128), 256, c)
    c = lax.fori_loop(0, whole, large, init)
    return lax.fori_loop(whole * big, count, small, c)

def fwd_kernel(tk, bounds, q_ref, qaug_ref, k_ref, kaug_ref, v_ref, ot_ref, lse_ref, s_scr, acc):
    qi = pl.program_id(1)
    start, count = bounds[qi, 0], bounds[qi, 1]
    tq = q_ref.shape[0]
    rhs = stack_heads(q_ref[...], qaug_ref[...])

    def scores(loc, off, size, m):
        lhs = jnp.concatenate([k_ref[pl.ds(off, size), :], kaug_ref[pl.ds(off, size), :]], axis=1)
        s = lax.dot_general(lhs, rhs, NT, preferred_element_type=F32)
        s_scr[pl.ds(loc, size), :] = s
        return jnp.maximum(m, jnp.max(s.reshape(size // 8, 8, 2 * tq), axis=0))

    m8 = two_level(start, count, tk, scores, jnp.full((8, 2 * tq), -3e38, F32))
    m = jnp.max(m8, axis=0, keepdims=True)
    acc[...] = jnp.zeros_like(acc)

    def mix(loc, off, size, l8):
        p = jnp.exp(s_scr[pl.ds(loc, size), :] - m)
        acc[...] += lax.dot_general(v_ref[pl.ds(off, size), :], p.astype(BF), TN, preferred_element_type=F32)
        return l8 + jnp.sum(p.reshape(size // 8, 8, 2 * tq), axis=0)

    l8 = two_level(start, count, tk, mix, jnp.zeros((8, 2 * tq), F32))
    l = jnp.sum(l8, axis=0, keepdims=True)
    ot_ref[...] = pick_heads(acc[...] / l, tq)
    lse = m + jnp.log(l)
    lse_ref[0] = jnp.concatenate([lse[:, :tq], lse[:, tq:]], axis=0)

def attn_fwd(bounds, q, qaug, k, kaug, v, *, tq=512, tk=768):
    T, D = q.shape
    S = k.shape[0]
    pairs = D // 128
    return pl.pallas_call(
        functools.partial(fwd_kernel, tk),
        out_shape=(jax.ShapeDtypeStruct((D, T), F32), jax.ShapeDtypeStruct((pairs, 2, T), F32)),
        grid_spec=pltpu.PrefetchScalarGridSpec(
            num_scalar_prefetch=1, grid=(pairs, T // tq),
            in_specs=[pl.BlockSpec((tq, 128), lambda h, i, b: (i, h)),
                      pl.BlockSpec((tq, 128), lambda h, i, b: (i, 0)),
                      pl.BlockSpec((S, 128), lambda h, i, b: (0, h)),
                      pl.BlockSpec((S, 128), lambda h, i, b: (0, 0)),
                      pl.BlockSpec((S, 128), lambda h, i, b: (0, h))],
            out_specs=(pl.BlockSpec((128, tq), lambda h, i, b: (h, i)),
                       pl.BlockSpec((1, 2, tq), lambda h, i, b: (h, 0, i))),
            scratch_shapes=[pltpu.VMEM((S, 2 * tq), F32), pltpu.VMEM((128, 2 * tq), F32)]),
        name="attend",
    )(bounds, q, qaug, k, kaug, v)

def bwd_kernel(tk, bounds, q_ref, qaug_ref, do_ref, lse_ref, ot_ref, k_ref, kaug_ref, v_ref,
               dqt_ref, dk_ref, dv_ref, dk_acc, dv_acc, dq_acc):
    qi = pl.program_id(1)
    start, count = bounds[qi, 0], bounds[qi, 1]
    tq = q_ref.shape[0]

    @pl.when(qi == 0)
    def _():
        dk_acc[...] = jnp.zeros_like(dk_acc)
        dv_acc[...] = jnp.zeros_like(dv_acc)

    qs = stack_heads(q_ref[...])
    qrhs = stack_heads(q_ref[...], qaug_ref[...])
    dos = stack_heads(do_ref[...])
    lse = jnp.concatenate([lse_ref[0, 0:1, :], lse_ref[0, 1:2, :]], axis=1)
    mixed = ot_ref[...] * do_ref[...].astype(F32).T
    delta = jnp.concatenate(
        [jnp.sum(mixed[:64], axis=0, keepdims=True), jnp.sum(mixed[64:], axis=0, keepdims=True)], axis=1
    )
    dq_acc[...] = jnp.zeros_like(dq_acc)

    def step(loc, off, size, carry):
        rows = pl.ds(off, size)
        lhs = jnp.concatenate([k_ref[rows, :], kaug_ref[rows, :]], axis=1)
        x = lax.dot_general(lhs, qrhs, NT, preferred_element_type=F32)
        y = lax.dot_general(v_ref[rows, :], dos, NT, preferred_element_type=F32)
        p = jnp.exp(x - lse)
        ds = (p * (y - delta)).astype(BF)
        pb = p.astype(BF)
        dv_acc[rows, :] += lax.dot_general(pb, dos, NN, preferred_element_type=F32)
        dk_acc[rows, :] += lax.dot_general(ds, qs, NN, preferred_element_type=F32)
        dq_acc[...] += lax.dot_general(k_ref[rows, :], ds, TN, preferred_element_type=F32)
        return carry

    two_level(start, count, tk, step, 0)
    dqt_ref[...] = (pick_heads(dq_acc[...], tq) * 0.125).astype(BF)

    @pl.when(qi == pl.num_programs(1) - 1)
    def _():
        dk_ref[...] = dk_acc[...].astype(BF)
        dv_ref[...] = dv_acc[...].astype(BF)

def attn_bwd(bounds, q, qaug, do, lse, ot, k, kaug, v, *, tq=512, tk=768):
    T, D = q.shape
    S = k.shape[0]
    pairs = D // 128
    row = lambda h, i, b: (h, 0, i)
    return pl.pallas_call(
        functools.partial(bwd_kernel, tk),
        out_shape=(jax.ShapeDtypeStruct((D, T), BF), jax.ShapeDtypeStruct((S, D), BF), jax.ShapeDtypeStruct((S, D), BF)),
        grid_spec=pltpu.PrefetchScalarGridSpec(
            num_scalar_prefetch=1, grid=(pairs, T // tq),
            in_specs=[pl.BlockSpec((tq, 128), lambda h, i, b: (i, h)),
                      pl.BlockSpec((tq, 128), lambda h, i, b: (i, 0)),
                      pl.BlockSpec((tq, 128), lambda h, i, b: (i, h)),
                      pl.BlockSpec((1, 2, tq), row),
                      pl.BlockSpec((128, tq), lambda h, i, b: (h, i)),
                      pl.BlockSpec((S, 128), lambda h, i, b: (0, h)),
                      pl.BlockSpec((S, 128), lambda h, i, b: (0, 0)),
                      pl.BlockSpec((S, 128), lambda h, i, b: (0, h))],
            out_specs=(pl.BlockSpec((128, tq), lambda h, i, b: (h, i)),
                       pl.BlockSpec((S, 128), lambda h, i, b: (0, h)),
                       pl.BlockSpec((S, 128), lambda h, i, b: (0, h))),
            scratch_shapes=[pltpu.VMEM((S, 128), F32), pltpu.VMEM((S, 128), F32), pltpu.VMEM((128, 2 * tq), F32)]),
        name="attend_back",
    )(bounds, q, qaug, do, lse, ot, k, kaug, v)


def local(
    tokens,
    cotangent,
    doc_starts,
    query_weight,
    key_weight,
    value_weight,
    out_weight,
    up_weight,
    down_weight,
    query_bias,
    value_bias,
    out_bias,
    attn_gain,
    attn_shift,
    up_bias,
    down_bias,
    final_gain,
    final_shift,
):
    inputs = tokens[0]
    doc_start = doc_starts[0]
    tok_rows = inputs.shape[0]
    stream_rows = tok_rows * lax.axis_size("ctx")
    first_row = lax.axis_index("ctx") * tok_rows
    tile = min(tok_rows, 512)
    bounds = key_range(doc_start, first_row, tok_rows, stream_rows, tile)
    query_doc, key_doc = document_lanes(doc_start, first_row, tok_rows, stream_rows)

    def gather(x):
        return lax.all_gather(x, "wsh", axis=0, tiled=True)

    all_tokens = lax.all_gather(inputs, "ctx", axis=0, tiled=True)
    qkv_w = gather(jnp.concatenate([query_weight, key_weight, value_weight], axis=1))
    query_w, key_w, value_w = qkv_w[:, :D], qkv_w[:, D : 2 * D], qkv_w[:, 2 * D :]
    small = gather(
        jnp.stack([query_bias, value_bias, out_bias, attn_gain, attn_shift, down_bias, final_gain, final_shift], axis=1)
    ).astype(F32)
    query_b, value_b, out_b, attn_g, attn_s, down_b, final_g, final_s = [small[:, i] for i in range(8)]
    up_b = gather(up_bias).astype(F32)
    out_w = gather(out_weight)
    up_w = gather(up_weight)
    down_w = gather(down_weight)

    queries = (jnp.dot(inputs, query_w, preferred_element_type=F32) + query_b).astype(BF) * jnp.asarray(SCALE, BF)
    keys = jnp.dot(all_tokens, key_w, preferred_element_type=F32).astype(BF)
    values = (jnp.dot(all_tokens, value_w, preferred_element_type=F32) + value_b).astype(BF)
    mixed_t, log_rows = attn_fwd(bounds, queries, query_doc, keys, key_doc, values, tq=tile)
    attn_t = mixed_t.astype(BF)
    inputs_f = inputs.astype(F32)
    branch = lax.dot_general(attn_t, out_w, TN, preferred_element_type=F32) + out_b
    first_norm, first_pull = jax.vjp(layer_norm, inputs_f + branch, attn_g, attn_s)
    first_b = first_norm.astype(BF)
    up_f = jnp.dot(first_b, up_w, preferred_element_type=F32) + up_b
    act_f, act_pull = jax.vjp(gelu_act, up_f)
    act_b = act_f.astype(BF)
    down_f = jnp.dot(act_b, down_w, preferred_element_type=F32) + down_b
    final_f, final_pull = jax.vjp(layer_norm, first_norm + down_f, final_g, final_s)
    layer_out = final_f.astype(BF)

    grad_sum2, grad_final_g, grad_final_s = final_pull(cotangent[0].astype(F32))
    grad_down = grad_sum2.astype(BF)
    grad_down_w = jnp.einsum("tf,td->fd", act_b, grad_down, preferred_element_type=F32)
    grad_down_b = jnp.sum(grad_down.astype(F32), axis=0)
    grad_act = jnp.einsum("td,fd->tf", grad_down, down_w, preferred_element_type=F32)
    (grad_up_f,) = act_pull(grad_act)
    grad_up = grad_up_f.astype(BF)
    grad_up_w = jnp.einsum("td,tf->df", first_b, grad_up, preferred_element_type=F32)
    grad_up_b = jnp.sum(grad_up.astype(F32), axis=0)
    grad_first = grad_sum2 + jnp.einsum("tf,df->td", grad_up, up_w, preferred_element_type=F32)
    grad_sum1, grad_attn_g, grad_attn_s = first_pull(grad_first)
    grad_branch = grad_sum1.astype(BF)
    grad_out_w = jnp.dot(attn_t, grad_branch, preferred_element_type=F32)
    grad_out_b = jnp.sum(grad_branch.astype(F32), axis=0)
    grad_attn = jnp.einsum("te,de->td", grad_branch, out_w, preferred_element_type=F32).astype(BF)
    grad_q_t, grad_k, grad_v = attn_bwd(
        bounds, queries, query_doc, grad_attn, log_rows, mixed_t, keys, key_doc, values, tq=tile
    )
    grad_all = jnp.einsum("te,de->td", grad_k, key_w, preferred_element_type=F32)
    grad_all = grad_all + jnp.einsum("te,de->td", grad_v, value_w, preferred_element_type=F32)
    grad_own = lax.psum_scatter(grad_all.astype(BF), "ctx", scatter_dimension=0, tiled=True)
    grad_query_w = jnp.einsum("td,et->de", inputs, grad_q_t, preferred_element_type=F32)
    grad_key_w = jnp.einsum("td,te->de", all_tokens, grad_k, preferred_element_type=F32)
    grad_value_w = jnp.einsum("td,te->de", all_tokens, grad_v, preferred_element_type=F32)
    grad_query_b = jnp.sum(grad_q_t.astype(F32), axis=1)
    grad_value_b = jnp.sum(grad_v.astype(F32), axis=0)
    grad_inputs = grad_sum1 + lax.dot_general(
        grad_q_t, query_w, (((0,), (1,)), ((), ())), preferred_element_type=F32
    )
    grad_inputs = grad_inputs + grad_own.astype(F32)

    def total(g):
        part = lax.psum_scatter(g.astype(BF), "wsh", scatter_dimension=0, tiled=True)
        return lax.psum(part, "ctx").astype(F32)

    grads = [
        grad_query_w, grad_key_w, grad_value_w, grad_out_w, grad_up_w, grad_down_w,
        grad_query_b, grad_value_b, grad_out_b, grad_attn_g, grad_attn_s, grad_up_b,
        grad_down_b, grad_final_g, grad_final_s,
    ]
    return (
        layer_out.reshape(1, tok_rows, D),
        grad_inputs.astype(BF).reshape(1, tok_rows, D),
        *[total(g) for g in grads],
    )


def solution(mesh):
    rows, mat, vec = P("wsh", "ctx", None), P("wsh", None), P("wsh")
    return jax.shard_map(
        local,
        mesh=mesh,
        in_specs=(rows, rows, mat) + (mat,) * 6 + (vec,) * 9,
        out_specs=(rows, rows) + (mat,) * 6 + (vec,) * 9,
        check_vma=False,
    )
```

```python
import functools

import jax
import jax.numpy as jnp
from jax import lax
from jax.experimental import pallas as pl
from jax.experimental.pallas import tpu as pltpu
from jax.sharding import PartitionSpec as P

D = 768
HEADS = 12
HD = 64
SCALE = 0.125
EPS = 1e-12
ROOT_HALF = 0.7071067811865476
BF = jnp.bfloat16
F32 = jnp.float32
NT = (((1,), (1,)), ((), ()))
NN = (((1,), (0,)), ((), ()))
TN = (((0,), (0,)), ((), ()))


def layer_norm(values, gain_vec, shift_vec):
    average = jnp.mean(values, axis=-1, keepdims=True)
    centred = values - average
    variance = jnp.mean(centred * centred, axis=-1, keepdims=True)
    return centred * lax.rsqrt(variance + EPS) * gain_vec + shift_vec


def gelu_act(values):
    return 0.5 * values * (1.0 + lax.erf(values * ROOT_HALF))


def key_range(doc_start, first_row, rows, stream_rows, tile):
    pos = jnp.arange(rows // tile, dtype=jnp.int32) * tile + first_row
    last = pos + tile - 1
    low = jnp.max(jnp.where(doc_start[None, :] <= pos[:, None], doc_start[None, :], 0), axis=1)
    high = jnp.min(
        jnp.where(doc_start[None, :] > last[:, None], doc_start[None, :], stream_rows), axis=1
    )
    first = low // 128 * 128
    count = (high - first + 255) // 256
    first = jnp.minimum(first, stream_rows - count * 256)
    return jnp.stack([first, count], axis=1).astype(jnp.int32)


def document_lanes(doc_start, first_row, rows, stream_rows):
    far = jnp.full((128 - doc_start.shape[0],), 2**30, jnp.int32)
    starts = jnp.concatenate([doc_start, far])
    ends = jnp.concatenate([doc_start[1:], jnp.full((1,), stream_rows, jnp.int32), far])
    query_pos = first_row + jnp.arange(rows, dtype=jnp.int32)[:, None]
    key_pos = jnp.arange(stream_rows, dtype=jnp.int32)[:, None]
    query_doc = ((query_pos >= starts) & (query_pos < ends)).astype(BF)
    key_doc = jnp.where((key_pos >= starts) & (key_pos < ends), 0.0, -1e30).astype(BF)
    return query_doc, key_doc


def stack_heads(x, extra=None):
    lane = lax.broadcasted_iota(jnp.int32, x.shape, 1)
    zero = jnp.zeros_like(x)
    lo = jnp.where(lane < 64, x, zero)
    hi = jnp.where(lane < 64, zero, x)
    if extra is not None:
        lo = jnp.concatenate([lo, extra], axis=1)
        hi = jnp.concatenate([hi, extra], axis=1)
    return jnp.concatenate([lo, hi], axis=0)

def pick_heads(x, tq):
    return jnp.concatenate([x[:64, :tq], x[64:, tq:]], axis=0)

def two_level(start, count, tk, body, init):
    big = tk // 256
    whole = count // big
    def large(t, c):
        return body(pl.multiple_of(t * tk, 256), pl.multiple_of(start + t * tk, 128), tk, c)
    def small(t, c):
        return body(pl.multiple_of(t * 256, 256), pl.multiple_of(start + t * 256, 128), 256, c)
    c = lax.fori_loop(0, whole, large, init)
    return lax.fori_loop(whole * big, count, small, c)

def fwd_kernel(tk, bounds, q_ref, qaug_ref, k_ref, kaug_ref, v_ref, ot_ref, lse_ref, s_scr, acc):
    qi = pl.program_id(1)
    start, count = bounds[qi, 0], bounds[qi, 1]
    tq = q_ref.shape[0]
    rhs = stack_heads(q_ref[...], qaug_ref[...])

    def scores(loc, off, size, m):
        lhs = jnp.concatenate([k_ref[pl.ds(off, size), :], kaug_ref[pl.ds(off, size), :]], axis=1)
        s = lax.dot_general(lhs, rhs, NT, preferred_element_type=F32)
        s_scr[pl.ds(loc, size), :] = s
        return jnp.maximum(m, jnp.max(s.reshape(size // 8, 8, 2 * tq), axis=0))

    m8 = two_level(start, count, tk, scores, jnp.full((8, 2 * tq), -3e38, F32))
    m = jnp.max(m8, axis=0, keepdims=True)
    acc[...] = jnp.zeros_like(acc)

    def mix(loc, off, size, l8):
        p = jnp.exp(s_scr[pl.ds(loc, size), :] - m)
        acc[...] += lax.dot_general(v_ref[pl.ds(off, size), :], p.astype(BF), TN, preferred_element_type=F32)
        return l8 + jnp.sum(p.reshape(size // 8, 8, 2 * tq), axis=0)

    l8 = two_level(start, count, tk, mix, jnp.zeros((8, 2 * tq), F32))
    l = jnp.sum(l8, axis=0, keepdims=True)
    ot_ref[...] = pick_heads(acc[...] / l, tq)
    lse = m + jnp.log(l)
    lse_ref[0] = jnp.concatenate([lse[:, :tq], lse[:, tq:]], axis=0)

def attn_fwd(bounds, q, qaug, k, kaug, v, *, tq=512, tk=768):
    T, D = q.shape
    S = k.shape[0]
    pairs = D // 128
    return pl.pallas_call(
        functools.partial(fwd_kernel, tk),
        out_shape=(jax.ShapeDtypeStruct((D, T), F32), jax.ShapeDtypeStruct((pairs, 2, T), F32)),
        grid_spec=pltpu.PrefetchScalarGridSpec(
            num_scalar_prefetch=1, grid=(pairs, T // tq),
            in_specs=[pl.BlockSpec((tq, 128), lambda h, i, b: (i, h)),
                      pl.BlockSpec((tq, 128), lambda h, i, b: (i, 0)),
                      pl.BlockSpec((S, 128), lambda h, i, b: (0, h)),
                      pl.BlockSpec((S, 128), lambda h, i, b: (0, 0)),
                      pl.BlockSpec((S, 128), lambda h, i, b: (0, h))],
            out_specs=(pl.BlockSpec((128, tq), lambda h, i, b: (h, i)),
                       pl.BlockSpec((1, 2, tq), lambda h, i, b: (h, 0, i))),
            scratch_shapes=[pltpu.VMEM((S, 2 * tq), F32), pltpu.VMEM((128, 2 * tq), F32)]),
        name="attend",
    )(bounds, q, qaug, k, kaug, v)

def bwd_kernel(tk, bounds, q_ref, qaug_ref, do_ref, lse_ref, ot_ref, k_ref, kaug_ref, v_ref,
               dqt_ref, dk_ref, dv_ref, dk_acc, dv_acc, dq_acc):
    qi = pl.program_id(1)
    start, count = bounds[qi, 0], bounds[qi, 1]
    tq = q_ref.shape[0]

    @pl.when(qi == 0)
    def _():
        dk_acc[...] = jnp.zeros_like(dk_acc)
        dv_acc[...] = jnp.zeros_like(dv_acc)

    qs = stack_heads(q_ref[...])
    qrhs = stack_heads(q_ref[...], qaug_ref[...])
    dos = stack_heads(do_ref[...])
    lse = jnp.concatenate([lse_ref[0, 0:1, :], lse_ref[0, 1:2, :]], axis=1)
    mixed = ot_ref[...] * do_ref[...].astype(F32).T
    delta = jnp.concatenate(
        [jnp.sum(mixed[:64], axis=0, keepdims=True), jnp.sum(mixed[64:], axis=0, keepdims=True)], axis=1
    )
    dq_acc[...] = jnp.zeros_like(dq_acc)

    def step(loc, off, size, carry):
        rows = pl.ds(off, size)
        lhs = jnp.concatenate([k_ref[rows, :], kaug_ref[rows, :]], axis=1)
        x = lax.dot_general(lhs, qrhs, NT, preferred_element_type=F32)
        y = lax.dot_general(v_ref[rows, :], dos, NT, preferred_element_type=F32)
        p = jnp.exp(x - lse)
        ds = (p * (y - delta)).astype(BF)
        pb = p.astype(BF)
        dv_acc[rows, :] += lax.dot_general(pb, dos, NN, preferred_element_type=F32)
        dk_acc[rows, :] += lax.dot_general(ds, qs, NN, preferred_element_type=F32)
        dq_acc[...] += lax.dot_general(k_ref[rows, :], ds, TN, preferred_element_type=F32)
        return carry

    two_level(start, count, tk, step, 0)
    dqt_ref[...] = (pick_heads(dq_acc[...], tq) * 0.125).astype(BF)

    @pl.when(qi == pl.num_programs(1) - 1)
    def _():
        dk_ref[...] = dk_acc[...].astype(BF)
        dv_ref[...] = dv_acc[...].astype(BF)

def attn_bwd(bounds, q, qaug, do, lse, ot, k, kaug, v, *, tq=512, tk=768):
    T, D = q.shape
    S = k.shape[0]
    pairs = D // 128
    row = lambda h, i, b: (h, 0, i)
    return pl.pallas_call(
        functools.partial(bwd_kernel, tk),
        out_shape=(jax.ShapeDtypeStruct((D, T), BF), jax.ShapeDtypeStruct((S, D), BF), jax.ShapeDtypeStruct((S, D), BF)),
        grid_spec=pltpu.PrefetchScalarGridSpec(
            num_scalar_prefetch=1, grid=(pairs, T // tq),
            in_specs=[pl.BlockSpec((tq, 128), lambda h, i, b: (i, h)),
                      pl.BlockSpec((tq, 128), lambda h, i, b: (i, 0)),
                      pl.BlockSpec((tq, 128), lambda h, i, b: (i, h)),
                      pl.BlockSpec((1, 2, tq), row),
                      pl.BlockSpec((128, tq), lambda h, i, b: (h, i)),
                      pl.BlockSpec((S, 128), lambda h, i, b: (0, h)),
                      pl.BlockSpec((S, 128), lambda h, i, b: (0, 0)),
                      pl.BlockSpec((S, 128), lambda h, i, b: (0, h))],
            out_specs=(pl.BlockSpec((128, tq), lambda h, i, b: (h, i)),
                       pl.BlockSpec((S, 128), lambda h, i, b: (0, h)),
                       pl.BlockSpec((S, 128), lambda h, i, b: (0, h))),
            scratch_shapes=[pltpu.VMEM((S, 128), F32), pltpu.VMEM((S, 128), F32), pltpu.VMEM((128, 2 * tq), F32)]),
        name="attend_back",
    )(bounds, q, qaug, do, lse, ot, k, kaug, v)


def reach(n_ctx):
    return n_ctx // 2


def reduce_kernel(chunks, n_parts, *refs):
    parts = refs[:n_parts]
    vec_ref, rows_ref, out_ref, vec_out, own_ref = refs[n_parts : n_parts + 5]
    (mine, buf_a, buf_h, buf_b, buf_s, keep, buf_c, buf_u, buf_d, buf_f,
     vmine, vbuf_a, vbuf_h, vbuf_b, vbuf_s, vbuf_c, vbuf_u, vbuf_d,
     rmine, rbuf_x, rbuf_s, rbuf_z, rkeep,
     sem_l, sem_a, sem_b, sem_c, sem_d, sem_e, sem_f, sem_v, sem_rl, sem_rx, sem_rz) = refs[n_parts + 5 :]
    n_chunks = len(chunks)
    n_ctx, n_wsh = lax.axis_size("ctx"), lax.axis_size("wsh")
    zs = n_ctx // 2
    a, w = lax.axis_index("ctx"), lax.axis_index("wsh")
    z, x = a // 2, lax.rem(a, 2)
    y, c = w // 2, lax.rem(w, 2)
    core_peer = (a, y * 2 + (1 - c))
    y_peer = (a, (1 - y) * 2 + c)
    x_peer = (z * 2 + (1 - x), w)

    def z_peer(d):
        other = lax.rem(z + d, zs)
        return other, (other * 2 + x, w)

    def slot(dest, src):
        return lax.rem(src - dest + zs, zs) - 1

    rows = out_ref.shape[1]
    half = out_ref.shape[2] // 2
    piece = rows // zs
    MESH = pl.DeviceIdType.MESH
    barrier = pltpu.get_barrier_semaphore()
    for dev in [core_peer, y_peer, x_peer] + [z_peer(d)[1] for d in range(1, zs)]:
        pl.semaphore_signal(barrier, inc=1, device_id=dev, device_id_type=MESH)
    pl.semaphore_wait(barrier, zs + 2)

    def send(src, dst, sems, idx, dev):
        return pltpu.make_async_remote_copy(
            src_ref=src, dst_ref=dst, send_sem=sems.at[(0,) + idx], recv_sem=sems.at[(1,) + idx],
            device_id=dev, device_id_type=MESH)

    def wait_in(ref, sems, idx):
        send(ref, ref, sems, idx, core_peer).wait_recv()

    def wait_out(ref, sems, idx):
        send(ref, ref, sems, idx, core_peer).wait_send()

    for yy in range(2):
        pltpu.make_async_copy(vec_ref.at[yy * 2 + c], vmine.at[yy], sem_v.at[0, 0]).start()
        send(vec_ref.at[yy * 2 + (1 - c)], vbuf_a.at[yy], sem_v, (1,), core_peer).start()
    for k, (p, row0, col0) in enumerate(chunks):
        for yy in range(2):
            where = (pl.ds(row0, rows), pl.ds(col0, 2 * half))
            pltpu.make_async_copy(parts[p].at[(yy * 2 + c,) + where], mine.at[k, yy], sem_l.at[k]).start()
            send(parts[p].at[(yy * 2 + (1 - c),) + where], buf_a.at[k, yy], sem_a, (k,), core_peer).start()

    n_slices = sem_rl.shape[0]
    tall = own_ref.shape[0] // n_slices
    near = reach(n_ctx)

    def runs_start(t):
        rs = pl.ds(pl.multiple_of(t * tall, tall), tall)
        for zz in range(zs):
            run = zz * 2 + (1 - x)

            @pl.when(jnp.abs(run - a) <= near)
            def _():
                send(rows_ref.at[run, rs, :], rbuf_x.at[zz, rs, :], sem_rx, (t, zz), x_peer).start()

            @pl.when(jnp.abs(2 * (zz - z)) <= near)
            def _():
                pltpu.make_async_copy(rows_ref.at[zz * 2 + x, rs, :], rmine.at[zz, rs, :], sem_rl.at[t, zz]).start()

    def runs_pass(t):
        rs = pl.ds(pl.multiple_of(t * tall, tall), tall)
        for zz in range(zs):
            @pl.when(jnp.abs(2 * (zz - z)) <= near)
            def _():
                pltpu.make_async_copy(rmine.at[zz, rs, :], rmine.at[zz, rs, :], sem_rl.at[t, zz]).wait()
                rkeep[...] = rmine[zz, rs, :].astype(F32)

                @pl.when(jnp.abs(zz * 2 + x - (z * 2 + 1 - x)) <= near)
                def _():
                    wait_in(rbuf_x.at[zz, rs, :], sem_rx, (t, zz))
                    rkeep[...] += rbuf_x[zz, rs, :].astype(F32)

                @pl.when(zz == z)
                def _():
                    own_ref[rs, :] = rkeep[...]

                @pl.when(zz != z)
                def _():
                    rbuf_s[zz, rs, :] = rkeep[...].astype(BF)
                    send(rbuf_s.at[zz, rs, :], rbuf_z.at[slot(zz, z), rs, :], sem_rz, (t, slot(zz, z)),
                         (zz * 2 + x, w)).start()

    def runs_end(t):
        rs = pl.ds(pl.multiple_of(t * tall, tall), tall)
        for d in range(1, zs):
            other, _unused = z_peer(d)

            @pl.when(jnp.abs(2 * (other - z)) <= near)
            def _():
                wait_in(rbuf_z.at[d - 1, rs, :], sem_rz, (t, d - 1))
                own_ref[rs, :] += rbuf_z[d - 1, rs, :].astype(F32)

    def stage_b(k):
        pltpu.make_async_copy(mine.at[k], mine.at[k], sem_l.at[k]).wait()
        wait_in(buf_a.at[k], sem_a, (k,))
        buf_h[k] = (mine[k, 1 - y].astype(F32) + buf_a[k, 1 - y].astype(F32)).astype(BF)
        send(buf_h.at[k], buf_b.at[k], sem_b, (k,), y_peer).start()

    def column(side):
        return pl.ds(pl.multiple_of(side * half, 128), half)

    def stage_c(k):
        wait_in(buf_b.at[k], sem_b, (k,))
        def total(side):
            cols = column(side)
            return (mine[k, y, :, cols].astype(F32) + buf_a[k, y, :, cols].astype(F32)
                    + buf_b[k, :, cols].astype(F32))
        buf_s[k] = total(1 - x).astype(BF)
        send(buf_s.at[k], buf_c.at[k], sem_c, (k,), x_peer).start()
        keep[k] = total(x)

    def stage_d(k):
        wait_in(buf_c.at[k], sem_c, (k,))
        s = keep[k] + buf_c[k].astype(F32)
        keep[k] = s
        buf_u[k] = s.astype(BF)
        for d in range(1, zs):
            other, dev = z_peer(d)
            send(buf_u.at[k, pl.ds(pl.multiple_of(other * piece, 16), piece), :], buf_d.at[k, slot(other, z)],
                 sem_d, (k, ), dev).start()

    def stage_e(k):
        wait_in(buf_d.at[k], sem_d, (k,))
        my = pl.ds(pl.multiple_of(z * piece, 16), piece)
        s = keep[k, my, :]
        for d in range(zs - 1):
            s = s + buf_d[k, d].astype(F32)
        buf_f[k] = s.astype(BF)
        out_ref[k, my, column(x)] = s.astype(BF)
        for d in range(1, zs):
            other, dev = z_peer(d)
            send(buf_f.at[k], out_ref.at[k, my, column(x)], sem_e, (k,), dev).start()

    def stage_f(k):
        wait_in(buf_d.at[k], sem_e, (k,))
        send(out_ref.at[k, :, column(x)], out_ref.at[k, :, column(x)], sem_f, (k,), x_peer).start()

    def stage_g(k):
        wait_in(out_ref.at[k, :, column(1 - x)], sem_f, (k,))

    def vec_b():
        pltpu.make_async_copy(vmine, vmine, sem_v.at[0, 0]).wait()
        wait_in(vbuf_a, sem_v, (1,))
        vbuf_h[...] = (vmine[1 - y].astype(F32) + vbuf_a[1 - y].astype(F32)).astype(BF)
        send(vbuf_h, vbuf_b, sem_v, (2,), y_peer).start()

    def vec_c():
        wait_in(vbuf_b, sem_v, (2,))
        vbuf_s[...] = (vmine[y].astype(F32) + vbuf_a[y].astype(F32) + vbuf_b[...].astype(F32)).astype(BF)
        send(vbuf_s, vbuf_c, sem_v, (3,), x_peer).start()

    def vec_d():
        wait_in(vbuf_c, sem_v, (3,))
        s = (vbuf_s[...].astype(F32) + vbuf_c[...].astype(F32)).astype(BF)
        vbuf_u[...] = s
        vbuf_d[z] = s
        for d in range(1, zs):
            _unused, dev = z_peer(d)
            send(vbuf_u, vbuf_d.at[z], sem_v, (4,), dev).start()

    def vec_e():
        wait_in(vbuf_d.at[pl.ds(0, zs - 1)], sem_v, (4,))
        s = vbuf_d[0].astype(F32)
        for d in range(1, zs):
            s = s + vbuf_d[d].astype(F32)
        vec_out[...] = s

    def guarded(fn, k, n):
        @pl.when((k >= 0) & (k < n))
        def _():
            fn(k)

    vec_b()

    def step(t, carry):
        guarded(runs_start, t, n_slices)
        guarded(stage_b, t, n_chunks)
        guarded(runs_pass, t - 1, n_slices)
        guarded(stage_c, t - 2, n_chunks)
        guarded(runs_end, t - 2, n_slices)
        guarded(stage_d, t - 3, n_chunks)
        guarded(stage_e, t - 4, n_chunks)
        guarded(stage_f, t - 5, n_chunks)
        guarded(stage_g, t - 6, n_chunks)
        guarded(lambda k: vec_c(), t - 1, 1)
        guarded(lambda k: vec_d(), t - 2, 1)
        guarded(lambda k: vec_e(), t - 3, 1)
        return carry

    lax.fori_loop(0, max(n_chunks + 6, n_slices + 3, 5), step, 0)

    wait_out(vbuf_a, sem_v, (1,))
    wait_out(vbuf_h, sem_v, (2,))
    wait_out(vbuf_s, sem_v, (3,))
    wait_out(vbuf_d.at[pl.ds(0, zs - 1)], sem_v, (4,))

    def drain(k, carry):
        wait_out(buf_a.at[k], sem_a, (k,))
        wait_out(buf_b.at[k], sem_b, (k,))
        wait_out(buf_c.at[k], sem_c, (k,))
        wait_out(buf_d.at[k], sem_d, (k,))
        wait_out(buf_d.at[k], sem_e, (k,))
        wait_out(out_ref.at[k, :, column(x)], sem_f, (k,))
        return carry

    lax.fori_loop(0, n_chunks, drain, 0)

    def drain_runs(t, carry):
        rs = pl.ds(pl.multiple_of(t * tall, tall), tall)
        for zz in range(zs):
            @pl.when(jnp.abs(zz * 2 + (1 - x) - a) <= near)
            def _():
                wait_out(rbuf_x.at[zz, rs, :], sem_rx, (t, zz))

            @pl.when((zz != z) & (jnp.abs(2 * (zz - z)) <= near))
            def _():
                wait_out(rbuf_s.at[zz, rs, :], sem_rz, (t, slot(zz, z)))
        return carry

    lax.fori_loop(0, n_slices, drain_runs, 0)


def reduce_grads(parts, chunks, vec, runs):
    n_ctx, n_wsh = lax.axis_size("ctx"), lax.axis_size("wsh")
    zs = n_ctx // 2
    rows = chunks[0][1]
    chunk_list = [(p, r, col) for p, _rows, r, col in chunks]
    n = len(chunks)
    half, piece = D // 2, rows // zs
    tall = runs.shape[1]
    n_slices = 8
    vm = pltpu.VMEM
    dma = pltpu.SemaphoreType.DMA
    vrows = vec.shape[1]
    any_spec = pl.BlockSpec(memory_space=pl.ANY)
    vm_spec = pl.BlockSpec(memory_space=pltpu.VMEM)
    return pl.pallas_call(
        functools.partial(reduce_kernel, chunk_list, len(parts)),
        out_shape=(
            jax.ShapeDtypeStruct((n, rows, D), BF),
            jax.ShapeDtypeStruct((vrows, D), F32),
            jax.ShapeDtypeStruct((tall, D), F32),
        ),
        in_specs=[any_spec] * (len(parts) + 2),
        out_specs=(vm_spec,) * 3,
        scratch_shapes=[
            vm((n, 2, rows, D), BF), vm((n, 2, rows, D), BF), vm((n, rows, D), BF), vm((n, rows, D), BF),
            vm((n, rows, half), BF), vm((n, rows, half), F32), vm((n, rows, half), BF), vm((n, rows, half), BF),
            vm((n, zs - 1, piece, half), BF), vm((n, piece, half), BF),
            vm((2, vrows, D), BF), vm((2, vrows, D), BF), vm((vrows, D), BF), vm((vrows, D), BF),
            vm((vrows, D), BF), vm((vrows, D), BF), vm((vrows, D), BF), vm((zs, vrows, D), BF),
            vm((zs, tall, D), BF), vm((zs, tall, D), BF), vm((zs, tall, D), BF), vm((zs - 1, tall, D), BF),
            vm((tall // n_slices, D), F32),
            dma((n,)), dma((2, n)), dma((2, n)), dma((2, n)), dma((2, n)), dma((2, n)), dma((2, n)), dma((2, 5)),
            dma((n_slices, zs)), dma((2, n_slices, zs)), dma((2, n_slices, zs)),
        ],
        compiler_params=pltpu.CompilerParams(collective_id=2, has_side_effects=True, vmem_limit_bytes=62 * 2**20),
        name="reduce_grads",
    )(*parts, vec, runs)


def reduce_all(matrices, vectors, grad_all):
    n_ctx, n_wsh = lax.axis_size("ctx"), lax.axis_size("wsh")
    zs = max(n_ctx // 2, 1)
    own = D // n_wsh
    if n_wsh != 4 or n_ctx % 2 or own % (zs * 16) or (grad_all.shape[0] // n_ctx) % 128:

        def total(g):
            part = lax.psum_scatter(g.astype(BF), "wsh", scatter_dimension=0, tiled=True)
            return lax.psum(part, "ctx").astype(F32)

        grad_own = lax.psum_scatter(grad_all, "ctx", scatter_dimension=0, tiled=True)
        return [total(g) for g in matrices + vectors], grad_own.astype(F32)

    parts, chunks, spans = [], [], []
    for p, g in enumerate(matrices):
        tall, wide = g.shape[0] // n_wsh, g.shape[1]
        parts.append(g.astype(BF).reshape(n_wsh, tall, wide))
        spans.append((len(chunks), tall // own, wide // D))
        for r in range(tall // own):
            for col in range(wide // D):
                chunks.append((p, own, r * own, col * D))
    vec = jnp.concatenate([v.reshape(n_wsh, -1) for v in vectors], axis=1)
    width = vec.shape[1]
    tall = -(-width // (16 * D)) * 16
    vec = jnp.pad(vec, ((0, 0), (0, tall * D - width))).astype(BF).reshape(n_wsh, tall, D)
    summed, vec_sum, grad_own = reduce_grads(
        parts, chunks, vec, grad_all.reshape(n_ctx, grad_all.shape[0] // n_ctx, D)
    )
    sums = []
    for first, down, across in spans:
        block = summed[first : first + down * across]
        if across > 1:
            block = jnp.concatenate([block[i] for i in range(across)], axis=1)
        sums.append(block.reshape(down * own, across * D).astype(F32))
    flat, place = vec_sum.reshape(-1), 0
    for v in vectors:
        size = v.shape[0] // n_wsh
        sums.append(flat[place : place + size])
        place += size
    return sums, grad_own


def local(
    tokens,
    cotangent,
    doc_starts,
    query_weight,
    key_weight,
    value_weight,
    out_weight,
    up_weight,
    down_weight,
    query_bias,
    value_bias,
    out_bias,
    attn_gain,
    attn_shift,
    up_bias,
    down_bias,
    final_gain,
    final_shift,
):
    inputs = tokens[0]
    doc_start = doc_starts[0]
    tok_rows = inputs.shape[0]
    stream_rows = tok_rows * lax.axis_size("ctx")
    first_row = lax.axis_index("ctx") * tok_rows
    tile = min(tok_rows, 512)
    bounds = key_range(doc_start, first_row, tok_rows, stream_rows, tile)
    query_doc, key_doc = document_lanes(doc_start, first_row, tok_rows, stream_rows)

    def gather(x):
        return lax.all_gather(x, "wsh", axis=0, tiled=True)

    all_tokens = lax.all_gather(inputs, "ctx", axis=0, tiled=True)
    qkv_w = gather(jnp.concatenate([query_weight, key_weight, value_weight], axis=1))
    query_w, key_w, value_w = qkv_w[:, :D], qkv_w[:, D : 2 * D], qkv_w[:, 2 * D :]
    small = gather(
        jnp.stack([query_bias, value_bias, out_bias, attn_gain, attn_shift, down_bias, final_gain, final_shift], axis=1)
    ).astype(F32)
    query_b, value_b, out_b, attn_g, attn_s, down_b, final_g, final_s = [small[:, i] for i in range(8)]
    up_b = gather(up_bias).astype(F32)
    out_w = gather(out_weight)
    up_w = gather(up_weight)
    down_w = gather(down_weight)

    queries = (jnp.dot(inputs, query_w, preferred_element_type=F32) + query_b).astype(BF) * jnp.asarray(SCALE, BF)
    keys = jnp.dot(all_tokens, key_w, preferred_element_type=F32).astype(BF)
    values = (jnp.dot(all_tokens, value_w, preferred_element_type=F32) + value_b).astype(BF)
    mixed_t, log_rows = attn_fwd(bounds, queries, query_doc, keys, key_doc, values, tq=tile)
    attn_t = mixed_t.astype(BF)
    inputs_f = inputs.astype(F32)
    branch = lax.dot_general(attn_t, out_w, TN, preferred_element_type=F32) + out_b
    first_norm, first_pull = jax.vjp(layer_norm, inputs_f + branch, attn_g, attn_s)
    first_b = first_norm.astype(BF)
    up_f = jnp.dot(first_b, up_w, preferred_element_type=F32) + up_b
    act_f, act_pull = jax.vjp(gelu_act, up_f)
    act_b = act_f.astype(BF)
    down_f = jnp.dot(act_b, down_w, preferred_element_type=F32) + down_b
    final_f, final_pull = jax.vjp(layer_norm, first_norm + down_f, final_g, final_s)
    layer_out = final_f.astype(BF)

    grad_sum2, grad_final_g, grad_final_s = final_pull(cotangent[0].astype(F32))
    grad_down = grad_sum2.astype(BF)
    grad_down_w = jnp.einsum("tf,td->fd", act_b, grad_down, preferred_element_type=F32)
    grad_down_b = jnp.sum(grad_down.astype(F32), axis=0)
    grad_act = jnp.einsum("td,fd->tf", grad_down, down_w, preferred_element_type=F32)
    (grad_up_f,) = act_pull(grad_act)
    grad_up = grad_up_f.astype(BF)
    grad_up_w = jnp.einsum("td,tf->df", first_b, grad_up, preferred_element_type=F32)
    grad_up_b = jnp.sum(grad_up.astype(F32), axis=0)
    grad_first = grad_sum2 + jnp.einsum("tf,df->td", grad_up, up_w, preferred_element_type=F32)
    grad_sum1, grad_attn_g, grad_attn_s = first_pull(grad_first)
    grad_branch = grad_sum1.astype(BF)
    grad_out_w = jnp.dot(attn_t, grad_branch, preferred_element_type=F32)
    grad_out_b = jnp.sum(grad_branch.astype(F32), axis=0)
    grad_attn = jnp.einsum("te,de->td", grad_branch, out_w, preferred_element_type=F32).astype(BF)
    grad_q_t, grad_k, grad_v = attn_bwd(
        bounds, queries, query_doc, grad_attn, log_rows, mixed_t, keys, key_doc, values, tq=tile
    )
    grad_all = jnp.einsum("te,de->td", grad_k, key_w, preferred_element_type=F32)
    grad_all = grad_all + jnp.einsum("te,de->td", grad_v, value_w, preferred_element_type=F32)
    grad_query_w = jnp.einsum("td,et->de", inputs, grad_q_t, preferred_element_type=F32)
    grad_key_w = jnp.einsum("td,te->de", all_tokens, grad_k, preferred_element_type=F32)
    grad_value_w = jnp.einsum("td,te->de", all_tokens, grad_v, preferred_element_type=F32)
    grad_query_b = jnp.sum(grad_q_t.astype(F32), axis=1)
    grad_value_b = jnp.sum(grad_v.astype(F32), axis=0)
    grad_inputs = grad_sum1 + lax.dot_general(
        grad_q_t, query_w, (((0,), (1,)), ((), ())), preferred_element_type=F32
    )
    matrices = (grad_query_w, grad_key_w, grad_value_w, grad_out_w, grad_up_w, grad_down_w)
    vectors = (
        grad_query_b, grad_value_b, grad_out_b, grad_attn_g, grad_attn_s,
        grad_up_b, grad_down_b, grad_final_g, grad_final_s,
    )
    sums, grad_own = reduce_all(matrices, vectors, grad_all.astype(BF))
    grad_inputs = grad_inputs + grad_own
    return (
        layer_out.reshape(1, tok_rows, D),
        grad_inputs.astype(BF).reshape(1, tok_rows, D),
        *sums,
    )


def solution(mesh):
    rows, mat, vec = P("wsh", "ctx", None), P("wsh", None), P("wsh")
    return jax.shard_map(
        local,
        mesh=mesh,
        in_specs=(rows, rows, mat) + (mat,) * 6 + (vec,) * 9,
        out_specs=(rows, rows) + (mat,) * 6 + (vec,) * 9,
        check_vma=False,
    )
```

```python
import functools

import jax
import jax.numpy as jnp
from jax import lax
from jax.experimental import pallas as pl
from jax.experimental.pallas import tpu as pltpu
from jax.sharding import PartitionSpec as P

D = 768
HEADS = 12
HD = 64
SCALE = 0.125
EPS = 1e-12
ROOT_HALF = 0.7071067811865476
BF = jnp.bfloat16
F32 = jnp.float32
NT = (((1,), (1,)), ((), ()))
NN = (((1,), (0,)), ((), ()))
TN = (((0,), (0,)), ((), ()))


def layer_norm(values, gain_vec, shift_vec):
    average = jnp.mean(values, axis=-1, keepdims=True)
    centred = values - average
    variance = jnp.mean(centred * centred, axis=-1, keepdims=True)
    return centred * lax.rsqrt(variance + EPS) * gain_vec + shift_vec


def gelu_act(values):
    return 0.5 * values * (1.0 + lax.erf(values * ROOT_HALF))


def key_range(doc_start, first_row, rows, stream_rows, tile):
    pos = jnp.arange(rows // tile, dtype=jnp.int32) * tile + first_row
    last = pos + tile - 1
    low = jnp.max(jnp.where(doc_start[None, :] <= pos[:, None], doc_start[None, :], 0), axis=1)
    high = jnp.min(
        jnp.where(doc_start[None, :] > last[:, None], doc_start[None, :], stream_rows), axis=1
    )
    first = low // 128 * 128
    count = (high - first + 255) // 256
    first = jnp.minimum(first, stream_rows - count * 256)
    return jnp.stack([first, count], axis=1).astype(jnp.int32)


def document_lanes(doc_start, first_row, rows, stream_rows):
    far = jnp.full((128 - doc_start.shape[0],), 2**30, jnp.int32)
    starts = jnp.concatenate([doc_start, far])
    ends = jnp.concatenate([doc_start[1:], jnp.full((1,), stream_rows, jnp.int32), far])
    query_pos = first_row + jnp.arange(rows, dtype=jnp.int32)[:, None]
    key_pos = jnp.arange(stream_rows, dtype=jnp.int32)[:, None]
    query_doc = ((query_pos >= starts) & (query_pos < ends)).astype(BF)
    key_doc = jnp.where((key_pos >= starts) & (key_pos < ends), 0.0, -1e30).astype(BF)
    return query_doc, key_doc


def stack_heads(x, extra=None):
    lane = lax.broadcasted_iota(jnp.int32, x.shape, 1)
    zero = jnp.zeros_like(x)
    lo = jnp.where(lane < 64, x, zero)
    hi = jnp.where(lane < 64, zero, x)
    if extra is not None:
        lo = jnp.concatenate([lo, extra], axis=1)
        hi = jnp.concatenate([hi, extra], axis=1)
    return jnp.concatenate([lo, hi], axis=0)

def pick_heads(x, tq):
    return jnp.concatenate([x[:64, :tq], x[64:, tq:]], axis=0)

def two_level(start, count, tk, body, init):
    big = tk // 256
    whole = count // big
    def large(t, c):
        return body(pl.multiple_of(t * tk, 256), pl.multiple_of(start + t * tk, 128), tk, c)
    def small(t, c):
        return body(pl.multiple_of(t * 256, 256), pl.multiple_of(start + t * 256, 128), 256, c)
    c = lax.fori_loop(0, whole, large, init)
    return lax.fori_loop(whole * big, count, small, c)

def fwd_kernel(tk, bounds, q_ref, qaug_ref, k_ref, kaug_ref, v_ref, ot_ref, lse_ref, s_scr, acc):
    qi = pl.program_id(1)
    start, count = bounds[qi, 0], bounds[qi, 1]
    tq = q_ref.shape[0]
    rhs = stack_heads(q_ref[...], qaug_ref[...])

    def scores(loc, off, size, m):
        lhs = jnp.concatenate([k_ref[pl.ds(off, size), :], kaug_ref[pl.ds(off, size), :]], axis=1)
        s = lax.dot_general(lhs, rhs, NT, preferred_element_type=F32)
        s_scr[pl.ds(loc, size), :] = s
        return jnp.maximum(m, jnp.max(s.reshape(size // 8, 8, 2 * tq), axis=0))

    m8 = two_level(start, count, tk, scores, jnp.full((8, 2 * tq), -3e38, F32))
    m = jnp.max(m8, axis=0, keepdims=True)
    acc[...] = jnp.zeros_like(acc)

    def mix(loc, off, size, l8):
        p = jnp.exp(s_scr[pl.ds(loc, size), :] - m)
        acc[...] += lax.dot_general(v_ref[pl.ds(off, size), :], p.astype(BF), TN, preferred_element_type=F32)
        return l8 + jnp.sum(p.reshape(size // 8, 8, 2 * tq), axis=0)

    l8 = two_level(start, count, tk, mix, jnp.zeros((8, 2 * tq), F32))
    l = jnp.sum(l8, axis=0, keepdims=True)
    ot_ref[...] = pick_heads(acc[...] / l, tq)
    lse = m + jnp.log(l)
    lse_ref[0] = jnp.concatenate([lse[:, :tq], lse[:, tq:]], axis=0)

def attn_fwd(bounds, q, qaug, k, kaug, v, *, tq=512, tk=768):
    T, D = q.shape
    S = k.shape[0]
    pairs = D // 128
    return pl.pallas_call(
        functools.partial(fwd_kernel, tk),
        out_shape=(jax.ShapeDtypeStruct((D, T), F32), jax.ShapeDtypeStruct((pairs, 2, T), F32)),
        grid_spec=pltpu.PrefetchScalarGridSpec(
            num_scalar_prefetch=1, grid=(pairs, T // tq),
            in_specs=[pl.BlockSpec((tq, 128), lambda h, i, b: (i, h)),
                      pl.BlockSpec((tq, 128), lambda h, i, b: (i, 0)),
                      pl.BlockSpec((S, 128), lambda h, i, b: (0, h)),
                      pl.BlockSpec((S, 128), lambda h, i, b: (0, 0)),
                      pl.BlockSpec((S, 128), lambda h, i, b: (0, h))],
            out_specs=(pl.BlockSpec((128, tq), lambda h, i, b: (h, i)),
                       pl.BlockSpec((1, 2, tq), lambda h, i, b: (h, 0, i))),
            scratch_shapes=[pltpu.VMEM((S, 2 * tq), F32), pltpu.VMEM((128, 2 * tq), F32)]),
        name="attend",
    )(bounds, q, qaug, k, kaug, v)

def bwd_kernel(tk, bounds, q_ref, qaug_ref, do_ref, lse_ref, ot_ref, k_ref, kaug_ref, v_ref,
               dqt_ref, dk_ref, dv_ref, dk_acc, dv_acc, dq_acc):
    qi = pl.program_id(1)
    start, count = bounds[qi, 0], bounds[qi, 1]
    tq = q_ref.shape[0]

    @pl.when(qi == 0)
    def _():
        dk_acc[...] = jnp.zeros_like(dk_acc)
        dv_acc[...] = jnp.zeros_like(dv_acc)

    qs = stack_heads(q_ref[...])
    qrhs = stack_heads(q_ref[...], qaug_ref[...])
    dos = stack_heads(do_ref[...])
    lse = jnp.concatenate([lse_ref[0, 0:1, :], lse_ref[0, 1:2, :]], axis=1)
    mixed = ot_ref[...] * do_ref[...].astype(F32).T
    delta = jnp.concatenate(
        [jnp.sum(mixed[:64], axis=0, keepdims=True), jnp.sum(mixed[64:], axis=0, keepdims=True)], axis=1
    )
    dq_acc[...] = jnp.zeros_like(dq_acc)

    def step(loc, off, size, carry):
        rows = pl.ds(off, size)
        lhs = jnp.concatenate([k_ref[rows, :], kaug_ref[rows, :]], axis=1)
        x = lax.dot_general(lhs, qrhs, NT, preferred_element_type=F32)
        y = lax.dot_general(v_ref[rows, :], dos, NT, preferred_element_type=F32)
        p = jnp.exp(x - lse)
        ds = (p * (y - delta)).astype(BF)
        pb = p.astype(BF)
        dv_acc[rows, :] += lax.dot_general(pb, dos, NN, preferred_element_type=F32)
        dk_acc[rows, :] += lax.dot_general(ds, qs, NN, preferred_element_type=F32)
        dq_acc[...] += lax.dot_general(k_ref[rows, :], ds, TN, preferred_element_type=F32)
        return carry

    two_level(start, count, tk, step, 0)
    dqt_ref[...] = (pick_heads(dq_acc[...], tq) * 0.125).astype(BF)

    @pl.when(qi == pl.num_programs(1) - 1)
    def _():
        dk_ref[...] = dk_acc[...].astype(BF)
        dv_ref[...] = dv_acc[...].astype(BF)

def attn_bwd(bounds, q, qaug, do, lse, ot, k, kaug, v, *, tq=512, tk=768):
    T, D = q.shape
    S = k.shape[0]
    pairs = D // 128
    row = lambda h, i, b: (h, 0, i)
    return pl.pallas_call(
        functools.partial(bwd_kernel, tk),
        out_shape=(jax.ShapeDtypeStruct((D, T), BF), jax.ShapeDtypeStruct((S, D), BF), jax.ShapeDtypeStruct((S, D), BF)),
        grid_spec=pltpu.PrefetchScalarGridSpec(
            num_scalar_prefetch=1, grid=(pairs, T // tq),
            in_specs=[pl.BlockSpec((tq, 128), lambda h, i, b: (i, h)),
                      pl.BlockSpec((tq, 128), lambda h, i, b: (i, 0)),
                      pl.BlockSpec((tq, 128), lambda h, i, b: (i, h)),
                      pl.BlockSpec((1, 2, tq), row),
                      pl.BlockSpec((128, tq), lambda h, i, b: (h, i)),
                      pl.BlockSpec((S, 128), lambda h, i, b: (0, h)),
                      pl.BlockSpec((S, 128), lambda h, i, b: (0, 0)),
                      pl.BlockSpec((S, 128), lambda h, i, b: (0, h))],
            out_specs=(pl.BlockSpec((128, tq), lambda h, i, b: (h, i)),
                       pl.BlockSpec((S, 128), lambda h, i, b: (0, h)),
                       pl.BlockSpec((S, 128), lambda h, i, b: (0, h))),
            scratch_shapes=[pltpu.VMEM((S, 128), F32), pltpu.VMEM((S, 128), F32), pltpu.VMEM((128, 2 * tq), F32)]),
        name="attend_back",
    )(bounds, q, qaug, do, lse, ot, k, kaug, v)


def reach(n_ctx):
    return n_ctx // 2


def reduce_kernel(chunks, n_parts, *refs):
    parts = refs[:n_parts]
    vec_ref, rows_ref, out_ref, vec_out, own_ref = refs[n_parts : n_parts + 5]
    (mine, buf_a, buf_h, buf_b, buf_s, keep, buf_c, buf_u, buf_d, buf_f,
     vmine, vbuf_a, vbuf_h, vbuf_b, vbuf_s, vbuf_c, vbuf_u, vbuf_d,
     rmine, rbuf_x, rbuf_s, rbuf_z, rkeep,
     sem_l, sem_a, sem_b, sem_c, sem_d, sem_e, sem_f, sem_v, sem_rl, sem_rx, sem_rz) = refs[n_parts + 5 :]
    n_chunks = len(chunks)
    n_ctx, n_wsh = lax.axis_size("ctx"), lax.axis_size("wsh")
    zs = n_ctx // 2
    a, w = lax.axis_index("ctx"), lax.axis_index("wsh")
    z, x = a // 2, lax.rem(a, 2)
    y, c = w // 2, lax.rem(w, 2)
    core_peer = (a, y * 2 + (1 - c))
    y_peer = (a, (1 - y) * 2 + c)
    x_peer = (z * 2 + (1 - x), w)

    def z_peer(d):
        other = lax.rem(z + d, zs)
        return other, (other * 2 + x, w)

    def slot(dest, src):
        return lax.rem(src - dest + zs, zs) - 1

    rows = out_ref.shape[1]
    half = out_ref.shape[2] // 2
    piece = rows // zs
    MESH = pl.DeviceIdType.MESH
    barrier = pltpu.get_barrier_semaphore()
    for dev in [core_peer, y_peer, x_peer] + [z_peer(d)[1] for d in range(1, zs)]:
        pl.semaphore_signal(barrier, inc=1, device_id=dev, device_id_type=MESH)
    pl.semaphore_wait(barrier, zs + 2)

    def send(src, dst, sems, idx, dev):
        return pltpu.make_async_remote_copy(
            src_ref=src, dst_ref=dst, send_sem=sems.at[(0,) + idx], recv_sem=sems.at[(1,) + idx],
            device_id=dev, device_id_type=MESH)

    def wait_in(ref, sems, idx):
        send(ref, ref, sems, idx, core_peer).wait_recv()

    def wait_out(ref, sems, idx):
        send(ref, ref, sems, idx, core_peer).wait_send()

    for yy in range(2):
        pltpu.make_async_copy(vec_ref.at[yy * 2 + c], vmine.at[yy], sem_v.at[0, 0]).start()
        send(vec_ref.at[yy * 2 + (1 - c)], vbuf_a.at[yy], sem_v, (1,), core_peer).start()
    for k, (p, row0, col0) in enumerate(chunks):
        for yy in range(2):
            where = (pl.ds(row0, rows), pl.ds(col0, 2 * half))
            pltpu.make_async_copy(parts[p].at[(yy * 2 + c,) + where], mine.at[k, yy], sem_l.at[k]).start()
            send(parts[p].at[(yy * 2 + (1 - c),) + where], buf_a.at[k, yy], sem_a, (k,), core_peer).start()

    n_slices = sem_rl.shape[0]
    tall = own_ref.shape[0] // n_slices
    near = reach(n_ctx)

    def runs_start(t):
        rs = pl.ds(pl.multiple_of(t * tall, tall), tall)
        for zz in range(zs):
            run = zz * 2 + (1 - x)

            @pl.when(jnp.abs(run - a) <= near)
            def _():
                send(rows_ref.at[run, rs, :], rbuf_x.at[zz, rs, :], sem_rx, (t, zz), x_peer).start()

            @pl.when(jnp.abs(2 * (zz - z)) <= near)
            def _():
                pltpu.make_async_copy(rows_ref.at[zz * 2 + x, rs, :], rmine.at[zz, rs, :], sem_rl.at[t, zz]).start()

    def runs_pass(t):
        rs = pl.ds(pl.multiple_of(t * tall, tall), tall)
        for zz in range(zs):
            @pl.when(jnp.abs(2 * (zz - z)) <= near)
            def _():
                pltpu.make_async_copy(rmine.at[zz, rs, :], rmine.at[zz, rs, :], sem_rl.at[t, zz]).wait()
                rkeep[...] = rmine[zz, rs, :].astype(F32)

                @pl.when(jnp.abs(zz * 2 + x - (z * 2 + 1 - x)) <= near)
                def _():
                    wait_in(rbuf_x.at[zz, rs, :], sem_rx, (t, zz))
                    rkeep[...] += rbuf_x[zz, rs, :].astype(F32)

                @pl.when(zz == z)
                def _():
                    own_ref[rs, :] = rkeep[...]

                @pl.when(zz != z)
                def _():
                    rbuf_s[zz, rs, :] = rkeep[...].astype(BF)
                    send(rbuf_s.at[zz, rs, :], rbuf_z.at[slot(zz, z), rs, :], sem_rz, (t, slot(zz, z)),
                         (zz * 2 + x, w)).start()

    def runs_end(t):
        rs = pl.ds(pl.multiple_of(t * tall, tall), tall)
        for d in range(1, zs):
            other, _unused = z_peer(d)

            @pl.when(jnp.abs(2 * (other - z)) <= near)
            def _():
                wait_in(rbuf_z.at[d - 1, rs, :], sem_rz, (t, d - 1))
                own_ref[rs, :] += rbuf_z[d - 1, rs, :].astype(F32)

    def stage_b(k):
        pltpu.make_async_copy(mine.at[k], mine.at[k], sem_l.at[k]).wait()
        wait_in(buf_a.at[k], sem_a, (k,))
        buf_h[k] = (mine[k, 1 - y].astype(F32) + buf_a[k, 1 - y].astype(F32)).astype(BF)
        send(buf_h.at[k], buf_b.at[k], sem_b, (k,), y_peer).start()

    def column(side):
        return pl.ds(pl.multiple_of(side * half, 128), half)

    def stage_c(k):
        wait_in(buf_b.at[k], sem_b, (k,))
        def total(side):
            cols = column(side)
            return (mine[k, y, :, cols].astype(F32) + buf_a[k, y, :, cols].astype(F32)
                    + buf_b[k, :, cols].astype(F32))
        buf_s[k] = total(1 - x).astype(BF)
        send(buf_s.at[k], buf_c.at[k], sem_c, (k,), x_peer).start()
        keep[k] = total(x)

    def stage_d(k):
        wait_in(buf_c.at[k], sem_c, (k,))
        s = keep[k] + buf_c[k].astype(F32)
        keep[k] = s
        buf_u[k] = s.astype(BF)
        for d in range(1, zs):
            other, dev = z_peer(d)
            send(buf_u.at[k, pl.ds(pl.multiple_of(other * piece, 16), piece), :], buf_d.at[k, slot(other, z)],
                 sem_d, (k, ), dev).start()

    def stage_e(k):
        wait_in(buf_d.at[k], sem_d, (k,))
        my = pl.ds(pl.multiple_of(z * piece, 16), piece)
        s = keep[k, my, :]
        for d in range(zs - 1):
            s = s + buf_d[k, d].astype(F32)
        buf_f[k] = s.astype(BF)
        out_ref[k, my, column(x)] = s.astype(BF)
        for d in range(1, zs):
            other, dev = z_peer(d)
            send(buf_f.at[k], out_ref.at[k, my, column(x)], sem_e, (k,), dev).start()

    def stage_f(k):
        wait_in(buf_d.at[k], sem_e, (k,))
        send(out_ref.at[k, :, column(x)], out_ref.at[k, :, column(x)], sem_f, (k,), x_peer).start()

    def stage_g(k):
        wait_in(out_ref.at[k, :, column(1 - x)], sem_f, (k,))

    def vec_b():
        pltpu.make_async_copy(vmine, vmine, sem_v.at[0, 0]).wait()
        wait_in(vbuf_a, sem_v, (1,))
        vbuf_h[...] = (vmine[1 - y].astype(F32) + vbuf_a[1 - y].astype(F32)).astype(BF)
        send(vbuf_h, vbuf_b, sem_v, (2,), y_peer).start()

    def vec_c():
        wait_in(vbuf_b, sem_v, (2,))
        vbuf_s[...] = (vmine[y].astype(F32) + vbuf_a[y].astype(F32) + vbuf_b[...].astype(F32)).astype(BF)
        send(vbuf_s, vbuf_c, sem_v, (3,), x_peer).start()

    def vec_d():
        wait_in(vbuf_c, sem_v, (3,))
        s = (vbuf_s[...].astype(F32) + vbuf_c[...].astype(F32)).astype(BF)
        vbuf_u[...] = s
        vbuf_d[z] = s
        for d in range(1, zs):
            _unused, dev = z_peer(d)
            send(vbuf_u, vbuf_d.at[z], sem_v, (4,), dev).start()

    def vec_e():
        wait_in(vbuf_d.at[pl.ds(0, zs - 1)], sem_v, (4,))
        s = vbuf_d[0].astype(F32)
        for d in range(1, zs):
            s = s + vbuf_d[d].astype(F32)
        vec_out[...] = s

    def guarded(fn, k, n):
        @pl.when((k >= 0) & (k < n))
        def _():
            fn(k)

    vec_b()

    def step(t, carry):
        guarded(runs_start, t, n_slices)
        guarded(stage_b, t, n_chunks)
        guarded(runs_pass, t - 1, n_slices)
        guarded(stage_c, t - 2, n_chunks)
        guarded(runs_end, t - 2, n_slices)
        guarded(stage_d, t - 3, n_chunks)
        guarded(stage_e, t - 4, n_chunks)
        guarded(stage_f, t - 5, n_chunks)
        guarded(stage_g, t - 6, n_chunks)
        guarded(lambda k: vec_c(), t - 1, 1)
        guarded(lambda k: vec_d(), t - 2, 1)
        guarded(lambda k: vec_e(), t - 3, 1)
        return carry

    lax.fori_loop(0, max(n_chunks + 6, n_slices + 3, 5), step, 0)

    wait_out(vbuf_a, sem_v, (1,))
    wait_out(vbuf_h, sem_v, (2,))
    wait_out(vbuf_s, sem_v, (3,))
    wait_out(vbuf_d.at[pl.ds(0, zs - 1)], sem_v, (4,))

    def drain(k, carry):
        wait_out(buf_a.at[k], sem_a, (k,))
        wait_out(buf_b.at[k], sem_b, (k,))
        wait_out(buf_c.at[k], sem_c, (k,))
        wait_out(buf_d.at[k], sem_d, (k,))
        wait_out(buf_d.at[k], sem_e, (k,))
        wait_out(out_ref.at[k, :, column(x)], sem_f, (k,))
        return carry

    lax.fori_loop(0, n_chunks, drain, 0)

    def drain_runs(t, carry):
        rs = pl.ds(pl.multiple_of(t * tall, tall), tall)
        for zz in range(zs):
            @pl.when(jnp.abs(zz * 2 + (1 - x) - a) <= near)
            def _():
                wait_out(rbuf_x.at[zz, rs, :], sem_rx, (t, zz))

            @pl.when((zz != z) & (jnp.abs(2 * (zz - z)) <= near))
            def _():
                wait_out(rbuf_s.at[zz, rs, :], sem_rz, (t, slot(zz, z)))
        return carry

    lax.fori_loop(0, n_slices, drain_runs, 0)


def reduce_grads(parts, chunks, vec, runs):
    n_ctx, n_wsh = lax.axis_size("ctx"), lax.axis_size("wsh")
    zs = n_ctx // 2
    rows = chunks[0][1]
    chunk_list = [(p, r, col) for p, _rows, r, col in chunks]
    n = len(chunks)
    half, piece = D // 2, rows // zs
    tall = runs.shape[1]
    n_slices = 8
    vm = pltpu.VMEM
    dma = pltpu.SemaphoreType.DMA
    vrows = vec.shape[1]
    any_spec = pl.BlockSpec(memory_space=pl.ANY)
    vm_spec = pl.BlockSpec(memory_space=pltpu.VMEM)
    return pl.pallas_call(
        functools.partial(reduce_kernel, chunk_list, len(parts)),
        out_shape=(
            jax.ShapeDtypeStruct((n, rows, D), BF),
            jax.ShapeDtypeStruct((vrows, D), F32),
            jax.ShapeDtypeStruct((tall, D), F32),
        ),
        in_specs=[any_spec] * (len(parts) + 2),
        out_specs=(vm_spec,) * 3,
        scratch_shapes=[
            vm((n, 2, rows, D), BF), vm((n, 2, rows, D), BF), vm((n, rows, D), BF), vm((n, rows, D), BF),
            vm((n, rows, half), BF), vm((n, rows, half), F32), vm((n, rows, half), BF), vm((n, rows, half), BF),
            vm((n, zs - 1, piece, half), BF), vm((n, piece, half), BF),
            vm((2, vrows, D), BF), vm((2, vrows, D), BF), vm((vrows, D), BF), vm((vrows, D), BF),
            vm((vrows, D), BF), vm((vrows, D), BF), vm((vrows, D), BF), vm((zs, vrows, D), BF),
            vm((zs, tall, D), BF), vm((zs, tall, D), BF), vm((zs, tall, D), BF), vm((zs - 1, tall, D), BF),
            vm((tall // n_slices, D), F32),
            dma((n,)), dma((2, n)), dma((2, n)), dma((2, n)), dma((2, n)), dma((2, n)), dma((2, n)), dma((2, 5)),
            dma((n_slices, zs)), dma((2, n_slices, zs)), dma((2, n_slices, zs)),
        ],
        compiler_params=pltpu.CompilerParams(collective_id=2, has_side_effects=True, vmem_limit_bytes=62 * 2**20),
        name="reduce_grads",
    )(*parts, vec, runs)


def gather_kernel(cut, tok_ref, vec_ref, wk_ref, wv_ref, wq_ref,
                  tok_out, k_out, v_out, q_out, w_out, vec_out,
                  tok, kbuf, vbuf, qbuf, wbuf, vecs,
                  sem_in, sem_out, sem_w, sem_l, sem_o):
    n_ctx = lax.axis_size("ctx")
    zs = n_ctx // 2
    a, w = lax.axis_index("ctx"), lax.axis_index("wsh")
    z, x = a // 2, lax.rem(a, 2)
    y, c = w // 2, lax.rem(w, 2)
    core_peer = (a, y * 2 + (1 - c))
    y_peer = (a, (1 - y) * 2 + c)
    x_peer = (z * 2 + (1 - x), w)
    up, down = (a + 2, w), (a - 2, w)
    near = reach(n_ctx)
    MESH = pl.DeviceIdType.MESH
    n_slices = sem_in.shape[1]
    tall = tok.shape[1] // n_slices
    own = wk_ref.shape[0]
    far = 4 * (near // 2 + 1)

    barrier = pltpu.get_barrier_semaphore()
    around = [(lax.rem(z + d, zs) * 2 + x, w) for d in (1, zs - 1)]
    for dev in [core_peer, y_peer, x_peer] + around:
        pl.semaphore_signal(barrier, inc=1, device_id=dev, device_id_type=MESH)
    pl.semaphore_wait(barrier, 5)

    def relative(u):
        dz = (u // 4) * (1 - 2 * lax.rem(u, 2))
        other = lax.rem(u // 2, 2)
        run = 2 * (z + dz) + (x + other - 2 * x * other)
        there = (z + dz >= 0) & (z + dz < zs) & (jnp.abs(run - a) <= near) & ((u >= 4) | (lax.rem(u, 2) == 0))
        return run, dz, other, there

    def rows(s):
        return pl.ds(pl.multiple_of(s * tall, tall), tall)

    def remote(src, dst, send_sem, recv_sem, dev):
        return pltpu.make_async_remote_copy(
            src_ref=src, dst_ref=dst, send_sem=send_sem, recv_sem=recv_sem, device_id=dev, device_id_type=MESH)

    def routes(u, s):
        run, dz, other, there = relative(u)
        z_first = s < cut
        to_x = there & (z_first | (dz == 0)) & (other == 0) & (jnp.abs(run - x_peer[0]) <= near)
        along = there & ((other == 0) | jnp.logical_not(z_first))
        to_up = along & (dz <= 0) & (z + 1 < zs) & (jnp.abs(run - (a + 2)) <= near)
        to_down = along & (dz >= 0) & (z > 0) & (jnp.abs(run - (a - 2)) <= near)
        return run, ((0, x_peer, to_x), (1, up, to_up), (2, down, to_down))

    def pass_on(u, s):
        run, where = routes(u, s)
        for d, dev, ok in where:
            @pl.when(ok)
            def _():
                source = tok_ref if isinstance(u, int) and u == 0 else tok.at[run]
                remote(source.at[rows(s), :], tok.at[run, rows(s), :], sem_out.at[d, u, s], sem_in.at[run, s], dev).start()

    def await_slice(u, s):
        run, _dz, _other, there = relative(u)

        @pl.when(there)
        def _():
            remote(tok.at[run, rows(s), :], tok.at[run, rows(s), :], sem_out.at[0, 0, 0], sem_in.at[run, s], x_peer).wait_recv()

    def start_own(s, carry):
        pass_on(0, s)
        return carry

    def weight_rows(owner):
        return pl.ds(pl.multiple_of(owner * own, 16), own)

    vec_own = vecs.at[w]
    remote(vec_ref, vec_own, sem_w.at[0, 0, 3], sem_w.at[1, 0, 3], core_peer).start()
    remote(vec_ref, vec_own, sem_w.at[0, 1, 3], sem_w.at[1, 1, 3], y_peer).start()
    pltpu.make_async_copy(vec_ref, vec_own, sem_l.at[3]).start()
    for m, ref in enumerate((wk_ref, wv_ref, wq_ref)):
        there = wbuf.at[m, weight_rows(w), :]
        remote(ref, there, sem_w.at[0, 1, m], sem_w.at[1, 1, m], y_peer).start()
        remote(ref, there, sem_w.at[0, 0, m], sem_w.at[1, 0, m], core_peer).start()
        pltpu.make_async_copy(ref, there, sem_l.at[m]).start()
    lax.fori_loop(0, n_slices, start_own, 0)
    pltpu.make_async_copy(tok_ref, tok.at[a], sem_l.at[4]).start()

    for j in range(n_ctx):
        @pl.when(jnp.abs(j - a) > near)
        def _():
            tok[j] = jnp.zeros_like(tok[j])

    def shard(m, owner):
        return vecs.at[owner] if m == 3 else wbuf.at[m, weight_rows(owner), :]

    def weight_arrival(m, kind):
        part = shard(m, w)
        return remote(part, part, sem_w.at[0, kind, m], sem_w.at[1, kind, m], core_peer)

    across = (1 - y) * 2 + c

    def weight_forward(m):
        weight_arrival(m, 1).wait_recv()
        remote(shard(m, across), shard(m, across), sem_w.at[0, 2, m], sem_w.at[1, 2, m], core_peer).start()

    def weight_end(m):
        weight_arrival(m, 0).wait_recv()
        weight_arrival(m, 2).wait_recv()
        pltpu.make_async_copy(shard(m, w), shard(m, w), sem_l.at[m]).wait()

    weight_forward(3)
    weight_forward(0)
    weight_forward(1)
    weight_end(3)
    total = vecs[0].astype(F32)
    for owner in range(1, 4):
        total = total + vecs[owner].astype(F32)
    vec_out[...] = total
    pltpu.make_async_copy(tok_ref, tok.at[a], sem_l.at[4]).wait()
    weight_end(0)
    weight_end(1)

    def relay(first, last):
        def one(i, carry):
            s = i // (last - first)
            u = first + lax.rem(i, last - first)
            await_slice(u, s)
            pass_on(u, s)
            return carry

        lax.fori_loop(0, n_slices * (last - first), one, 0)

    step_rows = 128
    steps = tok.shape[1] // step_rows

    def project(u, carry):
        run, _dz, _other, there = relative(u)

        @pl.when(u == 1)
        def _():
            relay(2, 6)

        @pl.when(u == 6)
        def _():
            weight_forward(2)
            weight_end(2)
            relay(6, 10)

        @pl.when(there)
        def _():
            @pl.when(u >= 10)
            def _():
                def one(s, carry):
                    await_slice(u, s)
                    return carry

                lax.fori_loop(0, n_slices, one, 0)

            def part(i, carry):
                r = pl.ds(pl.multiple_of(i * step_rows, step_rows), step_rows)
                t = tok[run, r, :]
                kbuf[run, r, :] = jnp.dot(t, wbuf[0], preferred_element_type=F32).astype(BF)
                vbuf[run, r, :] = (jnp.dot(t, wbuf[1], preferred_element_type=F32) + vec_out[1:2, :]).astype(BF)
                return carry

            lax.fori_loop(0, steps, part, 0)
            for i, (src, dst) in enumerate(((kbuf, k_out), (vbuf, v_out), (tok, tok_out))):
                pltpu.make_async_copy(src.at[run], dst.at[run], sem_o.at[i, run]).start()

        return carry

    for j in range(n_ctx):
        @pl.when(jnp.abs(j - a) > near)
        def _():
            kbuf[j] = jnp.zeros_like(kbuf[j])
            vbuf[j] = jnp.zeros_like(vbuf[j])
            for i, (src, dst) in enumerate(((kbuf, k_out), (vbuf, v_out), (tok, tok_out))):
                pltpu.make_async_copy(src.at[j], dst.at[j], sem_o.at[i, j]).start()

    lax.fori_loop(0, far, project, 0)

    def query_part(i, carry):
        r = pl.ds(pl.multiple_of(i * step_rows, step_rows), step_rows)
        q = (jnp.dot(tok[a, r, :], wbuf[2], preferred_element_type=F32) + vec_out[0:1, :]).astype(BF)
        qbuf[r, :] = q * jnp.asarray(SCALE, BF)
        return carry

    lax.fori_loop(0, steps, query_part, 0)
    pltpu.make_async_copy(qbuf, q_out, sem_l.at[5]).start()
    pltpu.make_async_copy(wbuf, w_out, sem_l.at[6]).start()

    for m in range(4):
        for kind in range(3):
            weight_arrival(m, kind).wait_send()

    def drain(i, carry):
        s = i // far
        u = lax.rem(i, far)
        run, where = routes(u, s)
        for d, dev, ok in where:
            @pl.when(ok & (u < 10))
            def _():
                remote(tok.at[run, rows(s), :], tok.at[run, rows(s), :], sem_out.at[d, u, s], sem_in.at[run, s], dev).wait_send()
        return carry

    lax.fori_loop(0, n_slices * far, drain, 0)
    for j in range(n_ctx):
        for i, (src, dst) in enumerate(((kbuf, k_out), (vbuf, v_out), (tok, tok_out))):
            pltpu.make_async_copy(src.at[j], dst.at[j], sem_o.at[i, j]).wait()
    pltpu.make_async_copy(qbuf, q_out, sem_l.at[5]).wait()
    pltpu.make_async_copy(wbuf, w_out, sem_l.at[6]).wait()


def gather_project(inputs, vec, key_weight, value_weight, query_weight):
    n_ctx, n_wsh = lax.axis_size("ctx"), lax.axis_size("wsh")
    tall = inputs.shape[0]
    n_slices = 8
    far = 4 * (reach(n_ctx) // 2 + 1)
    vm, dma = pltpu.VMEM, pltpu.SemaphoreType.DMA
    any_spec = pl.BlockSpec(memory_space=pl.ANY)
    vm_spec = pl.BlockSpec(memory_space=pltpu.VMEM)
    runs = (n_ctx, tall, D)
    shape = jax.ShapeDtypeStruct
    return pl.pallas_call(
        functools.partial(gather_kernel, 5),
        out_shape=(shape(runs, BF), shape(runs, BF), shape(runs, BF), shape((tall, D), BF), shape((3, D, D), BF),
                   shape(vec.shape, F32)),
        in_specs=[any_spec] * 5,
        out_specs=(any_spec,) * 5 + (vm_spec,),
        scratch_shapes=[
            vm(runs, BF), vm(runs, BF), vm(runs, BF), vm((tall, D), BF), vm((3, D, D), BF), vm((n_wsh,) + vec.shape, BF),
            dma((n_ctx, n_slices)), dma((3, far, n_slices)), dma((2, 3, 4)), dma((7,)), dma((3, n_ctx)),
        ],
        compiler_params=pltpu.CompilerParams(collective_id=1, has_side_effects=True, vmem_limit_bytes=48 * 2**20),
        name="gather_project",
    )(inputs, vec, key_weight, value_weight, query_weight)


def reduce_all(matrices, vectors, grad_all):
    n_ctx, n_wsh = lax.axis_size("ctx"), lax.axis_size("wsh")
    zs = max(n_ctx // 2, 1)
    own = D // n_wsh
    if n_wsh != 4 or n_ctx % 2 or own % (zs * 16) or (grad_all.shape[0] // n_ctx) % 128:

        def total(g):
            part = lax.psum_scatter(g.astype(BF), "wsh", scatter_dimension=0, tiled=True)
            return lax.psum(part, "ctx").astype(F32)

        grad_own = lax.psum_scatter(grad_all, "ctx", scatter_dimension=0, tiled=True)
        return [total(g) for g in matrices + vectors], grad_own.astype(F32)

    parts, chunks, spans = [], [], []
    for p, g in enumerate(matrices):
        tall, wide = g.shape[0] // n_wsh, g.shape[1]
        parts.append(g.astype(BF).reshape(n_wsh, tall, wide))
        spans.append((len(chunks), tall // own, wide // D))
        for r in range(tall // own):
            for col in range(wide // D):
                chunks.append((p, own, r * own, col * D))
    vec = jnp.concatenate([v.reshape(n_wsh, -1) for v in vectors], axis=1)
    width = vec.shape[1]
    tall = -(-width // (16 * D)) * 16
    vec = jnp.pad(vec, ((0, 0), (0, tall * D - width))).astype(BF).reshape(n_wsh, tall, D)
    summed, vec_sum, grad_own = reduce_grads(
        parts, chunks, vec, grad_all.reshape(n_ctx, grad_all.shape[0] // n_ctx, D)
    )
    sums = []
    for first, down, across in spans:
        block = summed[first : first + down * across]
        if across > 1:
            block = jnp.concatenate([block[i] for i in range(across)], axis=1)
        sums.append(block.reshape(down * own, across * D).astype(F32))
    flat, place = vec_sum.reshape(-1), 0
    for v in vectors:
        size = v.shape[0] // n_wsh
        sums.append(flat[place : place + size])
        place += size
    return sums, grad_own


def local(
    tokens,
    cotangent,
    doc_starts,
    query_weight,
    key_weight,
    value_weight,
    out_weight,
    up_weight,
    down_weight,
    query_bias,
    value_bias,
    out_bias,
    attn_gain,
    attn_shift,
    up_bias,
    down_bias,
    final_gain,
    final_shift,
):
    inputs = tokens[0]
    doc_start = doc_starts[0]
    tok_rows = inputs.shape[0]
    stream_rows = tok_rows * lax.axis_size("ctx")
    first_row = lax.axis_index("ctx") * tok_rows
    tile = min(tok_rows, 512)
    bounds = key_range(doc_start, first_row, tok_rows, stream_rows, tile)
    query_doc, key_doc = document_lanes(doc_start, first_row, tok_rows, stream_rows)

    n_ctx, n_wsh = lax.axis_size("ctx"), lax.axis_size("wsh")
    own = D // n_wsh

    def gather(x):
        return lax.all_gather(x, "wsh", axis=0, tiled=True)

    small = jnp.stack(
        [query_bias, value_bias, out_bias, attn_gain, attn_shift, down_bias, final_gain, final_shift]
    )
    if n_wsh == 4 and n_ctx % 4 == 0 and own % 16 == 0 and tok_rows % 512 == 0:
        w = lax.axis_index("wsh")
        at = lax.broadcasted_iota(jnp.int32, (8, D), 1) // own == w
        vec = jnp.where(at, jnp.tile(small, (1, n_wsh)), jnp.zeros((), BF))
        at = lax.broadcasted_iota(jnp.int32, (8, D), 0) == w
        vec = jnp.concatenate([vec, jnp.where(at, up_bias[None, :], jnp.zeros((), BF))], axis=0)
        all_tokens, keys, values, queries, kvq_w, vec = gather_project(
            inputs, vec, key_weight, value_weight, query_weight
        )
        all_tokens, keys, values = [r.reshape(stream_rows, D) for r in (all_tokens, keys, values)]
        key_w, value_w, query_w = kvq_w[0], kvq_w[1], kvq_w[2]
        query_b, value_b, out_b, attn_g, attn_s, down_b, final_g, final_s = [vec[i] for i in range(8)]
        up_b = vec[8 : 8 + n_wsh].reshape(-1)
    else:
        all_tokens = lax.all_gather(inputs, "ctx", axis=0, tiled=True)
        query_w, key_w, value_w = gather(query_weight), gather(key_weight), gather(value_weight)
        small = gather(small.T).astype(F32)
        query_b, value_b, out_b, attn_g, attn_s, down_b, final_g, final_s = [small[:, i] for i in range(8)]
        up_b = gather(up_bias).astype(F32)
        queries = jnp.dot(inputs, query_w, preferred_element_type=F32) + query_b
        queries = queries.astype(BF) * jnp.asarray(SCALE, BF)
        keys = jnp.dot(all_tokens, key_w, preferred_element_type=F32).astype(BF)
        values = (jnp.dot(all_tokens, value_w, preferred_element_type=F32) + value_b).astype(BF)
    out_w = gather(out_weight)
    up_w = gather(up_weight)
    down_w = gather(down_weight)

    mixed_t, log_rows = attn_fwd(bounds, queries, query_doc, keys, key_doc, values, tq=tile)
    attn_t = mixed_t.astype(BF)
    inputs_f = inputs.astype(F32)
    branch = lax.dot_general(attn_t, out_w, TN, preferred_element_type=F32) + out_b
    first_norm, first_pull = jax.vjp(layer_norm, inputs_f + branch, attn_g, attn_s)
    first_b = first_norm.astype(BF)
    up_f = jnp.dot(first_b, up_w, preferred_element_type=F32) + up_b
    act_f, act_pull = jax.vjp(gelu_act, up_f)
    act_b = act_f.astype(BF)
    down_f = jnp.dot(act_b, down_w, preferred_element_type=F32) + down_b
    final_f, final_pull = jax.vjp(layer_norm, first_norm + down_f, final_g, final_s)
    layer_out = final_f.astype(BF)

    grad_sum2, grad_final_g, grad_final_s = final_pull(cotangent[0].astype(F32))
    grad_down = grad_sum2.astype(BF)
    grad_down_w = jnp.einsum("tf,td->fd", act_b, grad_down, preferred_element_type=F32)
    grad_down_b = jnp.sum(grad_down.astype(F32), axis=0)
    grad_act = jnp.einsum("td,fd->tf", grad_down, down_w, preferred_element_type=F32)
    (grad_up_f,) = act_pull(grad_act)
    grad_up = grad_up_f.astype(BF)
    grad_up_w = jnp.einsum("td,tf->df", first_b, grad_up, preferred_element_type=F32)
    grad_up_b = jnp.sum(grad_up.astype(F32), axis=0)
    grad_first = grad_sum2 + jnp.einsum("tf,df->td", grad_up, up_w, preferred_element_type=F32)
    grad_sum1, grad_attn_g, grad_attn_s = first_pull(grad_first)
    grad_branch = grad_sum1.astype(BF)
    grad_out_w = jnp.dot(attn_t, grad_branch, preferred_element_type=F32)
    grad_out_b = jnp.sum(grad_branch.astype(F32), axis=0)
    grad_attn = jnp.einsum("te,de->td", grad_branch, out_w, preferred_element_type=F32).astype(BF)
    grad_q_t, grad_k, grad_v = attn_bwd(
        bounds, queries, query_doc, grad_attn, log_rows, mixed_t, keys, key_doc, values, tq=tile
    )
    grad_all = jnp.einsum("te,de->td", grad_k, key_w, preferred_element_type=F32)
    grad_all = grad_all + jnp.einsum("te,de->td", grad_v, value_w, preferred_element_type=F32)
    grad_query_w = jnp.einsum("td,et->de", inputs, grad_q_t, preferred_element_type=F32)
    grad_key_w = jnp.einsum("td,te->de", all_tokens, grad_k, preferred_element_type=F32)
    grad_value_w = jnp.einsum("td,te->de", all_tokens, grad_v, preferred_element_type=F32)
    grad_query_b = jnp.sum(grad_q_t.astype(F32), axis=1)
    grad_value_b = jnp.sum(grad_v.astype(F32), axis=0)
    grad_inputs = grad_sum1 + lax.dot_general(
        grad_q_t, query_w, (((0,), (1,)), ((), ())), preferred_element_type=F32
    )
    matrices = (grad_query_w, grad_key_w, grad_value_w, grad_out_w, grad_up_w, grad_down_w)
    vectors = (
        grad_query_b, grad_value_b, grad_out_b, grad_attn_g, grad_attn_s,
        grad_up_b, grad_down_b, grad_final_g, grad_final_s,
    )
    sums, grad_own = reduce_all(matrices, vectors, grad_all.astype(BF))
    grad_inputs = grad_inputs + grad_own
    return (
        layer_out.reshape(1, tok_rows, D),
        grad_inputs.astype(BF).reshape(1, tok_rows, D),
        *sums,
    )


def solution(mesh):
    rows, mat, vec = P("wsh", "ctx", None), P("wsh", None), P("wsh")
    return jax.shard_map(
        local,
        mesh=mesh,
        in_specs=(rows, rows, mat) + (mat,) * 6 + (vec,) * 9,
        out_specs=(rows, rows) + (mat,) * 6 + (vec,) * 9,
        check_vma=False,
    )
```

```python
import functools

import jax
import jax.numpy as jnp
from jax import lax
from jax.experimental import pallas as pl
from jax.experimental.pallas import tpu as pltpu
from jax.sharding import PartitionSpec as P

D = 768
HEADS = 12
HD = 64
SCALE = 0.125
EPS = 1e-12
ROOT_HALF = 0.7071067811865476
BF = jnp.bfloat16
F32 = jnp.float32
NT = (((1,), (1,)), ((), ()))
NN = (((1,), (0,)), ((), ()))
TN = (((0,), (0,)), ((), ()))


def layer_norm(values, gain_vec, shift_vec):
    average = jnp.mean(values, axis=-1, keepdims=True)
    centred = values - average
    variance = jnp.mean(centred * centred, axis=-1, keepdims=True)
    return centred * lax.rsqrt(variance + EPS) * gain_vec + shift_vec


def gelu_act(values):
    return 0.5 * values * (1.0 + lax.erf(values * ROOT_HALF))


def key_range(doc_start, first_row, rows, stream_rows, tile):
    pos = jnp.arange(rows // tile, dtype=jnp.int32) * tile + first_row
    last = pos + tile - 1
    low = jnp.max(jnp.where(doc_start[None, :] <= pos[:, None], doc_start[None, :], 0), axis=1)
    high = jnp.min(
        jnp.where(doc_start[None, :] > last[:, None], doc_start[None, :], stream_rows), axis=1
    )
    first = low // 128 * 128
    count = (high - first + 255) // 256
    first = jnp.minimum(first, stream_rows - count * 256)
    return jnp.stack([first, count], axis=1).astype(jnp.int32)


def document_lanes(doc_start, first_row, rows, stream_rows):
    far = jnp.full((128 - doc_start.shape[0],), 2**30, jnp.int32)
    starts = jnp.concatenate([doc_start, far])
    ends = jnp.concatenate([doc_start[1:], jnp.full((1,), stream_rows, jnp.int32), far])
    query_pos = first_row + jnp.arange(rows, dtype=jnp.int32)[:, None]
    key_pos = jnp.arange(stream_rows, dtype=jnp.int32)[:, None]
    query_doc = ((query_pos >= starts) & (query_pos < ends)).astype(BF)
    key_doc = jnp.where((key_pos >= starts) & (key_pos < ends), 0.0, -1e30).astype(BF)
    return query_doc, key_doc


def stack_heads(x, extra=None):
    lane = lax.broadcasted_iota(jnp.int32, x.shape, 1)
    zero = jnp.zeros_like(x)
    lo = jnp.where(lane < 64, x, zero)
    hi = jnp.where(lane < 64, zero, x)
    if extra is not None:
        lo = jnp.concatenate([lo, extra], axis=1)
        hi = jnp.concatenate([hi, extra], axis=1)
    return jnp.concatenate([lo, hi], axis=0)

def pick_heads(x, tq):
    return jnp.concatenate([x[:64, :tq], x[64:, tq:]], axis=0)

def two_level(start, count, tk, body, init):
    big = tk // 256
    whole = count // big
    def large(t, c):
        return body(pl.multiple_of(t * tk, 256), pl.multiple_of(start + t * tk, 128), tk, c)
    def small(t, c):
        return body(pl.multiple_of(t * 256, 256), pl.multiple_of(start + t * 256, 128), 256, c)
    c = lax.fori_loop(0, whole, large, init)
    return lax.fori_loop(whole * big, count, small, c)

def fwd_kernel(tk, bounds, q_ref, qaug_ref, k_ref, kaug_ref, v_ref, ot_ref, lse_ref, s_scr, acc):
    qi = pl.program_id(1)
    start, count = bounds[qi, 0], bounds[qi, 1]
    tq = q_ref.shape[0]
    rhs = stack_heads(q_ref[...], qaug_ref[...])

    def scores(loc, off, size, m):
        lhs = jnp.concatenate([k_ref[pl.ds(off, size), :], kaug_ref[pl.ds(off, size), :]], axis=1)
        s = lax.dot_general(lhs, rhs, NT, preferred_element_type=F32)
        s_scr[pl.ds(loc, size), :] = s
        return jnp.maximum(m, jnp.max(s.reshape(size // 8, 8, 2 * tq), axis=0))

    m8 = two_level(start, count, tk, scores, jnp.full((8, 2 * tq), -3e38, F32))
    m = jnp.max(m8, axis=0, keepdims=True)
    acc[...] = jnp.zeros_like(acc)

    def mix(loc, off, size, l8):
        p = jnp.exp(s_scr[pl.ds(loc, size), :] - m)
        acc[...] += lax.dot_general(v_ref[pl.ds(off, size), :], p.astype(BF), TN, preferred_element_type=F32)
        return l8 + jnp.sum(p.reshape(size // 8, 8, 2 * tq), axis=0)

    l8 = two_level(start, count, tk, mix, jnp.zeros((8, 2 * tq), F32))
    l = jnp.sum(l8, axis=0, keepdims=True)
    ot_ref[...] = pick_heads(acc[...] / l, tq)
    lse = m + jnp.log(l)
    lse_ref[0] = jnp.concatenate([lse[:, :tq], lse[:, tq:]], axis=0)

def attn_fwd(bounds, q, qaug, k, kaug, v, *, tq=512, tk=768):
    T, D = q.shape
    S = k.shape[0]
    pairs = D // 128
    return pl.pallas_call(
        functools.partial(fwd_kernel, tk),
        out_shape=(jax.ShapeDtypeStruct((D, T), F32), jax.ShapeDtypeStruct((pairs, 2, T), F32)),
        grid_spec=pltpu.PrefetchScalarGridSpec(
            num_scalar_prefetch=1, grid=(pairs, T // tq),
            in_specs=[pl.BlockSpec((tq, 128), lambda h, i, b: (i, h)),
                      pl.BlockSpec((tq, 128), lambda h, i, b: (i, 0)),
                      pl.BlockSpec((S, 128), lambda h, i, b: (0, h)),
                      pl.BlockSpec((S, 128), lambda h, i, b: (0, 0)),
                      pl.BlockSpec((S, 128), lambda h, i, b: (0, h))],
            out_specs=(pl.BlockSpec((128, tq), lambda h, i, b: (h, i)),
                       pl.BlockSpec((1, 2, tq), lambda h, i, b: (h, 0, i))),
            scratch_shapes=[pltpu.VMEM((S, 2 * tq), F32), pltpu.VMEM((128, 2 * tq), F32)]),
        name="attend",
    )(bounds, q, qaug, k, kaug, v)

def bwd_kernel(tk, bounds, q_ref, qaug_ref, do_ref, lse_ref, ot_ref, k_ref, kaug_ref, v_ref,
               dq_ref, dk_ref, dv_ref, dk_acc, dv_acc, dq_acc):
    qi = pl.program_id(1)
    start, count = bounds[qi, 0], bounds[qi, 1]
    tq = q_ref.shape[0]

    @pl.when(qi == 0)
    def _():
        dk_acc[...] = jnp.zeros_like(dk_acc)
        dv_acc[...] = jnp.zeros_like(dv_acc)

    qs = stack_heads(q_ref[...])
    qrhs = stack_heads(q_ref[...], qaug_ref[...])
    dos = stack_heads(do_ref[...])
    lse = jnp.concatenate([lse_ref[0, 0:1, :], lse_ref[0, 1:2, :]], axis=1)
    mixed = ot_ref[...] * do_ref[...].astype(F32).T
    delta = jnp.concatenate(
        [jnp.sum(mixed[:64], axis=0, keepdims=True), jnp.sum(mixed[64:], axis=0, keepdims=True)], axis=1
    )
    dq_acc[...] = jnp.zeros_like(dq_acc)

    def step(loc, off, size, carry):
        rows = pl.ds(off, size)
        lhs = jnp.concatenate([k_ref[rows, :], kaug_ref[rows, :]], axis=1)
        x = lax.dot_general(lhs, qrhs, NT, preferred_element_type=F32)
        y = lax.dot_general(v_ref[rows, :], dos, NT, preferred_element_type=F32)
        p = jnp.exp(x - lse)
        ds = (p * (y - delta)).astype(BF)
        pb = p.astype(BF)
        dv_acc[rows, :] += lax.dot_general(pb, dos, NN, preferred_element_type=F32)
        dk_acc[rows, :] += lax.dot_general(ds, qs, NN, preferred_element_type=F32)
        dq_acc[...] += lax.dot_general(k_ref[rows, :], ds, TN, preferred_element_type=F32)
        return carry

    two_level(start, count, tk, step, 0)
    dq_ref[...] = (pick_heads(dq_acc[...], tq) * SCALE).T.astype(BF)

    @pl.when(qi == pl.num_programs(1) - 1)
    def _():
        dk_ref[...] = dk_acc[...].astype(BF)
        dv_ref[...] = dv_acc[...].astype(BF)

def attn_bwd(bounds, q, qaug, do, lse, ot, k, kaug, v, *, tq=512, tk=768):
    T, D = q.shape
    S = k.shape[0]
    pairs = D // 128
    row = lambda h, i, b: (h, 0, i)
    return pl.pallas_call(
        functools.partial(bwd_kernel, tk),
        out_shape=(jax.ShapeDtypeStruct((T, D), BF), jax.ShapeDtypeStruct((S, D), BF), jax.ShapeDtypeStruct((S, D), BF)),
        grid_spec=pltpu.PrefetchScalarGridSpec(
            num_scalar_prefetch=1, grid=(pairs, T // tq),
            in_specs=[pl.BlockSpec((tq, 128), lambda h, i, b: (i, h)),
                      pl.BlockSpec((tq, 128), lambda h, i, b: (i, 0)),
                      pl.BlockSpec((tq, 128), lambda h, i, b: (i, h)),
                      pl.BlockSpec((1, 2, tq), row),
                      pl.BlockSpec((128, tq), lambda h, i, b: (h, i)),
                      pl.BlockSpec((S, 128), lambda h, i, b: (0, h)),
                      pl.BlockSpec((S, 128), lambda h, i, b: (0, 0)),
                      pl.BlockSpec((S, 128), lambda h, i, b: (0, h))],
            out_specs=(pl.BlockSpec((tq, 128), lambda h, i, b: (i, h)),
                       pl.BlockSpec((S, 128), lambda h, i, b: (0, h)),
                       pl.BlockSpec((S, 128), lambda h, i, b: (0, h))),
            scratch_shapes=[pltpu.VMEM((S, 128), F32), pltpu.VMEM((S, 128), F32), pltpu.VMEM((128, 2 * tq), F32)]),
        name="attend_back",
    )(bounds, q, qaug, do, lse, ot, k, kaug, v)


def reach(n_ctx):
    return n_ctx // 2


def finish_kernel(n_up, up_ref, vec_ref, dk_ref, dv_ref, tok_ref, dq_ref, w_ref, own_in_ref, mine_tok_ref,
                  out_ref, vec_out, wide_out, grad_ref,
                  mine, buf_a, buf_h, buf_b, buf_s, keep, buf_c, buf_u, buf_d, buf_f, gbf,
                  sums, heard, line,
                  loads, weights, acc, dq, own, bias,
                  rsend, rmine, rbuf_x, rbuf_z,
                  sem_l, sem_a, sem_b, sem_c, sem_d, sem_e, sem_f, sem_v, sem_rx, sem_rz, sem_load, sem_in):
    n_chunks = out_ref.shape[0]
    n_ctx, n_wsh = lax.axis_size("ctx"), lax.axis_size("wsh")
    zs = n_ctx // 2
    a, w = lax.axis_index("ctx"), lax.axis_index("wsh")
    z, x = a // 2, lax.rem(a, 2)
    y, c = w // 2, lax.rem(w, 2)
    core_peer = (a, y * 2 + (1 - c))
    y_peer = (a, (1 - y) * 2 + c)
    x_peer = (z * 2 + (1 - x), w)
    near = reach(n_ctx)
    hops = near // 2
    MESH = pl.DeviceIdType.MESH

    def z_peer(d):
        other = lax.rem(z + d, zs)
        return other, (other * 2 + x, w)

    def slot(dest, src):
        return lax.rem(src - dest + zs, zs) - 1

    rows = out_ref.shape[1]
    half = out_ref.shape[2] // 2
    piece = rows // zs
    tall = own.shape[0]
    n_slices = sem_rx.shape[2]
    part = tall // n_slices

    barrier = pltpu.get_barrier_semaphore()
    for dev in [core_peer, y_peer, x_peer] + [z_peer(d)[1] for d in range(1, zs)]:
        pl.semaphore_signal(barrier, inc=1, device_id=dev, device_id_type=MESH)
    pl.semaphore_wait(barrier, zs + 2)

    def send(src, dst, sems, idx, dev):
        return pltpu.make_async_remote_copy(
            src_ref=src, dst_ref=dst, send_sem=sems.at[(0,) + idx], recv_sem=sems.at[(1,) + idx],
            device_id=dev, device_id_type=MESH)

    def wait_in(ref, sems, idx):
        send(ref, ref, sems, idx, core_peer).wait_recv()

    def wait_out(ref, sems, idx):
        send(ref, ref, sems, idx, core_peer).wait_send()

    def distance(i):
        return (hops - i // 4) * (1 - 2 * lax.rem(i // 2, 2))

    def position(i):
        dz = distance(i)
        mine_too = lax.rem(i, 2)
        run = 2 * (z + dz) + (1 - x) * (1 - mine_too) + x * mine_too
        there = (z + dz >= 0) & (z + dz < zs) & (jnp.abs(run - a) <= near)
        return run, mine_too, i // 2, there

    n_pos = 4 * hops + 2

    def load(i):
        run, _mine_too, _turn, there = position(i)
        return there, [
            pltpu.make_async_copy(src.at[run], loads.at[lax.rem(i, 2), j], sem_load.at[lax.rem(i, 2), j])
            for j, src in enumerate((dk_ref, dv_ref, tok_ref))
        ]

    def load_start(i):
        there, copies = load(i)

        @pl.when(there & (i < n_pos))
        def _():
            for copy in copies:
                copy.start()

    load_start(0)
    fetch = [pltpu.make_async_copy(w_ref, weights, sem_in.at[0]), pltpu.make_async_copy(dq_ref, dq, sem_in.at[1]),
             pltpu.make_async_copy(own_in_ref, own, sem_in.at[2])]
    for copy in fetch:
        copy.start()
    for k in range(n_up):
        for yy in range(2):
            where = (slice(None), pl.ds(k * 2 * half, 2 * half))
            pltpu.make_async_copy(up_ref.at[(yy * 2 + c,) + where], mine.at[k, yy], sem_l.at[k]).start()
            send(up_ref.at[(yy * 2 + (1 - c),) + where], buf_a.at[k, yy], sem_a, (k,), core_peer).start()
    acc[...] = jnp.zeros_like(acc)
    bias[...] = jnp.zeros_like(bias)
    fetch[0].wait()

    def unit(i):
        run, mine_too, turn, there = position(i)
        at = lax.rem(i, 2)
        load_start(i + 1)

        @pl.when(there)
        def _():
            for copy in load(i)[1]:
                copy.wait()

            def tokens_part(r, carry):
                rs = pl.ds(pl.multiple_of(r * 128, 128), 128)
                g = lax.dot_general(loads[at, 0, rs, :], weights[0], NT, preferred_element_type=F32)
                g = g + lax.dot_general(loads[at, 1, rs, :], weights[1], NT, preferred_element_type=F32)

                @pl.when(mine_too == 1)
                def _():
                    rmine[turn, rs, :] = g.astype(BF)

                @pl.when(mine_too == 0)
                def _():
                    rsend[turn, rs, :] = g.astype(BF)

                bias[0:8, :] += jnp.sum(loads[at, 1, rs, :].astype(F32).reshape(16, 8, 2 * half), axis=0)
                return carry

            lax.fori_loop(0, tall // 128, tokens_part, 0)

            @pl.when(mine_too == 0)
            def _():
                for s in range(n_slices):
                    rs = pl.ds(s * part, part)
                    send(rsend.at[turn, rs, :], rbuf_x.at[turn, rs, :], sem_rx, (turn, s), x_peer).start()

            def weights_part(r, carry):
                fs = pl.ds(pl.multiple_of(r * 256, 256), 256)
                flipped = loads[at, 2, :, fs].T
                for j in range(2):
                    acc[j, fs, :] += lax.dot_general(flipped, loads[at, j], NN, preferred_element_type=F32)
                return carry

            lax.fori_loop(0, 2 * half // 256, weights_part, 0)

    def runs(e):
        turn, s = e // n_slices, lax.rem(e, n_slices)
        rs = pl.ds(pl.multiple_of(s * part, part), part)
        dz = distance(2 * turn)
        other = z + dz

        @pl.when((other >= 0) & (other < zs))
        def _():
            joined = jnp.abs(2 * dz + 2 * x - 1) <= near

            @pl.when(joined)
            def _():
                wait_in(rbuf_x.at[turn, rs, :], sem_rx, (turn, s))
                sum_ = rmine[turn, rs, :].astype(F32) + rbuf_x[turn, rs, :].astype(F32)

                @pl.when(dz == 0)
                def _():
                    own[rs, :] += sum_

                @pl.when(dz != 0)
                def _():
                    rmine[turn, rs, :] = sum_.astype(BF)

            @pl.when(dz != 0)
            def _():
                send(rmine.at[turn, rs, :], rbuf_z.at[slot(other, z), rs, :], sem_rz, (slot(other, z), s),
                     (other * 2 + x, w)).start()

    def runs_end(e):
        d, s = 1 + e // n_slices, lax.rem(e, n_slices)
        rs = pl.ds(pl.multiple_of(s * part, part), part)
        other = lax.rem(z + d, zs)

        @pl.when(jnp.abs(2 * (other - z)) <= near)
        def _():
            wait_in(rbuf_z.at[d - 1, rs, :], sem_rz, (d - 1, s))
            own[rs, :] += rbuf_z[d - 1, rs, :].astype(F32)

    def stage_b(k):
        pltpu.make_async_copy(mine.at[k], mine.at[k], sem_l.at[k]).wait()
        wait_in(buf_a.at[k], sem_a, (k,))
        buf_h[k] = (mine[k, 1 - y].astype(F32) + buf_a[k, 1 - y].astype(F32)).astype(BF)
        send(buf_h.at[k], buf_b.at[k], sem_b, (k,), y_peer).start()

    def column(side):
        return pl.ds(pl.multiple_of(side * half, 128), half)

    def stage_c(k):
        wait_in(buf_b.at[k], sem_b, (k,))

        def total(side):
            cols = column(side)
            return (mine[k, y, :, cols].astype(F32) + buf_a[k, y, :, cols].astype(F32)
                    + buf_b[k, :, cols].astype(F32))

        buf_s[k] = total(1 - x).astype(BF)
        send(buf_s.at[k], buf_c.at[k], sem_c, (k,), x_peer).start()
        keep[k] = total(x)

    def stage_d(k):
        wait_in(buf_c.at[k], sem_c, (k,))
        s = keep[k] + buf_c[k].astype(F32)
        keep[k] = s
        buf_u[k] = s.astype(BF)
        for d in range(1, zs):
            other, dev = z_peer(d)
            send(buf_u.at[k, pl.ds(pl.multiple_of(other * piece, 16), piece), :], buf_d.at[k, slot(other, z)],
                 sem_d, (k,), dev).start()

    def stage_e(k):
        wait_in(buf_d.at[k], sem_d, (k,))
        my = pl.ds(pl.multiple_of(z * piece, 16), piece)
        s = keep[k, my, :]
        for d in range(zs - 1):
            s = s + buf_d[k, d].astype(F32)
        buf_f[k] = s.astype(BF)
        out_ref[k, my, column(x)] = s.astype(BF)
        for d in range(1, zs):
            _other, dev = z_peer(d)
            send(buf_f.at[k], out_ref.at[k, my, column(x)], sem_e, (k,), dev).start()

    def stage_f(k):
        wait_in(buf_d.at[k], sem_e, (k,))
        send(out_ref.at[k, :, column(x)], out_ref.at[k, :, column(x)], sem_f, (k,), x_peer).start()

    def stage_g(k):
        wait_in(out_ref.at[k, :, column(1 - x)], sem_f, (k,))

    def guarded(fn, k, low, high):
        @pl.when((k >= low) & (k < high))
        def _():
            fn(k)

    def first_step(t, carry):
        guarded(unit, t, 0, n_pos)
        guarded(stage_b, t, 0, n_up)
        guarded(stage_c, t - 2, 0, n_up)
        guarded(runs, t - 5, 0, n_slices)
        guarded(stage_d, t - 5, 0, n_up)
        guarded(stage_e, t - 7, 0, n_up)
        return carry

    lax.fori_loop(0, n_up + 7, first_step, 0)

    fetch[1].wait()
    fetch[2].wait()
    own_tok = pltpu.make_async_copy(mine_tok_ref, loads.at[0, 2], sem_load.at[0, 2])
    own_tok.start()

    def to_bf(j, target):
        for owner in range(n_wsh):
            gbf[target, owner] = acc[j, owner * rows : (owner + 1) * rows, :].astype(BF)

    def chunk_start(k, j):
        for yy in range(2):
            pltpu.make_async_copy(gbf.at[j, yy * 2 + c], mine.at[k, yy], sem_l.at[k]).start()
            send(gbf.at[j, yy * 2 + (1 - c)], buf_a.at[k, yy], sem_a, (k,), core_peer).start()

    for j in range(2):
        to_bf(j, j)
        chunk_start(n_up + j, j)
    own_tok.wait()

    def query_part(r, carry):
        fs = pl.ds(pl.multiple_of(r * 256, 256), 256)
        acc[0, fs, :] = lax.dot_general(loads[0, 2, :, fs].T, dq[...], NN, preferred_element_type=F32)
        return carry

    lax.fori_loop(0, 2 * half // 256, query_part, 0)
    to_bf(0, 2)
    chunk_start(n_up + 2, 2)

    def query_tokens(r, carry):
        rs = pl.ds(pl.multiple_of(r * 128, 128), 128)
        own[rs, :] += lax.dot_general(dq[rs, :], weights[2], NT, preferred_element_type=F32)
        bias[8:16, :] += jnp.sum(dq[rs, :].astype(F32).reshape(16, 8, 2 * half), axis=0)
        return carry

    lax.fori_loop(0, tall // 128, query_tokens, 0)

    sums[0] = vec_ref[...]
    sums[0, 0:1, :] = jnp.sum(bias[8:16, :], axis=0, keepdims=True)
    sums[0, 1:2, :] = jnp.sum(bias[0:8, :], axis=0, keepdims=True)
    pair = (core_peer, y_peer, x_peer)

    def vec_send(stage):
        send(sums.at[stage], heard.at[stage], sem_v, (stage,), pair[stage]).start()

    def vec_stage(stage):
        wait_in(heard.at[stage], sem_v, (stage,))
        total = sums[stage] + heard[stage]
        sums[stage + 1] = total
        if stage < 2:
            vec_send(stage + 1)
        else:
            line[z] = total
            for d in range(1, zs):
                _other, dev = z_peer(d)
                send(sums.at[3], line.at[z], sem_v, (3,), dev).start()

    def vec_last():
        wait_in(line.at[pl.ds(0, zs - 1)], sem_v, (3,))
        total = line[0]
        for d in range(1, zs):
            total = total + line[d]
        small, wide = total[0:8, 0:rows], total[8:9, :]
        for owner in range(1, n_wsh):
            small = jnp.where(w == owner, total[0:8, owner * rows : (owner + 1) * rows], small)
            wide = jnp.where(w == owner, total[8 + owner : 9 + owner, :], wide)
        vec_out[...] = small
        wide_out[...] = wide

    vec_send(0)

    def second_step(t, carry):
        guarded(stage_b, n_up + t, n_up, n_chunks)
        for stage in range(3):
            guarded(lambda k: vec_stage(stage), t - 1 - stage, 0, 1)
        for j in range(2):
            guarded(runs, n_slices + 2 * t + j, n_slices, (2 * hops + 1) * n_slices)
        guarded(stage_f, t, 0, n_up)
        guarded(stage_c, n_up + t - 2, n_up, n_chunks)
        guarded(stage_d, n_up + t - 5, n_up, n_chunks)
        guarded(stage_e, n_up + t - 8, n_up, n_chunks)
        guarded(stage_f, n_up + t - 11, n_up, n_chunks)
        guarded(lambda k: vec_last(), t - 6, 0, 1)
        return carry

    lax.fori_loop(0, n_chunks - n_up + 11, second_step, 0)

    def each_end(e, carry):
        runs_end(e)
        return carry

    lax.fori_loop(0, (zs - 1) * n_slices, each_end, 0)
    grad_ref[...] = own[...].astype(BF)

    def drain(k, carry):
        stage_g(k)
        wait_out(buf_a.at[k], sem_a, (k,))
        wait_out(buf_b.at[k], sem_b, (k,))
        wait_out(buf_c.at[k], sem_c, (k,))
        wait_out(buf_d.at[k], sem_d, (k,))
        wait_out(buf_d.at[k], sem_e, (k,))
        wait_out(out_ref.at[k, :, column(x)], sem_f, (k,))
        return carry

    lax.fori_loop(0, n_chunks, drain, 0)
    for stage in range(3):
        wait_out(heard.at[stage], sem_v, (stage,))
    wait_out(line.at[pl.ds(0, zs - 1)], sem_v, (3,))

    def drain_runs(e, carry):
        turn, s = e // n_slices, lax.rem(e, n_slices)
        rs = pl.ds(pl.multiple_of(s * part, part), part)
        _run, _mine_too, _turn, there = position(2 * turn)

        @pl.when(there)
        def _():
            wait_out(rbuf_x.at[turn, rs, :], sem_rx, (turn, s))

        dz = distance(2 * turn)

        @pl.when((dz != 0) & (z + dz >= 0) & (z + dz < zs))
        def _():
            wait_out(rmine.at[turn, rs, :], sem_rz, (slot(z + dz, z), s))

        return carry

    lax.fori_loop(0, (2 * hops + 1) * n_slices, drain_runs, 0)


def finish(up_parts, vec, grad_k, grad_v, all_tokens, grad_q, kvq_w, own_grad, inputs):
    n_ctx, n_wsh = lax.axis_size("ctx"), lax.axis_size("wsh")
    zs, hops = n_ctx // 2, reach(n_ctx) // 2
    rows, n_up = up_parts.shape[1], up_parts.shape[2] // D
    n = n_up + 3
    half, piece, tall = D // 2, rows // zs, inputs.shape[0]
    turns, n_slices = 2 * hops + 1, 4
    vm, dma, shape = pltpu.VMEM, pltpu.SemaphoreType.DMA, jax.ShapeDtypeStruct
    any_spec = pl.BlockSpec(memory_space=pl.ANY)
    vm_spec = pl.BlockSpec(memory_space=pltpu.VMEM)
    return pl.pallas_call(
        functools.partial(finish_kernel, n_up),
        out_shape=(shape((n, rows, D), BF), shape((8, rows), F32), shape((1, D), F32), shape((tall, D), BF)),
        in_specs=[any_spec, vm_spec] + [any_spec] * 7,
        out_specs=(vm_spec,) * 4,
        scratch_shapes=[
            vm((n, 2, rows, D), BF), vm((n, 2, rows, D), BF), vm((n, rows, D), BF), vm((n, rows, D), BF),
            vm((n, rows, half), BF), vm((n, rows, half), F32), vm((n, rows, half), BF), vm((n, rows, half), BF),
            vm((n, zs - 1, piece, half), BF), vm((n, piece, half), BF), vm((3, n_wsh, rows, D), BF),
            vm((4,) + vec.shape, F32), vm((3,) + vec.shape, F32), vm((zs,) + vec.shape, F32),
            vm((2, 3, tall, D), BF), vm((3, D, D), BF), vm((2, D, D), F32), vm((tall, D), BF), vm((tall, D), F32),
            vm((16, D), F32),
            vm((turns, tall, D), BF), vm((turns, tall, D), BF), vm((turns, tall, D), BF), vm((zs - 1, tall, D), BF),
            dma((n,)), dma((2, n)), dma((2, n)), dma((2, n)), dma((2, n)), dma((2, n)), dma((2, n)), dma((2, 4)),
            dma((2, turns, n_slices)), dma((2, zs - 1, n_slices)), dma((2, 3)), dma((3,)),
        ],
        compiler_params=pltpu.CompilerParams(collective_id=2, has_side_effects=True, vmem_limit_bytes=63 * 2**20),
        name="finish",
    )(up_parts, vec, grad_k, grad_v, all_tokens, grad_q, kvq_w, own_grad, inputs)


def gather_kernel(cut, tok_ref, vec_ref, wk_ref, wv_ref, wq_ref,
                  tok_out, k_out, v_out, q_out, w_out, vec_out,
                  tok, kbuf, vbuf, qbuf, wbuf, vecs,
                  sem_in, sem_out, sem_w, sem_l, sem_o):
    n_ctx = lax.axis_size("ctx")
    zs = n_ctx // 2
    a, w = lax.axis_index("ctx"), lax.axis_index("wsh")
    z, x = a // 2, lax.rem(a, 2)
    y, c = w // 2, lax.rem(w, 2)
    core_peer = (a, y * 2 + (1 - c))
    y_peer = (a, (1 - y) * 2 + c)
    x_peer = (z * 2 + (1 - x), w)
    up, down = (a + 2, w), (a - 2, w)
    near = reach(n_ctx)
    MESH = pl.DeviceIdType.MESH
    n_slices = sem_in.shape[1]
    tall = tok.shape[1] // n_slices
    own = wk_ref.shape[0]
    far = 4 * (near // 2 + 1)

    barrier = pltpu.get_barrier_semaphore()
    around = [(lax.rem(z + d, zs) * 2 + x, w) for d in (1, zs - 1)]
    for dev in [core_peer, y_peer, x_peer] + around:
        pl.semaphore_signal(barrier, inc=1, device_id=dev, device_id_type=MESH)
    pl.semaphore_wait(barrier, 5)

    def relative(u):
        dz = (u // 4) * (1 - 2 * lax.rem(u, 2))
        other = lax.rem(u // 2, 2)
        run = 2 * (z + dz) + (x + other - 2 * x * other)
        there = (z + dz >= 0) & (z + dz < zs) & (jnp.abs(run - a) <= near) & ((u >= 4) | (lax.rem(u, 2) == 0))
        return run, dz, other, there

    def rows(s):
        return pl.ds(pl.multiple_of(s * tall, tall), tall)

    def remote(src, dst, send_sem, recv_sem, dev):
        return pltpu.make_async_remote_copy(
            src_ref=src, dst_ref=dst, send_sem=send_sem, recv_sem=recv_sem, device_id=dev, device_id_type=MESH)

    def routes(u, s):
        run, dz, other, there = relative(u)
        z_first = s < cut
        to_x = there & (z_first | (dz == 0)) & (other == 0) & (jnp.abs(run - x_peer[0]) <= near)
        along = there & ((other == 0) | jnp.logical_not(z_first))
        to_up = along & (dz <= 0) & (z + 1 < zs) & (jnp.abs(run - (a + 2)) <= near)
        to_down = along & (dz >= 0) & (z > 0) & (jnp.abs(run - (a - 2)) <= near)
        return run, ((0, x_peer, to_x), (1, up, to_up), (2, down, to_down))

    def pass_on(u, s):
        run, where = routes(u, s)
        for d, dev, ok in where:
            @pl.when(ok)
            def _():
                source = tok_ref if isinstance(u, int) and u == 0 else tok.at[run]
                remote(source.at[rows(s), :], tok.at[run, rows(s), :], sem_out.at[d, u, s], sem_in.at[run, s], dev).start()

    def await_slice(u, s):
        run, _dz, _other, there = relative(u)

        @pl.when(there)
        def _():
            remote(tok.at[run, rows(s), :], tok.at[run, rows(s), :], sem_out.at[0, 0, 0], sem_in.at[run, s], x_peer).wait_recv()

    def start_own(s, carry):
        pass_on(0, s)
        return carry

    def weight_rows(owner):
        return pl.ds(pl.multiple_of(owner * own, 16), own)

    vec_own = vecs.at[w]
    remote(vec_ref, vec_own, sem_w.at[0, 0, 3], sem_w.at[1, 0, 3], core_peer).start()
    remote(vec_ref, vec_own, sem_w.at[0, 1, 3], sem_w.at[1, 1, 3], y_peer).start()
    pltpu.make_async_copy(vec_ref, vec_own, sem_l.at[3]).start()
    for m, ref in enumerate((wk_ref, wv_ref, wq_ref)):
        there = wbuf.at[m, weight_rows(w), :]
        remote(ref, there, sem_w.at[0, 1, m], sem_w.at[1, 1, m], y_peer).start()
        remote(ref, there, sem_w.at[0, 0, m], sem_w.at[1, 0, m], core_peer).start()
        pltpu.make_async_copy(ref, there, sem_l.at[m]).start()
    lax.fori_loop(0, n_slices, start_own, 0)
    pltpu.make_async_copy(tok_ref, tok.at[a], sem_l.at[4]).start()

    for j in range(n_ctx):
        @pl.when(jnp.abs(j - a) > near)
        def _():
            tok[j] = jnp.zeros_like(tok[j])

    def shard(m, owner):
        return vecs.at[owner] if m == 3 else wbuf.at[m, weight_rows(owner), :]

    def weight_arrival(m, kind):
        part = shard(m, w)
        return remote(part, part, sem_w.at[0, kind, m], sem_w.at[1, kind, m], core_peer)

    across = (1 - y) * 2 + c

    def weight_forward(m):
        weight_arrival(m, 1).wait_recv()
        remote(shard(m, across), shard(m, across), sem_w.at[0, 2, m], sem_w.at[1, 2, m], core_peer).start()

    def weight_end(m):
        weight_arrival(m, 0).wait_recv()
        weight_arrival(m, 2).wait_recv()
        pltpu.make_async_copy(shard(m, w), shard(m, w), sem_l.at[m]).wait()

    weight_forward(3)
    weight_forward(0)
    weight_forward(1)
    weight_end(3)
    total = vecs[0].astype(F32)
    for owner in range(1, 4):
        total = total + vecs[owner].astype(F32)
    vec_out[...] = total
    pltpu.make_async_copy(tok_ref, tok.at[a], sem_l.at[4]).wait()
    weight_end(0)
    weight_end(1)

    def relay(first, last):
        def one(i, carry):
            s = i // (last - first)
            u = first + lax.rem(i, last - first)
            await_slice(u, s)
            pass_on(u, s)
            return carry

        lax.fori_loop(0, n_slices * (last - first), one, 0)

    step_rows = 128
    steps = tok.shape[1] // step_rows

    def project(u, carry):
        run, _dz, _other, there = relative(u)

        @pl.when(u == 1)
        def _():
            relay(2, 6)

        @pl.when(u == 6)
        def _():
            weight_forward(2)
            weight_end(2)
            relay(6, 10)

        @pl.when(there)
        def _():
            @pl.when(u >= 10)
            def _():
                def one(s, carry):
                    await_slice(u, s)
                    return carry

                lax.fori_loop(0, n_slices, one, 0)

            def part(i, carry):
                r = pl.ds(pl.multiple_of(i * step_rows, step_rows), step_rows)
                t = tok[run, r, :]
                kbuf[run, r, :] = jnp.dot(t, wbuf[0], preferred_element_type=F32).astype(BF)
                vbuf[run, r, :] = (jnp.dot(t, wbuf[1], preferred_element_type=F32) + vec_out[1:2, :]).astype(BF)
                return carry

            lax.fori_loop(0, steps, part, 0)
            for i, (src, dst) in enumerate(((kbuf, k_out), (vbuf, v_out), (tok, tok_out))):
                pltpu.make_async_copy(src.at[run], dst.at[run], sem_o.at[i, run]).start()

        return carry

    for j in range(n_ctx):
        @pl.when(jnp.abs(j - a) > near)
        def _():
            kbuf[j] = jnp.zeros_like(kbuf[j])
            vbuf[j] = jnp.zeros_like(vbuf[j])
            for i, (src, dst) in enumerate(((kbuf, k_out), (vbuf, v_out), (tok, tok_out))):
                pltpu.make_async_copy(src.at[j], dst.at[j], sem_o.at[i, j]).start()

    lax.fori_loop(0, far, project, 0)

    def query_part(i, carry):
        r = pl.ds(pl.multiple_of(i * step_rows, step_rows), step_rows)
        q = (jnp.dot(tok[a, r, :], wbuf[2], preferred_element_type=F32) + vec_out[0:1, :]).astype(BF)
        qbuf[r, :] = q * jnp.asarray(SCALE, BF)
        return carry

    lax.fori_loop(0, steps, query_part, 0)
    pltpu.make_async_copy(qbuf, q_out, sem_l.at[5]).start()
    pltpu.make_async_copy(wbuf, w_out, sem_l.at[6]).start()

    for m in range(4):
        for kind in range(3):
            weight_arrival(m, kind).wait_send()

    def drain(i, carry):
        s = i // far
        u = lax.rem(i, far)
        run, where = routes(u, s)
        for d, dev, ok in where:
            @pl.when(ok & (u < 10))
            def _():
                remote(tok.at[run, rows(s), :], tok.at[run, rows(s), :], sem_out.at[d, u, s], sem_in.at[run, s], dev).wait_send()
        return carry

    lax.fori_loop(0, n_slices * far, drain, 0)
    for j in range(n_ctx):
        for i, (src, dst) in enumerate(((kbuf, k_out), (vbuf, v_out), (tok, tok_out))):
            pltpu.make_async_copy(src.at[j], dst.at[j], sem_o.at[i, j]).wait()
    pltpu.make_async_copy(qbuf, q_out, sem_l.at[5]).wait()
    pltpu.make_async_copy(wbuf, w_out, sem_l.at[6]).wait()


def gather_project(inputs, vec, key_weight, value_weight, query_weight):
    n_ctx, n_wsh = lax.axis_size("ctx"), lax.axis_size("wsh")
    tall = inputs.shape[0]
    n_slices = 8
    far = 4 * (reach(n_ctx) // 2 + 1)
    vm, dma = pltpu.VMEM, pltpu.SemaphoreType.DMA
    any_spec = pl.BlockSpec(memory_space=pl.ANY)
    vm_spec = pl.BlockSpec(memory_space=pltpu.VMEM)
    runs = (n_ctx, tall, D)
    shape = jax.ShapeDtypeStruct
    return pl.pallas_call(
        functools.partial(gather_kernel, 5),
        out_shape=(shape(runs, BF), shape(runs, BF), shape(runs, BF), shape((tall, D), BF), shape((3, D, D), BF),
                   shape(vec.shape, F32)),
        in_specs=[any_spec] * 5,
        out_specs=(any_spec,) * 5 + (vm_spec,),
        scratch_shapes=[
            vm(runs, BF), vm(runs, BF), vm(runs, BF), vm((tall, D), BF), vm((3, D, D), BF), vm((n_wsh,) + vec.shape, BF),
            dma((n_ctx, n_slices)), dma((3, far, n_slices)), dma((2, 3, 4)), dma((7,)), dma((3, n_ctx)),
        ],
        compiler_params=pltpu.CompilerParams(collective_id=1, has_side_effects=True, vmem_limit_bytes=48 * 2**20),
        name="gather_project",
    )(inputs, vec, key_weight, value_weight, query_weight)


def local(
    tokens,
    cotangent,
    doc_starts,
    query_weight,
    key_weight,
    value_weight,
    out_weight,
    up_weight,
    down_weight,
    query_bias,
    value_bias,
    out_bias,
    attn_gain,
    attn_shift,
    up_bias,
    down_bias,
    final_gain,
    final_shift,
):
    inputs = tokens[0]
    doc_start = doc_starts[0]
    tok_rows = inputs.shape[0]
    stream_rows = tok_rows * lax.axis_size("ctx")
    first_row = lax.axis_index("ctx") * tok_rows
    tile = min(tok_rows, 512)
    bounds = key_range(doc_start, first_row, tok_rows, stream_rows, tile)
    query_doc, key_doc = document_lanes(doc_start, first_row, tok_rows, stream_rows)

    n_ctx, n_wsh = lax.axis_size("ctx"), lax.axis_size("wsh")
    own = D // n_wsh

    def gather(x):
        return lax.all_gather(x, "wsh", axis=0, tiled=True)

    small = jnp.stack(
        [query_bias, value_bias, out_bias, attn_gain, attn_shift, down_bias, final_gain, final_shift]
    )
    fast = n_wsh == 4 and n_ctx % 4 == 0 and own % (n_ctx // 2 * 16) == 0 and tok_rows % 512 == 0
    if fast:
        w = lax.axis_index("wsh")
        at = lax.broadcasted_iota(jnp.int32, (8, D), 1) // own == w
        vec = jnp.where(at, jnp.tile(small, (1, n_wsh)), jnp.zeros((), BF))
        at = lax.broadcasted_iota(jnp.int32, (8, D), 0) == w
        vec = jnp.concatenate([vec, jnp.where(at, up_bias[None, :], jnp.zeros((), BF))], axis=0)
        all_tokens, keys, values, queries, kvq_w, vec = gather_project(
            inputs, vec, key_weight, value_weight, query_weight
        )
        all_tokens, keys, values = [r.reshape(stream_rows, D) for r in (all_tokens, keys, values)]
        key_w, value_w, query_w = kvq_w[0], kvq_w[1], kvq_w[2]
        query_b, value_b, out_b, attn_g, attn_s, down_b, final_g, final_s = [vec[i] for i in range(8)]
        up_b = vec[8 : 8 + n_wsh].reshape(-1)
    else:
        all_tokens = lax.all_gather(inputs, "ctx", axis=0, tiled=True)
        query_w, key_w, value_w = gather(query_weight), gather(key_weight), gather(value_weight)
        small = gather(small.T).astype(F32)
        query_b, value_b, out_b, attn_g, attn_s, down_b, final_g, final_s = [small[:, i] for i in range(8)]
        up_b = gather(up_bias).astype(F32)
        queries = jnp.dot(inputs, query_w, preferred_element_type=F32) + query_b
        queries = queries.astype(BF) * jnp.asarray(SCALE, BF)
        keys = jnp.dot(all_tokens, key_w, preferred_element_type=F32).astype(BF)
        values = (jnp.dot(all_tokens, value_w, preferred_element_type=F32) + value_b).astype(BF)
    out_w = gather(out_weight)
    up_w = gather(up_weight)
    down_w = gather(down_weight)

    mixed_t, log_rows = attn_fwd(bounds, queries, query_doc, keys, key_doc, values, tq=tile)
    attn_t = mixed_t.astype(BF)
    inputs_f = inputs.astype(F32)
    branch = lax.dot_general(attn_t, out_w, TN, preferred_element_type=F32) + out_b
    first_norm, first_pull = jax.vjp(layer_norm, inputs_f + branch, attn_g, attn_s)
    first_b = first_norm.astype(BF)
    up_f = jnp.dot(first_b, up_w, preferred_element_type=F32) + up_b
    act_f, act_pull = jax.vjp(gelu_act, up_f)
    act_b = act_f.astype(BF)
    down_f = jnp.dot(act_b, down_w, preferred_element_type=F32) + down_b
    final_f, final_pull = jax.vjp(layer_norm, first_norm + down_f, final_g, final_s)
    layer_out = final_f.astype(BF)

    grad_sum2, grad_final_g, grad_final_s = final_pull(cotangent[0].astype(F32))
    grad_down = grad_sum2.astype(BF)
    grad_down_w = jnp.einsum("tf,td->fd", act_b, grad_down, preferred_element_type=F32)
    grad_down_b = jnp.sum(grad_down.astype(F32), axis=0)
    grad_act = jnp.einsum("td,fd->tf", grad_down, down_w, preferred_element_type=F32)
    (grad_up_f,) = act_pull(grad_act)
    grad_up = grad_up_f.astype(BF)
    grad_up_w = jnp.einsum("td,tf->df", first_b, grad_up, preferred_element_type=F32)
    grad_up_b = jnp.sum(grad_up.astype(F32), axis=0)
    grad_first = grad_sum2 + jnp.einsum("tf,df->td", grad_up, up_w, preferred_element_type=F32)
    grad_sum1, grad_attn_g, grad_attn_s = first_pull(grad_first)
    grad_branch = grad_sum1.astype(BF)
    grad_out_w = jnp.dot(attn_t, grad_branch, preferred_element_type=F32)
    grad_out_b = jnp.sum(grad_branch.astype(F32), axis=0)
    grad_attn = jnp.einsum("te,de->td", grad_branch, out_w, preferred_element_type=F32).astype(BF)
    grad_q, grad_k, grad_v = attn_bwd(
        bounds, queries, query_doc, grad_attn, log_rows, mixed_t, keys, key_doc, values, tq=tile
    )
    def total(g):
        part = lax.psum_scatter(g.astype(BF), "wsh", scatter_dimension=0, tiled=True)
        return lax.psum(part, "ctx").astype(F32)

    if fast:
        none = jnp.zeros((D,), F32)
        vec = jnp.stack([none, none, grad_out_b, grad_attn_g, grad_attn_s, grad_down_b, grad_final_g, grad_final_s])
        vec = jnp.concatenate([vec, grad_up_b.reshape(n_wsh, -1), jnp.zeros((8 - n_wsh, D), F32)], axis=0)
        summed, small, wide, grad_inputs = finish(
            grad_up_w.astype(BF).reshape(n_wsh, own, -1), vec, grad_k.reshape(n_ctx, tok_rows, D),
            grad_v.reshape(n_ctx, tok_rows, D), all_tokens.reshape(n_ctx, tok_rows, D), grad_q, kvq_w, grad_sum1, inputs,
        )
        n_up = summed.shape[0] - 3
        up_sum = jnp.concatenate([summed[i] for i in range(n_up)], axis=1)
        sums = [
            summed[n_up + 2].astype(F32), summed[n_up].astype(F32), summed[n_up + 1].astype(F32), total(grad_out_w),
            up_sum.astype(F32), total(grad_down_w), small[0], small[1], small[2], small[3], small[4], wide[0],
            small[5], small[6], small[7],
        ]
    else:
        grad_all = jnp.einsum("te,de->td", grad_k, key_w, preferred_element_type=F32)
        grad_all = grad_all + jnp.einsum("te,de->td", grad_v, value_w, preferred_element_type=F32)
        grad_own = lax.psum_scatter(grad_all.astype(BF), "ctx", scatter_dimension=0, tiled=True)
        grad_query_w = jnp.einsum("td,te->de", inputs, grad_q, preferred_element_type=F32)
        grad_key_w = jnp.einsum("td,te->de", all_tokens, grad_k, preferred_element_type=F32)
        grad_value_w = jnp.einsum("td,te->de", all_tokens, grad_v, preferred_element_type=F32)
        grad_query_b = jnp.sum(grad_q.astype(F32), axis=0)
        grad_value_b = jnp.sum(grad_v.astype(F32), axis=0)
        grad_inputs = grad_sum1 + jnp.einsum("te,de->td", grad_q, query_w, preferred_element_type=F32)
        grad_inputs = grad_inputs + grad_own.astype(F32)
        sums = [
            total(g)
            for g in (
                grad_query_w, grad_key_w, grad_value_w, grad_out_w, grad_up_w, grad_down_w,
                grad_query_b, grad_value_b, grad_out_b, grad_attn_g, grad_attn_s, grad_up_b,
                grad_down_b, grad_final_g, grad_final_s,
            )
        ]
    return (
        layer_out.reshape(1, tok_rows, D),
        grad_inputs.astype(BF).reshape(1, tok_rows, D),
        *sums,
    )


def solution(mesh):
    rows, mat, vec = P("wsh", "ctx", None), P("wsh", None), P("wsh")
    return jax.shard_map(
        local,
        mesh=mesh,
        in_specs=(rows, rows, mat) + (mat,) * 6 + (vec,) * 9,
        out_specs=(rows, rows) + (mat,) * 6 + (vec,) * 9,
        check_vma=False,
    )
```

```python
import functools

import jax
import jax.numpy as jnp
from jax import lax
from jax.experimental import pallas as pl
from jax.experimental.pallas import tpu as pltpu
from jax.sharding import PartitionSpec as P

D = 768
HEADS = 12
HD = 64
SCALE = 0.125
EPS = 1e-12
ROOT_HALF = 0.7071067811865476
BF = jnp.bfloat16
F32 = jnp.float32
NT = (((1,), (1,)), ((), ()))
NN = (((1,), (0,)), ((), ()))
TN = (((0,), (0,)), ((), ()))


def layer_norm(values, gain_vec, shift_vec):
    average = jnp.mean(values, axis=-1, keepdims=True)
    centred = values - average
    variance = jnp.mean(centred * centred, axis=-1, keepdims=True)
    return centred * lax.rsqrt(variance + EPS) * gain_vec + shift_vec


def gelu_act(values):
    return 0.5 * values * (1.0 + lax.erf(values * ROOT_HALF))


def key_range(doc_start, first_row, rows, stream_rows, tile):
    pos = jnp.arange(rows // tile, dtype=jnp.int32) * tile + first_row
    last = pos + tile - 1
    low = jnp.max(jnp.where(doc_start[None, :] <= pos[:, None], doc_start[None, :], 0), axis=1)
    high = jnp.min(
        jnp.where(doc_start[None, :] > last[:, None], doc_start[None, :], stream_rows), axis=1
    )
    first = low // 128 * 128
    count = (high - first + 255) // 256
    first = jnp.minimum(first, stream_rows - count * 256)
    return jnp.stack([first, count], axis=1).astype(jnp.int32)


def document_lanes(doc_start, first_row, rows, stream_rows):
    far = jnp.full((128 - doc_start.shape[0],), 2**30, jnp.int32)
    starts = jnp.concatenate([doc_start, far])
    ends = jnp.concatenate([doc_start[1:], jnp.full((1,), stream_rows, jnp.int32), far])
    query_pos = first_row + jnp.arange(rows, dtype=jnp.int32)[:, None]
    key_pos = jnp.arange(stream_rows, dtype=jnp.int32)[:, None]
    query_doc = ((query_pos >= starts) & (query_pos < ends)).astype(BF)
    key_doc = jnp.where((key_pos >= starts) & (key_pos < ends), 0.0, -1e30).astype(BF)
    return query_doc, key_doc


def stack_heads(x, extra=None):
    lane = lax.broadcasted_iota(jnp.int32, x.shape, 1)
    zero = jnp.zeros_like(x)
    lo = jnp.where(lane < 64, x, zero)
    hi = jnp.where(lane < 64, zero, x)
    if extra is not None:
        lo = jnp.concatenate([lo, extra], axis=1)
        hi = jnp.concatenate([hi, extra], axis=1)
    return jnp.concatenate([lo, hi], axis=0)

def pick_heads(x, tq):
    return jnp.concatenate([x[:64, :tq], x[64:, tq:]], axis=0)

def two_level(start, count, tk, body, init):
    big = tk // 256
    whole = count // big
    def large(t, c):
        return body(pl.multiple_of(t * tk, 256), pl.multiple_of(start + t * tk, 128), tk, c)
    def small(t, c):
        return body(pl.multiple_of(t * 256, 256), pl.multiple_of(start + t * 256, 128), 256, c)
    c = lax.fori_loop(0, whole, large, init)
    return lax.fori_loop(whole * big, count, small, c)

def fwd_kernel(tk, bounds, q_ref, qaug_ref, k_ref, kaug_ref, v_ref, ot_ref, lse_ref, s_scr, acc):
    qi = pl.program_id(1)
    start, count = bounds[qi, 0], bounds[qi, 1]
    tq = q_ref.shape[0]
    rhs = stack_heads(q_ref[...], qaug_ref[...])

    def scores(loc, off, size, m):
        lhs = jnp.concatenate([k_ref[pl.ds(off, size), :], kaug_ref[pl.ds(off, size), :]], axis=1)
        s = lax.dot_general(lhs, rhs, NT, preferred_element_type=F32)
        s_scr[pl.ds(loc, size), :] = s
        return jnp.maximum(m, jnp.max(s.reshape(size // 8, 8, 2 * tq), axis=0))

    m8 = two_level(start, count, tk, scores, jnp.full((8, 2 * tq), -3e38, F32))
    m = jnp.max(m8, axis=0, keepdims=True)
    acc[...] = jnp.zeros_like(acc)

    def mix(loc, off, size, l8):
        p = jnp.exp(s_scr[pl.ds(loc, size), :] - m)
        acc[...] += lax.dot_general(v_ref[pl.ds(off, size), :], p.astype(BF), TN, preferred_element_type=F32)
        return l8 + jnp.sum(p.reshape(size // 8, 8, 2 * tq), axis=0)

    l8 = two_level(start, count, tk, mix, jnp.zeros((8, 2 * tq), F32))
    l = jnp.sum(l8, axis=0, keepdims=True)
    ot_ref[...] = pick_heads(acc[...] / l, tq)
    lse = m + jnp.log(l)
    lse_ref[0] = jnp.concatenate([lse[:, :tq], lse[:, tq:]], axis=0)

def attn_fwd(bounds, q, qaug, k, kaug, v, *, tq=512, tk=768):
    T, D = q.shape
    S = k.shape[0]
    pairs = D // 128
    return pl.pallas_call(
        functools.partial(fwd_kernel, tk),
        out_shape=(jax.ShapeDtypeStruct((D, T), F32), jax.ShapeDtypeStruct((pairs, 2, T), F32)),
        grid_spec=pltpu.PrefetchScalarGridSpec(
            num_scalar_prefetch=1, grid=(pairs, T // tq),
            in_specs=[pl.BlockSpec((tq, 128), lambda h, i, b: (i, h)),
                      pl.BlockSpec((tq, 128), lambda h, i, b: (i, 0)),
                      pl.BlockSpec((S, 128), lambda h, i, b: (0, h)),
                      pl.BlockSpec((S, 128), lambda h, i, b: (0, 0)),
                      pl.BlockSpec((S, 128), lambda h, i, b: (0, h))],
            out_specs=(pl.BlockSpec((128, tq), lambda h, i, b: (h, i)),
                       pl.BlockSpec((1, 2, tq), lambda h, i, b: (h, 0, i))),
            scratch_shapes=[pltpu.VMEM((S, 2 * tq), F32), pltpu.VMEM((128, 2 * tq), F32)]),
        name="attend",
    )(bounds, q, qaug, k, kaug, v)

def bwd_kernel(tk, bounds, q_ref, qaug_ref, do_ref, lse_ref, ot_ref, k_ref, kaug_ref, v_ref,
               dq_ref, dk_ref, dv_ref, dk_acc, dv_acc, dq_acc):
    qi = pl.program_id(1)
    start, count = bounds[qi, 0], bounds[qi, 1]
    tq = q_ref.shape[0]

    @pl.when(qi == 0)
    def _():
        dk_acc[...] = jnp.zeros_like(dk_acc)
        dv_acc[...] = jnp.zeros_like(dv_acc)

    qs = stack_heads(q_ref[...])
    qrhs = stack_heads(q_ref[...], qaug_ref[...])
    dos = stack_heads(do_ref[...])
    lse = jnp.concatenate([lse_ref[0, 0:1, :], lse_ref[0, 1:2, :]], axis=1)
    mixed = ot_ref[...] * do_ref[...].astype(F32).T
    delta = jnp.concatenate(
        [jnp.sum(mixed[:64], axis=0, keepdims=True), jnp.sum(mixed[64:], axis=0, keepdims=True)], axis=1
    )
    dq_acc[...] = jnp.zeros_like(dq_acc)

    def step(loc, off, size, carry):
        rows = pl.ds(off, size)
        lhs = jnp.concatenate([k_ref[rows, :], kaug_ref[rows, :]], axis=1)
        x = lax.dot_general(lhs, qrhs, NT, preferred_element_type=F32)
        y = lax.dot_general(v_ref[rows, :], dos, NT, preferred_element_type=F32)
        p = jnp.exp(x - lse)
        ds = (p * (y - delta)).astype(BF)
        pb = p.astype(BF)
        dv_acc[rows, :] += lax.dot_general(pb, dos, NN, preferred_element_type=F32)
        dk_acc[rows, :] += lax.dot_general(ds, qs, NN, preferred_element_type=F32)
        dq_acc[...] += lax.dot_general(k_ref[rows, :], ds, TN, preferred_element_type=F32)
        return carry

    two_level(start, count, tk, step, 0)
    dq_ref[...] = (pick_heads(dq_acc[...], tq) * SCALE).T.astype(BF)

    @pl.when(qi == pl.num_programs(1) - 1)
    def _():
        dk_ref[...] = dk_acc[...].astype(BF)
        dv_ref[...] = dv_acc[...].astype(BF)

def attn_bwd(bounds, q, qaug, do, lse, ot, k, kaug, v, *, tq=512, tk=768):
    T, D = q.shape
    S = k.shape[0]
    pairs = D // 128
    row = lambda h, i, b: (h, 0, i)
    return pl.pallas_call(
        functools.partial(bwd_kernel, tk),
        out_shape=(jax.ShapeDtypeStruct((T, D), BF), jax.ShapeDtypeStruct((S, D), BF), jax.ShapeDtypeStruct((S, D), BF)),
        grid_spec=pltpu.PrefetchScalarGridSpec(
            num_scalar_prefetch=1, grid=(pairs, T // tq),
            in_specs=[pl.BlockSpec((tq, 128), lambda h, i, b: (i, h)),
                      pl.BlockSpec((tq, 128), lambda h, i, b: (i, 0)),
                      pl.BlockSpec((tq, 128), lambda h, i, b: (i, h)),
                      pl.BlockSpec((1, 2, tq), row),
                      pl.BlockSpec((128, tq), lambda h, i, b: (h, i)),
                      pl.BlockSpec((S, 128), lambda h, i, b: (0, h)),
                      pl.BlockSpec((S, 128), lambda h, i, b: (0, 0)),
                      pl.BlockSpec((S, 128), lambda h, i, b: (0, h))],
            out_specs=(pl.BlockSpec((tq, 128), lambda h, i, b: (i, h)),
                       pl.BlockSpec((S, 128), lambda h, i, b: (0, h)),
                       pl.BlockSpec((S, 128), lambda h, i, b: (0, h))),
            scratch_shapes=[pltpu.VMEM((S, 128), F32), pltpu.VMEM((S, 128), F32), pltpu.VMEM((128, 2 * tq), F32)]),
        name="attend_back",
    )(bounds, q, qaug, do, lse, ot, k, kaug, v)


def reach(n_ctx):
    return n_ctx // 2


def finish_kernel(sources, n_parts, *refs):
    parts = refs[:n_parts]
    (vec_ref, dk_ref, dv_ref, tok_ref, dq_ref, w_ref, own_in_ref, mine_tok_ref,
     out_ref, vec_out, wide_out, grad_ref,
     mine, buf_a, buf_h, buf_b, buf_s, buf_c, buf_d, buf_e, gbf,
     sums, heard, line,
     loads, weights, acc, dq, own, bias,
     run_part, from_x, from_z, far_z, last_x,
     sem_l, sem_a, sem_b, sem_c, sem_d, sem_v, sem_x, sem_z, sem_far, sem_load, sem_in) = refs[n_parts:]
    n_ready = len(sources)
    n_chunks = out_ref.shape[0]
    n_ctx, n_wsh = lax.axis_size("ctx"), lax.axis_size("wsh")
    zs = n_ctx // 2
    a, w = lax.axis_index("ctx"), lax.axis_index("wsh")
    z, x = a // 2, lax.rem(a, 2)
    y, c = w // 2, lax.rem(w, 2)
    core_peer = (a, y * 2 + (1 - c))
    y_peer = (a, (1 - y) * 2 + c)
    x_peer = (z * 2 + (1 - x), w)
    low, high = lax.rem(z, 2), z // 2
    pair_peer = ((z + 1 - 2 * low) * 2 + x, w)
    skip_peer = (lax.rem(z + 2, zs) * 2 + x, w)
    up_peer, down_peer = (a + 2, w), (a - 2, w)
    near = reach(n_ctx)
    hops = near // 2
    MESH = pl.DeviceIdType.MESH

    rows = out_ref.shape[1]
    half = out_ref.shape[2] // 2
    piece = rows // zs
    tall = own.shape[0]
    cut = from_x.shape[1]

    def z_peer(d):
        return (lax.rem(z + d, zs) * 2 + x, w)

    barrier = pltpu.get_barrier_semaphore()
    for dev in [core_peer, y_peer, x_peer] + [z_peer(d) for d in range(1, zs)]:
        pl.semaphore_signal(barrier, inc=1, device_id=dev, device_id_type=MESH)
    pl.semaphore_wait(barrier, zs + 2)

    def send(src, dst, sems, idx, dev):
        return pltpu.make_async_remote_copy(
            src_ref=src, dst_ref=dst, send_sem=sems.at[(0,) + idx], recv_sem=sems.at[(1,) + idx],
            device_id=dev, device_id_type=MESH)

    def wait_in(ref, sems, idx):
        send(ref, ref, sems, idx, core_peer).wait_recv()

    def wait_out(ref, sems, idx):
        send(ref, ref, sems, idx, core_peer).wait_send()

    def distance(i):
        return (hops - i // 4) * (1 - 2 * lax.rem(i // 2, 2))

    def position(i):
        dz = distance(i)
        mine_too = lax.rem(i, 2)
        run = 2 * (z + dz) + (1 - x) * (1 - mine_too) + x * mine_too
        return run, mine_too, (z + dz >= 0) & (z + dz < zs) & (jnp.abs(run - a) <= near)

    n_pos = 4 * hops + 2

    def load(i):
        run, _mine_too, there = position(i)
        return there, [
            pltpu.make_async_copy(src.at[run], loads.at[lax.rem(i, 2), j], sem_load.at[lax.rem(i, 2), j])
            for j, src in enumerate((dk_ref, dv_ref, tok_ref))
        ]

    def load_start(i):
        there, copies = load(i)

        @pl.when(there & (i < n_pos))
        def _():
            for copy in copies:
                copy.start()

    def share(k, owner):
        if k < n_ready:
            p, row0, col0 = sources[k]
            return parts[p].at[owner, pl.ds(row0, rows), pl.ds(col0, 2 * half)]
        return gbf.at[k - n_ready, owner]

    def share_load(k):
        for yy in range(2):
            pltpu.make_async_copy(share(k, yy * 2 + c), mine.at[k % 4, yy], sem_l.at[k]).start()

    def share_send(k):
        for yy in range(2):
            send(share(k, yy * 2 + (1 - c)), buf_a.at[k, yy], sem_a, (k,), core_peer).start()

    load_start(0)
    fetch = [pltpu.make_async_copy(w_ref, weights, sem_in.at[0]), pltpu.make_async_copy(dq_ref, dq, sem_in.at[1]),
             pltpu.make_async_copy(own_in_ref, own, sem_in.at[2])]
    for copy in fetch:
        copy.start()
    for k in range(n_ready):
        share_send(k)
        if k < 4:
            share_load(k)
    acc[...] = jnp.zeros_like(acc)
    bias[...] = jnp.zeros_like(bias)
    fetch[0].wait()

    near_rows, far_rows = pl.ds(0, cut), pl.ds(cut, tall - cut)

    def unit(i):
        run, mine_too, there = position(i)
        at = lax.rem(i, 2)
        load_start(i + 1)

        @pl.when(there)
        def _():
            for copy in load(i)[1]:
                copy.wait()

            def tokens_part(r, carry):
                rs = pl.ds(pl.multiple_of(r * 128, 128), 128)
                g = lax.dot_general(loads[at, 0, rs, :], weights[0], NT, preferred_element_type=F32)
                g = g + lax.dot_general(loads[at, 1, rs, :], weights[1], NT, preferred_element_type=F32)
                run_part[i, rs, :] = g.astype(BF)
                bias[0:8, :] += jnp.sum(loads[at, 1, rs, :].astype(F32).reshape(16, 8, 2 * half), axis=0)
                return carry

            lax.fori_loop(0, tall // 128, tokens_part, 0)

            @pl.when(mine_too == 0)
            def _():
                send(run_part.at[i, near_rows, :], from_x.at[i // 2], sem_x, (i // 2,), x_peer).start()

            @pl.when(i < 4)
            def _():
                far_send(i)

            def weights_part(r, carry):
                fs = pl.ds(pl.multiple_of(r * 256, 256), 256)
                flipped = loads[at, 2, :, fs].T
                for j in range(2):
                    acc[j, fs, :] += lax.dot_general(flipped, loads[at, j], NN, preferred_element_type=F32)
                return carry

            lax.fori_loop(0, 2 * half // 256, weights_part, 0)

    def from_below(i):
        dz = distance(i)
        step = 1 - 2 * lax.rem(i // 2, 2)
        sender, target = z - step, z - step + dz
        side = jnp.abs(2 * dz + (1 - 2 * x) * (1 - lax.rem(i, 2))) <= near
        return (sender >= 0) & (sender < zs) & (target >= 0) & (target < zs) & side

    def toward(i, copy_of):
        step = 1 - 2 * lax.rem(i // 2, 2)

        @pl.when(step == 1)
        def _():
            copy_of(up_peer).start()

        @pl.when(step == -1)
        def _():
            copy_of(down_peer).start()

    def far_send(i):
        toward(i, lambda dev: send(run_part.at[i, far_rows, :], far_z.at[i], sem_far, (i,), dev))

    def far_pass(i):
        _run, _mine_too, there = position(i)

        @pl.when(there)
        def _():
            @pl.when(from_below(i - 4))
            def _():
                wait_in(far_z.at[i - 4], sem_far, (i - 4,))
                run_part[i, far_rows, :] = (
                    run_part[i, far_rows, :].astype(F32) + far_z[i - 4].astype(F32)).astype(BF)

            far_send(i)

    def far_end():
        for col in range(2):
            total = n_pos - 2 + col
            for src in (4 + col, 6 + col):
                @pl.when(from_below(src))
                def _():
                    wait_in(far_z.at[src], sem_far, (src,))
                    run_part[total, far_rows, :] = (
                        run_part[total, far_rows, :].astype(F32) + far_z[src].astype(F32)).astype(BF)
            if col == 0:
                send(run_part.at[total, far_rows, :], last_x, sem_x, (n_pos // 2,), x_peer).start()
        own[far_rows, :] += run_part[n_pos - 1, far_rows, :].astype(F32)

    def near_pass(n):
        dz = distance(2 * n)
        i = 2 * n + 1

        @pl.when((z + dz >= 0) & (z + dz < zs))
        def _():
            @pl.when(jnp.abs(2 * dz + 2 * x - 1) <= near)
            def _():
                wait_in(from_x.at[n], sem_x, (n,))
                run_part[i, near_rows, :] = (
                    run_part[i, near_rows, :].astype(F32) + from_x[n].astype(F32)).astype(BF)

            @pl.when((n >= 2) & from_below(i - 4))
            def _():
                wait_in(from_z.at[n - 2], sem_z, (n - 2,))
                run_part[i, near_rows, :] = (
                    run_part[i, near_rows, :].astype(F32) + from_z[n - 2].astype(F32)).astype(BF)

            toward(i, lambda dev: send(run_part.at[i, near_rows, :], from_z.at[n], sem_z, (n,), dev))

    def near_own():
        n = n_pos // 2 - 1
        wait_in(from_x.at[n], sem_x, (n,))
        own[near_rows, :] += run_part[n_pos - 1, near_rows, :].astype(F32) + from_x[n].astype(F32)

    def near_end():
        for n in (2, 3):
            @pl.when(from_below(2 * n + 1))
            def _():
                wait_in(from_z.at[n], sem_z, (n,))
                own[near_rows, :] += from_z[n].astype(F32)

    def add(p, q):
        return (p.astype(F32) + q.astype(F32)).astype(BF)

    def column(side):
        return pl.ds(pl.multiple_of(side * half, 128), half)

    def band(start, size):
        return pl.ds(pl.multiple_of(start, 16), size)

    def stage_b(k):
        at = lax.rem(k, 4)
        pltpu.make_async_copy(mine.at[at], mine.at[at], sem_l.at[k]).wait()
        wait_in(buf_a.at[k], sem_a, (k,))
        buf_h[k] = add(mine[at, 1 - y], buf_a[k, 1 - y])
        send(buf_h.at[k], buf_b.at[k], sem_b, (k,), y_peer).start()
        buf_a[k, y] = add(mine[at, y], buf_a[k, y])

    def stage_c(k):
        wait_in(buf_b.at[k], sem_b, (k,))
        buf_s[k] = add(buf_a[k, y, :, column(1 - x)], buf_b[k, :, column(1 - x)])
        send(buf_s.at[k], buf_c.at[k], sem_c, (0, k), x_peer).start()

    my_two, other_two = band(low * 2 * piece, 2 * piece), band((1 - low) * 2 * piece, 2 * piece)
    my_one, other_one = band(high * piece, piece), band((1 - high) * piece, piece)
    my_rows = band(low * 2 * piece + high * piece, piece)

    def stage_d(k):
        wait_in(buf_c.at[k], sem_c, (0, k))
        cols = column(x)
        joined = buf_a[k, y, :, cols].astype(F32) + buf_b[k, :, cols].astype(F32) + buf_c[k].astype(F32)
        buf_c[k] = joined.astype(BF)
        send(buf_c.at[k, other_two, :], buf_d.at[k], sem_d, (0, k), pair_peer).start()

    def stage_d2(k):
        wait_in(buf_d.at[k], sem_d, (0, k))
        buf_d[k] = add(buf_d[k], buf_c[k, my_two, :])
        send(buf_d.at[k, other_one, :], buf_e.at[k], sem_d, (1, k), skip_peer).start()

    def stage_e(k):
        wait_in(buf_e.at[k], sem_d, (1, k))
        buf_e[k] = add(buf_e[k], buf_d[k, my_one, :])
        out_ref[k, my_rows, column(x)] = buf_e[k]
        send(buf_e.at[k], out_ref.at[k, my_rows, column(x)], sem_d, (2, k), skip_peer).start()

    def stage_e2(k):
        wait_in(buf_e.at[k], sem_d, (2, k))
        there = out_ref.at[k, my_two, column(x)]
        send(there, there, sem_d, (3, k), pair_peer).start()

    def stage_f(k):
        wait_in(buf_d.at[k], sem_d, (3, k))
        there = out_ref.at[k, :, column(x)]
        send(there, there, sem_c, (1, k), x_peer).start()

    def guarded(fn, k, first, last):
        @pl.when((k >= first) & (k < last))
        def _():
            fn(k)

    def chunk_step(m):
        for lag, stage in enumerate((stage_c, stage_d, stage_d2, stage_e, stage_e2, stage_f)):
            guarded(stage, m - (lag and lag + 5), 0, n_chunks)

    def first_step(t, carry):
        guarded(unit, t, 0, n_pos)
        for j in range(2):
            guarded(stage_b, 2 * t + j, 0, n_ready)
        for k in range(4, n_ready):
            @pl.when(t == (k - 4) // 2)
            def _():
                share_load(k)

        @pl.when(lax.rem(t, 2) == 1)
        def _():
            guarded(near_pass, t // 2 - 1, 0, 4)

        guarded(far_pass, t - 2, 4, 8)

        @pl.when((lax.rem(t, 2) == 0) & (t >= 2))
        def _():
            chunk_step(t // 2 - 1)

        return carry

    lax.fori_loop(0, n_pos, first_step, 0)
    done = n_pos // 2 - 1

    fetch[1].wait()
    fetch[2].wait()
    own_tok = pltpu.make_async_copy(mine_tok_ref, loads.at[0, 2], sem_load.at[0, 2])
    own_tok.start()

    def to_bf(j, target):
        for owner in range(n_wsh):
            gbf[target, owner] = acc[j, owner * rows : (owner + 1) * rows, :].astype(BF)
        share_load(n_ready + target)
        share_send(n_ready + target)

    to_bf(0, 0)
    to_bf(1, 1)
    own_tok.wait()

    def query_part(r, carry):
        fs = pl.ds(pl.multiple_of(r * 256, 256), 256)
        acc[0, fs, :] = lax.dot_general(loads[0, 2, :, fs].T, dq[...], NN, preferred_element_type=F32)
        return carry

    lax.fori_loop(0, 2 * half // 256, query_part, 0)
    to_bf(0, 2)

    def query_tokens(r, carry):
        rs = pl.ds(pl.multiple_of(r * 128, 128), 128)
        own[rs, :] += lax.dot_general(dq[rs, :], weights[2], NT, preferred_element_type=F32)
        bias[8:16, :] += jnp.sum(dq[rs, :].astype(F32).reshape(16, 8, 2 * half), axis=0)
        return carry

    lax.fori_loop(0, tall // 128, query_tokens, 0)

    sums[0] = vec_ref[...]
    sums[0, 0:1, :] = jnp.sum(bias[8:16, :], axis=0, keepdims=True)
    sums[0, 1:2, :] = jnp.sum(bias[0:8, :], axis=0, keepdims=True)
    pair = (core_peer, y_peer, x_peer)

    def vec_send(stage):
        send(sums.at[stage], heard.at[stage], sem_v, (stage,), pair[stage]).start()

    def vec_stage(stage):
        wait_in(heard.at[stage], sem_v, (stage,))
        total = sums[stage] + heard[stage]
        sums[stage + 1] = total
        if stage < 2:
            vec_send(stage + 1)
        else:
            line[z] = total
            for d in range(1, zs):
                send(sums.at[3], line.at[z], sem_v, (3,), z_peer(d)).start()

    def vec_last():
        wait_in(line.at[pl.ds(0, zs - 1)], sem_v, (3,))
        total = line[0]
        for d in range(1, zs):
            total = total + line[d]
        small, wide = total[0:8, 0:rows], total[8:9, :]
        for owner in range(1, n_wsh):
            small = jnp.where(w == owner, total[0:8, owner * rows : (owner + 1) * rows], small)
            wide = jnp.where(w == owner, total[8 + owner : 9 + owner, :], wide)
        vec_out[...] = small
        wide_out[...] = wide

    vec_send(0)

    def second_step(m, carry):
        guarded(stage_b, m - done + n_ready, n_ready, n_chunks)
        chunk_step(m)
        guarded(lambda k: near_own(), m - done, 0, 1)
        for stage in range(3):
            guarded(lambda k: vec_stage(stage), m - done - 1 - stage, 0, 1)
        guarded(lambda k: near_end(), m - done - 3, 0, 1)
        guarded(lambda k: far_end(), m - done - 4, 0, 1)
        guarded(lambda k: vec_last(), m - done - 5, 0, 1)
        return carry

    lax.fori_loop(done, n_chunks + 10, second_step, 0)
    wait_in(last_x, sem_x, (n_pos // 2,))
    own[far_rows, :] += last_x[...].astype(F32)
    grad_ref[...] = own[...].astype(BF)

    def drain(k, carry):
        wait_in(buf_s.at[k], sem_c, (1, k))
        wait_out(buf_a.at[k], sem_a, (k,))
        wait_out(buf_b.at[k], sem_b, (k,))
        wait_out(buf_s.at[k], sem_c, (0, k))
        wait_out(buf_s.at[k], sem_c, (1, k))
        wait_out(buf_d.at[k], sem_d, (0, k))
        wait_out(buf_e.at[k], sem_d, (1, k))
        wait_out(buf_e.at[k], sem_d, (2, k))
        wait_out(buf_d.at[k], sem_d, (3, k))
        return carry

    lax.fori_loop(0, n_chunks, drain, 0)
    for stage in range(3):
        wait_out(heard.at[stage], sem_v, (stage,))
    wait_out(line.at[pl.ds(0, zs - 1)], sem_v, (3,))
    wait_out(last_x, sem_x, (n_pos // 2,))

    def drain_runs(i, carry):
        _run, mine_too, there = position(i)

        @pl.when(there)
        def _():
            wait_out(far_z.at[i], sem_far, (i,))

            @pl.when(mine_too == 1)
            def _():
                wait_out(from_z.at[i // 2], sem_z, (i // 2,))

        return carry

    lax.fori_loop(0, n_pos - 2, drain_runs, 0)

    def drain_x(n, carry):
        _run, _mine_too, there = position(2 * n)

        @pl.when(there)
        def _():
            wait_out(from_x.at[n], sem_x, (n,))

        return carry

    lax.fori_loop(0, n_pos // 2, drain_x, 0)


def finish(matrices, vec, grad_k, grad_v, all_tokens, grad_q, kvq_w, own_grad, inputs):
    n_ctx, n_wsh = lax.axis_size("ctx"), lax.axis_size("wsh")
    zs, hops = n_ctx // 2, reach(n_ctx) // 2
    rows = D // n_wsh
    parts, sources, spans = [], [], []
    for p, g in enumerate(matrices):
        down, across = g.shape[0] // D, g.shape[1] // D
        parts.append(g.astype(BF).reshape(n_wsh, down * rows, across * D))
        spans.append((len(sources), down, across))
        sources += [(p, r * rows, col * D) for r in range(down) for col in range(across)]
    n = len(sources) + 3
    spans += [(len(sources) + j, 1, 1) for j in range(3)]
    half, piece, tall = D // 2, rows // zs, inputs.shape[0]
    n_pos, cut = 4 * hops + 2, tall // 2
    vm, dma, shape = pltpu.VMEM, pltpu.SemaphoreType.DMA, jax.ShapeDtypeStruct
    any_spec = pl.BlockSpec(memory_space=pl.ANY)
    vm_spec = pl.BlockSpec(memory_space=pltpu.VMEM)
    summed, small, wide, grad_own = pl.pallas_call(
        functools.partial(finish_kernel, sources, len(parts)),
        out_shape=(shape((n, rows, D), BF), shape((8, rows), F32), shape((1, D), F32), shape((tall, D), BF)),
        in_specs=[any_spec] * len(parts) + [vm_spec] + [any_spec] * 7,
        out_specs=(vm_spec,) * 4,
        scratch_shapes=[
            vm((4, 2, rows, D), BF), vm((n, 2, rows, D), BF), vm((n, rows, D), BF), vm((n, rows, D), BF),
            vm((n, rows, half), BF), vm((n, rows, half), BF), vm((n, 2 * piece, half), BF), vm((n, piece, half), BF),
            vm((3, n_wsh, rows, D), BF),
            vm((4,) + vec.shape, F32), vm((3,) + vec.shape, F32), vm((zs,) + vec.shape, F32),
            vm((2, 3, tall, D), BF), vm((3, D, D), BF), vm((2, D, D), F32), vm((tall, D), BF), vm((tall, D), F32),
            vm((16, D), F32),
            vm((n_pos, tall, D), BF), vm((n_pos // 2, cut, D), BF), vm((4, cut, D), BF),
            vm((n_pos - 2, tall - cut, D), BF), vm((tall - cut, D), BF),
            dma((n,)), dma((2, n)), dma((2, n)), dma((2, 2, n)), dma((2, 4, n)), dma((2, 4)),
            dma((2, n_pos // 2 + 1)), dma((2, 4)), dma((2, n_pos - 2)), dma((2, 3)), dma((3,)),
        ],
        compiler_params=pltpu.CompilerParams(collective_id=2, has_side_effects=True, vmem_limit_bytes=63 * 2**20),
        name="finish",
    )(*parts, vec, grad_k, grad_v, all_tokens, grad_q, kvq_w, own_grad, inputs)
    sums = []
    for first, down, across in spans:
        block = summed[first : first + down * across]
        if across > 1:
            block = jnp.concatenate([block[i] for i in range(across)], axis=1)
        sums.append(block.reshape(down * rows, across * D).astype(F32))
    return sums, small, wide, grad_own


def gather_kernel(cut, tok_ref, vec_ref, wk_ref, wv_ref, wq_ref,
                  tok_out, k_out, v_out, q_out, w_out, vec_out,
                  tok, kbuf, vbuf, qbuf, wbuf, vecs,
                  sem_in, sem_out, sem_w, sem_l, sem_o):
    n_ctx = lax.axis_size("ctx")
    zs = n_ctx // 2
    a, w = lax.axis_index("ctx"), lax.axis_index("wsh")
    z, x = a // 2, lax.rem(a, 2)
    y, c = w // 2, lax.rem(w, 2)
    core_peer = (a, y * 2 + (1 - c))
    y_peer = (a, (1 - y) * 2 + c)
    x_peer = (z * 2 + (1 - x), w)
    up, down = (a + 2, w), (a - 2, w)
    near = reach(n_ctx)
    MESH = pl.DeviceIdType.MESH
    n_slices = sem_in.shape[1]
    tall = tok.shape[1] // n_slices
    own = wk_ref.shape[0]
    far = 4 * (near // 2 + 1)

    barrier = pltpu.get_barrier_semaphore()
    around = [(lax.rem(z + d, zs) * 2 + x, w) for d in (1, zs - 1)]
    for dev in [core_peer, y_peer, x_peer] + around:
        pl.semaphore_signal(barrier, inc=1, device_id=dev, device_id_type=MESH)
    pl.semaphore_wait(barrier, 5)

    def relative(u):
        dz = (u // 4) * (1 - 2 * lax.rem(u, 2))
        other = lax.rem(u // 2, 2)
        run = 2 * (z + dz) + (x + other - 2 * x * other)
        there = (z + dz >= 0) & (z + dz < zs) & (jnp.abs(run - a) <= near) & ((u >= 4) | (lax.rem(u, 2) == 0))
        return run, dz, other, there

    def rows(s):
        return pl.ds(pl.multiple_of(s * tall, tall), tall)

    def remote(src, dst, send_sem, recv_sem, dev):
        return pltpu.make_async_remote_copy(
            src_ref=src, dst_ref=dst, send_sem=send_sem, recv_sem=recv_sem, device_id=dev, device_id_type=MESH)

    def routes(u, s):
        run, dz, other, there = relative(u)
        z_first = s < cut
        to_x = there & (z_first | (dz == 0)) & (other == 0) & (jnp.abs(run - x_peer[0]) <= near)
        along = there & ((other == 0) | jnp.logical_not(z_first))
        to_up = along & (dz <= 0) & (z + 1 < zs) & (jnp.abs(run - (a + 2)) <= near)
        to_down = along & (dz >= 0) & (z > 0) & (jnp.abs(run - (a - 2)) <= near)
        return run, ((0, x_peer, to_x), (1, up, to_up), (2, down, to_down))

    def pass_on(u, s):
        run, where = routes(u, s)
        for d, dev, ok in where:
            @pl.when(ok)
            def _():
                source = tok_ref if isinstance(u, int) and u == 0 else tok.at[run]
                remote(source.at[rows(s), :], tok.at[run, rows(s), :], sem_out.at[d, u, s], sem_in.at[run, s], dev).start()

    def await_slice(u, s):
        run, _dz, _other, there = relative(u)

        @pl.when(there)
        def _():
            remote(tok.at[run, rows(s), :], tok.at[run, rows(s), :], sem_out.at[0, 0, 0], sem_in.at[run, s], x_peer).wait_recv()

    def start_own(s, carry):
        pass_on(0, s)
        return carry

    def weight_rows(owner):
        return pl.ds(pl.multiple_of(owner * own, 16), own)

    vec_own = vecs.at[w]
    remote(vec_ref, vec_own, sem_w.at[0, 0, 3], sem_w.at[1, 0, 3], core_peer).start()
    remote(vec_ref, vec_own, sem_w.at[0, 1, 3], sem_w.at[1, 1, 3], y_peer).start()
    pltpu.make_async_copy(vec_ref, vec_own, sem_l.at[3]).start()
    for m, ref in enumerate((wk_ref, wv_ref, wq_ref)):
        there = wbuf.at[m, weight_rows(w), :]
        remote(ref, there, sem_w.at[0, 1, m], sem_w.at[1, 1, m], y_peer).start()
        remote(ref, there, sem_w.at[0, 0, m], sem_w.at[1, 0, m], core_peer).start()
        pltpu.make_async_copy(ref, there, sem_l.at[m]).start()
    lax.fori_loop(0, n_slices, start_own, 0)
    pltpu.make_async_copy(tok_ref, tok.at[a], sem_l.at[4]).start()

    for j in range(n_ctx):
        @pl.when(jnp.abs(j - a) > near)
        def _():
            tok[j] = jnp.zeros_like(tok[j])

    def shard(m, owner):
        return vecs.at[owner] if m == 3 else wbuf.at[m, weight_rows(owner), :]

    def weight_arrival(m, kind):
        part = shard(m, w)
        return remote(part, part, sem_w.at[0, kind, m], sem_w.at[1, kind, m], core_peer)

    across = (1 - y) * 2 + c

    def weight_forward(m):
        weight_arrival(m, 1).wait_recv()
        remote(shard(m, across), shard(m, across), sem_w.at[0, 2, m], sem_w.at[1, 2, m], core_peer).start()

    def weight_end(m):
        weight_arrival(m, 0).wait_recv()
        weight_arrival(m, 2).wait_recv()
        pltpu.make_async_copy(shard(m, w), shard(m, w), sem_l.at[m]).wait()

    def relay(first, last):
        def one(i, carry):
            s = i // (last - first)
            u = first + lax.rem(i, last - first)
            await_slice(u, s)
            pass_on(u, s)
            return carry

        lax.fori_loop(0, n_slices * (last - first), one, 0)

    relay(2, 6)
    weight_forward(3)
    weight_forward(0)
    weight_forward(1)
    weight_end(3)
    total = vecs[0].astype(F32)
    for owner in range(1, 4):
        total = total + vecs[owner].astype(F32)
    vec_out[...] = total
    pltpu.make_async_copy(tok_ref, tok.at[a], sem_l.at[4]).wait()
    weight_end(0)
    weight_end(1)

    step_rows = 128
    steps = tok.shape[1] // step_rows

    def query_part(i, carry):
        r = pl.ds(pl.multiple_of(i * step_rows, step_rows), step_rows)
        q = (jnp.dot(tok[a, r, :], wbuf[2], preferred_element_type=F32) + vec_out[0:1, :]).astype(BF)
        qbuf[r, :] = q * jnp.asarray(SCALE, BF)
        return carry

    def project(u, carry):
        run, _dz, _other, there = relative(u)

        @pl.when(u == 6)
        def _():
            weight_forward(2)
            weight_end(2)
            lax.fori_loop(0, steps, query_part, 0)
            pltpu.make_async_copy(qbuf, q_out, sem_l.at[5]).start()
            relay(6, 10)

        @pl.when(there)
        def _():
            @pl.when(u >= 10)
            def _():
                def one(s, carry):
                    await_slice(u, s)
                    return carry

                lax.fori_loop(0, n_slices, one, 0)

            def part(i, carry):
                r = pl.ds(pl.multiple_of(i * step_rows, step_rows), step_rows)
                t = tok[run, r, :]
                kbuf[run, r, :] = jnp.dot(t, wbuf[0], preferred_element_type=F32).astype(BF)
                vbuf[run, r, :] = (jnp.dot(t, wbuf[1], preferred_element_type=F32) + vec_out[1:2, :]).astype(BF)
                return carry

            lax.fori_loop(0, steps, part, 0)
            for i, (src, dst) in enumerate(((kbuf, k_out), (vbuf, v_out), (tok, tok_out))):
                pltpu.make_async_copy(src.at[run], dst.at[run], sem_o.at[i, run]).start()

        return carry

    for j in range(n_ctx):
        @pl.when(jnp.abs(j - a) > near)
        def _():
            kbuf[j] = jnp.zeros_like(kbuf[j])
            vbuf[j] = jnp.zeros_like(vbuf[j])
            for i, (src, dst) in enumerate(((kbuf, k_out), (vbuf, v_out), (tok, tok_out))):
                pltpu.make_async_copy(src.at[j], dst.at[j], sem_o.at[i, j]).start()

    lax.fori_loop(0, far, project, 0)

    pltpu.make_async_copy(wbuf, w_out, sem_l.at[6]).start()

    for m in range(4):
        for kind in range(3):
            weight_arrival(m, kind).wait_send()

    def drain(i, carry):
        s = i // far
        u = lax.rem(i, far)
        run, where = routes(u, s)
        for d, dev, ok in where:
            @pl.when(ok & (u < 10))
            def _():
                remote(tok.at[run, rows(s), :], tok.at[run, rows(s), :], sem_out.at[d, u, s], sem_in.at[run, s], dev).wait_send()
        return carry

    lax.fori_loop(0, n_slices * far, drain, 0)
    for j in range(n_ctx):
        for i, (src, dst) in enumerate(((kbuf, k_out), (vbuf, v_out), (tok, tok_out))):
            pltpu.make_async_copy(src.at[j], dst.at[j], sem_o.at[i, j]).wait()
    pltpu.make_async_copy(qbuf, q_out, sem_l.at[5]).wait()
    pltpu.make_async_copy(wbuf, w_out, sem_l.at[6]).wait()


def gather_project(inputs, vec, key_weight, value_weight, query_weight):
    n_ctx, n_wsh = lax.axis_size("ctx"), lax.axis_size("wsh")
    tall = inputs.shape[0]
    n_slices = 8
    far = 4 * (reach(n_ctx) // 2 + 1)
    vm, dma = pltpu.VMEM, pltpu.SemaphoreType.DMA
    any_spec = pl.BlockSpec(memory_space=pl.ANY)
    vm_spec = pl.BlockSpec(memory_space=pltpu.VMEM)
    runs = (n_ctx, tall, D)
    shape = jax.ShapeDtypeStruct
    return pl.pallas_call(
        functools.partial(gather_kernel, 5),
        out_shape=(shape(runs, BF), shape(runs, BF), shape(runs, BF), shape((tall, D), BF), shape((3, D, D), BF),
                   shape(vec.shape, F32)),
        in_specs=[any_spec] * 5,
        out_specs=(any_spec,) * 5 + (vm_spec,),
        scratch_shapes=[
            vm(runs, BF), vm(runs, BF), vm(runs, BF), vm((tall, D), BF), vm((3, D, D), BF), vm((n_wsh,) + vec.shape, BF),
            dma((n_ctx, n_slices)), dma((3, far, n_slices)), dma((2, 3, 4)), dma((7,)), dma((3, n_ctx)),
        ],
        compiler_params=pltpu.CompilerParams(collective_id=1, has_side_effects=True, vmem_limit_bytes=48 * 2**20),
        name="gather_project",
    )(inputs, vec, key_weight, value_weight, query_weight)


def local(
    tokens,
    cotangent,
    doc_starts,
    query_weight,
    key_weight,
    value_weight,
    out_weight,
    up_weight,
    down_weight,
    query_bias,
    value_bias,
    out_bias,
    attn_gain,
    attn_shift,
    up_bias,
    down_bias,
    final_gain,
    final_shift,
):
    inputs = tokens[0]
    doc_start = doc_starts[0]
    tok_rows = inputs.shape[0]
    stream_rows = tok_rows * lax.axis_size("ctx")
    first_row = lax.axis_index("ctx") * tok_rows
    tile = min(tok_rows, 512)
    bounds = key_range(doc_start, first_row, tok_rows, stream_rows, tile)
    query_doc, key_doc = document_lanes(doc_start, first_row, tok_rows, stream_rows)

    n_ctx, n_wsh = lax.axis_size("ctx"), lax.axis_size("wsh")
    own = D // n_wsh

    def gather(x):
        return lax.all_gather(x, "wsh", axis=0, tiled=True)

    small = jnp.stack(
        [query_bias, value_bias, out_bias, attn_gain, attn_shift, down_bias, final_gain, final_shift]
    )
    fast = n_wsh == 4 and n_ctx == 8 and own % (n_ctx // 2 * 16) == 0 and tok_rows % 512 == 0
    if fast:
        w = lax.axis_index("wsh")
        at = lax.broadcasted_iota(jnp.int32, (8, D), 1) // own == w
        vec = jnp.where(at, jnp.tile(small, (1, n_wsh)), jnp.zeros((), BF))
        at = lax.broadcasted_iota(jnp.int32, (8, D), 0) == w
        vec = jnp.concatenate([vec, jnp.where(at, up_bias[None, :], jnp.zeros((), BF))], axis=0)
        all_tokens, keys, values, queries, kvq_w, vec = gather_project(
            inputs, vec, key_weight, value_weight, query_weight
        )
        all_tokens, keys, values = [r.reshape(stream_rows, D) for r in (all_tokens, keys, values)]
        key_w, value_w, query_w = kvq_w[0], kvq_w[1], kvq_w[2]
        query_b, value_b, out_b, attn_g, attn_s, down_b, final_g, final_s = [vec[i] for i in range(8)]
        up_b = vec[8 : 8 + n_wsh].reshape(-1)
    else:
        all_tokens = lax.all_gather(inputs, "ctx", axis=0, tiled=True)
        query_w, key_w, value_w = gather(query_weight), gather(key_weight), gather(value_weight)
        small = gather(small.T).astype(F32)
        query_b, value_b, out_b, attn_g, attn_s, down_b, final_g, final_s = [small[:, i] for i in range(8)]
        up_b = gather(up_bias).astype(F32)
        queries = jnp.dot(inputs, query_w, preferred_element_type=F32) + query_b
        queries = queries.astype(BF) * jnp.asarray(SCALE, BF)
        keys = jnp.dot(all_tokens, key_w, preferred_element_type=F32).astype(BF)
        values = (jnp.dot(all_tokens, value_w, preferred_element_type=F32) + value_b).astype(BF)
    out_w = gather(out_weight)
    up_w = gather(up_weight)
    down_w = gather(down_weight)

    mixed_t, log_rows = attn_fwd(bounds, queries, query_doc, keys, key_doc, values, tq=tile)
    attn_t = mixed_t.astype(BF)
    inputs_f = inputs.astype(F32)
    branch = lax.dot_general(attn_t, out_w, TN, preferred_element_type=F32) + out_b
    first_norm, first_pull = jax.vjp(layer_norm, inputs_f + branch, attn_g, attn_s)
    first_b = first_norm.astype(BF)
    up_f = jnp.dot(first_b, up_w, preferred_element_type=F32) + up_b
    act_f, act_pull = jax.vjp(gelu_act, up_f)
    act_b = act_f.astype(BF)
    down_f = jnp.dot(act_b, down_w, preferred_element_type=F32) + down_b
    final_f, final_pull = jax.vjp(layer_norm, first_norm + down_f, final_g, final_s)
    layer_out = final_f.astype(BF)

    grad_sum2, grad_final_g, grad_final_s = final_pull(cotangent[0].astype(F32))
    grad_down = grad_sum2.astype(BF)
    grad_down_w = jnp.einsum("tf,td->fd", act_b, grad_down, preferred_element_type=F32)
    grad_down_b = jnp.sum(grad_down.astype(F32), axis=0)
    grad_act = jnp.einsum("td,fd->tf", grad_down, down_w, preferred_element_type=F32)
    (grad_up_f,) = act_pull(grad_act)
    grad_up = grad_up_f.astype(BF)
    grad_up_w = jnp.einsum("td,tf->df", first_b, grad_up, preferred_element_type=F32)
    grad_up_b = jnp.sum(grad_up.astype(F32), axis=0)
    grad_first = grad_sum2 + jnp.einsum("tf,df->td", grad_up, up_w, preferred_element_type=F32)
    grad_sum1, grad_attn_g, grad_attn_s = first_pull(grad_first)
    grad_branch = grad_sum1.astype(BF)
    grad_out_w = jnp.dot(attn_t, grad_branch, preferred_element_type=F32)
    grad_out_b = jnp.sum(grad_branch.astype(F32), axis=0)
    grad_attn = jnp.einsum("te,de->td", grad_branch, out_w, preferred_element_type=F32).astype(BF)
    grad_q, grad_k, grad_v = attn_bwd(
        bounds, queries, query_doc, grad_attn, log_rows, mixed_t, keys, key_doc, values, tq=tile
    )
    def total(g):
        part = lax.psum_scatter(g.astype(BF), "wsh", scatter_dimension=0, tiled=True)
        return lax.psum(part, "ctx").astype(F32)

    if fast:
        none = jnp.zeros((D,), F32)
        vec = jnp.stack([none, none, grad_out_b, grad_attn_g, grad_attn_s, grad_down_b, grad_final_g, grad_final_s])
        vec = jnp.concatenate([vec, grad_up_b.reshape(n_wsh, -1), jnp.zeros((8 - n_wsh, D), F32)], axis=0)
        mats, small, wide, grad_inputs = finish(
            (grad_up_w, grad_out_w, grad_down_w), vec, grad_k.reshape(n_ctx, tok_rows, D),
            grad_v.reshape(n_ctx, tok_rows, D), all_tokens.reshape(n_ctx, tok_rows, D), grad_q, kvq_w, grad_sum1, inputs,
        )
        up_sum, out_sum, down_sum, key_sum, value_sum, query_sum = mats
        sums = [
            query_sum, key_sum, value_sum, out_sum, up_sum, down_sum, small[0], small[1], small[2], small[3], small[4],
            wide[0], small[5], small[6], small[7],
        ]
    else:
        grad_all = jnp.einsum("te,de->td", grad_k, key_w, preferred_element_type=F32)
        grad_all = grad_all + jnp.einsum("te,de->td", grad_v, value_w, preferred_element_type=F32)
        grad_own = lax.psum_scatter(grad_all.astype(BF), "ctx", scatter_dimension=0, tiled=True)
        grad_query_w = jnp.einsum("td,te->de", inputs, grad_q, preferred_element_type=F32)
        grad_key_w = jnp.einsum("td,te->de", all_tokens, grad_k, preferred_element_type=F32)
        grad_value_w = jnp.einsum("td,te->de", all_tokens, grad_v, preferred_element_type=F32)
        grad_query_b = jnp.sum(grad_q.astype(F32), axis=0)
        grad_value_b = jnp.sum(grad_v.astype(F32), axis=0)
        grad_inputs = grad_sum1 + jnp.einsum("te,de->td", grad_q, query_w, preferred_element_type=F32)
        grad_inputs = grad_inputs + grad_own.astype(F32)
        sums = [
            total(g)
            for g in (
                grad_query_w, grad_key_w, grad_value_w, grad_out_w, grad_up_w, grad_down_w,
                grad_query_b, grad_value_b, grad_out_b, grad_attn_g, grad_attn_s, grad_up_b,
                grad_down_b, grad_final_g, grad_final_s,
            )
        ]
    return (
        layer_out.reshape(1, tok_rows, D),
        grad_inputs.astype(BF).reshape(1, tok_rows, D),
        *sums,
    )


def solution(mesh):
    rows, mat, vec = P("wsh", "ctx", None), P("wsh", None), P("wsh")
    return jax.shard_map(
        local,
        mesh=mesh,
        in_specs=(rows, rows, mat) + (mat,) * 6 + (vec,) * 9,
        out_specs=(rows, rows) + (mat,) * 6 + (vec,) * 9,
        check_vma=False,
    )
```

```python
import functools

import jax
import jax.numpy as jnp
from jax import lax
from jax.experimental import pallas as pl
from jax.experimental.pallas import tpu as pltpu
from jax.sharding import PartitionSpec as P

D = 768
HEADS = 12
HD = 64
SCALE = 0.125
EPS = 1e-12
ROOT_HALF = 0.7071067811865476
BF = jnp.bfloat16
F32 = jnp.float32
NT = (((1,), (1,)), ((), ()))
NN = (((1,), (0,)), ((), ()))
TN = (((0,), (0,)), ((), ()))


def layer_norm(values, gain_vec, shift_vec):
    average = jnp.mean(values, axis=-1, keepdims=True)
    centred = values - average
    variance = jnp.mean(centred * centred, axis=-1, keepdims=True)
    return centred * lax.rsqrt(variance + EPS) * gain_vec + shift_vec


def gelu_act(values):
    return 0.5 * values * (1.0 + lax.erf(values * ROOT_HALF))


def key_range(doc_start, first_row, rows, stream_rows, tile):
    pos = jnp.arange(rows // tile, dtype=jnp.int32) * tile + first_row
    last = pos + tile - 1
    low = jnp.max(jnp.where(doc_start[None, :] <= pos[:, None], doc_start[None, :], 0), axis=1)
    high = jnp.min(
        jnp.where(doc_start[None, :] > last[:, None], doc_start[None, :], stream_rows), axis=1
    )
    first = low // 128 * 128
    count = (high - first + 255) // 256
    first = jnp.minimum(first, stream_rows - count * 256)
    return jnp.stack([first, count], axis=1).astype(jnp.int32)


def document_lanes(doc_start, first_row, rows, stream_rows):
    far = jnp.full((128 - doc_start.shape[0],), 2**30, jnp.int32)
    starts = jnp.concatenate([doc_start, far])
    ends = jnp.concatenate([doc_start[1:], jnp.full((1,), stream_rows, jnp.int32), far])
    query_pos = first_row + jnp.arange(rows, dtype=jnp.int32)[:, None]
    key_pos = jnp.arange(stream_rows, dtype=jnp.int32)[:, None]
    query_doc = ((query_pos >= starts) & (query_pos < ends)).astype(BF)
    key_doc = jnp.where((key_pos >= starts) & (key_pos < ends), 0.0, -1e30).astype(BF)
    return query_doc, key_doc


def stack_heads(x, extra=None):
    lane = lax.broadcasted_iota(jnp.int32, x.shape, 1)
    zero = jnp.zeros_like(x)
    lo = jnp.where(lane < 64, x, zero)
    hi = jnp.where(lane < 64, zero, x)
    if extra is not None:
        lo = jnp.concatenate([lo, extra], axis=1)
        hi = jnp.concatenate([hi, extra], axis=1)
    return jnp.concatenate([lo, hi], axis=0)

def pick_heads(x, tq):
    return jnp.concatenate([x[:64, :tq], x[64:, tq:]], axis=0)

def two_level(start, count, tk, body, init):
    big = tk // 256
    whole = count // big
    def large(t, c):
        return body(pl.multiple_of(t * tk, 256), pl.multiple_of(start + t * tk, 128), tk, c)
    def small(t, c):
        return body(pl.multiple_of(t * 256, 256), pl.multiple_of(start + t * 256, 128), 256, c)
    c = lax.fori_loop(0, whole, large, init)
    return lax.fori_loop(whole * big, count, small, c)

def fwd_kernel(tk, bounds, q_ref, qaug_ref, k_ref, kaug_ref, v_ref, ot_ref, lse_ref, s_scr, acc):
    qi = pl.program_id(1)
    start, count = bounds[qi, 0], bounds[qi, 1]
    tq = q_ref.shape[0]
    rhs = stack_heads(q_ref[...], qaug_ref[...])

    def scores(loc, off, size, m):
        lhs = jnp.concatenate([k_ref[pl.ds(off, size), :], kaug_ref[pl.ds(off, size), :]], axis=1)
        s = lax.dot_general(lhs, rhs, NT, preferred_element_type=F32)
        s_scr[pl.ds(loc, size), :] = s
        return jnp.maximum(m, jnp.max(s.reshape(size // 8, 8, 2 * tq), axis=0))

    m8 = two_level(start, count, tk, scores, jnp.full((8, 2 * tq), -3e38, F32))
    m = jnp.max(m8, axis=0, keepdims=True)
    acc[...] = jnp.zeros_like(acc)

    def mix(loc, off, size, l8):
        p = jnp.exp(s_scr[pl.ds(loc, size), :] - m)
        acc[...] += lax.dot_general(v_ref[pl.ds(off, size), :], p.astype(BF), TN, preferred_element_type=F32)
        return l8 + jnp.sum(p.reshape(size // 8, 8, 2 * tq), axis=0)

    l8 = two_level(start, count, tk, mix, jnp.zeros((8, 2 * tq), F32))
    l = jnp.sum(l8, axis=0, keepdims=True)
    ot_ref[...] = pick_heads(acc[...] / l, tq)
    lse = m + jnp.log(l)
    lse_ref[0] = jnp.concatenate([lse[:, :tq], lse[:, tq:]], axis=0)

def attn_fwd(bounds, q, qaug, k, kaug, v, *, tq=512, tk=768):
    T, D = q.shape
    S = k.shape[0]
    pairs = D // 128
    return pl.pallas_call(
        functools.partial(fwd_kernel, tk),
        out_shape=(jax.ShapeDtypeStruct((D, T), F32), jax.ShapeDtypeStruct((pairs, 2, T), F32)),
        grid_spec=pltpu.PrefetchScalarGridSpec(
            num_scalar_prefetch=1, grid=(pairs, T // tq),
            in_specs=[pl.BlockSpec((tq, 128), lambda h, i, b: (i, h)),
                      pl.BlockSpec((tq, 128), lambda h, i, b: (i, 0)),
                      pl.BlockSpec((S, 128), lambda h, i, b: (0, h)),
                      pl.BlockSpec((S, 128), lambda h, i, b: (0, 0)),
                      pl.BlockSpec((S, 128), lambda h, i, b: (0, h))],
            out_specs=(pl.BlockSpec((128, tq), lambda h, i, b: (h, i)),
                       pl.BlockSpec((1, 2, tq), lambda h, i, b: (h, 0, i))),
            scratch_shapes=[pltpu.VMEM((S, 2 * tq), F32), pltpu.VMEM((128, 2 * tq), F32)]),
        name="attend",
    )(bounds, q, qaug, k, kaug, v)

def bwd_kernel(tk, bounds, q_ref, qaug_ref, do_ref, lse_ref, ot_ref, k_ref, kaug_ref, v_ref,
               dq_ref, dk_ref, dv_ref, dk_acc, dv_acc, dq_acc):
    qi = pl.program_id(1)
    start, count = bounds[qi, 0], bounds[qi, 1]
    tq = q_ref.shape[0]

    @pl.when(qi == 0)
    def _():
        dk_acc[...] = jnp.zeros_like(dk_acc)
        dv_acc[...] = jnp.zeros_like(dv_acc)

    qs = stack_heads(q_ref[...])
    qrhs = stack_heads(q_ref[...], qaug_ref[...])
    dos = stack_heads(do_ref[...])
    lse = jnp.concatenate([lse_ref[0, 0:1, :], lse_ref[0, 1:2, :]], axis=1)
    mixed = ot_ref[...] * do_ref[...].astype(F32).T
    delta = jnp.concatenate(
        [jnp.sum(mixed[:64], axis=0, keepdims=True), jnp.sum(mixed[64:], axis=0, keepdims=True)], axis=1
    )
    dq_acc[...] = jnp.zeros_like(dq_acc)

    def step(loc, off, size, carry):
        rows = pl.ds(off, size)
        lhs = jnp.concatenate([k_ref[rows, :], kaug_ref[rows, :]], axis=1)
        x = lax.dot_general(lhs, qrhs, NT, preferred_element_type=F32)
        y = lax.dot_general(v_ref[rows, :], dos, NT, preferred_element_type=F32)
        p = jnp.exp(x - lse)
        ds = (p * (y - delta)).astype(BF)
        pb = p.astype(BF)
        dv_acc[rows, :] += lax.dot_general(pb, dos, NN, preferred_element_type=F32)
        dk_acc[rows, :] += lax.dot_general(ds, qs, NN, preferred_element_type=F32)
        dq_acc[...] += lax.dot_general(k_ref[rows, :], ds, TN, preferred_element_type=F32)
        return carry

    two_level(start, count, tk, step, 0)
    dq_ref[...] = (pick_heads(dq_acc[...], tq) * SCALE).T.astype(BF)

    @pl.when(qi == pl.num_programs(1) - 1)
    def _():
        dk_ref[...] = dk_acc[...].astype(BF)
        dv_ref[...] = dv_acc[...].astype(BF)

def attn_bwd(bounds, q, qaug, do, lse, ot, k, kaug, v, *, tq=512, tk=768):
    T, D = q.shape
    S = k.shape[0]
    pairs = D // 128
    row = lambda h, i, b: (h, 0, i)
    return pl.pallas_call(
        functools.partial(bwd_kernel, tk),
        out_shape=(jax.ShapeDtypeStruct((T, D), BF), jax.ShapeDtypeStruct((S, D), BF), jax.ShapeDtypeStruct((S, D), BF)),
        grid_spec=pltpu.PrefetchScalarGridSpec(
            num_scalar_prefetch=1, grid=(pairs, T // tq),
            in_specs=[pl.BlockSpec((tq, 128), lambda h, i, b: (i, h)),
                      pl.BlockSpec((tq, 128), lambda h, i, b: (i, 0)),
                      pl.BlockSpec((tq, 128), lambda h, i, b: (i, h)),
                      pl.BlockSpec((1, 2, tq), row),
                      pl.BlockSpec((128, tq), lambda h, i, b: (h, i)),
                      pl.BlockSpec((S, 128), lambda h, i, b: (0, h)),
                      pl.BlockSpec((S, 128), lambda h, i, b: (0, 0)),
                      pl.BlockSpec((S, 128), lambda h, i, b: (0, h))],
            out_specs=(pl.BlockSpec((tq, 128), lambda h, i, b: (i, h)),
                       pl.BlockSpec((S, 128), lambda h, i, b: (0, h)),
                       pl.BlockSpec((S, 128), lambda h, i, b: (0, h))),
            scratch_shapes=[pltpu.VMEM((S, 128), F32), pltpu.VMEM((S, 128), F32), pltpu.VMEM((128, 2 * tq), F32)]),
        name="attend_back",
    )(bounds, q, qaug, do, lse, ot, k, kaug, v)


def middle_kernel(attn_ref, in_ref, cot_ref, vec_ref, wo_ref, wu_ref, down_own, down_far,
                  out_ref, sum1_ref, do_ref, grads_ref, up_out, down_out, attn_out,
                  wo, wu, wd, attn_b, first, hat1, scale1, first_b, act, slope, sum2, down_b, up_b, first_b2, first_t,
                  g_up, g_down, g_out, sem_w, sem_d, sem_o):
    rows, wide = in_ref.shape[0], wu.shape[1]
    a, w = lax.axis_index("ctx"), lax.axis_index("wsh")
    y, c = w // 2, lax.rem(w, 2)
    core_peer = (a, y * 2 + (1 - c))
    tall = down_own.shape[0]
    MESH = pl.DeviceIdType.MESH
    barrier = pltpu.get_barrier_semaphore()
    pl.semaphore_signal(barrier, inc=1, device_id=core_peer, device_id_type=MESH)
    pl.semaphore_wait(barrier, 1)
    passed = []
    for s, (ref, owner) in enumerate(((down_own, w), (down_far, (1 - y) * 2 + c))):
        there = wd.at[pl.ds(pl.multiple_of(owner * tall, 16), tall), :]
        passed.append(pltpu.make_async_remote_copy(
            src_ref=ref, dst_ref=there, send_sem=sem_d.at[0, s], recv_sem=sem_d.at[1, s],
            device_id=core_peer, device_id_type=MESH))
        passed[-1].start()
        pltpu.make_async_copy(ref, there, sem_w.at[2 + s]).start()
    loading = [pltpu.make_async_copy(wo_ref, wo, sem_w.at[0]), pltpu.make_async_copy(wu_ref, wu, sem_w.at[1])]
    for copy in loading:
        copy.start()

    def arrived(j):
        if j < 2:
            loading[j].wait()
        else:
            for s, owner in enumerate((w, (1 - y) * 2 + c)):
                there = wd.at[pl.ds(pl.multiple_of(owner * tall, 16), tall), :]
                pltpu.make_async_copy(there, there, sem_w.at[2 + s]).wait()
                passed[s].wait_recv()

    grads_ref[...] = jnp.zeros_like(grads_ref)
    attn_b[...] = attn_ref[...].astype(BF)
    out_b, attn_g, attn_s, down_bias, final_g, final_s = [vec_ref[i : i + 1, :] for i in range(2, 8)]
    arrived(0)
    block = 128

    def over_rows(fn):
        def one(i, carry):
            fn(pl.ds(pl.multiple_of(i * block, block), block))
            return carry

        lax.fori_loop(0, rows // block, one, 0)

    def norm(values):
        average = jnp.mean(values, axis=-1, keepdims=True)
        centred = values - average
        scale = lax.rsqrt(jnp.mean(centred * centred, axis=-1, keepdims=True) + EPS)
        return centred * scale, scale

    def norm_back(grad, hat, scale, gain):
        g = grad * gain
        return scale * (g - jnp.mean(g, axis=-1, keepdims=True) - hat * jnp.mean(g * hat, axis=-1, keepdims=True))

    def note(row, values):
        grads_ref[row : row + 1, :] += jnp.sum(values, axis=0, keepdims=True)

    def branch_part(r):
        a = attn_b[:, r].T
        v = lax.dot_general(a, wo[...], NN, preferred_element_type=F32) + out_b + in_ref[r, :].astype(F32)
        hat, scale = norm(v)
        hat1[r, :] = hat
        scale1[r, :] = scale
        f = hat * attn_g + attn_s
        first[r, :] = f
        first_b[r, :] = f.astype(BF)

    over_rows(branch_part)
    arrived(1)
    cols = vec_ref.shape[1]

    def over_wide(fn):
        def one(i, carry):
            fn(pl.ds(pl.multiple_of(i * cols, cols), cols), i)
            return carry

        lax.fori_loop(0, wide // cols, one, 0)

    def up_part(n, i):
        u = lax.dot_general(first_b[...], wu[:, n], NN, preferred_element_type=F32) + vec_ref[pl.ds(8 + i, 1), :]
        half = 0.5 * (1.0 + lax.erf(u * ROOT_HALF))
        act[:, n] = (u * half).astype(BF)
        slope[:, n] = half + u * (0.3989422804014327 * jnp.exp(-0.5 * u * u))

    over_wide(up_part)
    arrived(2)

    def down_part(r):
        v = lax.dot_general(act[r, :], wd[...], NN, preferred_element_type=F32) + down_bias + first[r, :]
        hat, scale = norm(v)
        out_ref[r, :] = (hat * final_g + final_s).astype(BF)
        cot = cot_ref[r, :].astype(F32)
        note(6, cot * hat)
        note(7, cot)
        g = norm_back(cot, hat, scale, final_g)
        sum2[r, :] = g
        rounded = g.astype(BF)
        down_b[r, :] = rounded
        note(5, rounded.astype(F32))

    over_rows(down_part)

    def up_back(n, i):
        g = lax.dot_general(down_b[...], wd[n, :], NT, preferred_element_type=F32) * slope[:, n]
        rounded = g.astype(BF)
        up_b[:, n] = rounded
        grads_ref[pl.ds(8 + i, 1), :] = jnp.sum(rounded.astype(F32), axis=0, keepdims=True)

    over_wide(up_back)

    def first_part(r):
        g = sum2[r, :] + lax.dot_general(up_b[r, :], wu[...], NT, preferred_element_type=F32)
        hat = hat1[r, :]
        note(3, g * hat)
        note(4, g)
        s1 = norm_back(g, hat, scale1[r, :], attn_g)
        sum1_ref[r, :] = s1
        rounded = s1.astype(BF)
        note(2, rounded.astype(F32))
        first_b2[r, :] = rounded

    over_rows(first_part)

    def do_part(r):
        do_ref[r, :] = lax.dot_general(first_b2[r, :], wo[...], NT, preferred_element_type=F32).astype(BF)

    over_rows(do_part)

    def wide_grads(n, i):
        g_down[n, :] = lax.dot_general(act[:, n].T, down_b[...], NN, preferred_element_type=F32).astype(BF)
        pltpu.make_async_copy(g_down.at[n, :], down_out.at[n, :], sem_o.at[0, i]).start()
        g_up[:, n] = lax.dot_general(first_t[...], up_b[:, n], NN, preferred_element_type=F32).astype(BF)
        pltpu.make_async_copy(g_up.at[:, n], up_out.at[:, n], sem_o.at[1, i]).start()

    first_t[...] = first_b[...].T
    over_wide(wide_grads)
    g_out[...] = lax.dot_general(attn_b[...], first_b2[...], NN, preferred_element_type=F32).astype(BF)
    pltpu.make_async_copy(g_out, attn_out, sem_o.at[2, 0]).start()

    def wide_end(n, i):
        pltpu.make_async_copy(g_down.at[n, :], down_out.at[n, :], sem_o.at[0, i]).wait()
        pltpu.make_async_copy(g_up.at[:, n], up_out.at[:, n], sem_o.at[1, i]).wait()

    over_wide(wide_end)
    pltpu.make_async_copy(g_out, attn_out, sem_o.at[2, 0]).wait()
    for copy in passed:
        copy.wait_send()


def middle(attn_t, inputs, cotangent, vec, out_w, up_w, down_own, down_far):
    rows = inputs.shape[0]
    wide = up_w.shape[1]
    vm, dma, shape = pltpu.VMEM, pltpu.SemaphoreType.DMA, jax.ShapeDtypeStruct
    any_spec = pl.BlockSpec(memory_space=pl.ANY)
    vm_spec = pl.BlockSpec(memory_space=pltpu.VMEM)
    return pl.pallas_call(
        middle_kernel,
        out_shape=(shape((rows, D), BF), shape((rows, D), F32), shape((rows, D), BF), shape((16, D), F32),
                   shape((D, wide), BF), shape((wide, D), BF), shape((D, D), BF)),
        in_specs=[vm_spec] * 4 + [any_spec] * 4,
        out_specs=(vm_spec,) * 4 + (any_spec,) * 3,
        scratch_shapes=[
            vm((D, D), BF), vm((D, wide), BF), vm((wide, D), BF), vm((D, rows), BF), vm((rows, D), F32),
            vm((rows, D), F32), vm((rows, 1), F32), vm((rows, D), BF), vm((rows, wide), BF), vm((rows, wide), F32),
            vm((rows, D), F32), vm((rows, D), BF), vm((rows, wide), BF), vm((rows, D), BF), vm((D, rows), BF),
            vm((D, wide), BF), vm((wide, D), BF), vm((D, D), BF), dma((4,)), dma((2, 2)), dma((3, wide // D)),
        ],
        compiler_params=pltpu.CompilerParams(collective_id=3, has_side_effects=True, vmem_limit_bytes=56 * 2**20),
        name="middle",
    )(attn_t, inputs, cotangent, vec, out_w, up_w, down_own, down_far)


def reach(n_ctx):
    return n_ctx // 2


def finish_kernel(sources, n_parts, *refs):
    parts = refs[:n_parts]
    (vec_ref, dk_ref, dv_ref, tok_ref, dq_ref, w_ref, own_in_ref, mine_tok_ref,
     out_ref, vec_out, wide_out, grad_ref,
     mine, buf_a, buf_h, buf_b, buf_s, buf_c, buf_d, buf_e, gbf,
     sums, heard, line,
     loads, weights, acc, dq, own, bias,
     run_part, from_x, from_z, far_z, last_x,
     sem_l, sem_a, sem_b, sem_c, sem_d, sem_v, sem_x, sem_z, sem_far, sem_load, sem_in) = refs[n_parts:]
    n_ready = len(sources)
    n_chunks = out_ref.shape[0]
    n_ctx, n_wsh = lax.axis_size("ctx"), lax.axis_size("wsh")
    zs = n_ctx // 2
    a, w = lax.axis_index("ctx"), lax.axis_index("wsh")
    z, x = a // 2, lax.rem(a, 2)
    y, c = w // 2, lax.rem(w, 2)
    core_peer = (a, y * 2 + (1 - c))
    y_peer = (a, (1 - y) * 2 + c)
    x_peer = (z * 2 + (1 - x), w)
    low, high = lax.rem(z, 2), z // 2
    pair_peer = ((z + 1 - 2 * low) * 2 + x, w)
    skip_peer = (lax.rem(z + 2, zs) * 2 + x, w)
    up_peer, down_peer = (a + 2, w), (a - 2, w)
    near = reach(n_ctx)
    hops = near // 2
    MESH = pl.DeviceIdType.MESH

    rows = out_ref.shape[1]
    half = out_ref.shape[2] // 2
    piece = rows // zs
    tall = own.shape[0]
    cut = from_x.shape[1]

    def z_peer(d):
        return (lax.rem(z + d, zs) * 2 + x, w)

    barrier = pltpu.get_barrier_semaphore()
    for dev in [core_peer, y_peer, x_peer] + [z_peer(d) for d in range(1, zs)]:
        pl.semaphore_signal(barrier, inc=1, device_id=dev, device_id_type=MESH)
    pl.semaphore_wait(barrier, zs + 2)

    def send(src, dst, sems, idx, dev):
        return pltpu.make_async_remote_copy(
            src_ref=src, dst_ref=dst, send_sem=sems.at[(0,) + idx], recv_sem=sems.at[(1,) + idx],
            device_id=dev, device_id_type=MESH)

    def wait_in(ref, sems, idx):
        send(ref, ref, sems, idx, core_peer).wait_recv()

    def wait_out(ref, sems, idx):
        send(ref, ref, sems, idx, core_peer).wait_send()

    def distance(i):
        return (hops - i // 4) * (1 - 2 * lax.rem(i // 2, 2))

    def position(i):
        dz = distance(i)
        mine_too = lax.rem(i, 2)
        run = 2 * (z + dz) + (1 - x) * (1 - mine_too) + x * mine_too
        return run, mine_too, (z + dz >= 0) & (z + dz < zs) & (jnp.abs(run - a) <= near)

    n_pos = 4 * hops + 2

    def load(i):
        run, _mine_too, there = position(i)
        return there, [
            pltpu.make_async_copy(src.at[run], loads.at[lax.rem(i, 2), j], sem_load.at[lax.rem(i, 2), j])
            for j, src in enumerate((dk_ref, dv_ref, tok_ref))
        ]

    def load_start(i):
        there, copies = load(i)

        @pl.when(there & (i < n_pos))
        def _():
            for copy in copies:
                copy.start()

    def share(k, owner):
        if k < n_ready:
            p, row0, col0 = sources[k]
            return parts[p].at[owner, pl.ds(row0, rows), pl.ds(col0, 2 * half)]
        return gbf.at[k - n_ready, owner]

    def share_load(k):
        for yy in range(2):
            pltpu.make_async_copy(share(k, yy * 2 + c), mine.at[k % 4, yy], sem_l.at[k]).start()

    def share_send(k):
        for yy in range(2):
            send(share(k, yy * 2 + (1 - c)), buf_a.at[k, yy], sem_a, (k,), core_peer).start()

    load_start(0)
    fetch = [pltpu.make_async_copy(w_ref, weights, sem_in.at[0]), pltpu.make_async_copy(dq_ref, dq, sem_in.at[1]),
             pltpu.make_async_copy(own_in_ref, own, sem_in.at[2])]
    for copy in fetch:
        copy.start()
    for k in range(n_ready):
        share_send(k)
        if k < 4:
            share_load(k)
    acc[...] = jnp.zeros_like(acc)
    bias[...] = jnp.zeros_like(bias)
    fetch[0].wait()

    near_rows, far_rows = pl.ds(0, cut), pl.ds(cut, tall - cut)

    def unit(i):
        run, mine_too, there = position(i)
        at = lax.rem(i, 2)
        load_start(i + 1)

        @pl.when(there)
        def _():
            for copy in load(i)[1]:
                copy.wait()

            def tokens_part(r, carry):
                rs = pl.ds(pl.multiple_of(r * 128, 128), 128)
                g = lax.dot_general(loads[at, 0, rs, :], weights[0], NT, preferred_element_type=F32)
                g = g + lax.dot_general(loads[at, 1, rs, :], weights[1], NT, preferred_element_type=F32)
                run_part[i, rs, :] = g.astype(BF)
                bias[0:8, :] += jnp.sum(loads[at, 1, rs, :].astype(F32).reshape(16, 8, 2 * half), axis=0)
                return carry

            lax.fori_loop(0, tall // 128, tokens_part, 0)

            @pl.when(mine_too == 0)
            def _():
                send(run_part.at[i, near_rows, :], from_x.at[i // 2], sem_x, (i // 2,), x_peer).start()

            @pl.when(i < 4)
            def _():
                far_send(i)

            def weights_part(r, carry):
                fs = pl.ds(pl.multiple_of(r * 256, 256), 256)
                flipped = loads[at, 2, :, fs].T
                for j in range(2):
                    acc[j, fs, :] += lax.dot_general(flipped, loads[at, j], NN, preferred_element_type=F32)
                return carry

            lax.fori_loop(0, 2 * half // 256, weights_part, 0)

    def from_below(i):
        dz = distance(i)
        step = 1 - 2 * lax.rem(i // 2, 2)
        sender, target = z - step, z - step + dz
        side = jnp.abs(2 * dz + (1 - 2 * x) * (1 - lax.rem(i, 2))) <= near
        return (sender >= 0) & (sender < zs) & (target >= 0) & (target < zs) & side

    def toward(i, copy_of):
        step = 1 - 2 * lax.rem(i // 2, 2)

        @pl.when(step == 1)
        def _():
            copy_of(up_peer).start()

        @pl.when(step == -1)
        def _():
            copy_of(down_peer).start()

    def far_send(i):
        toward(i, lambda dev: send(run_part.at[i, far_rows, :], far_z.at[i], sem_far, (i,), dev))

    def far_pass(i):
        _run, _mine_too, there = position(i)

        @pl.when(there)
        def _():
            @pl.when(from_below(i - 4))
            def _():
                wait_in(far_z.at[i - 4], sem_far, (i - 4,))
                run_part[i, far_rows, :] = (
                    run_part[i, far_rows, :].astype(F32) + far_z[i - 4].astype(F32)).astype(BF)

            far_send(i)

    def far_end():
        for col in range(2):
            total = n_pos - 2 + col
            for src in (4 + col, 6 + col):
                @pl.when(from_below(src))
                def _():
                    wait_in(far_z.at[src], sem_far, (src,))
                    run_part[total, far_rows, :] = (
                        run_part[total, far_rows, :].astype(F32) + far_z[src].astype(F32)).astype(BF)
            if col == 0:
                send(run_part.at[total, far_rows, :], last_x, sem_x, (n_pos // 2,), x_peer).start()
        own[far_rows, :] += run_part[n_pos - 1, far_rows, :].astype(F32)

    def near_pass(n):
        dz = distance(2 * n)
        i = 2 * n + 1

        @pl.when((z + dz >= 0) & (z + dz < zs))
        def _():
            @pl.when(jnp.abs(2 * dz + 2 * x - 1) <= near)
            def _():
                wait_in(from_x.at[n], sem_x, (n,))
                run_part[i, near_rows, :] = (
                    run_part[i, near_rows, :].astype(F32) + from_x[n].astype(F32)).astype(BF)

            @pl.when((n >= 2) & from_below(i - 4))
            def _():
                wait_in(from_z.at[n - 2], sem_z, (n - 2,))
                run_part[i, near_rows, :] = (
                    run_part[i, near_rows, :].astype(F32) + from_z[n - 2].astype(F32)).astype(BF)

            toward(i, lambda dev: send(run_part.at[i, near_rows, :], from_z.at[n], sem_z, (n,), dev))

    def near_own():
        n = n_pos // 2 - 1
        wait_in(from_x.at[n], sem_x, (n,))
        own[near_rows, :] += run_part[n_pos - 1, near_rows, :].astype(F32) + from_x[n].astype(F32)

    def near_end():
        for n in (2, 3):
            @pl.when(from_below(2 * n + 1))
            def _():
                wait_in(from_z.at[n], sem_z, (n,))
                own[near_rows, :] += from_z[n].astype(F32)

    def add(p, q):
        return (p.astype(F32) + q.astype(F32)).astype(BF)

    def column(side):
        return pl.ds(pl.multiple_of(side * half, 128), half)

    def band(start, size):
        return pl.ds(pl.multiple_of(start, 16), size)

    def stage_b(k):
        at = lax.rem(k, 4)
        pltpu.make_async_copy(mine.at[at], mine.at[at], sem_l.at[k]).wait()
        wait_in(buf_a.at[k], sem_a, (k,))
        buf_h[k] = add(mine[at, 1 - y], buf_a[k, 1 - y])
        send(buf_h.at[k], buf_b.at[k], sem_b, (k,), y_peer).start()
        buf_a[k, y] = add(mine[at, y], buf_a[k, y])

    def stage_c(k):
        wait_in(buf_b.at[k], sem_b, (k,))
        buf_s[k] = add(buf_a[k, y, :, column(1 - x)], buf_b[k, :, column(1 - x)])
        send(buf_s.at[k], buf_c.at[k], sem_c, (0, k), x_peer).start()

    my_two, other_two = band(low * 2 * piece, 2 * piece), band((1 - low) * 2 * piece, 2 * piece)
    my_one, other_one = band(high * piece, piece), band((1 - high) * piece, piece)
    my_rows = band(low * 2 * piece + high * piece, piece)

    def stage_d(k):
        wait_in(buf_c.at[k], sem_c, (0, k))
        cols = column(x)
        joined = buf_a[k, y, :, cols].astype(F32) + buf_b[k, :, cols].astype(F32) + buf_c[k].astype(F32)
        buf_c[k] = joined.astype(BF)
        send(buf_c.at[k, other_two, :], buf_d.at[k], sem_d, (0, k), pair_peer).start()

    def stage_d2(k):
        wait_in(buf_d.at[k], sem_d, (0, k))
        buf_d[k] = add(buf_d[k], buf_c[k, my_two, :])
        send(buf_d.at[k, other_one, :], buf_e.at[k], sem_d, (1, k), skip_peer).start()

    def stage_e(k):
        wait_in(buf_e.at[k], sem_d, (1, k))
        buf_e[k] = add(buf_e[k], buf_d[k, my_one, :])
        out_ref[k, my_rows, column(x)] = buf_e[k]
        send(buf_e.at[k], out_ref.at[k, my_rows, column(x)], sem_d, (2, k), skip_peer).start()

    def stage_e2(k):
        wait_in(buf_e.at[k], sem_d, (2, k))
        there = out_ref.at[k, my_two, column(x)]
        send(there, there, sem_d, (3, k), pair_peer).start()

    def stage_f(k):
        wait_in(buf_d.at[k], sem_d, (3, k))
        there = out_ref.at[k, :, column(x)]
        send(there, there, sem_c, (1, k), x_peer).start()

    def guarded(fn, k, first, last):
        @pl.when((k >= first) & (k < last))
        def _():
            fn(k)

    def chunk_step(m):
        for lag, stage in enumerate((stage_c, stage_d, stage_d2, stage_e, stage_e2, stage_f)):
            guarded(stage, m - (lag and lag + 5), 0, n_chunks)

    def first_step(t, carry):
        guarded(unit, t, 0, n_pos)
        for j in range(2):
            guarded(stage_b, 2 * t + j, 0, n_ready)
        for k in range(4, n_ready):
            @pl.when(t == (k - 4) // 2)
            def _():
                share_load(k)

        @pl.when(lax.rem(t, 2) == 1)
        def _():
            guarded(near_pass, t // 2 - 1, 0, 4)

        guarded(far_pass, t - 2, 4, 8)

        @pl.when((lax.rem(t, 2) == 0) & (t >= 2))
        def _():
            chunk_step(t // 2 - 1)

        return carry

    lax.fori_loop(0, n_pos, first_step, 0)
    done = n_pos // 2 - 1

    fetch[1].wait()
    fetch[2].wait()
    own_tok = pltpu.make_async_copy(mine_tok_ref, loads.at[0, 2], sem_load.at[0, 2])
    own_tok.start()

    def to_bf(j, target):
        for owner in range(n_wsh):
            gbf[target, owner] = acc[j, owner * rows : (owner + 1) * rows, :].astype(BF)
        share_load(n_ready + target)
        share_send(n_ready + target)

    to_bf(0, 0)
    to_bf(1, 1)
    own_tok.wait()

    def query_part(r, carry):
        fs = pl.ds(pl.multiple_of(r * 256, 256), 256)
        acc[0, fs, :] = lax.dot_general(loads[0, 2, :, fs].T, dq[...], NN, preferred_element_type=F32)
        return carry

    lax.fori_loop(0, 2 * half // 256, query_part, 0)
    to_bf(0, 2)

    def query_tokens(r, carry):
        rs = pl.ds(pl.multiple_of(r * 128, 128), 128)
        own[rs, :] += lax.dot_general(dq[rs, :], weights[2], NT, preferred_element_type=F32)
        bias[8:16, :] += jnp.sum(dq[rs, :].astype(F32).reshape(16, 8, 2 * half), axis=0)
        return carry

    lax.fori_loop(0, tall // 128, query_tokens, 0)

    sums[0] = vec_ref[...]
    sums[0, 0:1, :] = jnp.sum(bias[8:16, :], axis=0, keepdims=True)
    sums[0, 1:2, :] = jnp.sum(bias[0:8, :], axis=0, keepdims=True)
    pair = (core_peer, y_peer, x_peer)

    def vec_send(stage):
        send(sums.at[stage], heard.at[stage], sem_v, (stage,), pair[stage]).start()

    def vec_stage(stage):
        wait_in(heard.at[stage], sem_v, (stage,))
        total = sums[stage] + heard[stage]
        sums[stage + 1] = total
        if stage < 2:
            vec_send(stage + 1)
        else:
            line[z] = total
            for d in range(1, zs):
                send(sums.at[3], line.at[z], sem_v, (3,), z_peer(d)).start()

    def vec_last():
        wait_in(line.at[pl.ds(0, zs - 1)], sem_v, (3,))
        total = line[0]
        for d in range(1, zs):
            total = total + line[d]
        small, wide = total[0:8, 0:rows], total[8:9, :]
        for owner in range(1, n_wsh):
            small = jnp.where(w == owner, total[0:8, owner * rows : (owner + 1) * rows], small)
            wide = jnp.where(w == owner, total[8 + owner : 9 + owner, :], wide)
        vec_out[...] = small
        wide_out[...] = wide

    vec_send(0)

    def second_step(m, carry):
        guarded(stage_b, m - done + n_ready, n_ready, n_chunks)
        chunk_step(m)
        guarded(lambda k: near_own(), m - done, 0, 1)
        for stage in range(3):
            guarded(lambda k: vec_stage(stage), m - done - 1 - stage, 0, 1)
        guarded(lambda k: near_end(), m - done - 3, 0, 1)
        guarded(lambda k: far_end(), m - done - 4, 0, 1)
        guarded(lambda k: vec_last(), m - done - 5, 0, 1)
        return carry

    lax.fori_loop(done, n_chunks + 10, second_step, 0)
    wait_in(last_x, sem_x, (n_pos // 2,))
    own[far_rows, :] += last_x[...].astype(F32)
    grad_ref[...] = own[...].astype(BF)

    def drain(k, carry):
        wait_in(buf_s.at[k], sem_c, (1, k))
        wait_out(buf_a.at[k], sem_a, (k,))
        wait_out(buf_b.at[k], sem_b, (k,))
        wait_out(buf_s.at[k], sem_c, (0, k))
        wait_out(buf_s.at[k], sem_c, (1, k))
        wait_out(buf_d.at[k], sem_d, (0, k))
        wait_out(buf_e.at[k], sem_d, (1, k))
        wait_out(buf_e.at[k], sem_d, (2, k))
        wait_out(buf_d.at[k], sem_d, (3, k))
        return carry

    lax.fori_loop(0, n_chunks, drain, 0)
    for stage in range(3):
        wait_out(heard.at[stage], sem_v, (stage,))
    wait_out(line.at[pl.ds(0, zs - 1)], sem_v, (3,))
    wait_out(last_x, sem_x, (n_pos // 2,))

    def drain_runs(i, carry):
        _run, mine_too, there = position(i)

        @pl.when(there)
        def _():
            wait_out(far_z.at[i], sem_far, (i,))

            @pl.when(mine_too == 1)
            def _():
                wait_out(from_z.at[i // 2], sem_z, (i // 2,))

        return carry

    lax.fori_loop(0, n_pos - 2, drain_runs, 0)

    def drain_x(n, carry):
        _run, _mine_too, there = position(2 * n)

        @pl.when(there)
        def _():
            wait_out(from_x.at[n], sem_x, (n,))

        return carry

    lax.fori_loop(0, n_pos // 2, drain_x, 0)


def finish(matrices, vec, grad_k, grad_v, all_tokens, grad_q, kvq_w, own_grad, inputs):
    n_ctx, n_wsh = lax.axis_size("ctx"), lax.axis_size("wsh")
    zs, hops = n_ctx // 2, reach(n_ctx) // 2
    rows = D // n_wsh
    parts, sources, spans = [], [], []
    for p, g in enumerate(matrices):
        down, across = g.shape[0] // D, g.shape[1] // D
        parts.append(g.astype(BF).reshape(n_wsh, down * rows, across * D))
        spans.append((len(sources), down, across))
        sources += [(p, r * rows, col * D) for r in range(down) for col in range(across)]
    n = len(sources) + 3
    spans += [(len(sources) + j, 1, 1) for j in range(3)]
    half, piece, tall = D // 2, rows // zs, inputs.shape[0]
    n_pos, cut = 4 * hops + 2, tall // 2
    vm, dma, shape = pltpu.VMEM, pltpu.SemaphoreType.DMA, jax.ShapeDtypeStruct
    any_spec = pl.BlockSpec(memory_space=pl.ANY)
    vm_spec = pl.BlockSpec(memory_space=pltpu.VMEM)
    summed, small, wide, grad_own = pl.pallas_call(
        functools.partial(finish_kernel, sources, len(parts)),
        out_shape=(shape((n, rows, D), BF), shape((8, rows), F32), shape((1, D), F32), shape((tall, D), BF)),
        in_specs=[any_spec] * len(parts) + [vm_spec] + [any_spec] * 7,
        out_specs=(vm_spec,) * 4,
        scratch_shapes=[
            vm((4, 2, rows, D), BF), vm((n, 2, rows, D), BF), vm((n, rows, D), BF), vm((n, rows, D), BF),
            vm((n, rows, half), BF), vm((n, rows, half), BF), vm((n, 2 * piece, half), BF), vm((n, piece, half), BF),
            vm((3, n_wsh, rows, D), BF),
            vm((4,) + vec.shape, F32), vm((3,) + vec.shape, F32), vm((zs,) + vec.shape, F32),
            vm((2, 3, tall, D), BF), vm((3, D, D), BF), vm((2, D, D), F32), vm((tall, D), BF), vm((tall, D), F32),
            vm((16, D), F32),
            vm((n_pos, tall, D), BF), vm((n_pos // 2, cut, D), BF), vm((4, cut, D), BF),
            vm((n_pos - 2, tall - cut, D), BF), vm((tall - cut, D), BF),
            dma((n,)), dma((2, n)), dma((2, n)), dma((2, 2, n)), dma((2, 4, n)), dma((2, 4)),
            dma((2, n_pos // 2 + 1)), dma((2, 4)), dma((2, n_pos - 2)), dma((2, 3)), dma((3,)),
        ],
        compiler_params=pltpu.CompilerParams(collective_id=2, has_side_effects=True, vmem_limit_bytes=63 * 2**20),
        name="finish",
    )(*parts, vec, grad_k, grad_v, all_tokens, grad_q, kvq_w, own_grad, inputs)
    sums = []
    for first, down, across in spans:
        block = summed[first : first + down * across]
        if across > 1:
            block = jnp.concatenate([block[i] for i in range(across)], axis=1)
        sums.append(block.reshape(down * rows, across * D).astype(F32))
    return sums, small, wide, grad_own


def gather_kernel(cut, tok_ref, vec_ref, wk_ref, wv_ref, wq_ref, wo_ref, wu_ref,
                  tok_out, k_out, v_out, q_out, w_out, vec_out, wo_out, wu_out,
                  tok, kbuf, vbuf, qbuf, wbuf, vecs, wo, wu,
                  sem_in, sem_out, sem_w, sem_l, sem_o):
    n_ctx = lax.axis_size("ctx")
    zs = n_ctx // 2
    a, w = lax.axis_index("ctx"), lax.axis_index("wsh")
    z, x = a // 2, lax.rem(a, 2)
    y, c = w // 2, lax.rem(w, 2)
    core_peer = (a, y * 2 + (1 - c))
    y_peer = (a, (1 - y) * 2 + c)
    x_peer = (z * 2 + (1 - x), w)
    up, down = (a + 2, w), (a - 2, w)
    near = reach(n_ctx)
    MESH = pl.DeviceIdType.MESH
    n_slices = sem_in.shape[1]
    tall = tok.shape[1] // n_slices
    own = wk_ref.shape[0]
    far = 4 * (near // 2 + 1)

    barrier = pltpu.get_barrier_semaphore()
    around = [(lax.rem(z + d, zs) * 2 + x, w) for d in (1, zs - 1)]
    for dev in [core_peer, y_peer, x_peer] + around:
        pl.semaphore_signal(barrier, inc=1, device_id=dev, device_id_type=MESH)
    pl.semaphore_wait(barrier, 5)

    def relative(u):
        dz = (u // 4) * (1 - 2 * lax.rem(u, 2))
        other = lax.rem(u // 2, 2)
        run = 2 * (z + dz) + (x + other - 2 * x * other)
        there = (z + dz >= 0) & (z + dz < zs) & (jnp.abs(run - a) <= near) & ((u >= 4) | (lax.rem(u, 2) == 0))
        return run, dz, other, there

    def rows(s):
        return pl.ds(pl.multiple_of(s * tall, tall), tall)

    def remote(src, dst, send_sem, recv_sem, dev):
        return pltpu.make_async_remote_copy(
            src_ref=src, dst_ref=dst, send_sem=send_sem, recv_sem=recv_sem, device_id=dev, device_id_type=MESH)

    def routes(u, s):
        run, dz, other, there = relative(u)
        z_first = s < cut
        to_x = there & (z_first | (dz == 0)) & (other == 0) & (jnp.abs(run - x_peer[0]) <= near)
        along = there & ((other == 0) | jnp.logical_not(z_first))
        to_up = along & (dz <= 0) & (z + 1 < zs) & (jnp.abs(run - (a + 2)) <= near)
        to_down = along & (dz >= 0) & (z > 0) & (jnp.abs(run - (a - 2)) <= near)
        return run, ((0, x_peer, to_x), (1, up, to_up), (2, down, to_down))

    def pass_on(u, s):
        run, where = routes(u, s)
        for d, dev, ok in where:
            @pl.when(ok)
            def _():
                source = tok_ref if isinstance(u, int) and u == 0 else tok.at[run]
                remote(source.at[rows(s), :], tok.at[run, rows(s), :], sem_out.at[d, u, s], sem_in.at[run, s], dev).start()

    def await_slice(u, s):
        run, _dz, _other, there = relative(u)

        @pl.when(there)
        def _():
            remote(tok.at[run, rows(s), :], tok.at[run, rows(s), :], sem_out.at[0, 0, 0], sem_in.at[run, s], x_peer).wait_recv()

    def start_own(s, carry):
        pass_on(0, s)
        return carry

    def weight_rows(owner):
        return pl.ds(pl.multiple_of(owner * own, 16), own)

    def shard(m, owner):
        if m == 3:
            return vecs.at[owner]
        return (wbuf.at[0], wbuf.at[1], wbuf.at[2], None, wo, wu)[m].at[weight_rows(owner), :]

    shards = (wk_ref, wv_ref, wq_ref, vec_ref, wo_ref, wu_ref)
    for m in (3, 0, 1, 2, 4, 5):
        remote(shards[m], shard(m, w), sem_w.at[0, 1, m], sem_w.at[1, 1, m], y_peer).start()
        remote(shards[m], shard(m, w), sem_w.at[0, 0, m], sem_w.at[1, 0, m], core_peer).start()
        pltpu.make_async_copy(shards[m], shard(m, w), sem_w.at[0, 3, m]).start()
    lax.fori_loop(0, n_slices, start_own, 0)
    pltpu.make_async_copy(tok_ref, tok.at[a], sem_l.at[4]).start()

    for j in range(n_ctx):
        @pl.when(jnp.abs(j - a) > near)
        def _():
            tok[j] = jnp.zeros_like(tok[j])

    def weight_arrival(m, kind):
        part = shard(m, w)
        return remote(part, part, sem_w.at[0, kind, m], sem_w.at[1, kind, m], core_peer)

    across = (1 - y) * 2 + c

    def weight_forward(m):
        weight_arrival(m, 1).wait_recv()
        remote(shard(m, across), shard(m, across), sem_w.at[0, 2, m], sem_w.at[1, 2, m], core_peer).start()

    def weight_end(m):
        weight_arrival(m, 0).wait_recv()
        weight_arrival(m, 2).wait_recv()
        pltpu.make_async_copy(shard(m, w), shard(m, w), sem_w.at[0, 3, m]).wait()

    def relay(first, last):
        def one(i, carry):
            s = i // (last - first)
            u = first + lax.rem(i, last - first)
            await_slice(u, s)
            pass_on(u, s)
            return carry

        lax.fori_loop(0, n_slices * (last - first), one, 0)

    relay(2, 6)
    weight_forward(3)
    weight_forward(0)
    weight_forward(1)
    weight_end(3)
    total = vecs[0].astype(F32)
    for owner in range(1, 4):
        total = total + vecs[owner].astype(F32)
    vec_out[...] = total
    pltpu.make_async_copy(tok_ref, tok.at[a], sem_l.at[4]).wait()
    weight_end(0)
    weight_end(1)

    step_rows = 128
    steps = tok.shape[1] // step_rows

    def query_part(i, carry):
        r = pl.ds(pl.multiple_of(i * step_rows, step_rows), step_rows)
        q = (jnp.dot(tok[a, r, :], wbuf[2], preferred_element_type=F32) + vec_out[0:1, :]).astype(BF)
        qbuf[r, :] = q * jnp.asarray(SCALE, BF)
        return carry

    def project(u, carry):
        run, _dz, _other, there = relative(u)

        @pl.when(u == 6)
        def _():
            weight_forward(2)
            weight_end(2)
            lax.fori_loop(0, steps, query_part, 0)
            pltpu.make_async_copy(qbuf, q_out, sem_l.at[5]).start()
            relay(6, 10)

        @pl.when(there)
        def _():
            @pl.when(u >= 10)
            def _():
                def one(s, carry):
                    await_slice(u, s)
                    return carry

                lax.fori_loop(0, n_slices, one, 0)

            def part(i, carry):
                r = pl.ds(pl.multiple_of(i * step_rows, step_rows), step_rows)
                t = tok[run, r, :]
                kbuf[run, r, :] = jnp.dot(t, wbuf[0], preferred_element_type=F32).astype(BF)
                vbuf[run, r, :] = (jnp.dot(t, wbuf[1], preferred_element_type=F32) + vec_out[1:2, :]).astype(BF)
                return carry

            lax.fori_loop(0, steps, part, 0)
            for i, (src, dst) in enumerate(((kbuf, k_out), (vbuf, v_out), (tok, tok_out))):
                pltpu.make_async_copy(src.at[run], dst.at[run], sem_o.at[i, run]).start()

        return carry

    for j in range(n_ctx):
        @pl.when(jnp.abs(j - a) > near)
        def _():
            kbuf[j] = jnp.zeros_like(kbuf[j])
            vbuf[j] = jnp.zeros_like(vbuf[j])
            for i, (src, dst) in enumerate(((kbuf, k_out), (vbuf, v_out), (tok, tok_out))):
                pltpu.make_async_copy(src.at[j], dst.at[j], sem_o.at[i, j]).start()

    lax.fori_loop(0, far, project, 0)

    pltpu.make_async_copy(wbuf, w_out, sem_l.at[6]).start()

    for m in (4, 5):
        weight_forward(m)
    for m, full, target in ((4, wo, wo_out), (5, wu, wu_out)):
        weight_end(m)
        pltpu.make_async_copy(full, target, sem_l.at[m - 4]).start()
    for m in range(6):
        for kind in range(3):
            weight_arrival(m, kind).wait_send()

    def drain(i, carry):
        s = i // far
        u = lax.rem(i, far)
        run, where = routes(u, s)
        for d, dev, ok in where:
            @pl.when(ok & (u < 10))
            def _():
                remote(tok.at[run, rows(s), :], tok.at[run, rows(s), :], sem_out.at[d, u, s], sem_in.at[run, s], dev).wait_send()
        return carry

    lax.fori_loop(0, n_slices * far, drain, 0)
    for j in range(n_ctx):
        for i, (src, dst) in enumerate(((kbuf, k_out), (vbuf, v_out), (tok, tok_out))):
            pltpu.make_async_copy(src.at[j], dst.at[j], sem_o.at[i, j]).wait()
    pltpu.make_async_copy(qbuf, q_out, sem_l.at[5]).wait()
    pltpu.make_async_copy(wbuf, w_out, sem_l.at[6]).wait()
    pltpu.make_async_copy(wo, wo_out, sem_l.at[0]).wait()
    pltpu.make_async_copy(wu, wu_out, sem_l.at[1]).wait()


def gather_project(inputs, vec, key_weight, value_weight, query_weight, out_weight, up_weight):
    n_ctx, n_wsh = lax.axis_size("ctx"), lax.axis_size("wsh")
    tall = inputs.shape[0]
    n_slices = 8
    far = 4 * (reach(n_ctx) // 2 + 1)
    vm, dma = pltpu.VMEM, pltpu.SemaphoreType.DMA
    any_spec = pl.BlockSpec(memory_space=pl.ANY)
    vm_spec = pl.BlockSpec(memory_space=pltpu.VMEM)
    runs = (n_ctx, tall, D)
    shape = jax.ShapeDtypeStruct
    return pl.pallas_call(
        functools.partial(gather_kernel, 5),
        out_shape=(shape(runs, BF), shape(runs, BF), shape(runs, BF), shape((tall, D), BF), shape((3, D, D), BF),
                   shape(vec.shape, F32), shape((D, D), BF), shape((D, up_weight.shape[1]), BF)),
        in_specs=[any_spec] * 7,
        out_specs=(any_spec,) * 5 + (vm_spec,) + (any_spec,) * 2,
        scratch_shapes=[
            vm(runs, BF), vm(runs, BF), vm(runs, BF), vm((tall, D), BF), vm((3, D, D), BF), vm((n_wsh,) + vec.shape, BF),
            vm((D, D), BF), vm((D, up_weight.shape[1]), BF),
            dma((n_ctx, n_slices)), dma((3, far, n_slices)), dma((2, 4, 6)), dma((7,)), dma((3, n_ctx)),
        ],
        compiler_params=pltpu.CompilerParams(collective_id=1, has_side_effects=True, vmem_limit_bytes=48 * 2**20),
        name="gather_project",
    )(inputs, vec, key_weight, value_weight, query_weight, out_weight, up_weight)


def local(
    tokens,
    cotangent,
    doc_starts,
    query_weight,
    key_weight,
    value_weight,
    out_weight,
    up_weight,
    down_weight,
    query_bias,
    value_bias,
    out_bias,
    attn_gain,
    attn_shift,
    up_bias,
    down_bias,
    final_gain,
    final_shift,
):
    inputs = tokens[0]
    doc_start = doc_starts[0]
    tok_rows = inputs.shape[0]
    stream_rows = tok_rows * lax.axis_size("ctx")
    first_row = lax.axis_index("ctx") * tok_rows
    tile = min(tok_rows, 512)
    bounds = key_range(doc_start, first_row, tok_rows, stream_rows, tile)
    query_doc, key_doc = document_lanes(doc_start, first_row, tok_rows, stream_rows)

    n_ctx, n_wsh = lax.axis_size("ctx"), lax.axis_size("wsh")
    own = D // n_wsh

    def gather(x):
        return lax.all_gather(x, "wsh", axis=0, tiled=True)

    small = jnp.stack(
        [query_bias, value_bias, out_bias, attn_gain, attn_shift, down_bias, final_gain, final_shift]
    )
    fast = n_wsh == 4 and n_ctx == 8 and own % (n_ctx // 2 * 16) == 0 and tok_rows % 512 == 0
    if fast:
        w = lax.axis_index("wsh")
        at = lax.broadcasted_iota(jnp.int32, (8, D), 1) // own == w
        vec = jnp.where(at, jnp.tile(small, (1, n_wsh)), jnp.zeros((), BF))
        at = lax.broadcasted_iota(jnp.int32, (8, D), 0) == w
        vec = jnp.concatenate([vec, jnp.where(at, up_bias[None, :], jnp.zeros((), BF))], axis=0)
        all_tokens, keys, values, queries, kvq_w, vec, out_w, up_w = gather_project(
            inputs, vec, key_weight, value_weight, query_weight, out_weight, up_weight
        )
        down_own, _unused = lax.optimization_barrier((down_weight, vec))
        down_far = lax.ppermute(down_own, "wsh", [(i, i ^ 2) for i in range(n_wsh)])
        all_tokens, keys, values = [r.reshape(stream_rows, D) for r in (all_tokens, keys, values)]
        key_w, value_w, query_w = kvq_w[0], kvq_w[1], kvq_w[2]
        query_b, value_b, out_b, attn_g, attn_s, down_b, final_g, final_s = [vec[i] for i in range(8)]
        up_b = vec[8 : 8 + n_wsh].reshape(-1)
    else:
        all_tokens = lax.all_gather(inputs, "ctx", axis=0, tiled=True)
        query_w, key_w, value_w = gather(query_weight), gather(key_weight), gather(value_weight)
        small = gather(small.T).astype(F32)
        query_b, value_b, out_b, attn_g, attn_s, down_b, final_g, final_s = [small[:, i] for i in range(8)]
        up_b = gather(up_bias).astype(F32)
        queries = jnp.dot(inputs, query_w, preferred_element_type=F32) + query_b
        queries = queries.astype(BF) * jnp.asarray(SCALE, BF)
        keys = jnp.dot(all_tokens, key_w, preferred_element_type=F32).astype(BF)
        values = (jnp.dot(all_tokens, value_w, preferred_element_type=F32) + value_b).astype(BF)
    mixed_t, log_rows = attn_fwd(bounds, queries, query_doc, keys, key_doc, values, tq=tile)
    if fast:
        layer_out, grad_sum1, grad_attn, vec_grads, grad_up_w, grad_down_w, grad_out_w = middle(
            mixed_t, inputs, cotangent[0], vec, out_w, up_w, down_own, down_far
        )
        grad_q, grad_k, grad_v = attn_bwd(
            bounds, queries, query_doc, grad_attn, log_rows, mixed_t, keys, key_doc, values, tq=tile
        )
        mats, small, wide, grad_inputs = finish(
            (grad_up_w, grad_out_w, grad_down_w), vec_grads, grad_k.reshape(n_ctx, tok_rows, D),
            grad_v.reshape(n_ctx, tok_rows, D), all_tokens.reshape(n_ctx, tok_rows, D), grad_q, kvq_w, grad_sum1, inputs,
        )
        up_sum, out_sum, down_sum, key_sum, value_sum, query_sum = mats
        return (
            layer_out.reshape(1, tok_rows, D), grad_inputs.reshape(1, tok_rows, D), query_sum, key_sum, value_sum,
            out_sum, up_sum, down_sum, small[0], small[1], small[2], small[3], small[4], wide[0],
            small[5], small[6], small[7],
        )

    out_w = gather(out_weight)
    up_w = gather(up_weight)
    down_w = gather(down_weight)
    attn_t = mixed_t.astype(BF)
    inputs_f = inputs.astype(F32)
    branch = lax.dot_general(attn_t, out_w, TN, preferred_element_type=F32) + out_b
    first_norm, first_pull = jax.vjp(layer_norm, inputs_f + branch, attn_g, attn_s)
    first_b = first_norm.astype(BF)
    up_f = jnp.dot(first_b, up_w, preferred_element_type=F32) + up_b
    act_f, act_pull = jax.vjp(gelu_act, up_f)
    act_b = act_f.astype(BF)
    down_f = jnp.dot(act_b, down_w, preferred_element_type=F32) + down_b
    final_f, final_pull = jax.vjp(layer_norm, first_norm + down_f, final_g, final_s)
    layer_out = final_f.astype(BF)

    grad_sum2, grad_final_g, grad_final_s = final_pull(cotangent[0].astype(F32))
    grad_down = grad_sum2.astype(BF)
    grad_down_w = jnp.einsum("tf,td->fd", act_b, grad_down, preferred_element_type=F32)
    grad_down_b = jnp.sum(grad_down.astype(F32), axis=0)
    grad_act = jnp.einsum("td,fd->tf", grad_down, down_w, preferred_element_type=F32)
    (grad_up_f,) = act_pull(grad_act)
    grad_up = grad_up_f.astype(BF)
    grad_up_w = jnp.einsum("td,tf->df", first_b, grad_up, preferred_element_type=F32)
    grad_up_b = jnp.sum(grad_up.astype(F32), axis=0)
    grad_first = grad_sum2 + jnp.einsum("tf,df->td", grad_up, up_w, preferred_element_type=F32)
    grad_sum1, grad_attn_g, grad_attn_s = first_pull(grad_first)
    grad_branch = grad_sum1.astype(BF)
    grad_out_w = jnp.dot(attn_t, grad_branch, preferred_element_type=F32)
    grad_out_b = jnp.sum(grad_branch.astype(F32), axis=0)
    grad_attn = jnp.einsum("te,de->td", grad_branch, out_w, preferred_element_type=F32).astype(BF)
    grad_q, grad_k, grad_v = attn_bwd(
        bounds, queries, query_doc, grad_attn, log_rows, mixed_t, keys, key_doc, values, tq=tile
    )
    def total(g):
        part = lax.psum_scatter(g.astype(BF), "wsh", scatter_dimension=0, tiled=True)
        return lax.psum(part, "ctx").astype(F32)

    grad_all = jnp.einsum("te,de->td", grad_k, key_w, preferred_element_type=F32)
    grad_all = grad_all + jnp.einsum("te,de->td", grad_v, value_w, preferred_element_type=F32)
    grad_own = lax.psum_scatter(grad_all.astype(BF), "ctx", scatter_dimension=0, tiled=True)
    grad_query_w = jnp.einsum("td,te->de", inputs, grad_q, preferred_element_type=F32)
    grad_key_w = jnp.einsum("td,te->de", all_tokens, grad_k, preferred_element_type=F32)
    grad_value_w = jnp.einsum("td,te->de", all_tokens, grad_v, preferred_element_type=F32)
    grad_query_b = jnp.sum(grad_q.astype(F32), axis=0)
    grad_value_b = jnp.sum(grad_v.astype(F32), axis=0)
    grad_inputs = grad_sum1 + jnp.einsum("te,de->td", grad_q, query_w, preferred_element_type=F32)
    grad_inputs = grad_inputs + grad_own.astype(F32)
    sums = [
        total(g)
        for g in (
            grad_query_w, grad_key_w, grad_value_w, grad_out_w, grad_up_w, grad_down_w,
            grad_query_b, grad_value_b, grad_out_b, grad_attn_g, grad_attn_s, grad_up_b,
            grad_down_b, grad_final_g, grad_final_s,
        )
    ]
    return (
        layer_out.reshape(1, tok_rows, D),
        grad_inputs.astype(BF).reshape(1, tok_rows, D),
        *sums,
    )


def solution(mesh):
    rows, mat, vec = P("wsh", "ctx", None), P("wsh", None), P("wsh")
    return jax.shard_map(
        local,
        mesh=mesh,
        in_specs=(rows, rows, mat) + (mat,) * 6 + (vec,) * 9,
        out_specs=(rows, rows) + (mat,) * 6 + (vec,) * 9,
        check_vma=False,
    )
```

```python
import functools

import jax
import jax.numpy as jnp
from jax import lax
from jax.experimental import pallas as pl
from jax.experimental.pallas import tpu as pltpu
from jax.sharding import PartitionSpec as P

D = 768
HEADS = 12
HD = 64
SCALE = 0.125
EPS = 1e-12
ROOT_HALF = 0.7071067811865476
BF = jnp.bfloat16
F32 = jnp.float32
NT = (((1,), (1,)), ((), ()))
NN = (((1,), (0,)), ((), ()))
TN = (((0,), (0,)), ((), ()))


def layer_norm(values, gain_vec, shift_vec):
    average = jnp.mean(values, axis=-1, keepdims=True)
    centred = values - average
    variance = jnp.mean(centred * centred, axis=-1, keepdims=True)
    return centred * lax.rsqrt(variance + EPS) * gain_vec + shift_vec


def gelu_act(values):
    return 0.5 * values * (1.0 + lax.erf(values * ROOT_HALF))


def key_range(docs, first_row, tile, stream_rows):
    last = first_row + tile - 1
    low, high = 0, stream_rows
    for d in range(1, docs.shape[0]):
        low = jnp.where(docs[d] <= first_row, docs[d], low)
    for d in range(docs.shape[0] - 1, 0, -1):
        high = jnp.where(docs[d] > last, docs[d], high)
    first = low // 128 * 128
    count = (high - first + 255) // 256
    return jnp.minimum(first, stream_rows - count * 256), count


def document_lanes(doc_start, first_row, rows, stream_rows):
    far = jnp.full((128 - doc_start.shape[0],), 2**30, jnp.int32)
    starts = jnp.concatenate([doc_start, far])
    ends = jnp.concatenate([doc_start[1:], jnp.full((1,), stream_rows, jnp.int32), far])
    query_pos = first_row + jnp.arange(rows, dtype=jnp.int32)[:, None]
    key_pos = jnp.arange(stream_rows, dtype=jnp.int32)[:, None]
    query_doc = ((query_pos >= starts) & (query_pos < ends)).astype(BF)
    key_doc = jnp.where((key_pos >= starts) & (key_pos < ends), 0.0, -1e30).astype(BF)
    return query_doc, key_doc


def stack_heads(x, extra=None):
    lane = lax.broadcasted_iota(jnp.int32, x.shape, 1)
    zero = jnp.zeros_like(x)
    lo = jnp.where(lane < 64, x, zero)
    hi = jnp.where(lane < 64, zero, x)
    if extra is not None:
        lo = jnp.concatenate([lo, extra], axis=1)
        hi = jnp.concatenate([hi, extra], axis=1)
    return jnp.concatenate([lo, hi], axis=0)

def pick_heads(x, tq):
    return jnp.concatenate([x[:64, :tq], x[64:, tq:]], axis=0)

def two_level(start, count, tk, body, init):
    big = tk // 256
    whole = count // big
    def large(t, c):
        return body(pl.multiple_of(t * tk, 256), pl.multiple_of(start + t * tk, 128), tk, c)
    def small(t, c):
        return body(pl.multiple_of(t * 256, 256), pl.multiple_of(start + t * 256, 128), 256, c)
    c = lax.fori_loop(0, whole, large, init)
    return lax.fori_loop(whole * big, count, small, c)

def fwd_kernel(tk, docs, q_ref, qaug_ref, k_ref, kaug_ref, v_ref, ot_ref, lse_ref, s_scr, acc):
    qi = pl.program_id(1)
    tq = q_ref.shape[0]
    first_row = lax.axis_index("ctx") * (tq * pl.num_programs(1)) + qi * tq
    start, count = key_range(docs, first_row, tq, k_ref.shape[0])
    rhs = stack_heads(q_ref[...], qaug_ref[...])

    def scores(loc, off, size, m):
        lhs = jnp.concatenate([k_ref[pl.ds(off, size), :], kaug_ref[pl.ds(off, size), :]], axis=1)
        s = lax.dot_general(lhs, rhs, NT, preferred_element_type=F32)
        s_scr[pl.ds(loc, size), :] = s
        return jnp.maximum(m, jnp.max(s.reshape(size // 8, 8, 2 * tq), axis=0))

    m8 = two_level(start, count, tk, scores, jnp.full((8, 2 * tq), -3e38, F32))
    m = jnp.max(m8, axis=0, keepdims=True)
    acc[...] = jnp.zeros_like(acc)

    def mix(loc, off, size, l8):
        p = jnp.exp(s_scr[pl.ds(loc, size), :] - m)
        acc[...] += lax.dot_general(v_ref[pl.ds(off, size), :], p.astype(BF), TN, preferred_element_type=F32)
        return l8 + jnp.sum(p.reshape(size // 8, 8, 2 * tq), axis=0)

    l8 = two_level(start, count, tk, mix, jnp.zeros((8, 2 * tq), F32))
    l = jnp.sum(l8, axis=0, keepdims=True)
    ot_ref[...] = pick_heads(acc[...] / l, tq)
    lse = m + jnp.log(l)
    lse_ref[0] = jnp.concatenate([lse[:, :tq], lse[:, tq:]], axis=0)

def attn_fwd(docs, q, qaug, k, kaug, v, *, tq=512, tk=768):
    T, D = q.shape
    S = k.shape[0]
    pairs = D // 128
    return pl.pallas_call(
        functools.partial(fwd_kernel, tk),
        out_shape=(jax.ShapeDtypeStruct((D, T), F32), jax.ShapeDtypeStruct((pairs, 2, T), F32)),
        grid_spec=pltpu.PrefetchScalarGridSpec(
            num_scalar_prefetch=1, grid=(pairs, T // tq),
            in_specs=[pl.BlockSpec((tq, 128), lambda h, i, b: (i, h)),
                      pl.BlockSpec((tq, 128), lambda h, i, b: (i, 0)),
                      pl.BlockSpec((S, 128), lambda h, i, b: (0, h)),
                      pl.BlockSpec((S, 128), lambda h, i, b: (0, 0)),
                      pl.BlockSpec((S, 128), lambda h, i, b: (0, h))],
            out_specs=(pl.BlockSpec((128, tq), lambda h, i, b: (h, i)),
                       pl.BlockSpec((1, 2, tq), lambda h, i, b: (h, 0, i))),
            scratch_shapes=[pltpu.VMEM((S, 2 * tq), F32), pltpu.VMEM((128, 2 * tq), F32)]),
        name="attend",
    )(docs, q, qaug, k, kaug, v)

def bwd_kernel(tk, docs, q_ref, qaug_ref, do_ref, lse_ref, ot_ref, k_ref, kaug_ref, v_ref,
               dq_ref, dk_ref, dv_ref, dk_acc, dv_acc, dq_acc):
    qi = pl.program_id(1)
    tq = q_ref.shape[0]
    first_row = lax.axis_index("ctx") * (tq * pl.num_programs(1)) + qi * tq
    start, count = key_range(docs, first_row, tq, k_ref.shape[0])

    @pl.when(qi == 0)
    def _():
        dk_acc[...] = jnp.zeros_like(dk_acc)
        dv_acc[...] = jnp.zeros_like(dv_acc)

    qs = stack_heads(q_ref[...])
    qrhs = stack_heads(q_ref[...], qaug_ref[...])
    dos = stack_heads(do_ref[...])
    lse = jnp.concatenate([lse_ref[0, 0:1, :], lse_ref[0, 1:2, :]], axis=1)
    mixed = ot_ref[...] * do_ref[...].astype(F32).T
    delta = jnp.concatenate(
        [jnp.sum(mixed[:64], axis=0, keepdims=True), jnp.sum(mixed[64:], axis=0, keepdims=True)], axis=1
    )
    dq_acc[...] = jnp.zeros_like(dq_acc)

    def step(loc, off, size, carry):
        rows = pl.ds(off, size)
        lhs = jnp.concatenate([k_ref[rows, :], kaug_ref[rows, :]], axis=1)
        x = lax.dot_general(lhs, qrhs, NT, preferred_element_type=F32)
        y = lax.dot_general(v_ref[rows, :], dos, NT, preferred_element_type=F32)
        p = jnp.exp(x - lse)
        ds = (p * (y - delta)).astype(BF)
        pb = p.astype(BF)
        dv_acc[rows, :] += lax.dot_general(pb, dos, NN, preferred_element_type=F32)
        dk_acc[rows, :] += lax.dot_general(ds, qs, NN, preferred_element_type=F32)
        dq_acc[...] += lax.dot_general(k_ref[rows, :], ds, TN, preferred_element_type=F32)
        return carry

    two_level(start, count, tk, step, 0)
    dq_ref[...] = (pick_heads(dq_acc[...], tq) * SCALE).T.astype(BF)

    @pl.when(qi == pl.num_programs(1) - 1)
    def _():
        dk_ref[...] = dk_acc[...].astype(BF)
        dv_ref[...] = dv_acc[...].astype(BF)

def attn_bwd(docs, q, qaug, do, lse, ot, k, kaug, v, *, tq=512, tk=768):
    T, D = q.shape
    S = k.shape[0]
    pairs = D // 128
    row = lambda h, i, b: (h, 0, i)
    return pl.pallas_call(
        functools.partial(bwd_kernel, tk),
        out_shape=(jax.ShapeDtypeStruct((T, D), BF), jax.ShapeDtypeStruct((S, D), BF), jax.ShapeDtypeStruct((S, D), BF)),
        grid_spec=pltpu.PrefetchScalarGridSpec(
            num_scalar_prefetch=1, grid=(pairs, T // tq),
            in_specs=[pl.BlockSpec((tq, 128), lambda h, i, b: (i, h)),
                      pl.BlockSpec((tq, 128), lambda h, i, b: (i, 0)),
                      pl.BlockSpec((tq, 128), lambda h, i, b: (i, h)),
                      pl.BlockSpec((1, 2, tq), row),
                      pl.BlockSpec((128, tq), lambda h, i, b: (h, i)),
                      pl.BlockSpec((S, 128), lambda h, i, b: (0, h)),
                      pl.BlockSpec((S, 128), lambda h, i, b: (0, 0)),
                      pl.BlockSpec((S, 128), lambda h, i, b: (0, h))],
            out_specs=(pl.BlockSpec((tq, 128), lambda h, i, b: (i, h)),
                       pl.BlockSpec((S, 128), lambda h, i, b: (0, h)),
                       pl.BlockSpec((S, 128), lambda h, i, b: (0, h))),
            scratch_shapes=[pltpu.VMEM((S, 128), F32), pltpu.VMEM((S, 128), F32), pltpu.VMEM((128, 2 * tq), F32)]),
        name="attend_back",
    )(docs, q, qaug, do, lse, ot, k, kaug, v)


def middle_kernel(attn_ref, in_ref, cot_ref, vec_ref, wo_ref, wu_ref, down_own, down_far,
                  out_ref, sum1_ref, do_ref, grads_ref, up_out, down_out, attn_out,
                  wo, wu, wd, attn_b, first, hat1, scale1, first_b, act, slope, sum2, down_b, up_b, first_b2, first_t,
                  g_up, g_down, g_out, sem_w, sem_d, sem_o):
    rows, wide = in_ref.shape[0], wu.shape[1]
    a, w = lax.axis_index("ctx"), lax.axis_index("wsh")
    y, c = w // 2, lax.rem(w, 2)
    core_peer = (a, y * 2 + (1 - c))
    tall = down_own.shape[0]
    MESH = pl.DeviceIdType.MESH
    barrier = pltpu.get_barrier_semaphore()
    pl.semaphore_signal(barrier, inc=1, device_id=core_peer, device_id_type=MESH)
    pl.semaphore_wait(barrier, 1)
    passed = []
    for s, (ref, owner) in enumerate(((down_own, w), (down_far, (1 - y) * 2 + c))):
        there = wd.at[pl.ds(pl.multiple_of(owner * tall, 16), tall), :]
        passed.append(pltpu.make_async_remote_copy(
            src_ref=ref, dst_ref=there, send_sem=sem_d.at[0, s], recv_sem=sem_d.at[1, s],
            device_id=core_peer, device_id_type=MESH))
        passed[-1].start()
        pltpu.make_async_copy(ref, there, sem_w.at[2 + s]).start()
    loading = [pltpu.make_async_copy(wo_ref, wo, sem_w.at[0]), pltpu.make_async_copy(wu_ref, wu, sem_w.at[1])]
    for copy in loading:
        copy.start()

    def arrived(j):
        if j < 2:
            loading[j].wait()
        else:
            for s, owner in enumerate((w, (1 - y) * 2 + c)):
                there = wd.at[pl.ds(pl.multiple_of(owner * tall, 16), tall), :]
                pltpu.make_async_copy(there, there, sem_w.at[2 + s]).wait()
                passed[s].wait_recv()

    grads_ref[...] = jnp.zeros_like(grads_ref)
    attn_b[...] = attn_ref[...].astype(BF)
    out_b, attn_g, attn_s, down_bias, final_g, final_s = [vec_ref[i : i + 1, :] for i in range(2, 8)]
    arrived(0)
    block = 128

    def over_rows(fn):
        def one(i, carry):
            fn(pl.ds(pl.multiple_of(i * block, block), block))
            return carry

        lax.fori_loop(0, rows // block, one, 0)

    def norm(values):
        average = jnp.mean(values, axis=-1, keepdims=True)
        centred = values - average
        scale = lax.rsqrt(jnp.mean(centred * centred, axis=-1, keepdims=True) + EPS)
        return centred * scale, scale

    def norm_back(grad, hat, scale, gain):
        g = grad * gain
        return scale * (g - jnp.mean(g, axis=-1, keepdims=True) - hat * jnp.mean(g * hat, axis=-1, keepdims=True))

    def note(row, values):
        grads_ref[row : row + 1, :] += jnp.sum(values, axis=0, keepdims=True)

    def branch_part(r):
        a = attn_b[:, r].T
        v = lax.dot_general(a, wo[...], NN, preferred_element_type=F32) + out_b + in_ref[r, :].astype(F32)
        hat, scale = norm(v)
        hat1[r, :] = hat
        scale1[r, :] = scale
        f = hat * attn_g + attn_s
        first[r, :] = f
        first_b[r, :] = f.astype(BF)

    over_rows(branch_part)
    arrived(1)
    cols = vec_ref.shape[1]

    def over_wide(fn):
        def one(i, carry):
            fn(pl.ds(pl.multiple_of(i * cols, cols), cols), i)
            return carry

        lax.fori_loop(0, wide // cols, one, 0)

    def up_part(n, i):
        u = lax.dot_general(first_b[...], wu[:, n], NN, preferred_element_type=F32) + vec_ref[pl.ds(8 + i, 1), :]
        half = 0.5 * (1.0 + lax.erf(u * ROOT_HALF))
        act[:, n] = (u * half).astype(BF)
        slope[:, n] = half + u * (0.3989422804014327 * jnp.exp(-0.5 * u * u))

    over_wide(up_part)
    arrived(2)

    def down_part(r):
        v = lax.dot_general(act[r, :], wd[...], NN, preferred_element_type=F32) + down_bias + first[r, :]
        hat, scale = norm(v)
        out_ref[r, :] = (hat * final_g + final_s).astype(BF)
        cot = cot_ref[r, :].astype(F32)
        note(6, cot * hat)
        note(7, cot)
        g = norm_back(cot, hat, scale, final_g)
        sum2[r, :] = g
        rounded = g.astype(BF)
        down_b[r, :] = rounded
        note(5, rounded.astype(F32))

    over_rows(down_part)

    def up_back(n, i):
        g = lax.dot_general(down_b[...], wd[n, :], NT, preferred_element_type=F32) * slope[:, n]
        rounded = g.astype(BF)
        up_b[:, n] = rounded
        grads_ref[pl.ds(8 + i, 1), :] = jnp.sum(rounded.astype(F32), axis=0, keepdims=True)

    over_wide(up_back)

    def first_part(r):
        g = sum2[r, :] + lax.dot_general(up_b[r, :], wu[...], NT, preferred_element_type=F32)
        hat = hat1[r, :]
        note(3, g * hat)
        note(4, g)
        s1 = norm_back(g, hat, scale1[r, :], attn_g)
        sum1_ref[r, :] = s1
        rounded = s1.astype(BF)
        note(2, rounded.astype(F32))
        first_b2[r, :] = rounded

    over_rows(first_part)

    def do_part(r):
        do_ref[r, :] = lax.dot_general(first_b2[r, :], wo[...], NT, preferred_element_type=F32).astype(BF)

    over_rows(do_part)

    def wide_grads(n, i):
        g_down[n, :] = lax.dot_general(act[:, n].T, down_b[...], NN, preferred_element_type=F32).astype(BF)
        pltpu.make_async_copy(g_down.at[n, :], down_out.at[n, :], sem_o.at[0, i]).start()
        g_up[:, n] = lax.dot_general(first_t[...], up_b[:, n], NN, preferred_element_type=F32).astype(BF)
        pltpu.make_async_copy(g_up.at[:, n], up_out.at[:, n], sem_o.at[1, i]).start()

    first_t[...] = first_b[...].T
    over_wide(wide_grads)
    g_out[...] = lax.dot_general(attn_b[...], first_b2[...], NN, preferred_element_type=F32).astype(BF)
    pltpu.make_async_copy(g_out, attn_out, sem_o.at[2, 0]).start()

    def wide_end(n, i):
        pltpu.make_async_copy(g_down.at[n, :], down_out.at[n, :], sem_o.at[0, i]).wait()
        pltpu.make_async_copy(g_up.at[:, n], up_out.at[:, n], sem_o.at[1, i]).wait()

    over_wide(wide_end)
    pltpu.make_async_copy(g_out, attn_out, sem_o.at[2, 0]).wait()
    for copy in passed:
        copy.wait_send()


def middle(attn_t, inputs, cotangent, vec, out_w, up_w, down_own, down_far):
    rows = inputs.shape[0]
    wide = up_w.shape[1]
    vm, dma, shape = pltpu.VMEM, pltpu.SemaphoreType.DMA, jax.ShapeDtypeStruct
    any_spec = pl.BlockSpec(memory_space=pltpu.HBM)
    vm_spec = pl.BlockSpec(memory_space=pltpu.VMEM)
    return pl.pallas_call(
        middle_kernel,
        out_shape=(shape((rows, D), BF), shape((rows, D), F32), shape((rows, D), BF), shape((16, D), F32),
                   shape((D, wide), BF), shape((wide, D), BF), shape((D, D), BF)),
        in_specs=[vm_spec] * 4 + [any_spec] * 4,
        out_specs=(vm_spec,) * 4 + (any_spec,) * 3,
        scratch_shapes=[
            vm((D, D), BF), vm((D, wide), BF), vm((wide, D), BF), vm((D, rows), BF), vm((rows, D), F32),
            vm((rows, D), F32), vm((rows, 1), F32), vm((rows, D), BF), vm((rows, wide), BF), vm((rows, wide), F32),
            vm((rows, D), F32), vm((rows, D), BF), vm((rows, wide), BF), vm((rows, D), BF), vm((D, rows), BF),
            vm((D, wide), BF), vm((wide, D), BF), vm((D, D), BF), dma((4,)), dma((2, 2)), dma((3, wide // D)),
        ],
        compiler_params=pltpu.CompilerParams(collective_id=3, has_side_effects=True, vmem_limit_bytes=63 * 2**20),
        name="middle",
    )(attn_t, inputs, cotangent, vec, out_w, up_w, down_own, down_far)


def reach(n_ctx):
    return n_ctx // 2


def finish_kernel(sources, n_parts, *refs):
    parts = refs[:n_parts]
    (vec_ref, dk_ref, dv_ref, tok_ref, dq_ref, w_ref, own_in_ref, mine_tok_ref,
     out_ref, vec_out, wide_out, grad_ref,
     mine, buf_a, buf_h, buf_b, buf_s, buf_c, buf_d, buf_e, gbf,
     sums, heard, line,
     loads, weights, acc, dq, own, bias,
     run_part, from_x, from_z, far_z, last_x,
     sem_l, sem_a, sem_b, sem_c, sem_d, sem_v, sem_x, sem_z, sem_far, sem_load, sem_in) = refs[n_parts:]
    n_ready = len(sources)
    n_chunks = out_ref.shape[0]
    n_ctx, n_wsh = lax.axis_size("ctx"), lax.axis_size("wsh")
    zs = n_ctx // 2
    a, w = lax.axis_index("ctx"), lax.axis_index("wsh")
    z, x = a // 2, lax.rem(a, 2)
    y, c = w // 2, lax.rem(w, 2)
    core_peer = (a, y * 2 + (1 - c))
    y_peer = (a, (1 - y) * 2 + c)
    x_peer = (z * 2 + (1 - x), w)
    low, high = lax.rem(z, 2), z // 2
    pair_peer = ((z + 1 - 2 * low) * 2 + x, w)
    skip_peer = (lax.rem(z + 2, zs) * 2 + x, w)
    up_peer, down_peer = (a + 2, w), (a - 2, w)
    near = reach(n_ctx)
    hops = near // 2
    MESH = pl.DeviceIdType.MESH

    rows = out_ref.shape[1]
    half = out_ref.shape[2] // 2
    piece = rows // zs
    tall = own.shape[0]
    cut = from_x.shape[1]

    def z_peer(d):
        return (lax.rem(z + d, zs) * 2 + x, w)

    barrier = pltpu.get_barrier_semaphore()
    for dev in [core_peer, y_peer, x_peer] + [z_peer(d) for d in range(1, zs)]:
        pl.semaphore_signal(barrier, inc=1, device_id=dev, device_id_type=MESH)
    pl.semaphore_wait(barrier, zs + 2)

    def send(src, dst, sems, idx, dev):
        return pltpu.make_async_remote_copy(
            src_ref=src, dst_ref=dst, send_sem=sems.at[(0,) + idx], recv_sem=sems.at[(1,) + idx],
            device_id=dev, device_id_type=MESH)

    def wait_in(ref, sems, idx):
        send(ref, ref, sems, idx, core_peer).wait_recv()

    def wait_out(ref, sems, idx):
        send(ref, ref, sems, idx, core_peer).wait_send()

    def distance(i):
        return (hops - i // 4) * (1 - 2 * lax.rem(i // 2, 2))

    def position(i):
        dz = distance(i)
        mine_too = lax.rem(i, 2)
        run = 2 * (z + dz) + (1 - x) * (1 - mine_too) + x * mine_too
        return run, mine_too, (z + dz >= 0) & (z + dz < zs) & (jnp.abs(run - a) <= near)

    n_pos = 4 * hops + 2

    def load(i):
        run, _mine_too, there = position(i)
        return there, [
            pltpu.make_async_copy(src.at[run], loads.at[lax.rem(i, 2), j], sem_load.at[lax.rem(i, 2), j])
            for j, src in enumerate((dk_ref, dv_ref, tok_ref))
        ]

    def load_start(i):
        there, copies = load(i)

        @pl.when(there & (i < n_pos))
        def _():
            for copy in copies:
                copy.start()

    def share(k, owner):
        if k < n_ready:
            p, row0, col0 = sources[k]
            return parts[p].at[owner, pl.ds(row0, rows), pl.ds(col0, 2 * half)]
        return gbf.at[k - n_ready, owner]

    def share_load(k):
        for yy in range(2):
            pltpu.make_async_copy(share(k, yy * 2 + c), mine.at[k % 4, yy], sem_l.at[k]).start()

    def share_send(k):
        for yy in range(2):
            send(share(k, yy * 2 + (1 - c)), buf_a.at[k, yy], sem_a, (k,), core_peer).start()

    load_start(0)
    fetch = [pltpu.make_async_copy(w_ref, weights, sem_in.at[0]), pltpu.make_async_copy(dq_ref, dq, sem_in.at[1]),
             pltpu.make_async_copy(own_in_ref, own, sem_in.at[2])]
    for copy in fetch:
        copy.start()
    for k in range(n_ready):
        share_send(k)
        if k < 4:
            share_load(k)
    acc[...] = jnp.zeros_like(acc)
    bias[...] = jnp.zeros_like(bias)
    fetch[0].wait()

    near_rows, far_rows = pl.ds(0, cut), pl.ds(cut, tall - cut)

    def unit(i):
        run, mine_too, there = position(i)
        at = lax.rem(i, 2)
        load_start(i + 1)

        @pl.when(there)
        def _():
            for copy in load(i)[1]:
                copy.wait()

            def tokens_part(r, carry):
                rs = pl.ds(pl.multiple_of(r * 128, 128), 128)
                g = lax.dot_general(loads[at, 0, rs, :], weights[0], NT, preferred_element_type=F32)
                g = g + lax.dot_general(loads[at, 1, rs, :], weights[1], NT, preferred_element_type=F32)
                run_part[i, rs, :] = g.astype(BF)
                bias[0:8, :] += jnp.sum(loads[at, 1, rs, :].astype(F32).reshape(16, 8, 2 * half), axis=0)
                return carry

            lax.fori_loop(0, tall // 128, tokens_part, 0)

            @pl.when(mine_too == 0)
            def _():
                send(run_part.at[i, near_rows, :], from_x.at[i // 2], sem_x, (i // 2,), x_peer).start()

            @pl.when(i < 4)
            def _():
                far_send(i)

            def weights_part(r, carry):
                fs = pl.ds(pl.multiple_of(r * 256, 256), 256)
                flipped = loads[at, 2, :, fs].T
                for j in range(2):
                    acc[j, fs, :] += lax.dot_general(flipped, loads[at, j], NN, preferred_element_type=F32)
                return carry

            lax.fori_loop(0, 2 * half // 256, weights_part, 0)

    def from_below(i):
        dz = distance(i)
        step = 1 - 2 * lax.rem(i // 2, 2)
        sender, target = z - step, z - step + dz
        side = jnp.abs(2 * dz + (1 - 2 * x) * (1 - lax.rem(i, 2))) <= near
        return (sender >= 0) & (sender < zs) & (target >= 0) & (target < zs) & side

    def toward(i, copy_of):
        step = 1 - 2 * lax.rem(i // 2, 2)

        @pl.when(step == 1)
        def _():
            copy_of(up_peer).start()

        @pl.when(step == -1)
        def _():
            copy_of(down_peer).start()

    def far_send(i):
        toward(i, lambda dev: send(run_part.at[i, far_rows, :], far_z.at[i], sem_far, (i,), dev))

    def far_pass(i):
        _run, _mine_too, there = position(i)

        @pl.when(there)
        def _():
            @pl.when(from_below(i - 4))
            def _():
                wait_in(far_z.at[i - 4], sem_far, (i - 4,))
                run_part[i, far_rows, :] = (
                    run_part[i, far_rows, :].astype(F32) + far_z[i - 4].astype(F32)).astype(BF)

            far_send(i)

    def far_end():
        for col in range(2):
            total = n_pos - 2 + col
            for src in (4 + col, 6 + col):
                @pl.when(from_below(src))
                def _():
                    wait_in(far_z.at[src], sem_far, (src,))
                    run_part[total, far_rows, :] = (
                        run_part[total, far_rows, :].astype(F32) + far_z[src].astype(F32)).astype(BF)
            if col == 0:
                send(run_part.at[total, far_rows, :], last_x, sem_x, (n_pos // 2,), x_peer).start()
        own[far_rows, :] += run_part[n_pos - 1, far_rows, :].astype(F32)

    def near_pass(n):
        dz = distance(2 * n)
        i = 2 * n + 1

        @pl.when((z + dz >= 0) & (z + dz < zs))
        def _():
            @pl.when(jnp.abs(2 * dz + 2 * x - 1) <= near)
            def _():
                wait_in(from_x.at[n], sem_x, (n,))
                run_part[i, near_rows, :] = (
                    run_part[i, near_rows, :].astype(F32) + from_x[n].astype(F32)).astype(BF)

            @pl.when((n >= 2) & from_below(i - 4))
            def _():
                wait_in(from_z.at[n - 2], sem_z, (n - 2,))
                run_part[i, near_rows, :] = (
                    run_part[i, near_rows, :].astype(F32) + from_z[n - 2].astype(F32)).astype(BF)

            toward(i, lambda dev: send(run_part.at[i, near_rows, :], from_z.at[n], sem_z, (n,), dev))

    def near_own():
        n = n_pos // 2 - 1
        wait_in(from_x.at[n], sem_x, (n,))
        own[near_rows, :] += run_part[n_pos - 1, near_rows, :].astype(F32) + from_x[n].astype(F32)

    def near_end():
        for n in (2, 3):
            @pl.when(from_below(2 * n + 1))
            def _():
                wait_in(from_z.at[n], sem_z, (n,))
                own[near_rows, :] += from_z[n].astype(F32)

    def add(p, q):
        return (p.astype(F32) + q.astype(F32)).astype(BF)

    def column(side):
        return pl.ds(pl.multiple_of(side * half, 128), half)

    def band(start, size):
        return pl.ds(pl.multiple_of(start, 16), size)

    def stage_b(k):
        at = lax.rem(k, 4)
        pltpu.make_async_copy(mine.at[at], mine.at[at], sem_l.at[k]).wait()
        wait_in(buf_a.at[k], sem_a, (k,))
        buf_h[k] = add(mine[at, 1 - y], buf_a[k, 1 - y])
        send(buf_h.at[k], buf_b.at[k], sem_b, (k,), y_peer).start()
        buf_a[k, y] = add(mine[at, y], buf_a[k, y])

    def stage_c(k):
        wait_in(buf_b.at[k], sem_b, (k,))
        buf_s[k] = add(buf_a[k, y, :, column(1 - x)], buf_b[k, :, column(1 - x)])
        send(buf_s.at[k], buf_c.at[k], sem_c, (0, k), x_peer).start()

    my_two, other_two = band(low * 2 * piece, 2 * piece), band((1 - low) * 2 * piece, 2 * piece)
    my_one, other_one = band(high * piece, piece), band((1 - high) * piece, piece)
    my_rows = band(low * 2 * piece + high * piece, piece)

    def stage_d(k):
        wait_in(buf_c.at[k], sem_c, (0, k))
        cols = column(x)
        joined = buf_a[k, y, :, cols].astype(F32) + buf_b[k, :, cols].astype(F32) + buf_c[k].astype(F32)
        buf_c[k] = joined.astype(BF)
        send(buf_c.at[k, other_two, :], buf_d.at[k], sem_d, (0, k), pair_peer).start()

    def stage_d2(k):
        wait_in(buf_d.at[k], sem_d, (0, k))
        buf_d[k] = add(buf_d[k], buf_c[k, my_two, :])
        send(buf_d.at[k, other_one, :], buf_e.at[k], sem_d, (1, k), skip_peer).start()

    def stage_e(k):
        wait_in(buf_e.at[k], sem_d, (1, k))
        buf_e[k] = add(buf_e[k], buf_d[k, my_one, :])
        out_ref[k, my_rows, column(x)] = buf_e[k]
        send(buf_e.at[k], out_ref.at[k, my_rows, column(x)], sem_d, (2, k), skip_peer).start()

    def stage_e2(k):
        wait_in(buf_e.at[k], sem_d, (2, k))
        there = out_ref.at[k, my_two, column(x)]
        send(there, there, sem_d, (3, k), pair_peer).start()

    def stage_f(k):
        wait_in(buf_d.at[k], sem_d, (3, k))
        there = out_ref.at[k, :, column(x)]
        send(there, there, sem_c, (1, k), x_peer).start()

    def guarded(fn, k, first, last):
        @pl.when((k >= first) & (k < last))
        def _():
            fn(k)

    def chunk_step(m):
        for lag, stage in enumerate((stage_c, stage_d, stage_d2, stage_e, stage_e2, stage_f)):
            guarded(stage, m - (lag and lag + 5), 0, n_chunks)

    def first_step(t, carry):
        guarded(unit, t, 0, n_pos)
        for j in range(2):
            guarded(stage_b, 2 * t + j, 0, n_ready)
        for k in range(4, n_ready):
            @pl.when(t == (k - 4) // 2)
            def _():
                share_load(k)

        @pl.when(lax.rem(t, 2) == 1)
        def _():
            guarded(near_pass, t // 2 - 1, 0, 4)

        guarded(far_pass, t - 2, 4, 8)

        @pl.when((lax.rem(t, 2) == 0) & (t >= 2))
        def _():
            chunk_step(t // 2 - 1)

        return carry

    lax.fori_loop(0, n_pos, first_step, 0)
    done = n_pos // 2 - 1

    fetch[1].wait()
    fetch[2].wait()
    own_tok = pltpu.make_async_copy(mine_tok_ref, loads.at[0, 2], sem_load.at[0, 2])
    own_tok.start()

    def to_bf(j, target):
        for owner in range(n_wsh):
            gbf[target, owner] = acc[j, owner * rows : (owner + 1) * rows, :].astype(BF)
        share_load(n_ready + target)
        share_send(n_ready + target)

    to_bf(0, 0)
    to_bf(1, 1)
    own_tok.wait()

    def query_part(r, carry):
        fs = pl.ds(pl.multiple_of(r * 256, 256), 256)
        acc[0, fs, :] = lax.dot_general(loads[0, 2, :, fs].T, dq[...], NN, preferred_element_type=F32)
        return carry

    lax.fori_loop(0, 2 * half // 256, query_part, 0)
    to_bf(0, 2)

    def query_tokens(r, carry):
        rs = pl.ds(pl.multiple_of(r * 128, 128), 128)
        own[rs, :] += lax.dot_general(dq[rs, :], weights[2], NT, preferred_element_type=F32)
        bias[8:16, :] += jnp.sum(dq[rs, :].astype(F32).reshape(16, 8, 2 * half), axis=0)
        return carry

    lax.fori_loop(0, tall // 128, query_tokens, 0)

    sums[0] = vec_ref[...]
    sums[0, 0:1, :] = jnp.sum(bias[8:16, :], axis=0, keepdims=True)
    sums[0, 1:2, :] = jnp.sum(bias[0:8, :], axis=0, keepdims=True)
    pair = (core_peer, y_peer, x_peer)

    def vec_send(stage):
        send(sums.at[stage], heard.at[stage], sem_v, (stage,), pair[stage]).start()

    def vec_stage(stage):
        wait_in(heard.at[stage], sem_v, (stage,))
        total = sums[stage] + heard[stage]
        sums[stage + 1] = total
        if stage < 2:
            vec_send(stage + 1)
        else:
            line[z] = total
            for d in range(1, zs):
                send(sums.at[3], line.at[z], sem_v, (3,), z_peer(d)).start()

    def vec_last():
        wait_in(line.at[pl.ds(0, zs - 1)], sem_v, (3,))
        total = line[0]
        for d in range(1, zs):
            total = total + line[d]
        small, wide = total[0:8, 0:rows], total[8:9, :]
        for owner in range(1, n_wsh):
            small = jnp.where(w == owner, total[0:8, owner * rows : (owner + 1) * rows], small)
            wide = jnp.where(w == owner, total[8 + owner : 9 + owner, :], wide)
        vec_out[...] = small
        wide_out[...] = wide

    vec_send(0)

    def second_step(m, carry):
        guarded(stage_b, m - done + n_ready, n_ready, n_chunks)
        chunk_step(m)
        guarded(lambda k: near_own(), m - done, 0, 1)
        for stage in range(3):
            guarded(lambda k: vec_stage(stage), m - done - 1 - stage, 0, 1)
        guarded(lambda k: near_end(), m - done - 3, 0, 1)
        guarded(lambda k: far_end(), m - done - 4, 0, 1)
        guarded(lambda k: vec_last(), m - done - 5, 0, 1)
        return carry

    lax.fori_loop(done, n_chunks + 10, second_step, 0)
    wait_in(last_x, sem_x, (n_pos // 2,))
    own[far_rows, :] += last_x[...].astype(F32)
    grad_ref[...] = own[...].astype(BF)

    def drain(k, carry):
        wait_in(buf_s.at[k], sem_c, (1, k))
        wait_out(buf_a.at[k], sem_a, (k,))
        wait_out(buf_b.at[k], sem_b, (k,))
        wait_out(buf_s.at[k], sem_c, (0, k))
        wait_out(buf_s.at[k], sem_c, (1, k))
        wait_out(buf_d.at[k], sem_d, (0, k))
        wait_out(buf_e.at[k], sem_d, (1, k))
        wait_out(buf_e.at[k], sem_d, (2, k))
        wait_out(buf_d.at[k], sem_d, (3, k))
        return carry

    lax.fori_loop(0, n_chunks, drain, 0)
    for stage in range(3):
        wait_out(heard.at[stage], sem_v, (stage,))
    wait_out(line.at[pl.ds(0, zs - 1)], sem_v, (3,))
    wait_out(last_x, sem_x, (n_pos // 2,))

    def drain_runs(i, carry):
        _run, mine_too, there = position(i)

        @pl.when(there)
        def _():
            wait_out(far_z.at[i], sem_far, (i,))

            @pl.when(mine_too == 1)
            def _():
                wait_out(from_z.at[i // 2], sem_z, (i // 2,))

        return carry

    lax.fori_loop(0, n_pos - 2, drain_runs, 0)

    def drain_x(n, carry):
        _run, _mine_too, there = position(2 * n)

        @pl.when(there)
        def _():
            wait_out(from_x.at[n], sem_x, (n,))

        return carry

    lax.fori_loop(0, n_pos // 2, drain_x, 0)


def widen_kernel(spans, in_ref, *outs):
    for (first, down, across), out in zip(spans, outs):
        for r in range(down):
            for col in range(across):
                out[r, :, col * D : (col + 1) * D] = in_ref[first + r * across + col].astype(F32)


def widen(summed, spans):
    n, rows, _width = summed.shape
    part = rows // 4
    outs = pl.pallas_call(
        functools.partial(widen_kernel, spans),
        grid=(4,),
        out_shape=[jax.ShapeDtypeStruct((down, rows, across * D), F32) for _first, down, across in spans],
        in_specs=[pl.BlockSpec((n, part, D), lambda i: (0, i, 0))],
        out_specs=[pl.BlockSpec((down, part, across * D), lambda i: (0, i, 0)) for _first, down, across in spans],
        name="widen",
    )(summed)
    return [o.reshape(-1, o.shape[2]) for o in outs]


def finish(matrices, vec, grad_k, grad_v, all_tokens, grad_q, kvq_w, own_grad, inputs):
    n_ctx, n_wsh = lax.axis_size("ctx"), lax.axis_size("wsh")
    zs, hops = n_ctx // 2, reach(n_ctx) // 2
    rows = D // n_wsh
    parts, sources, spans = [], [], []
    for p, g in enumerate(matrices):
        down, across = g.shape[0] // D, g.shape[1] // D
        parts.append(g.astype(BF).reshape(n_wsh, down * rows, across * D))
        spans.append((len(sources), down, across))
        sources += [(p, r * rows, col * D) for r in range(down) for col in range(across)]
    n = len(sources) + 3
    spans += [(len(sources) + j, 1, 1) for j in range(3)]
    half, piece, tall = D // 2, rows // zs, inputs.shape[0]
    n_pos, cut = 4 * hops + 2, tall // 2
    vm, dma, shape = pltpu.VMEM, pltpu.SemaphoreType.DMA, jax.ShapeDtypeStruct
    any_spec = pl.BlockSpec(memory_space=pltpu.HBM)
    vm_spec = pl.BlockSpec(memory_space=pltpu.VMEM)
    summed, small, wide, grad_own = pl.pallas_call(
        functools.partial(finish_kernel, sources, len(parts)),
        out_shape=(shape((n, rows, D), BF), shape((8, rows), F32), shape((1, D), F32), shape((tall, D), BF)),
        in_specs=[any_spec] * len(parts) + [vm_spec] + [any_spec] * 7,
        out_specs=(vm_spec,) * 4,
        scratch_shapes=[
            vm((4, 2, rows, D), BF), vm((n, 2, rows, D), BF), vm((n, rows, D), BF), vm((n, rows, D), BF),
            vm((n, rows, half), BF), vm((n, rows, half), BF), vm((n, 2 * piece, half), BF), vm((n, piece, half), BF),
            vm((3, n_wsh, rows, D), BF),
            vm((4,) + vec.shape, F32), vm((3,) + vec.shape, F32), vm((zs,) + vec.shape, F32),
            vm((2, 3, tall, D), BF), vm((3, D, D), BF), vm((2, D, D), F32), vm((tall, D), BF), vm((tall, D), F32),
            vm((16, D), F32),
            vm((n_pos, tall, D), BF), vm((n_pos // 2, cut, D), BF), vm((4, cut, D), BF),
            vm((n_pos - 2, tall - cut, D), BF), vm((tall - cut, D), BF),
            dma((n,)), dma((2, n)), dma((2, n)), dma((2, 2, n)), dma((2, 4, n)), dma((2, 4)),
            dma((2, n_pos // 2 + 1)), dma((2, 4)), dma((2, n_pos - 2)), dma((2, 3)), dma((3,)),
        ],
        compiler_params=pltpu.CompilerParams(collective_id=2, has_side_effects=True, vmem_limit_bytes=63 * 2**20),
        name="finish",
    )(*parts, vec, grad_k, grad_v, all_tokens, grad_q, kvq_w, own_grad, inputs)
    return widen(summed, spans), small, wide, grad_own


def gather_kernel(cut, tok_ref, docs_ref, wk_ref, wv_ref, wq_ref, wo_ref, wu_ref, vec_ref,
                  tok_out, k_out, v_out, q_out, w_out, vec_out, wo_out, wu_out, query_doc, key_doc,
                  tok, kbuf, vbuf, qbuf, wbuf, vecs, wo, wu, kdoc,
                  sem_in, sem_out, sem_w, sem_l, sem_o):
    n_ctx = lax.axis_size("ctx")
    zs = n_ctx // 2
    a, w = lax.axis_index("ctx"), lax.axis_index("wsh")
    z, x = a // 2, lax.rem(a, 2)
    y, c = w // 2, lax.rem(w, 2)
    core_peer = (a, y * 2 + (1 - c))
    y_peer = (a, (1 - y) * 2 + c)
    x_peer = (z * 2 + (1 - x), w)
    up, down = (a + 2, w), (a - 2, w)
    near = reach(n_ctx)
    MESH = pl.DeviceIdType.MESH
    n_slices = sem_in.shape[1]
    tall = tok.shape[1] // n_slices
    own = wk_ref.shape[0]
    far = 4 * (near // 2 + 1)

    barrier = pltpu.get_barrier_semaphore()
    around = [(lax.rem(z + d, zs) * 2 + x, w) for d in (1, zs - 1)]
    for dev in [core_peer, y_peer, x_peer] + around:
        pl.semaphore_signal(barrier, inc=1, device_id=dev, device_id_type=MESH)
    pl.semaphore_wait(barrier, 5)

    def relative(u):
        dz = (u // 4) * (1 - 2 * lax.rem(u, 2))
        other = lax.rem(u // 2, 2)
        run = 2 * (z + dz) + (x + other - 2 * x * other)
        there = (z + dz >= 0) & (z + dz < zs) & (jnp.abs(run - a) <= near) & ((u >= 4) | (lax.rem(u, 2) == 0))
        return run, dz, other, there

    def rows(s):
        return pl.ds(pl.multiple_of(s * tall, tall), tall)

    def remote(src, dst, send_sem, recv_sem, dev):
        return pltpu.make_async_remote_copy(
            src_ref=src, dst_ref=dst, send_sem=send_sem, recv_sem=recv_sem, device_id=dev, device_id_type=MESH)

    def routes(u, s):
        run, dz, other, there = relative(u)
        z_first = s < cut
        to_x = there & (z_first | (dz == 0)) & (other == 0) & (jnp.abs(run - x_peer[0]) <= near)
        along = there & ((other == 0) | jnp.logical_not(z_first))
        to_up = along & (dz <= 0) & (z + 1 < zs) & (jnp.abs(run - (a + 2)) <= near)
        to_down = along & (dz >= 0) & (z > 0) & (jnp.abs(run - (a - 2)) <= near)
        return run, ((0, x_peer, to_x), (1, up, to_up), (2, down, to_down))

    def pass_on(u, s):
        run, where = routes(u, s)
        for d, dev, ok in where:
            @pl.when(ok)
            def _():
                source = tok_ref if isinstance(u, int) and u == 0 else tok.at[run]
                remote(source.at[rows(s), :], tok.at[run, rows(s), :], sem_out.at[d, u, s], sem_in.at[run, s], dev).start()

    def await_slice(u, s):
        run, _dz, _other, there = relative(u)

        @pl.when(there)
        def _():
            remote(tok.at[run, rows(s), :], tok.at[run, rows(s), :], sem_out.at[0, 0, 0], sem_in.at[run, s], x_peer).wait_recv()

    def start_own(s, carry):
        pass_on(0, s)
        return carry

    def weight_rows(owner):
        return pl.ds(pl.multiple_of(owner * own, 16), own)

    def shard(m, owner):
        if m == 3:
            return vecs.at[owner]
        return (wbuf.at[0], wbuf.at[1], wbuf.at[2], None, wo, wu)[m].at[weight_rows(owner), :]

    vecs[w, 0 : vec_ref.shape[0], :] = vec_ref[...]
    shards = (wk_ref, wv_ref, wq_ref, vecs.at[w], wo_ref, wu_ref)
    for m in (3, 0, 1, 2, 4, 5):
        remote(shards[m], shard(m, w), sem_w.at[0, 1, m], sem_w.at[1, 1, m], y_peer).start()
        remote(shards[m], shard(m, w), sem_w.at[0, 0, m], sem_w.at[1, 0, m], core_peer).start()
        if m != 3:
            pltpu.make_async_copy(shards[m], shard(m, w), sem_w.at[0, 3, m]).start()
    lax.fori_loop(0, n_slices, start_own, 0)
    pltpu.make_async_copy(tok_ref, tok.at[a], sem_l.at[4]).start()

    for j in range(n_ctx):
        @pl.when(jnp.abs(j - a) > near)
        def _():
            tok[j] = jnp.zeros_like(tok[j])

    n_rows = tok.shape[1]

    def is_own_lane(first):
        pos = first + lax.broadcasted_iota(jnp.int32, (n_rows, 128), 0)
        doc = jnp.full((n_rows, 128), -1, jnp.int32)
        for d in range(docs_ref.shape[1]):
            doc = doc + jnp.where(pos >= docs_ref[0, d], 1, 0)
        return lax.broadcasted_iota(jnp.int32, (n_rows, 128), 1) == doc

    def key_lanes(j, carry):
        kdoc[pl.ds(pl.multiple_of(j * n_rows, n_rows), n_rows), :] = jnp.where(
            is_own_lane(j * n_rows), 0.0, -1e30).astype(BF)
        return carry

    lax.fori_loop(0, n_ctx, key_lanes, 0)
    pltpu.make_async_copy(kdoc, key_doc, sem_l.at[3]).start()
    query_doc[...] = jnp.where(is_own_lane(a * n_rows), 1.0, 0.0).astype(BF)

    def weight_arrival(m, kind):
        part = shard(m, w)
        return remote(part, part, sem_w.at[0, kind, m], sem_w.at[1, kind, m], core_peer)

    across = (1 - y) * 2 + c

    def weight_forward(m):
        weight_arrival(m, 1).wait_recv()
        remote(shard(m, across), shard(m, across), sem_w.at[0, 2, m], sem_w.at[1, 2, m], core_peer).start()

    def weight_end(m):
        weight_arrival(m, 0).wait_recv()
        weight_arrival(m, 2).wait_recv()
        if m != 3:
            pltpu.make_async_copy(shard(m, w), shard(m, w), sem_w.at[0, 3, m]).wait()

    def relay(first, last):
        def one(i, carry):
            s = i // (last - first)
            u = first + lax.rem(i, last - first)
            await_slice(u, s)
            pass_on(u, s)
            return carry

        lax.fori_loop(0, n_slices * (last - first), one, 0)

    relay(2, 6)
    weight_forward(3)
    weight_forward(0)
    weight_forward(1)
    weight_end(3)
    vec_out[0:8, :] = jnp.concatenate([vecs[o, 0:8, :] for o in range(4)], axis=1)
    for o in range(4):
        vec_out[8 + o : 9 + o, :] = jnp.concatenate([vecs[o, 8 + i : 9 + i, :] for i in range(4)], axis=1)
    pltpu.make_async_copy(tok_ref, tok.at[a], sem_l.at[4]).wait()
    weight_end(0)
    weight_end(1)

    step_rows = 128
    steps = tok.shape[1] // step_rows

    def query_part(i, carry):
        r = pl.ds(pl.multiple_of(i * step_rows, step_rows), step_rows)
        q = (jnp.dot(tok[a, r, :], wbuf[2], preferred_element_type=F32) + vec_out[0:1, :]).astype(BF)
        qbuf[r, :] = q * jnp.asarray(SCALE, BF)
        return carry

    def project(u, carry):
        run, _dz, _other, there = relative(u)

        @pl.when(u == 6)
        def _():
            weight_forward(2)
            weight_end(2)
            lax.fori_loop(0, steps, query_part, 0)
            pltpu.make_async_copy(qbuf, q_out, sem_l.at[5]).start()
            relay(6, 10)

        @pl.when(there)
        def _():
            @pl.when(u >= 10)
            def _():
                def one(s, carry):
                    await_slice(u, s)
                    return carry

                lax.fori_loop(0, n_slices, one, 0)

            def part(i, carry):
                r = pl.ds(pl.multiple_of(i * step_rows, step_rows), step_rows)
                t = tok[run, r, :]
                kbuf[run, r, :] = jnp.dot(t, wbuf[0], preferred_element_type=F32).astype(BF)
                vbuf[run, r, :] = (jnp.dot(t, wbuf[1], preferred_element_type=F32) + vec_out[1:2, :]).astype(BF)
                return carry

            lax.fori_loop(0, steps, part, 0)
            for i, (src, dst) in enumerate(((kbuf, k_out), (vbuf, v_out), (tok, tok_out))):
                pltpu.make_async_copy(src.at[run], dst.at[run], sem_o.at[i, run]).start()

        return carry

    for j in range(n_ctx):
        @pl.when(jnp.abs(j - a) > near)
        def _():
            kbuf[j] = jnp.zeros_like(kbuf[j])
            vbuf[j] = jnp.zeros_like(vbuf[j])
            for i, (src, dst) in enumerate(((kbuf, k_out), (vbuf, v_out), (tok, tok_out))):
                pltpu.make_async_copy(src.at[j], dst.at[j], sem_o.at[i, j]).start()

    lax.fori_loop(0, far, project, 0)

    pltpu.make_async_copy(wbuf, w_out, sem_l.at[6]).start()

    for m in (4, 5):
        weight_forward(m)
    for m, full, target in ((4, wo, wo_out), (5, wu, wu_out)):
        weight_end(m)
        pltpu.make_async_copy(full, target, sem_l.at[m - 4]).start()
    for m in range(6):
        for kind in range(3):
            weight_arrival(m, kind).wait_send()

    def drain(i, carry):
        s = i // far
        u = lax.rem(i, far)
        run, where = routes(u, s)
        for d, dev, ok in where:
            @pl.when(ok & (u < 10))
            def _():
                remote(tok.at[run, rows(s), :], tok.at[run, rows(s), :], sem_out.at[d, u, s], sem_in.at[run, s], dev).wait_send()
        return carry

    lax.fori_loop(0, n_slices * far, drain, 0)
    for j in range(n_ctx):
        for i, (src, dst) in enumerate(((kbuf, k_out), (vbuf, v_out), (tok, tok_out))):
            pltpu.make_async_copy(src.at[j], dst.at[j], sem_o.at[i, j]).wait()
    pltpu.make_async_copy(qbuf, q_out, sem_l.at[5]).wait()
    pltpu.make_async_copy(wbuf, w_out, sem_l.at[6]).wait()
    pltpu.make_async_copy(wo, wo_out, sem_l.at[0]).wait()
    pltpu.make_async_copy(wu, wu_out, sem_l.at[1]).wait()
    pltpu.make_async_copy(kdoc, key_doc, sem_l.at[3]).wait()


def gather_project(inputs, doc_starts, vectors, key_weight, value_weight, query_weight, out_weight, up_weight):
    n_ctx, n_wsh = lax.axis_size("ctx"), lax.axis_size("wsh")
    tall = inputs.shape[0]
    n_slices = 8
    far = 4 * (reach(n_ctx) // 2 + 1)
    vm, dma = pltpu.VMEM, pltpu.SemaphoreType.DMA
    any_spec = pl.BlockSpec(memory_space=pltpu.HBM)
    vm_spec = pl.BlockSpec(memory_space=pltpu.VMEM)
    runs = (n_ctx, tall, D)
    shape = jax.ShapeDtypeStruct
    return pl.pallas_call(
        functools.partial(gather_kernel, 5),
        out_shape=(shape(runs, BF), shape(runs, BF), shape(runs, BF), shape((tall, D), BF), shape((3, D, D), BF),
                   shape((16, D), F32), shape((D, D), BF), shape((D, up_weight.shape[1]), BF), shape((tall, 128), BF),
                   shape((n_ctx * tall, 128), BF)),
        in_specs=[any_spec, pl.BlockSpec(memory_space=pltpu.SMEM)] + [any_spec] * 5 + [vm_spec],
        out_specs=(any_spec,) * 5 + (vm_spec,) + (any_spec,) * 2 + (vm_spec, any_spec),
        scratch_shapes=[
            vm(runs, BF), vm(runs, BF), vm(runs, BF), vm((tall, D), BF), vm((3, D, D), BF), vm((n_wsh, 16, D // n_wsh), F32),
            vm((D, D), BF), vm((D, up_weight.shape[1]), BF), vm((n_ctx * tall, 128), BF),
            dma((n_ctx, n_slices)), dma((3, far, n_slices)), dma((2, 4, 6)), dma((7,)), dma((3, n_ctx)),
        ],
        compiler_params=pltpu.CompilerParams(collective_id=1, has_side_effects=True, vmem_limit_bytes=63 * 2**20),
        name="gather_project",
    )(inputs, doc_starts, key_weight, value_weight, query_weight, out_weight, up_weight, vectors)


def local(
    tokens,
    cotangent,
    doc_starts,
    query_weight,
    key_weight,
    value_weight,
    out_weight,
    up_weight,
    down_weight,
    query_bias,
    value_bias,
    out_bias,
    attn_gain,
    attn_shift,
    up_bias,
    down_bias,
    final_gain,
    final_shift,
):
    inputs = tokens[0]
    doc_start = doc_starts[0]
    tok_rows = inputs.shape[0]
    stream_rows = tok_rows * lax.axis_size("ctx")
    tile = min(tok_rows, 512)
    n_ctx, n_wsh = lax.axis_size("ctx"), lax.axis_size("wsh")
    own = D // n_wsh

    def gather(x):
        return lax.all_gather(x, "wsh", axis=0, tiled=True)

    fast = n_wsh == 4 and n_ctx == 8 and own % (n_ctx // 2 * 16) == 0 and tok_rows % 512 == 0
    if fast:
        small = (query_bias, value_bias, out_bias, attn_gain, attn_shift, down_bias, final_gain, final_shift)
        vectors = jnp.concatenate(small + (up_bias,)).astype(F32).reshape(8 + n_wsh, own)
        all_tokens, keys, values, queries, kvq_w, vec, out_w, up_w, query_doc, key_doc = gather_project(
            inputs, doc_starts, vectors, key_weight, value_weight, query_weight, out_weight, up_weight
        )
        down_own, _unused = lax.optimization_barrier((down_weight, vec))
        down_far = lax.ppermute(down_own, "wsh", [(i, i ^ 2) for i in range(n_wsh)])
        all_tokens, keys, values = [r.reshape(stream_rows, D) for r in (all_tokens, keys, values)]
    else:
        first_row = lax.axis_index("ctx") * tok_rows
        query_doc, key_doc = document_lanes(doc_start, first_row, tok_rows, stream_rows)
        small = jnp.stack(
            [query_bias, value_bias, out_bias, attn_gain, attn_shift, down_bias, final_gain, final_shift]
        )
        all_tokens = lax.all_gather(inputs, "ctx", axis=0, tiled=True)
        query_w, key_w, value_w = gather(query_weight), gather(key_weight), gather(value_weight)
        small = gather(small.T).astype(F32)
        query_b, value_b, out_b, attn_g, attn_s, down_b, final_g, final_s = [small[:, i] for i in range(8)]
        up_b = gather(up_bias).astype(F32)
        queries = jnp.dot(inputs, query_w, preferred_element_type=F32) + query_b
        queries = queries.astype(BF) * jnp.asarray(SCALE, BF)
        keys = jnp.dot(all_tokens, key_w, preferred_element_type=F32).astype(BF)
        values = (jnp.dot(all_tokens, value_w, preferred_element_type=F32) + value_b).astype(BF)
    mixed_t, log_rows = attn_fwd(doc_start, queries, query_doc, keys, key_doc, values, tq=tile)
    if fast:
        layer_out, grad_sum1, grad_attn, vec_grads, grad_up_w, grad_down_w, grad_out_w = middle(
            mixed_t, inputs, cotangent[0], vec, out_w, up_w, down_own, down_far
        )
        grad_q, grad_k, grad_v = attn_bwd(
            doc_start, queries, query_doc, grad_attn, log_rows, mixed_t, keys, key_doc, values, tq=tile
        )
        mats, small, wide, grad_inputs = finish(
            (grad_up_w, grad_out_w, grad_down_w), vec_grads, grad_k.reshape(n_ctx, tok_rows, D),
            grad_v.reshape(n_ctx, tok_rows, D), all_tokens.reshape(n_ctx, tok_rows, D), grad_q, kvq_w, grad_sum1, inputs,
        )
        up_sum, out_sum, down_sum, key_sum, value_sum, query_sum = mats
        return (
            layer_out.reshape(1, tok_rows, D), grad_inputs.reshape(1, tok_rows, D), query_sum, key_sum, value_sum,
            out_sum, up_sum, down_sum, small[0], small[1], small[2], small[3], small[4], wide[0],
            small[5], small[6], small[7],
        )

    out_w = gather(out_weight)
    up_w = gather(up_weight)
    down_w = gather(down_weight)
    attn_t = mixed_t.astype(BF)
    inputs_f = inputs.astype(F32)
    branch = lax.dot_general(attn_t, out_w, TN, preferred_element_type=F32) + out_b
    first_norm, first_pull = jax.vjp(layer_norm, inputs_f + branch, attn_g, attn_s)
    first_b = first_norm.astype(BF)
    up_f = jnp.dot(first_b, up_w, preferred_element_type=F32) + up_b
    act_f, act_pull = jax.vjp(gelu_act, up_f)
    act_b = act_f.astype(BF)
    down_f = jnp.dot(act_b, down_w, preferred_element_type=F32) + down_b
    final_f, final_pull = jax.vjp(layer_norm, first_norm + down_f, final_g, final_s)
    layer_out = final_f.astype(BF)

    grad_sum2, grad_final_g, grad_final_s = final_pull(cotangent[0].astype(F32))
    grad_down = grad_sum2.astype(BF)
    grad_down_w = jnp.einsum("tf,td->fd", act_b, grad_down, preferred_element_type=F32)
    grad_down_b = jnp.sum(grad_down.astype(F32), axis=0)
    grad_act = jnp.einsum("td,fd->tf", grad_down, down_w, preferred_element_type=F32)
    (grad_up_f,) = act_pull(grad_act)
    grad_up = grad_up_f.astype(BF)
    grad_up_w = jnp.einsum("td,tf->df", first_b, grad_up, preferred_element_type=F32)
    grad_up_b = jnp.sum(grad_up.astype(F32), axis=0)
    grad_first = grad_sum2 + jnp.einsum("tf,df->td", grad_up, up_w, preferred_element_type=F32)
    grad_sum1, grad_attn_g, grad_attn_s = first_pull(grad_first)
    grad_branch = grad_sum1.astype(BF)
    grad_out_w = jnp.dot(attn_t, grad_branch, preferred_element_type=F32)
    grad_out_b = jnp.sum(grad_branch.astype(F32), axis=0)
    grad_attn = jnp.einsum("te,de->td", grad_branch, out_w, preferred_element_type=F32).astype(BF)
    grad_q, grad_k, grad_v = attn_bwd(
        doc_start, queries, query_doc, grad_attn, log_rows, mixed_t, keys, key_doc, values, tq=tile
    )
    def total(g):
        part = lax.psum_scatter(g.astype(BF), "wsh", scatter_dimension=0, tiled=True)
        return lax.psum(part, "ctx").astype(F32)

    grad_all = jnp.einsum("te,de->td", grad_k, key_w, preferred_element_type=F32)
    grad_all = grad_all + jnp.einsum("te,de->td", grad_v, value_w, preferred_element_type=F32)
    grad_own = lax.psum_scatter(grad_all.astype(BF), "ctx", scatter_dimension=0, tiled=True)
    grad_query_w = jnp.einsum("td,te->de", inputs, grad_q, preferred_element_type=F32)
    grad_key_w = jnp.einsum("td,te->de", all_tokens, grad_k, preferred_element_type=F32)
    grad_value_w = jnp.einsum("td,te->de", all_tokens, grad_v, preferred_element_type=F32)
    grad_query_b = jnp.sum(grad_q.astype(F32), axis=0)
    grad_value_b = jnp.sum(grad_v.astype(F32), axis=0)
    grad_inputs = grad_sum1 + jnp.einsum("te,de->td", grad_q, query_w, preferred_element_type=F32)
    grad_inputs = grad_inputs + grad_own.astype(F32)
    sums = [
        total(g)
        for g in (
            grad_query_w, grad_key_w, grad_value_w, grad_out_w, grad_up_w, grad_down_w,
            grad_query_b, grad_value_b, grad_out_b, grad_attn_g, grad_attn_s, grad_up_b,
            grad_down_b, grad_final_g, grad_final_s,
        )
    ]
    return (
        layer_out.reshape(1, tok_rows, D),
        grad_inputs.astype(BF).reshape(1, tok_rows, D),
        *sums,
    )


def solution(mesh):
    rows, mat, vec = P("wsh", "ctx", None), P("wsh", None), P("wsh")
    return jax.shard_map(
        local,
        mesh=mesh,
        in_specs=(rows, rows, mat) + (mat,) * 6 + (vec,) * 9,
        out_specs=(rows, rows) + (mat,) * 6 + (vec,) * 9,
        check_vma=False,
    )
```

```python
import functools

import jax
import jax.numpy as jnp
from jax import lax
from jax.experimental import pallas as pl
from jax.experimental.pallas import tpu as pltpu
from jax.sharding import PartitionSpec as P

D = 768
HEADS = 12
HD = 64
SCALE = 0.125
EPS = 1e-12
ROOT_HALF = 0.7071067811865476
BF = jnp.bfloat16
F32 = jnp.float32
NT = (((1,), (1,)), ((), ()))
NN = (((1,), (0,)), ((), ()))
TN = (((0,), (0,)), ((), ()))


def layer_norm(values, gain_vec, shift_vec):
    average = jnp.mean(values, axis=-1, keepdims=True)
    centred = values - average
    variance = jnp.mean(centred * centred, axis=-1, keepdims=True)
    return centred * lax.rsqrt(variance + EPS) * gain_vec + shift_vec


def gelu_act(values):
    return 0.5 * values * (1.0 + lax.erf(values * ROOT_HALF))


def key_range(docs, first_row, tile, stream_rows):
    last = first_row + tile - 1
    low, high = 0, stream_rows
    for d in range(1, docs.shape[0]):
        low = jnp.where(docs[d] <= first_row, docs[d], low)
    for d in range(docs.shape[0] - 1, 0, -1):
        high = jnp.where(docs[d] > last, docs[d], high)
    first = low // 128 * 128
    count = (high - first + 255) // 256
    return jnp.minimum(first, stream_rows - count * 256), count


def document_lanes(doc_start, first_row, rows, stream_rows):
    far = jnp.full((128 - doc_start.shape[0],), 2**30, jnp.int32)
    starts = jnp.concatenate([doc_start, far])
    ends = jnp.concatenate([doc_start[1:], jnp.full((1,), stream_rows, jnp.int32), far])
    query_pos = first_row + jnp.arange(rows, dtype=jnp.int32)[:, None]
    key_pos = jnp.arange(stream_rows, dtype=jnp.int32)[:, None]
    query_doc = ((query_pos >= starts) & (query_pos < ends)).astype(BF)
    key_doc = jnp.where((key_pos >= starts) & (key_pos < ends), 0.0, -1e30).astype(BF)
    return query_doc, key_doc


def stack_heads(x, extra=None):
    lane = lax.broadcasted_iota(jnp.int32, x.shape, 1)
    zero = jnp.zeros_like(x)
    lo = jnp.where(lane < 64, x, zero)
    hi = jnp.where(lane < 64, zero, x)
    if extra is not None:
        lo = jnp.concatenate([lo, extra], axis=1)
        hi = jnp.concatenate([hi, extra], axis=1)
    return jnp.concatenate([lo, hi], axis=0)

def pick_heads(x, tq):
    return jnp.concatenate([x[:64, :tq], x[64:, tq:]], axis=0)

def two_level(start, count, tk, body, init):
    done, carried = 0, init
    for n in (6, 3, 1):
        if n * 256 > tk:
            continue

        def step(t, c, n=n, done=done):
            at = done + t * n
            return body(pl.multiple_of(at * 256, 256), pl.multiple_of(start + at * 256, 128), n * 256, c)

        trips = (count - done) // n
        carried = lax.fori_loop(0, trips, step, carried)
        done = done + trips * n
    return carried


def fwd_kernel(tk, docs, q_ref, qaug_ref, k_ref, kaug_ref, v_ref, ot_ref, lse_ref, s_scr, acc):
    qi = pl.program_id(1)
    tq = q_ref.shape[0]
    first_row = lax.axis_index("ctx") * (tq * pl.num_programs(1)) + qi * tq
    start, count = key_range(docs, first_row, tq, k_ref.shape[0])
    rhs = stack_heads(q_ref[...], qaug_ref[...])

    def scores(loc, off, size, m):
        lhs = jnp.concatenate([k_ref[pl.ds(off, size), :], kaug_ref[pl.ds(off, size), :]], axis=1)
        s = lax.dot_general(lhs, rhs, NT, preferred_element_type=F32)
        s_scr[pl.ds(loc, size), :] = s
        return jnp.maximum(m, jnp.max(s.reshape(size // 8, 8, 2 * tq), axis=0))

    m8 = two_level(start, count, tk, scores, jnp.full((8, 2 * tq), -3e38, F32))
    m = jnp.max(m8, axis=0, keepdims=True)
    acc[...] = jnp.zeros_like(acc)

    def mix(loc, off, size, l8):
        p = jnp.exp(s_scr[pl.ds(loc, size), :] - m)
        acc[...] += lax.dot_general(v_ref[pl.ds(off, size), :], p.astype(BF), TN, preferred_element_type=F32)
        return l8 + jnp.sum(p.reshape(size // 8, 8, 2 * tq), axis=0)

    l8 = two_level(start, count, tk, mix, jnp.zeros((8, 2 * tq), F32))
    l = jnp.sum(l8, axis=0, keepdims=True)
    ot_ref[...] = pick_heads(acc[...] / l, tq)
    lse = m + jnp.log(l)
    lse_ref[0] = jnp.concatenate([lse[:, :tq], lse[:, tq:]], axis=0)

def attn_fwd(docs, q, qaug, k, kaug, v, *, tq=256, tk=1536):
    T, D = q.shape
    S = k.shape[0]
    pairs = D // 128
    return pl.pallas_call(
        functools.partial(fwd_kernel, tk),
        out_shape=(jax.ShapeDtypeStruct((D, T), F32), jax.ShapeDtypeStruct((pairs, 2, T), F32)),
        grid_spec=pltpu.PrefetchScalarGridSpec(
            num_scalar_prefetch=1, grid=(pairs, T // tq),
            in_specs=[pl.BlockSpec((tq, 128), lambda h, i, b: (i, h)),
                      pl.BlockSpec((tq, 128), lambda h, i, b: (i, 0)),
                      pl.BlockSpec((S, 128), lambda h, i, b: (0, h)),
                      pl.BlockSpec((S, 128), lambda h, i, b: (0, 0)),
                      pl.BlockSpec((S, 128), lambda h, i, b: (0, h))],
            out_specs=(pl.BlockSpec((128, tq), lambda h, i, b: (h, i)),
                       pl.BlockSpec((1, 2, tq), lambda h, i, b: (h, 0, i))),
            scratch_shapes=[pltpu.VMEM((S, 2 * tq), F32), pltpu.VMEM((128, 2 * tq), F32)]),
        name="attend",
    )(docs, q, qaug, k, kaug, v)

def bwd_kernel(tk, docs, q_ref, qaug_ref, do_ref, lse_ref, ot_ref, k_ref, kaug_ref, v_ref,
               dq_ref, dk_ref, dv_ref, dk_acc, dv_acc, dq_acc):
    qi = pl.program_id(1)
    tq = q_ref.shape[0]
    first_row = lax.axis_index("ctx") * (tq * pl.num_programs(1)) + qi * tq
    start, count = key_range(docs, first_row, tq, k_ref.shape[0])

    @pl.when(qi == 0)
    def _():
        dk_acc[...] = jnp.zeros_like(dk_acc)
        dv_acc[...] = jnp.zeros_like(dv_acc)

    qs = stack_heads(q_ref[...])
    qrhs = stack_heads(q_ref[...], qaug_ref[...])
    dos = stack_heads(do_ref[...])
    lse = jnp.concatenate([lse_ref[0, 0:1, :], lse_ref[0, 1:2, :]], axis=1)
    mixed = ot_ref[...] * do_ref[...].astype(F32).T
    delta = jnp.concatenate(
        [jnp.sum(mixed[:64], axis=0, keepdims=True), jnp.sum(mixed[64:], axis=0, keepdims=True)], axis=1
    )
    dq_acc[...] = jnp.zeros_like(dq_acc)

    def step(loc, off, size, carry):
        rows = pl.ds(off, size)
        lhs = jnp.concatenate([k_ref[rows, :], kaug_ref[rows, :]], axis=1)
        x = lax.dot_general(lhs, qrhs, NT, preferred_element_type=F32)
        y = lax.dot_general(v_ref[rows, :], dos, NT, preferred_element_type=F32)
        p = jnp.exp(x - lse)
        ds = (p * (y - delta)).astype(BF)
        pb = p.astype(BF)
        dv_acc[rows, :] += lax.dot_general(pb, dos, NN, preferred_element_type=F32)
        dk_acc[rows, :] += lax.dot_general(ds, qs, NN, preferred_element_type=F32)
        dq_acc[...] += lax.dot_general(k_ref[rows, :], ds, TN, preferred_element_type=F32)
        return carry

    two_level(start, count, tk, step, 0)
    dq_ref[...] = (pick_heads(dq_acc[...], tq) * SCALE).T.astype(BF)

    @pl.when(qi == pl.num_programs(1) - 1)
    def _():
        dk_ref[...] = dk_acc[...].astype(BF)
        dv_ref[...] = dv_acc[...].astype(BF)

def attn_bwd(docs, q, qaug, do, lse, ot, k, kaug, v, *, tq=256, tk=1536):
    T, D = q.shape
    S = k.shape[0]
    pairs = D // 128
    row = lambda h, i, b: (h, 0, i)
    return pl.pallas_call(
        functools.partial(bwd_kernel, tk),
        out_shape=(jax.ShapeDtypeStruct((T, D), BF), jax.ShapeDtypeStruct((S, D), BF), jax.ShapeDtypeStruct((S, D), BF)),
        grid_spec=pltpu.PrefetchScalarGridSpec(
            num_scalar_prefetch=1, grid=(pairs, T // tq),
            in_specs=[pl.BlockSpec((tq, 128), lambda h, i, b: (i, h)),
                      pl.BlockSpec((tq, 128), lambda h, i, b: (i, 0)),
                      pl.BlockSpec((tq, 128), lambda h, i, b: (i, h)),
                      pl.BlockSpec((1, 2, tq), row),
                      pl.BlockSpec((128, tq), lambda h, i, b: (h, i)),
                      pl.BlockSpec((S, 128), lambda h, i, b: (0, h)),
                      pl.BlockSpec((S, 128), lambda h, i, b: (0, 0)),
                      pl.BlockSpec((S, 128), lambda h, i, b: (0, h))],
            out_specs=(pl.BlockSpec((tq, 128), lambda h, i, b: (i, h)),
                       pl.BlockSpec((S, 128), lambda h, i, b: (0, h)),
                       pl.BlockSpec((S, 128), lambda h, i, b: (0, h))),
            scratch_shapes=[pltpu.VMEM((S, 128), F32), pltpu.VMEM((S, 128), F32), pltpu.VMEM((128, 2 * tq), F32)]),
        name="attend_back",
    )(docs, q, qaug, do, lse, ot, k, kaug, v)


def middle_kernel(attn_ref, in_ref, cot_ref, vec_ref, wo_ref, wu_ref, down_own, down_far,
                  out_ref, sum1_ref, do_ref, grads_ref, up_out, down_out, attn_out,
                  wo, wu, wd, attn_b, first, hat1, scale1, first_b, act, slope, sum2, down_b, up_b, first_b2, first_t,
                  g_up, g_down, g_out, sem_w, sem_d, sem_o):
    rows, wide = in_ref.shape[0], wu.shape[1]
    a, w = lax.axis_index("ctx"), lax.axis_index("wsh")
    y, c = w // 2, lax.rem(w, 2)
    core_peer = (a, y * 2 + (1 - c))
    tall = down_own.shape[0]
    MESH = pl.DeviceIdType.MESH
    barrier = pltpu.get_barrier_semaphore()
    pl.semaphore_signal(barrier, inc=1, device_id=core_peer, device_id_type=MESH)
    pl.semaphore_wait(barrier, 1)
    passed = []
    for s, (ref, owner) in enumerate(((down_own, w), (down_far, (1 - y) * 2 + c))):
        there = wd.at[pl.ds(pl.multiple_of(owner * tall, 16), tall), :]
        passed.append(pltpu.make_async_remote_copy(
            src_ref=ref, dst_ref=there, send_sem=sem_d.at[0, s], recv_sem=sem_d.at[1, s],
            device_id=core_peer, device_id_type=MESH))
        passed[-1].start()
        pltpu.make_async_copy(ref, there, sem_w.at[2 + s]).start()
    loading = [pltpu.make_async_copy(wo_ref, wo, sem_w.at[0]), pltpu.make_async_copy(wu_ref, wu, sem_w.at[1])]
    for copy in loading:
        copy.start()

    def arrived(j):
        if j < 2:
            loading[j].wait()
        else:
            for s, owner in enumerate((w, (1 - y) * 2 + c)):
                there = wd.at[pl.ds(pl.multiple_of(owner * tall, 16), tall), :]
                pltpu.make_async_copy(there, there, sem_w.at[2 + s]).wait()
                passed[s].wait_recv()

    grads_ref[...] = jnp.zeros_like(grads_ref)
    attn_b[...] = attn_ref[...].astype(BF)
    out_b, attn_g, attn_s, down_bias, final_g, final_s = [vec_ref[i : i + 1, :] for i in range(2, 8)]
    arrived(0)
    block = 128

    def over_rows(fn):
        def one(i, carry):
            fn(pl.ds(pl.multiple_of(i * block, block), block))
            return carry

        lax.fori_loop(0, rows // block, one, 0)

    def norm(values):
        average = jnp.mean(values, axis=-1, keepdims=True)
        centred = values - average
        scale = lax.rsqrt(jnp.mean(centred * centred, axis=-1, keepdims=True) + EPS)
        return centred * scale, scale

    def norm_back(grad, hat, scale, gain):
        g = grad * gain
        return scale * (g - jnp.mean(g, axis=-1, keepdims=True) - hat * jnp.mean(g * hat, axis=-1, keepdims=True))

    def note(row, values):
        grads_ref[row : row + 1, :] += jnp.sum(values, axis=0, keepdims=True)

    def branch_part(r):
        a = attn_b[:, r].T
        v = lax.dot_general(a, wo[...], NN, preferred_element_type=F32) + out_b + in_ref[r, :].astype(F32)
        hat, scale = norm(v)
        hat1[r, :] = hat
        scale1[r, :] = scale
        f = hat * attn_g + attn_s
        first[r, :] = f
        first_b[r, :] = f.astype(BF)

    over_rows(branch_part)
    arrived(1)
    cols = vec_ref.shape[1]

    def over_wide(fn):
        def one(i, carry):
            fn(pl.ds(pl.multiple_of(i * cols, cols), cols), i)
            return carry

        lax.fori_loop(0, wide // cols, one, 0)

    def up_part(n, i):
        u = lax.dot_general(first_b[...], wu[:, n], NN, preferred_element_type=F32) + vec_ref[pl.ds(8 + i, 1), :]
        half = 0.5 * (1.0 + lax.erf(u * ROOT_HALF))
        act[:, n] = (u * half).astype(BF)
        slope[:, n] = half + u * (0.3989422804014327 * jnp.exp(-0.5 * u * u))

    over_wide(up_part)
    arrived(2)

    def down_part(r):
        v = lax.dot_general(act[r, :], wd[...], NN, preferred_element_type=F32) + down_bias + first[r, :]
        hat, scale = norm(v)
        out_ref[r, :] = (hat * final_g + final_s).astype(BF)
        cot = cot_ref[r, :].astype(F32)
        note(6, cot * hat)
        note(7, cot)
        g = norm_back(cot, hat, scale, final_g)
        sum2[r, :] = g
        rounded = g.astype(BF)
        down_b[r, :] = rounded
        note(5, rounded.astype(F32))

    over_rows(down_part)

    def up_back(n, i):
        g = lax.dot_general(down_b[...], wd[n, :], NT, preferred_element_type=F32) * slope[:, n]
        rounded = g.astype(BF)
        up_b[:, n] = rounded
        grads_ref[pl.ds(8 + i, 1), :] = jnp.sum(rounded.astype(F32), axis=0, keepdims=True)

    over_wide(up_back)

    def first_part(r):
        g = sum2[r, :] + lax.dot_general(up_b[r, :], wu[...], NT, preferred_element_type=F32)
        hat = hat1[r, :]
        note(3, g * hat)
        note(4, g)
        s1 = norm_back(g, hat, scale1[r, :], attn_g)
        sum1_ref[r, :] = s1
        rounded = s1.astype(BF)
        note(2, rounded.astype(F32))
        first_b2[r, :] = rounded

    over_rows(first_part)

    def do_part(r):
        do_ref[r, :] = lax.dot_general(first_b2[r, :], wo[...], NT, preferred_element_type=F32).astype(BF)

    over_rows(do_part)

    def wide_grads(n, i):
        g_down[n, :] = lax.dot_general(act[:, n].T, down_b[...], NN, preferred_element_type=F32).astype(BF)
        pltpu.make_async_copy(g_down.at[n, :], down_out.at[n, :], sem_o.at[0, i]).start()
        g_up[:, n] = lax.dot_general(first_t[...], up_b[:, n], NN, preferred_element_type=F32).astype(BF)
        pltpu.make_async_copy(g_up.at[:, n], up_out.at[:, n], sem_o.at[1, i]).start()

    first_t[...] = first_b[...].T
    over_wide(wide_grads)
    g_out[...] = lax.dot_general(attn_b[...], first_b2[...], NN, preferred_element_type=F32).astype(BF)
    pltpu.make_async_copy(g_out, attn_out, sem_o.at[2, 0]).start()

    def wide_end(n, i):
        pltpu.make_async_copy(g_down.at[n, :], down_out.at[n, :], sem_o.at[0, i]).wait()
        pltpu.make_async_copy(g_up.at[:, n], up_out.at[:, n], sem_o.at[1, i]).wait()

    over_wide(wide_end)
    pltpu.make_async_copy(g_out, attn_out, sem_o.at[2, 0]).wait()
    for copy in passed:
        copy.wait_send()


def middle(attn_t, inputs, cotangent, vec, out_w, up_w, down_own, down_far):
    rows = inputs.shape[0]
    wide = up_w.shape[1]
    vm, dma, shape = pltpu.VMEM, pltpu.SemaphoreType.DMA, jax.ShapeDtypeStruct
    any_spec = pl.BlockSpec(memory_space=pltpu.HBM)
    vm_spec = pl.BlockSpec(memory_space=pltpu.VMEM)
    return pl.pallas_call(
        middle_kernel,
        out_shape=(shape((rows, D), BF), shape((rows, D), F32), shape((rows, D), BF), shape((16, D), F32),
                   shape((D, wide), BF), shape((wide, D), BF), shape((D, D), BF)),
        in_specs=[vm_spec] * 4 + [any_spec] * 4,
        out_specs=(vm_spec,) * 4 + (any_spec,) * 3,
        scratch_shapes=[
            vm((D, D), BF), vm((D, wide), BF), vm((wide, D), BF), vm((D, rows), BF), vm((rows, D), F32),
            vm((rows, D), F32), vm((rows, 1), F32), vm((rows, D), BF), vm((rows, wide), BF), vm((rows, wide), F32),
            vm((rows, D), F32), vm((rows, D), BF), vm((rows, wide), BF), vm((rows, D), BF), vm((D, rows), BF),
            vm((D, wide), BF), vm((wide, D), BF), vm((D, D), BF), dma((4,)), dma((2, 2)), dma((3, wide // D)),
        ],
        compiler_params=pltpu.CompilerParams(collective_id=3, has_side_effects=True, vmem_limit_bytes=63 * 2**20),
        name="middle",
    )(attn_t, inputs, cotangent, vec, out_w, up_w, down_own, down_far)


def reach(n_ctx):
    return n_ctx // 2


def finish_kernel(sources, n_parts, *refs):
    parts = refs[:n_parts]
    (vec_ref, dk_ref, dv_ref, tok_ref, dq_ref, w_ref, own_in_ref, mine_tok_ref,
     out_ref, vec_out, wide_out, grad_ref,
     mine, buf_a, buf_h, buf_b, buf_s, buf_c, buf_d, buf_e, gbf,
     sums, heard, line,
     loads, weights, acc, dq, own, bias,
     run_part, from_x, from_z, far_z, last_x,
     sem_l, sem_a, sem_b, sem_c, sem_d, sem_v, sem_x, sem_z, sem_far, sem_load, sem_in) = refs[n_parts:]
    n_ready = len(sources)
    n_chunks = out_ref.shape[0]
    n_ctx, n_wsh = lax.axis_size("ctx"), lax.axis_size("wsh")
    zs = n_ctx // 2
    a, w = lax.axis_index("ctx"), lax.axis_index("wsh")
    z, x = a // 2, lax.rem(a, 2)
    y, c = w // 2, lax.rem(w, 2)
    core_peer = (a, y * 2 + (1 - c))
    y_peer = (a, (1 - y) * 2 + c)
    x_peer = (z * 2 + (1 - x), w)
    low, high = lax.rem(z, 2), z // 2
    pair_peer = ((z + 1 - 2 * low) * 2 + x, w)
    skip_peer = (lax.rem(z + 2, zs) * 2 + x, w)
    up_peer, down_peer = (a + 2, w), (a - 2, w)
    near = reach(n_ctx)
    hops = near // 2
    MESH = pl.DeviceIdType.MESH

    rows = out_ref.shape[1]
    half = out_ref.shape[2] // 2
    piece = rows // zs
    tall = own.shape[0]
    cut = from_x.shape[1]

    def z_peer(d):
        return (lax.rem(z + d, zs) * 2 + x, w)

    barrier = pltpu.get_barrier_semaphore()
    for dev in [core_peer, y_peer, x_peer] + [z_peer(d) for d in range(1, zs)]:
        pl.semaphore_signal(barrier, inc=1, device_id=dev, device_id_type=MESH)
    pl.semaphore_wait(barrier, zs + 2)

    def send(src, dst, sems, idx, dev):
        return pltpu.make_async_remote_copy(
            src_ref=src, dst_ref=dst, send_sem=sems.at[(0,) + idx], recv_sem=sems.at[(1,) + idx],
            device_id=dev, device_id_type=MESH)

    def wait_in(ref, sems, idx):
        send(ref, ref, sems, idx, core_peer).wait_recv()

    def wait_out(ref, sems, idx):
        send(ref, ref, sems, idx, core_peer).wait_send()

    def distance(i):
        return (hops - i // 4) * (1 - 2 * lax.rem(i // 2, 2))

    def position(i):
        dz = distance(i)
        mine_too = lax.rem(i, 2)
        run = 2 * (z + dz) + (1 - x) * (1 - mine_too) + x * mine_too
        return run, mine_too, (z + dz >= 0) & (z + dz < zs) & (jnp.abs(run - a) <= near)

    n_pos = 4 * hops + 2

    def load(i):
        run, _mine_too, there = position(i)
        return there, [
            pltpu.make_async_copy(src.at[run], loads.at[lax.rem(i, 2), j], sem_load.at[lax.rem(i, 2), j])
            for j, src in enumerate((dk_ref, dv_ref, tok_ref))
        ]

    def load_start(i):
        there, copies = load(i)

        @pl.when(there & (i < n_pos))
        def _():
            for copy in copies:
                copy.start()

    def share(k, owner):
        if k < n_ready:
            p, row0, col0 = sources[k]
            return parts[p].at[owner, pl.ds(row0, rows), pl.ds(col0, 2 * half)]
        return gbf.at[k - n_ready, owner]

    def share_load(k):
        for yy in range(2):
            pltpu.make_async_copy(share(k, yy * 2 + c), mine.at[k % 4, yy], sem_l.at[k]).start()

    def share_send(k):
        for yy in range(2):
            send(share(k, yy * 2 + (1 - c)), buf_a.at[k, yy], sem_a, (k,), core_peer).start()

    load_start(0)
    fetch = [pltpu.make_async_copy(w_ref, weights, sem_in.at[0]), pltpu.make_async_copy(dq_ref, dq, sem_in.at[1]),
             pltpu.make_async_copy(own_in_ref, own, sem_in.at[2])]
    for copy in fetch:
        copy.start()
    for k in range(n_ready):
        share_send(k)
        if k < 4:
            share_load(k)
    acc[...] = jnp.zeros_like(acc)
    bias[...] = jnp.zeros_like(bias)
    fetch[0].wait()

    near_rows, far_rows = pl.ds(0, cut), pl.ds(cut, tall - cut)

    def unit(i):
        run, mine_too, there = position(i)
        at = lax.rem(i, 2)
        load_start(i + 1)

        @pl.when(there)
        def _():
            for copy in load(i)[1]:
                copy.wait()

            def tokens_part(r, carry):
                rs = pl.ds(pl.multiple_of(r * 128, 128), 128)
                g = lax.dot_general(loads[at, 0, rs, :], weights[0], NT, preferred_element_type=F32)
                g = g + lax.dot_general(loads[at, 1, rs, :], weights[1], NT, preferred_element_type=F32)
                run_part[i, rs, :] = g.astype(BF)
                bias[0:8, :] += jnp.sum(loads[at, 1, rs, :].astype(F32).reshape(16, 8, 2 * half), axis=0)
                return carry

            lax.fori_loop(0, tall // 128, tokens_part, 0)

            @pl.when(mine_too == 0)
            def _():
                send(run_part.at[i, near_rows, :], from_x.at[i // 2], sem_x, (i // 2,), x_peer).start()

            @pl.when(i < 4)
            def _():
                far_send(i)

            def weights_part(r, carry):
                fs = pl.ds(pl.multiple_of(r * 256, 256), 256)
                flipped = loads[at, 2, :, fs].T
                for j in range(2):
                    acc[j, fs, :] += lax.dot_general(flipped, loads[at, j], NN, preferred_element_type=F32)
                return carry

            lax.fori_loop(0, 2 * half // 256, weights_part, 0)

    def from_below(i):
        dz = distance(i)
        step = 1 - 2 * lax.rem(i // 2, 2)
        sender, target = z - step, z - step + dz
        side = jnp.abs(2 * dz + (1 - 2 * x) * (1 - lax.rem(i, 2))) <= near
        return (sender >= 0) & (sender < zs) & (target >= 0) & (target < zs) & side

    def toward(i, copy_of):
        step = 1 - 2 * lax.rem(i // 2, 2)

        @pl.when(step == 1)
        def _():
            copy_of(up_peer).start()

        @pl.when(step == -1)
        def _():
            copy_of(down_peer).start()

    def far_send(i):
        toward(i, lambda dev: send(run_part.at[i, far_rows, :], far_z.at[i], sem_far, (i,), dev))

    def far_pass(i):
        _run, _mine_too, there = position(i)

        @pl.when(there)
        def _():
            @pl.when(from_below(i - 4))
            def _():
                wait_in(far_z.at[i - 4], sem_far, (i - 4,))
                run_part[i, far_rows, :] = (
                    run_part[i, far_rows, :].astype(F32) + far_z[i - 4].astype(F32)).astype(BF)

            far_send(i)

    def far_end():
        for col in range(2):
            total = n_pos - 2 + col
            for src in (4 + col, 6 + col):
                @pl.when(from_below(src))
                def _():
                    wait_in(far_z.at[src], sem_far, (src,))
                    run_part[total, far_rows, :] = (
                        run_part[total, far_rows, :].astype(F32) + far_z[src].astype(F32)).astype(BF)
            if col == 0:
                send(run_part.at[total, far_rows, :], last_x, sem_x, (n_pos // 2,), x_peer).start()
        own[far_rows, :] += run_part[n_pos - 1, far_rows, :].astype(F32)

    def near_pass(n):
        dz = distance(2 * n)
        i = 2 * n + 1

        @pl.when((z + dz >= 0) & (z + dz < zs))
        def _():
            @pl.when(jnp.abs(2 * dz + 2 * x - 1) <= near)
            def _():
                wait_in(from_x.at[n], sem_x, (n,))
                run_part[i, near_rows, :] = (
                    run_part[i, near_rows, :].astype(F32) + from_x[n].astype(F32)).astype(BF)

            @pl.when((n >= 2) & from_below(i - 4))
            def _():
                wait_in(from_z.at[n - 2], sem_z, (n - 2,))
                run_part[i, near_rows, :] = (
                    run_part[i, near_rows, :].astype(F32) + from_z[n - 2].astype(F32)).astype(BF)

            toward(i, lambda dev: send(run_part.at[i, near_rows, :], from_z.at[n], sem_z, (n,), dev))

    def near_own():
        n = n_pos // 2 - 1
        wait_in(from_x.at[n], sem_x, (n,))
        own[near_rows, :] += run_part[n_pos - 1, near_rows, :].astype(F32) + from_x[n].astype(F32)

    def near_end():
        for n in (2, 3):
            @pl.when(from_below(2 * n + 1))
            def _():
                wait_in(from_z.at[n], sem_z, (n,))
                own[near_rows, :] += from_z[n].astype(F32)

    def add(p, q):
        return (p.astype(F32) + q.astype(F32)).astype(BF)

    def column(side):
        return pl.ds(pl.multiple_of(side * half, 128), half)

    def band(start, size):
        return pl.ds(pl.multiple_of(start, 16), size)

    def stage_b(k):
        at = lax.rem(k, 4)
        pltpu.make_async_copy(mine.at[at], mine.at[at], sem_l.at[k]).wait()
        wait_in(buf_a.at[k], sem_a, (k,))
        buf_h[k] = add(mine[at, 1 - y], buf_a[k, 1 - y])
        send(buf_h.at[k], buf_b.at[k], sem_b, (k,), y_peer).start()
        buf_a[k, y] = add(mine[at, y], buf_a[k, y])

    def stage_c(k):
        wait_in(buf_b.at[k], sem_b, (k,))
        buf_s[k] = add(buf_a[k, y, :, column(1 - x)], buf_b[k, :, column(1 - x)])
        send(buf_s.at[k], buf_c.at[k], sem_c, (0, k), x_peer).start()

    my_two, other_two = band(low * 2 * piece, 2 * piece), band((1 - low) * 2 * piece, 2 * piece)
    my_one, other_one = band(high * piece, piece), band((1 - high) * piece, piece)
    my_rows = band(low * 2 * piece + high * piece, piece)

    def stage_d(k):
        wait_in(buf_c.at[k], sem_c, (0, k))
        cols = column(x)
        joined = buf_a[k, y, :, cols].astype(F32) + buf_b[k, :, cols].astype(F32) + buf_c[k].astype(F32)
        buf_c[k] = joined.astype(BF)
        send(buf_c.at[k, other_two, :], buf_d.at[k], sem_d, (0, k), pair_peer).start()

    def stage_d2(k):
        wait_in(buf_d.at[k], sem_d, (0, k))
        buf_d[k] = add(buf_d[k], buf_c[k, my_two, :])
        send(buf_d.at[k, other_one, :], buf_e.at[k], sem_d, (1, k), skip_peer).start()

    def stage_e(k):
        wait_in(buf_e.at[k], sem_d, (1, k))
        buf_e[k] = add(buf_e[k], buf_d[k, my_one, :])
        out_ref[k, my_rows, column(x)] = buf_e[k]
        send(buf_e.at[k], out_ref.at[k, my_rows, column(x)], sem_d, (2, k), skip_peer).start()

    def stage_e2(k):
        wait_in(buf_e.at[k], sem_d, (2, k))
        there = out_ref.at[k, my_two, column(x)]
        send(there, there, sem_d, (3, k), pair_peer).start()

    def stage_f(k):
        wait_in(buf_d.at[k], sem_d, (3, k))
        there = out_ref.at[k, :, column(x)]
        send(there, there, sem_c, (1, k), x_peer).start()

    def guarded(fn, k, first, last):
        @pl.when((k >= first) & (k < last))
        def _():
            fn(k)

    def chunk_step(m):
        for lag, stage in enumerate((stage_c, stage_d, stage_d2, stage_e, stage_e2, stage_f)):
            guarded(stage, m - (lag and lag + 5), 0, n_chunks)

    def first_step(t, carry):
        guarded(unit, t, 0, n_pos)
        for j in range(2):
            guarded(stage_b, 2 * t + j, 0, n_ready)
        for k in range(4, n_ready):
            @pl.when(t == (k - 4) // 2)
            def _():
                share_load(k)

        @pl.when(lax.rem(t, 2) == 1)
        def _():
            guarded(near_pass, t // 2 - 1, 0, 4)

        guarded(far_pass, t - 2, 4, 8)

        @pl.when((lax.rem(t, 2) == 0) & (t >= 2))
        def _():
            chunk_step(t // 2 - 1)

        return carry

    lax.fori_loop(0, n_pos, first_step, 0)
    done = n_pos // 2 - 1

    fetch[1].wait()
    fetch[2].wait()
    own_tok = pltpu.make_async_copy(mine_tok_ref, loads.at[0, 2], sem_load.at[0, 2])
    own_tok.start()

    def to_bf(j, target):
        for owner in range(n_wsh):
            gbf[target, owner] = acc[j, owner * rows : (owner + 1) * rows, :].astype(BF)
        share_load(n_ready + target)
        share_send(n_ready + target)

    to_bf(0, 0)
    to_bf(1, 1)
    own_tok.wait()

    def query_part(r, carry):
        fs = pl.ds(pl.multiple_of(r * 256, 256), 256)
        acc[0, fs, :] = lax.dot_general(loads[0, 2, :, fs].T, dq[...], NN, preferred_element_type=F32)
        return carry

    lax.fori_loop(0, 2 * half // 256, query_part, 0)
    to_bf(0, 2)

    def query_tokens(r, carry):
        rs = pl.ds(pl.multiple_of(r * 128, 128), 128)
        own[rs, :] += lax.dot_general(dq[rs, :], weights[2], NT, preferred_element_type=F32)
        bias[8:16, :] += jnp.sum(dq[rs, :].astype(F32).reshape(16, 8, 2 * half), axis=0)
        return carry

    lax.fori_loop(0, tall // 128, query_tokens, 0)

    sums[0] = vec_ref[...]
    sums[0, 0:1, :] = jnp.sum(bias[8:16, :], axis=0, keepdims=True)
    sums[0, 1:2, :] = jnp.sum(bias[0:8, :], axis=0, keepdims=True)
    pair = (core_peer, y_peer, x_peer)

    def vec_send(stage):
        send(sums.at[stage], heard.at[stage], sem_v, (stage,), pair[stage]).start()

    def vec_stage(stage):
        wait_in(heard.at[stage], sem_v, (stage,))
        total = sums[stage] + heard[stage]
        sums[stage + 1] = total
        if stage < 2:
            vec_send(stage + 1)
        else:
            line[z] = total
            for d in range(1, zs):
                send(sums.at[3], line.at[z], sem_v, (3,), z_peer(d)).start()

    def vec_last():
        wait_in(line.at[pl.ds(0, zs - 1)], sem_v, (3,))
        total = line[0]
        for d in range(1, zs):
            total = total + line[d]
        small, wide = total[0:8, 0:rows], total[8:9, :]
        for owner in range(1, n_wsh):
            small = jnp.where(w == owner, total[0:8, owner * rows : (owner + 1) * rows], small)
            wide = jnp.where(w == owner, total[8 + owner : 9 + owner, :], wide)
        vec_out[...] = small
        wide_out[...] = wide

    vec_send(0)

    def second_step(m, carry):
        guarded(stage_b, m - done + n_ready, n_ready, n_chunks)
        chunk_step(m)
        guarded(lambda k: near_own(), m - done, 0, 1)
        for stage in range(3):
            guarded(lambda k: vec_stage(stage), m - done - 1 - stage, 0, 1)
        guarded(lambda k: near_end(), m - done - 3, 0, 1)
        guarded(lambda k: far_end(), m - done - 4, 0, 1)
        guarded(lambda k: vec_last(), m - done - 5, 0, 1)
        return carry

    lax.fori_loop(done, n_chunks + 10, second_step, 0)
    wait_in(last_x, sem_x, (n_pos // 2,))
    own[far_rows, :] += last_x[...].astype(F32)
    grad_ref[...] = own[...].astype(BF)

    def drain(k, carry):
        wait_in(buf_s.at[k], sem_c, (1, k))
        wait_out(buf_a.at[k], sem_a, (k,))
        wait_out(buf_b.at[k], sem_b, (k,))
        wait_out(buf_s.at[k], sem_c, (0, k))
        wait_out(buf_s.at[k], sem_c, (1, k))
        wait_out(buf_d.at[k], sem_d, (0, k))
        wait_out(buf_e.at[k], sem_d, (1, k))
        wait_out(buf_e.at[k], sem_d, (2, k))
        wait_out(buf_d.at[k], sem_d, (3, k))
        return carry

    lax.fori_loop(0, n_chunks, drain, 0)
    for stage in range(3):
        wait_out(heard.at[stage], sem_v, (stage,))
    wait_out(line.at[pl.ds(0, zs - 1)], sem_v, (3,))
    wait_out(last_x, sem_x, (n_pos // 2,))

    def drain_runs(i, carry):
        _run, mine_too, there = position(i)

        @pl.when(there)
        def _():
            wait_out(far_z.at[i], sem_far, (i,))

            @pl.when(mine_too == 1)
            def _():
                wait_out(from_z.at[i // 2], sem_z, (i // 2,))

        return carry

    lax.fori_loop(0, n_pos - 2, drain_runs, 0)

    def drain_x(n, carry):
        _run, _mine_too, there = position(2 * n)

        @pl.when(there)
        def _():
            wait_out(from_x.at[n], sem_x, (n,))

        return carry

    lax.fori_loop(0, n_pos // 2, drain_x, 0)


def widen_kernel(spans, in_ref, *outs):
    for (first, down, across), out in zip(spans, outs):
        for r in range(down):
            for col in range(across):
                out[r, :, col * D : (col + 1) * D] = in_ref[first + r * across + col].astype(F32)


def widen(summed, spans):
    n, rows, _width = summed.shape
    part = rows // 4
    outs = pl.pallas_call(
        functools.partial(widen_kernel, spans),
        grid=(4,),
        out_shape=[jax.ShapeDtypeStruct((down, rows, across * D), F32) for _first, down, across in spans],
        in_specs=[pl.BlockSpec((n, part, D), lambda i: (0, i, 0))],
        out_specs=[pl.BlockSpec((down, part, across * D), lambda i: (0, i, 0)) for _first, down, across in spans],
        name="widen",
    )(summed)
    return [o.reshape(-1, o.shape[2]) for o in outs]


def finish(matrices, vec, grad_k, grad_v, all_tokens, grad_q, kvq_w, own_grad, inputs):
    n_ctx, n_wsh = lax.axis_size("ctx"), lax.axis_size("wsh")
    zs, hops = n_ctx // 2, reach(n_ctx) // 2
    rows = D // n_wsh
    parts, sources, spans = [], [], []
    for p, g in enumerate(matrices):
        down, across = g.shape[0] // D, g.shape[1] // D
        parts.append(g.astype(BF).reshape(n_wsh, down * rows, across * D))
        spans.append((len(sources), down, across))
        sources += [(p, r * rows, col * D) for r in range(down) for col in range(across)]
    n = len(sources) + 3
    spans += [(len(sources) + j, 1, 1) for j in range(3)]
    half, piece, tall = D // 2, rows // zs, inputs.shape[0]
    n_pos, cut = 4 * hops + 2, tall // 2
    vm, dma, shape = pltpu.VMEM, pltpu.SemaphoreType.DMA, jax.ShapeDtypeStruct
    any_spec = pl.BlockSpec(memory_space=pltpu.HBM)
    vm_spec = pl.BlockSpec(memory_space=pltpu.VMEM)
    summed, small, wide, grad_own = pl.pallas_call(
        functools.partial(finish_kernel, sources, len(parts)),
        out_shape=(shape((n, rows, D), BF), shape((8, rows), F32), shape((1, D), F32), shape((tall, D), BF)),
        in_specs=[any_spec] * len(parts) + [vm_spec] + [any_spec] * 7,
        out_specs=(vm_spec,) * 4,
        scratch_shapes=[
            vm((4, 2, rows, D), BF), vm((n, 2, rows, D), BF), vm((n, rows, D), BF), vm((n, rows, D), BF),
            vm((n, rows, half), BF), vm((n, rows, half), BF), vm((n, 2 * piece, half), BF), vm((n, piece, half), BF),
            vm((3, n_wsh, rows, D), BF),
            vm((4,) + vec.shape, F32), vm((3,) + vec.shape, F32), vm((zs,) + vec.shape, F32),
            vm((2, 3, tall, D), BF), vm((3, D, D), BF), vm((2, D, D), F32), vm((tall, D), BF), vm((tall, D), F32),
            vm((16, D), F32),
            vm((n_pos, tall, D), BF), vm((n_pos // 2, cut, D), BF), vm((4, cut, D), BF),
            vm((n_pos - 2, tall - cut, D), BF), vm((tall - cut, D), BF),
            dma((n,)), dma((2, n)), dma((2, n)), dma((2, 2, n)), dma((2, 4, n)), dma((2, 4)),
            dma((2, n_pos // 2 + 1)), dma((2, 4)), dma((2, n_pos - 2)), dma((2, 3)), dma((3,)),
        ],
        compiler_params=pltpu.CompilerParams(collective_id=2, has_side_effects=True, vmem_limit_bytes=63 * 2**20),
        name="finish",
    )(*parts, vec, grad_k, grad_v, all_tokens, grad_q, kvq_w, own_grad, inputs)
    return widen(summed, spans), small, wide, grad_own


def gather_kernel(cut, tok_ref, docs_ref, wk_ref, wv_ref, wq_ref, wo_ref, wu_ref, vec_ref,
                  tok_out, k_out, v_out, q_out, w_out, vec_out, wo_out, wu_out, query_doc, key_doc,
                  tok, kbuf, vbuf, qbuf, wbuf, vecs, wo, wu, kdoc,
                  sem_in, sem_out, sem_w, sem_l, sem_o):
    n_ctx = lax.axis_size("ctx")
    zs = n_ctx // 2
    a, w = lax.axis_index("ctx"), lax.axis_index("wsh")
    z, x = a // 2, lax.rem(a, 2)
    y, c = w // 2, lax.rem(w, 2)
    core_peer = (a, y * 2 + (1 - c))
    y_peer = (a, (1 - y) * 2 + c)
    x_peer = (z * 2 + (1 - x), w)
    up, down = (a + 2, w), (a - 2, w)
    near = reach(n_ctx)
    MESH = pl.DeviceIdType.MESH
    n_slices = sem_in.shape[1]
    tall = tok.shape[1] // n_slices
    own = wk_ref.shape[0]
    far = 4 * (near // 2 + 1)

    barrier = pltpu.get_barrier_semaphore()
    around = [(lax.rem(z + d, zs) * 2 + x, w) for d in (1, zs - 1)]
    for dev in [core_peer, y_peer, x_peer] + around:
        pl.semaphore_signal(barrier, inc=1, device_id=dev, device_id_type=MESH)
    pl.semaphore_wait(barrier, 5)

    def relative(u):
        dz = (u // 4) * (1 - 2 * lax.rem(u, 2))
        other = lax.rem(u // 2, 2)
        run = 2 * (z + dz) + (x + other - 2 * x * other)
        there = (z + dz >= 0) & (z + dz < zs) & (jnp.abs(run - a) <= near) & ((u >= 4) | (lax.rem(u, 2) == 0))
        return run, dz, other, there

    def rows(s):
        return pl.ds(pl.multiple_of(s * tall, tall), tall)

    def remote(src, dst, send_sem, recv_sem, dev):
        return pltpu.make_async_remote_copy(
            src_ref=src, dst_ref=dst, send_sem=send_sem, recv_sem=recv_sem, device_id=dev, device_id_type=MESH)

    def routes(u, s):
        run, dz, other, there = relative(u)
        z_first = s < cut
        to_x = there & (z_first | (dz == 0)) & (other == 0) & (jnp.abs(run - x_peer[0]) <= near)
        along = there & ((other == 0) | jnp.logical_not(z_first))
        to_up = along & (dz <= 0) & (z + 1 < zs) & (jnp.abs(run - (a + 2)) <= near)
        to_down = along & (dz >= 0) & (z > 0) & (jnp.abs(run - (a - 2)) <= near)
        return run, ((0, x_peer, to_x), (1, up, to_up), (2, down, to_down))

    def pass_on(u, s):
        run, where = routes(u, s)
        for d, dev, ok in where:
            @pl.when(ok)
            def _():
                source = tok_ref if isinstance(u, int) and u == 0 else tok.at[run]
                remote(source.at[rows(s), :], tok.at[run, rows(s), :], sem_out.at[d, u, s], sem_in.at[run, s], dev).start()

    def await_slice(u, s):
        run, _dz, _other, there = relative(u)

        @pl.when(there)
        def _():
            remote(tok.at[run, rows(s), :], tok.at[run, rows(s), :], sem_out.at[0, 0, 0], sem_in.at[run, s], x_peer).wait_recv()

    def start_own(s, carry):
        pass_on(0, s)
        return carry

    def weight_rows(owner):
        return pl.ds(pl.multiple_of(owner * own, 16), own)

    def shard(m, owner):
        if m == 3:
            return vecs.at[owner]
        return (wbuf.at[0], wbuf.at[1], wbuf.at[2], None, wo, wu)[m].at[weight_rows(owner), :]

    vecs[w, 0 : vec_ref.shape[0], :] = vec_ref[...]
    shards = (wk_ref, wv_ref, wq_ref, vecs.at[w], wo_ref, wu_ref)
    for m in (3, 0, 1, 2, 4, 5):
        remote(shards[m], shard(m, w), sem_w.at[0, 1, m], sem_w.at[1, 1, m], y_peer).start()
        remote(shards[m], shard(m, w), sem_w.at[0, 0, m], sem_w.at[1, 0, m], core_peer).start()
        if m != 3:
            pltpu.make_async_copy(shards[m], shard(m, w), sem_w.at[0, 3, m]).start()
    lax.fori_loop(0, n_slices, start_own, 0)
    pltpu.make_async_copy(tok_ref, tok.at[a], sem_l.at[4]).start()

    for j in range(n_ctx):
        @pl.when(jnp.abs(j - a) > near)
        def _():
            tok[j] = jnp.zeros_like(tok[j])

    n_rows = tok.shape[1]

    def is_own_lane(first):
        pos = first + lax.broadcasted_iota(jnp.int32, (n_rows, 128), 0)
        doc = jnp.full((n_rows, 128), -1, jnp.int32)
        for d in range(docs_ref.shape[1]):
            doc = doc + jnp.where(pos >= docs_ref[0, d], 1, 0)
        return lax.broadcasted_iota(jnp.int32, (n_rows, 128), 1) == doc

    def key_lanes(j, carry):
        kdoc[pl.ds(pl.multiple_of(j * n_rows, n_rows), n_rows), :] = jnp.where(
            is_own_lane(j * n_rows), 0.0, -1e30).astype(BF)
        return carry

    lax.fori_loop(0, n_ctx, key_lanes, 0)
    pltpu.make_async_copy(kdoc, key_doc, sem_l.at[3]).start()
    query_doc[...] = jnp.where(is_own_lane(a * n_rows), 1.0, 0.0).astype(BF)

    def weight_arrival(m, kind):
        part = shard(m, w)
        return remote(part, part, sem_w.at[0, kind, m], sem_w.at[1, kind, m], core_peer)

    across = (1 - y) * 2 + c

    def weight_forward(m):
        weight_arrival(m, 1).wait_recv()
        remote(shard(m, across), shard(m, across), sem_w.at[0, 2, m], sem_w.at[1, 2, m], core_peer).start()

    def weight_end(m):
        weight_arrival(m, 0).wait_recv()
        weight_arrival(m, 2).wait_recv()
        if m != 3:
            pltpu.make_async_copy(shard(m, w), shard(m, w), sem_w.at[0, 3, m]).wait()

    def relay(first, last):
        def one(i, carry):
            s = i // (last - first)
            u = first + lax.rem(i, last - first)
            await_slice(u, s)
            pass_on(u, s)
            return carry

        lax.fori_loop(0, n_slices * (last - first), one, 0)

    relay(2, 6)
    weight_forward(3)
    weight_forward(0)
    weight_forward(1)
    weight_end(3)
    vec_out[0:8, :] = jnp.concatenate([vecs[o, 0:8, :] for o in range(4)], axis=1)
    for o in range(4):
        vec_out[8 + o : 9 + o, :] = jnp.concatenate([vecs[o, 8 + i : 9 + i, :] for i in range(4)], axis=1)
    pltpu.make_async_copy(tok_ref, tok.at[a], sem_l.at[4]).wait()
    weight_end(0)
    weight_end(1)

    step_rows = 128
    steps = tok.shape[1] // step_rows

    def query_part(i, carry):
        r = pl.ds(pl.multiple_of(i * step_rows, step_rows), step_rows)
        q = (jnp.dot(tok[a, r, :], wbuf[2], preferred_element_type=F32) + vec_out[0:1, :]).astype(BF)
        qbuf[r, :] = q * jnp.asarray(SCALE, BF)
        return carry

    def project(u, carry):
        run, _dz, _other, there = relative(u)

        @pl.when(u == 6)
        def _():
            weight_forward(2)
            weight_end(2)
            lax.fori_loop(0, steps, query_part, 0)
            pltpu.make_async_copy(qbuf, q_out, sem_l.at[5]).start()
            relay(6, 10)

        @pl.when(there)
        def _():
            @pl.when(u >= 10)
            def _():
                def one(s, carry):
                    await_slice(u, s)
                    return carry

                lax.fori_loop(0, n_slices, one, 0)

            def part(i, carry):
                r = pl.ds(pl.multiple_of(i * step_rows, step_rows), step_rows)
                t = tok[run, r, :]
                kbuf[run, r, :] = jnp.dot(t, wbuf[0], preferred_element_type=F32).astype(BF)
                vbuf[run, r, :] = (jnp.dot(t, wbuf[1], preferred_element_type=F32) + vec_out[1:2, :]).astype(BF)
                return carry

            lax.fori_loop(0, steps, part, 0)
            for i, (src, dst) in enumerate(((kbuf, k_out), (vbuf, v_out), (tok, tok_out))):
                pltpu.make_async_copy(src.at[run], dst.at[run], sem_o.at[i, run]).start()

        return carry

    for j in range(n_ctx):
        @pl.when(jnp.abs(j - a) > near)
        def _():
            kbuf[j] = jnp.zeros_like(kbuf[j])
            vbuf[j] = jnp.zeros_like(vbuf[j])
            for i, (src, dst) in enumerate(((kbuf, k_out), (vbuf, v_out), (tok, tok_out))):
                pltpu.make_async_copy(src.at[j], dst.at[j], sem_o.at[i, j]).start()

    lax.fori_loop(0, far, project, 0)

    pltpu.make_async_copy(wbuf, w_out, sem_l.at[6]).start()

    for m in (4, 5):
        weight_forward(m)
    for m, full, target in ((4, wo, wo_out), (5, wu, wu_out)):
        weight_end(m)
        pltpu.make_async_copy(full, target, sem_l.at[m - 4]).start()
    for m in range(6):
        for kind in range(3):
            weight_arrival(m, kind).wait_send()

    def drain(i, carry):
        s = i // far
        u = lax.rem(i, far)
        run, where = routes(u, s)
        for d, dev, ok in where:
            @pl.when(ok & (u < 10))
            def _():
                remote(tok.at[run, rows(s), :], tok.at[run, rows(s), :], sem_out.at[d, u, s], sem_in.at[run, s], dev).wait_send()
        return carry

    lax.fori_loop(0, n_slices * far, drain, 0)
    for j in range(n_ctx):
        for i, (src, dst) in enumerate(((kbuf, k_out), (vbuf, v_out), (tok, tok_out))):
            pltpu.make_async_copy(src.at[j], dst.at[j], sem_o.at[i, j]).wait()
    pltpu.make_async_copy(qbuf, q_out, sem_l.at[5]).wait()
    pltpu.make_async_copy(wbuf, w_out, sem_l.at[6]).wait()
    pltpu.make_async_copy(wo, wo_out, sem_l.at[0]).wait()
    pltpu.make_async_copy(wu, wu_out, sem_l.at[1]).wait()
    pltpu.make_async_copy(kdoc, key_doc, sem_l.at[3]).wait()


def gather_project(inputs, doc_starts, vectors, key_weight, value_weight, query_weight, out_weight, up_weight):
    n_ctx, n_wsh = lax.axis_size("ctx"), lax.axis_size("wsh")
    tall = inputs.shape[0]
    n_slices = 8
    far = 4 * (reach(n_ctx) // 2 + 1)
    vm, dma = pltpu.VMEM, pltpu.SemaphoreType.DMA
    any_spec = pl.BlockSpec(memory_space=pltpu.HBM)
    vm_spec = pl.BlockSpec(memory_space=pltpu.VMEM)
    runs = (n_ctx, tall, D)
    shape = jax.ShapeDtypeStruct
    return pl.pallas_call(
        functools.partial(gather_kernel, 5),
        out_shape=(shape(runs, BF), shape(runs, BF), shape(runs, BF), shape((tall, D), BF), shape((3, D, D), BF),
                   shape((16, D), F32), shape((D, D), BF), shape((D, up_weight.shape[1]), BF), shape((tall, 128), BF),
                   shape((n_ctx * tall, 128), BF)),
        in_specs=[any_spec, pl.BlockSpec(memory_space=pltpu.SMEM)] + [any_spec] * 5 + [vm_spec],
        out_specs=(any_spec,) * 5 + (vm_spec,) + (any_spec,) * 2 + (vm_spec, any_spec),
        scratch_shapes=[
            vm(runs, BF), vm(runs, BF), vm(runs, BF), vm((tall, D), BF), vm((3, D, D), BF), vm((n_wsh, 16, D // n_wsh), F32),
            vm((D, D), BF), vm((D, up_weight.shape[1]), BF), vm((n_ctx * tall, 128), BF),
            dma((n_ctx, n_slices)), dma((3, far, n_slices)), dma((2, 4, 6)), dma((7,)), dma((3, n_ctx)),
        ],
        compiler_params=pltpu.CompilerParams(collective_id=1, has_side_effects=True, vmem_limit_bytes=63 * 2**20),
        name="gather_project",
    )(inputs, doc_starts, key_weight, value_weight, query_weight, out_weight, up_weight, vectors)


def local(
    tokens,
    cotangent,
    doc_starts,
    query_weight,
    key_weight,
    value_weight,
    out_weight,
    up_weight,
    down_weight,
    query_bias,
    value_bias,
    out_bias,
    attn_gain,
    attn_shift,
    up_bias,
    down_bias,
    final_gain,
    final_shift,
):
    inputs = tokens[0]
    doc_start = doc_starts[0]
    tok_rows = inputs.shape[0]
    stream_rows = tok_rows * lax.axis_size("ctx")
    tile = min(tok_rows, 256)
    n_ctx, n_wsh = lax.axis_size("ctx"), lax.axis_size("wsh")
    own = D // n_wsh

    def gather(x):
        return lax.all_gather(x, "wsh", axis=0, tiled=True)

    fast = n_wsh == 4 and n_ctx == 8 and own % (n_ctx // 2 * 16) == 0 and tok_rows % 512 == 0
    if fast:
        small = (query_bias, value_bias, out_bias, attn_gain, attn_shift, down_bias, final_gain, final_shift)
        vectors, place = jnp.zeros(((8 + n_wsh) * own,), F32), 0
        for v in small + (up_bias,):
            ends = (place, vectors.shape[0] - place - v.shape[0], 0)
            vectors = vectors + lax.pad(v.astype(F32), jnp.zeros((), F32), (ends,))
            place += v.shape[0]
        vectors = vectors.reshape(8 + n_wsh, own)
        all_tokens, keys, values, queries, kvq_w, vec, out_w, up_w, query_doc, key_doc = gather_project(
            inputs, doc_starts, vectors, key_weight, value_weight, query_weight, out_weight, up_weight
        )
        down_own, _unused = lax.optimization_barrier((down_weight, vec))
        down_far = lax.ppermute(down_own, "wsh", [(i, i ^ 2) for i in range(n_wsh)])
        all_tokens, keys, values = [r.reshape(stream_rows, D) for r in (all_tokens, keys, values)]
    else:
        first_row = lax.axis_index("ctx") * tok_rows
        query_doc, key_doc = document_lanes(doc_start, first_row, tok_rows, stream_rows)
        small = jnp.stack(
            [query_bias, value_bias, out_bias, attn_gain, attn_shift, down_bias, final_gain, final_shift]
        )
        all_tokens = lax.all_gather(inputs, "ctx", axis=0, tiled=True)
        query_w, key_w, value_w = gather(query_weight), gather(key_weight), gather(value_weight)
        small = gather(small.T).astype(F32)
        query_b, value_b, out_b, attn_g, attn_s, down_b, final_g, final_s = [small[:, i] for i in range(8)]
        up_b = gather(up_bias).astype(F32)
        queries = jnp.dot(inputs, query_w, preferred_element_type=F32) + query_b
        queries = queries.astype(BF) * jnp.asarray(SCALE, BF)
        keys = jnp.dot(all_tokens, key_w, preferred_element_type=F32).astype(BF)
        values = (jnp.dot(all_tokens, value_w, preferred_element_type=F32) + value_b).astype(BF)
    mixed_t, log_rows = attn_fwd(doc_start, queries, query_doc, keys, key_doc, values, tq=tile)
    if fast:
        layer_out, grad_sum1, grad_attn, vec_grads, grad_up_w, grad_down_w, grad_out_w = middle(
            mixed_t, inputs, cotangent[0], vec, out_w, up_w, down_own, down_far
        )
        grad_q, grad_k, grad_v = attn_bwd(
            doc_start, queries, query_doc, grad_attn, log_rows, mixed_t, keys, key_doc, values, tq=tile
        )
        mats, small, wide, grad_inputs = finish(
            (grad_up_w, grad_out_w, grad_down_w), vec_grads, grad_k.reshape(n_ctx, tok_rows, D),
            grad_v.reshape(n_ctx, tok_rows, D), all_tokens.reshape(n_ctx, tok_rows, D), grad_q, kvq_w, grad_sum1, inputs,
        )
        up_sum, out_sum, down_sum, key_sum, value_sum, query_sum = mats
        return (
            layer_out.reshape(1, tok_rows, D), grad_inputs.reshape(1, tok_rows, D), query_sum, key_sum, value_sum,
            out_sum, up_sum, down_sum, small[0], small[1], small[2], small[3], small[4], wide[0],
            small[5], small[6], small[7],
        )

    out_w = gather(out_weight)
    up_w = gather(up_weight)
    down_w = gather(down_weight)
    attn_t = mixed_t.astype(BF)
    inputs_f = inputs.astype(F32)
    branch = lax.dot_general(attn_t, out_w, TN, preferred_element_type=F32) + out_b
    first_norm, first_pull = jax.vjp(layer_norm, inputs_f + branch, attn_g, attn_s)
    first_b = first_norm.astype(BF)
    up_f = jnp.dot(first_b, up_w, preferred_element_type=F32) + up_b
    act_f, act_pull = jax.vjp(gelu_act, up_f)
    act_b = act_f.astype(BF)
    down_f = jnp.dot(act_b, down_w, preferred_element_type=F32) + down_b
    final_f, final_pull = jax.vjp(layer_norm, first_norm + down_f, final_g, final_s)
    layer_out = final_f.astype(BF)

    grad_sum2, grad_final_g, grad_final_s = final_pull(cotangent[0].astype(F32))
    grad_down = grad_sum2.astype(BF)
    grad_down_w = jnp.einsum("tf,td->fd", act_b, grad_down, preferred_element_type=F32)
    grad_down_b = jnp.sum(grad_down.astype(F32), axis=0)
    grad_act = jnp.einsum("td,fd->tf", grad_down, down_w, preferred_element_type=F32)
    (grad_up_f,) = act_pull(grad_act)
    grad_up = grad_up_f.astype(BF)
    grad_up_w = jnp.einsum("td,tf->df", first_b, grad_up, preferred_element_type=F32)
    grad_up_b = jnp.sum(grad_up.astype(F32), axis=0)
    grad_first = grad_sum2 + jnp.einsum("tf,df->td", grad_up, up_w, preferred_element_type=F32)
    grad_sum1, grad_attn_g, grad_attn_s = first_pull(grad_first)
    grad_branch = grad_sum1.astype(BF)
    grad_out_w = jnp.dot(attn_t, grad_branch, preferred_element_type=F32)
    grad_out_b = jnp.sum(grad_branch.astype(F32), axis=0)
    grad_attn = jnp.einsum("te,de->td", grad_branch, out_w, preferred_element_type=F32).astype(BF)
    grad_q, grad_k, grad_v = attn_bwd(
        doc_start, queries, query_doc, grad_attn, log_rows, mixed_t, keys, key_doc, values, tq=tile
    )
    def total(g):
        part = lax.psum_scatter(g.astype(BF), "wsh", scatter_dimension=0, tiled=True)
        return lax.psum(part, "ctx").astype(F32)

    grad_all = jnp.einsum("te,de->td", grad_k, key_w, preferred_element_type=F32)
    grad_all = grad_all + jnp.einsum("te,de->td", grad_v, value_w, preferred_element_type=F32)
    grad_own = lax.psum_scatter(grad_all.astype(BF), "ctx", scatter_dimension=0, tiled=True)
    grad_query_w = jnp.einsum("td,te->de", inputs, grad_q, preferred_element_type=F32)
    grad_key_w = jnp.einsum("td,te->de", all_tokens, grad_k, preferred_element_type=F32)
    grad_value_w = jnp.einsum("td,te->de", all_tokens, grad_v, preferred_element_type=F32)
    grad_query_b = jnp.sum(grad_q.astype(F32), axis=0)
    grad_value_b = jnp.sum(grad_v.astype(F32), axis=0)
    grad_inputs = grad_sum1 + jnp.einsum("te,de->td", grad_q, query_w, preferred_element_type=F32)
    grad_inputs = grad_inputs + grad_own.astype(F32)
    sums = [
        total(g)
        for g in (
            grad_query_w, grad_key_w, grad_value_w, grad_out_w, grad_up_w, grad_down_w,
            grad_query_b, grad_value_b, grad_out_b, grad_attn_g, grad_attn_s, grad_up_b,
            grad_down_b, grad_final_g, grad_final_s,
        )
    ]
    return (
        layer_out.reshape(1, tok_rows, D),
        grad_inputs.astype(BF).reshape(1, tok_rows, D),
        *sums,
    )


def solution(mesh):
    rows, mat, vec = P("wsh", "ctx", None), P("wsh", None), P("wsh")
    return jax.shard_map(
        local,
        mesh=mesh,
        in_specs=(rows, rows, mat) + (mat,) * 6 + (vec,) * 9,
        out_specs=(rows, rows) + (mat,) * 6 + (vec,) * 9,
        check_vma=False,
    )
```

```python
import functools

import jax
import jax.numpy as jnp
from jax import lax
from jax.experimental import pallas as pl
from jax.experimental.pallas import tpu as pltpu
from jax.sharding import PartitionSpec as P

D = 768
HEADS = 12
HD = 64
SCALE = 0.125
EPS = 1e-12
ROOT_HALF = 0.7071067811865476
BF = jnp.bfloat16
F32 = jnp.float32
NT = (((1,), (1,)), ((), ()))
NN = (((1,), (0,)), ((), ()))
TN = (((0,), (0,)), ((), ()))


def layer_norm(values, gain_vec, shift_vec):
    average = jnp.mean(values, axis=-1, keepdims=True)
    centred = values - average
    variance = jnp.mean(centred * centred, axis=-1, keepdims=True)
    return centred * lax.rsqrt(variance + EPS) * gain_vec + shift_vec


def gelu_act(values):
    return 0.5 * values * (1.0 + lax.erf(values * ROOT_HALF))


def key_range(docs, first_row, tile, stream_rows):
    last = first_row + tile - 1
    low, high = 0, stream_rows
    for d in range(1, docs.shape[0]):
        low = jnp.where(docs[d] <= first_row, docs[d], low)
    for d in range(docs.shape[0] - 1, 0, -1):
        high = jnp.where(docs[d] > last, docs[d], high)
    first = low // 128 * 128
    count = (high - first + 255) // 256
    return jnp.minimum(first, stream_rows - count * 256), count


def document_lanes(doc_start, first_row, rows, stream_rows):
    far = jnp.full((128 - doc_start.shape[0],), 2**30, jnp.int32)
    starts = jnp.concatenate([doc_start, far])
    ends = jnp.concatenate([doc_start[1:], jnp.full((1,), stream_rows, jnp.int32), far])
    query_pos = first_row + jnp.arange(rows, dtype=jnp.int32)[:, None]
    key_pos = jnp.arange(stream_rows, dtype=jnp.int32)[:, None]
    query_doc = ((query_pos >= starts) & (query_pos < ends)).astype(BF)
    key_doc = jnp.where((key_pos >= starts) & (key_pos < ends), 0.0, -1e30).astype(BF)
    return query_doc, key_doc


def stack_heads(x, extra=None):
    lane = lax.broadcasted_iota(jnp.int32, x.shape, 1)
    zero = jnp.zeros_like(x)
    lo = jnp.where(lane < 64, x, zero)
    hi = jnp.where(lane < 64, zero, x)
    if extra is not None:
        lo = jnp.concatenate([lo, extra], axis=1)
        hi = jnp.concatenate([hi, extra], axis=1)
    return jnp.concatenate([lo, hi], axis=0)

def pick_heads(x, tq):
    return jnp.concatenate([x[:64, :tq], x[64:, tq:]], axis=0)

def two_level(start, count, tk, body, init):
    done, carried = 0, init
    for n in (6, 3, 1):
        if n * 256 > tk:
            continue

        def step(t, c, n=n, done=done):
            at = done + t * n
            return body(pl.multiple_of(at * 256, 256), pl.multiple_of(start + at * 256, 128), n * 256, c)

        trips = (count - done) // n
        carried = lax.fori_loop(0, trips, step, carried)
        done = done + trips * n
    return carried


def fwd_kernel(tq, tk, docs, q_ref, qaug_ref, k_ref, kaug_ref, v_ref, ot_ref, lse_ref, s_scr, acc):
    def part(i, carry):
        rows = pl.ds(pl.multiple_of(i * tq, tq), tq)
        start, count = key_range(docs, lax.axis_index("ctx") * q_ref.shape[0] + i * tq, tq, k_ref.shape[0])
        rhs = stack_heads(q_ref[rows, :], qaug_ref[rows, :])

        def scores(loc, off, size, m):
            lhs = jnp.concatenate([k_ref[pl.ds(off, size), :], kaug_ref[pl.ds(off, size), :]], axis=1)
            s = lax.dot_general(lhs, rhs, NT, preferred_element_type=F32)
            s_scr[pl.ds(loc, size), :] = s
            return jnp.maximum(m, jnp.max(s.reshape(size // 8, 8, 2 * tq), axis=0))

        m8 = two_level(start, count, tk, scores, jnp.full((8, 2 * tq), -3e38, F32))
        m = jnp.max(m8, axis=0, keepdims=True)
        acc[...] = jnp.zeros_like(acc)

        def mix(loc, off, size, l8):
            p = jnp.exp(s_scr[pl.ds(loc, size), :] - m)
            acc[...] += lax.dot_general(v_ref[pl.ds(off, size), :], p.astype(BF), TN, preferred_element_type=F32)
            return l8 + jnp.sum(p.reshape(size // 8, 8, 2 * tq), axis=0)

        l8 = two_level(start, count, tk, mix, jnp.zeros((8, 2 * tq), F32))
        l = jnp.sum(l8, axis=0, keepdims=True)
        ot_ref[:, rows] = pick_heads(acc[...] / l, tq)
        lse = m + jnp.log(l)
        lse_ref[0, :, rows] = jnp.concatenate([lse[:, :tq], lse[:, tq:]], axis=0)
        return carry

    lax.fori_loop(0, q_ref.shape[0] // tq, part, 0)


def attn_fwd(docs, q, qaug, k, kaug, v, *, tq=256, tk=1536):
    T, D = q.shape
    S = k.shape[0]
    pairs = D // 128
    return pl.pallas_call(
        functools.partial(fwd_kernel, tq, tk),
        out_shape=(jax.ShapeDtypeStruct((D, T), F32), jax.ShapeDtypeStruct((pairs, 2, T), F32)),
        grid_spec=pltpu.PrefetchScalarGridSpec(
            num_scalar_prefetch=1, grid=(pairs,),
            in_specs=[pl.BlockSpec((T, 128), lambda h, b: (0, h)),
                      pl.BlockSpec((T, 128), lambda h, b: (0, 0)),
                      pl.BlockSpec((S, 128), lambda h, b: (0, h)),
                      pl.BlockSpec((S, 128), lambda h, b: (0, 0)),
                      pl.BlockSpec((S, 128), lambda h, b: (0, h))],
            out_specs=(pl.BlockSpec((128, T), lambda h, b: (h, 0)),
                       pl.BlockSpec((1, 2, T), lambda h, b: (h, 0, 0))),
            scratch_shapes=[pltpu.VMEM((S, 2 * tq), F32), pltpu.VMEM((128, 2 * tq), F32)]),
        name="attend",
    )(docs, q, qaug, k, kaug, v)


def bwd_kernel(tq, tk, docs, q_ref, qaug_ref, do_ref, lse_ref, ot_ref, k_ref, kaug_ref, v_ref,
               dq_ref, dk_ref, dv_ref, dk_acc, dv_acc, dq_acc, delta_scr):
    n_rows, n_keys = q_ref.shape[0], k_ref.shape[0]
    first_row = lax.axis_index("ctx") * n_rows
    low, high = n_keys, 0
    for i in range(n_rows // tq):
        start, count = key_range(docs, first_row + i * tq, tq, n_keys)
        low, high = jnp.minimum(low, start), jnp.maximum(high, start + count * 256)

    def over_seen(fn):
        def one(t, carry):
            fn(pl.ds(pl.multiple_of(low + t * 128, 128), 128))
            return carry

        lax.fori_loop(0, (high - low) // 128, one, 0)

    def clear(rows):
        dk_acc[rows, :] = jnp.zeros((128, 128), F32)
        dv_acc[rows, :] = jnp.zeros((128, 128), F32)

    over_seen(clear)
    mixed = ot_ref[...] * do_ref[...].astype(F32).T
    deltas = [jnp.sum(mixed[:64], axis=0, keepdims=True), jnp.sum(mixed[64:], axis=0, keepdims=True)]
    delta_scr[...] = jnp.concatenate(deltas, axis=0)

    def part(i, carry):
        part_rows = pl.ds(pl.multiple_of(i * tq, tq), tq)
        start, count = key_range(docs, first_row + i * tq, tq, n_keys)
        q, do = q_ref[part_rows, :], do_ref[part_rows, :]
        qs = stack_heads(q)
        qrhs = stack_heads(q, qaug_ref[part_rows, :])
        dos = stack_heads(do)
        lse = jnp.concatenate([lse_ref[0, 0:1, part_rows], lse_ref[0, 1:2, part_rows]], axis=1)
        delta = jnp.concatenate([delta_scr[0:1, part_rows], delta_scr[1:2, part_rows]], axis=1)
        dq_acc[...] = jnp.zeros_like(dq_acc)

        def step(loc, off, size, carry):
            rows = pl.ds(off, size)
            lhs = jnp.concatenate([k_ref[rows, :], kaug_ref[rows, :]], axis=1)
            x = lax.dot_general(lhs, qrhs, NT, preferred_element_type=F32)
            y = lax.dot_general(v_ref[rows, :], dos, NT, preferred_element_type=F32)
            p = jnp.exp(x - lse)
            ds = (p * (y - delta)).astype(BF)
            pb = p.astype(BF)
            dv_acc[rows, :] += lax.dot_general(pb, dos, NN, preferred_element_type=F32)
            dk_acc[rows, :] += lax.dot_general(ds, qs, NN, preferred_element_type=F32)
            dq_acc[...] += lax.dot_general(k_ref[rows, :], ds, TN, preferred_element_type=F32)
            return carry

        two_level(start, count, tk, step, 0)
        dq_ref[part_rows, :] = (pick_heads(dq_acc[...], tq) * SCALE).T.astype(BF)
        return carry

    lax.fori_loop(0, n_rows // tq, part, 0)
    dk_ref[...] = jnp.zeros_like(dk_ref)
    dv_ref[...] = jnp.zeros_like(dv_ref)

    def give(rows):
        dk_ref[rows, :] = dk_acc[rows, :].astype(BF)
        dv_ref[rows, :] = dv_acc[rows, :].astype(BF)

    over_seen(give)


def attn_bwd(docs, q, qaug, do, lse, ot, k, kaug, v, *, tq=256, tk=1536):
    T, D = q.shape
    S = k.shape[0]
    pairs = D // 128
    return pl.pallas_call(
        functools.partial(bwd_kernel, tq, tk),
        out_shape=(jax.ShapeDtypeStruct((T, D), BF), jax.ShapeDtypeStruct((S, D), BF), jax.ShapeDtypeStruct((S, D), BF)),
        grid_spec=pltpu.PrefetchScalarGridSpec(
            num_scalar_prefetch=1, grid=(pairs,),
            in_specs=[pl.BlockSpec((T, 128), lambda h, b: (0, h)),
                      pl.BlockSpec((T, 128), lambda h, b: (0, 0)),
                      pl.BlockSpec((T, 128), lambda h, b: (0, h)),
                      pl.BlockSpec((1, 2, T), lambda h, b: (h, 0, 0)),
                      pl.BlockSpec((128, T), lambda h, b: (h, 0)),
                      pl.BlockSpec((S, 128), lambda h, b: (0, h)),
                      pl.BlockSpec((S, 128), lambda h, b: (0, 0)),
                      pl.BlockSpec((S, 128), lambda h, b: (0, h))],
            out_specs=(pl.BlockSpec((T, 128), lambda h, b: (0, h)),
                       pl.BlockSpec((S, 128), lambda h, b: (0, h)),
                       pl.BlockSpec((S, 128), lambda h, b: (0, h))),
            scratch_shapes=[pltpu.VMEM((S, 128), F32), pltpu.VMEM((S, 128), F32), pltpu.VMEM((128, 2 * tq), F32),
                            pltpu.VMEM((2, T), F32)]),
        name="attend_back",
    )(docs, q, qaug, do, lse, ot, k, kaug, v)


def middle_kernel(attn_ref, in_ref, cot_ref, vec_ref, out_own, out_far, wu_ref, down_own, down_far,
                  out_ref, sum1_ref, do_ref, grads_ref, up_out, down_out, attn_out,
                  wo, wu, wd, attn_b, first, hat1, scale1, first_b, act, slope, sum2, down_b, up_b, first_b2, first_t,
                  g_up, g_down, g_out, sem_w, sem_d, sem_o):
    rows, wide = in_ref.shape[0], wu.shape[1]
    a, w = lax.axis_index("ctx"), lax.axis_index("wsh")
    y, c = w // 2, lax.rem(w, 2)
    core_peer = (a, y * 2 + (1 - c))
    MESH = pl.DeviceIdType.MESH
    owners = (w, (1 - y) * 2 + c)
    barrier = pltpu.get_barrier_semaphore()
    pl.semaphore_signal(barrier, inc=1, device_id=core_peer, device_id_type=MESH)
    pl.semaphore_wait(barrier, 1)

    def share(j, s, full, ref):
        tall = ref.shape[0]
        there = full.at[pl.ds(pl.multiple_of(owners[s] * tall, 16), tall), :]
        return (
            pltpu.make_async_copy(ref, there, sem_w.at[j, s]),
            pltpu.make_async_remote_copy(
                src_ref=ref, dst_ref=there, send_sem=sem_d.at[0, j, s], recv_sem=sem_d.at[1, j, s],
                device_id=core_peer, device_id_type=MESH),
        )

    shares = [[share(j, s, full, ref) for s, ref in enumerate(pair)]
              for j, (full, pair) in enumerate(((wo, (out_own, out_far)), (wd, (down_own, down_far))))]
    up_load = pltpu.make_async_copy(wu_ref, wu, sem_w.at[2, 0])
    for pair in shares:
        for kept, passed in pair:
            passed.start()
            kept.start()
    up_load.start()

    def arrived(j):
        if j == 1:
            up_load.wait()
        else:
            for kept, passed in shares[j // 2]:
                kept.wait()
                passed.wait_recv()

    grads_ref[...] = jnp.zeros_like(grads_ref)
    attn_b[...] = attn_ref[...].astype(BF)
    out_b, attn_g, attn_s, down_bias, final_g, final_s = [vec_ref[i : i + 1, :] for i in range(2, 8)]
    arrived(0)
    block = 128

    def over_rows(fn):
        def one(i, carry):
            fn(pl.ds(pl.multiple_of(i * block, block), block))
            return carry

        lax.fori_loop(0, rows // block, one, 0)

    def norm(values):
        average = jnp.mean(values, axis=-1, keepdims=True)
        centred = values - average
        scale = lax.rsqrt(jnp.mean(centred * centred, axis=-1, keepdims=True) + EPS)
        return centred * scale, scale

    def norm_back(grad, hat, scale, gain):
        g = grad * gain
        return scale * (g - jnp.mean(g, axis=-1, keepdims=True) - hat * jnp.mean(g * hat, axis=-1, keepdims=True))

    def note(row, values):
        grads_ref[row : row + 1, :] += jnp.sum(values, axis=0, keepdims=True)

    def branch_part(r):
        a = attn_b[:, r].T
        v = lax.dot_general(a, wo[...], NN, preferred_element_type=F32) + out_b + in_ref[r, :].astype(F32)
        hat, scale = norm(v)
        hat1[r, :] = hat
        scale1[r, :] = scale
        f = hat * attn_g + attn_s
        first[r, :] = f
        first_b[r, :] = f.astype(BF)

    over_rows(branch_part)
    arrived(1)
    cols = vec_ref.shape[1]

    def over_wide(fn):
        def one(i, carry):
            fn(pl.ds(pl.multiple_of(i * cols, cols), cols), i)
            return carry

        lax.fori_loop(0, wide // cols, one, 0)

    def up_part(n, i):
        u = lax.dot_general(first_b[...], wu[:, n], NN, preferred_element_type=F32) + vec_ref[pl.ds(8 + i, 1), :]
        half = 0.5 * (1.0 + lax.erf(u * ROOT_HALF))
        act[:, n] = (u * half).astype(BF)
        slope[:, n] = half + u * (0.3989422804014327 * jnp.exp(-0.5 * u * u))

    over_wide(up_part)
    arrived(2)

    def down_part(r):
        v = lax.dot_general(act[r, :], wd[...], NN, preferred_element_type=F32) + down_bias + first[r, :]
        hat, scale = norm(v)
        out_ref[r, :] = (hat * final_g + final_s).astype(BF)
        cot = cot_ref[r, :].astype(F32)
        note(6, cot * hat)
        note(7, cot)
        g = norm_back(cot, hat, scale, final_g)
        sum2[r, :] = g
        rounded = g.astype(BF)
        down_b[r, :] = rounded
        note(5, rounded.astype(F32))

    over_rows(down_part)

    def up_back(n, i):
        g = lax.dot_general(down_b[...], wd[n, :], NT, preferred_element_type=F32) * slope[:, n]
        rounded = g.astype(BF)
        up_b[:, n] = rounded
        grads_ref[pl.ds(8 + i, 1), :] = jnp.sum(rounded.astype(F32), axis=0, keepdims=True)

    over_wide(up_back)

    def first_part(r):
        g = sum2[r, :] + lax.dot_general(up_b[r, :], wu[...], NT, preferred_element_type=F32)
        hat = hat1[r, :]
        note(3, g * hat)
        note(4, g)
        s1 = norm_back(g, hat, scale1[r, :], attn_g)
        sum1_ref[r, :] = s1
        rounded = s1.astype(BF)
        note(2, rounded.astype(F32))
        first_b2[r, :] = rounded

    over_rows(first_part)

    def do_part(r):
        do_ref[r, :] = lax.dot_general(first_b2[r, :], wo[...], NT, preferred_element_type=F32).astype(BF)

    over_rows(do_part)

    def wide_grads(n, i):
        g_down[n, :] = lax.dot_general(act[:, n].T, down_b[...], NN, preferred_element_type=F32).astype(BF)
        pltpu.make_async_copy(g_down.at[n, :], down_out.at[n, :], sem_o.at[0, i]).start()
        g_up[:, n] = lax.dot_general(first_t[...], up_b[:, n], NN, preferred_element_type=F32).astype(BF)
        pltpu.make_async_copy(g_up.at[:, n], up_out.at[:, n], sem_o.at[1, i]).start()

    first_t[...] = first_b[...].T
    over_wide(wide_grads)
    g_out[...] = lax.dot_general(attn_b[...], first_b2[...], NN, preferred_element_type=F32).astype(BF)
    pltpu.make_async_copy(g_out, attn_out, sem_o.at[2, 0]).start()

    def wide_end(n, i):
        pltpu.make_async_copy(g_down.at[n, :], down_out.at[n, :], sem_o.at[0, i]).wait()
        pltpu.make_async_copy(g_up.at[:, n], up_out.at[:, n], sem_o.at[1, i]).wait()

    over_wide(wide_end)
    pltpu.make_async_copy(g_out, attn_out, sem_o.at[2, 0]).wait()
    for pair in shares:
        for _kept, passed in pair:
            passed.wait_send()


def middle(attn_t, inputs, cotangent, vec, out_own, out_far, up_w, down_own, down_far):
    rows = inputs.shape[0]
    wide = up_w.shape[1]
    vm, dma, shape = pltpu.VMEM, pltpu.SemaphoreType.DMA, jax.ShapeDtypeStruct
    any_spec = pl.BlockSpec(memory_space=pltpu.HBM)
    vm_spec = pl.BlockSpec(memory_space=pltpu.VMEM)
    return pl.pallas_call(
        middle_kernel,
        out_shape=(shape((rows, D), BF), shape((rows, D), F32), shape((rows, D), BF), shape((16, D), F32),
                   shape((D, wide), BF), shape((wide, D), BF), shape((D, D), BF)),
        in_specs=[vm_spec] * 4 + [any_spec] * 5,
        out_specs=(vm_spec,) * 4 + (any_spec,) * 3,
        scratch_shapes=[
            vm((D, D), BF), vm((D, wide), BF), vm((wide, D), BF), vm((D, rows), BF), vm((rows, D), F32),
            vm((rows, D), F32), vm((rows, 1), F32), vm((rows, D), BF), vm((rows, wide), BF), vm((rows, wide), F32),
            vm((rows, D), F32), vm((rows, D), BF), vm((rows, wide), BF), vm((rows, D), BF), vm((D, rows), BF),
            vm((D, wide), BF), vm((wide, D), BF), vm((D, D), BF), dma((3, 2)), dma((2, 2, 2)), dma((3, wide // D)),
        ],
        compiler_params=pltpu.CompilerParams(collective_id=3, has_side_effects=True, vmem_limit_bytes=63 * 2**20),
        name="middle",
    )(attn_t, inputs, cotangent, vec, out_own, out_far, up_w, down_own, down_far)


def reach(n_ctx):
    return n_ctx // 2


def finish_kernel(sources, n_parts, *refs):
    parts = refs[:n_parts]
    (vec_ref, dk_ref, dv_ref, tok_ref, dq_ref, w_ref, own_in_ref, mine_tok_ref,
     out_ref, vec_out, wide_out, grad_ref,
     mine, buf_a, buf_h, buf_b, buf_s, buf_c, buf_d, buf_e, gbf,
     sums, heard, line,
     loads, weights, acc, dq, own, bias,
     run_part, from_x, from_z, far_z, last_x,
     sem_l, sem_a, sem_b, sem_c, sem_d, sem_v, sem_x, sem_z, sem_far, sem_load, sem_in) = refs[n_parts:]
    n_ready = len(sources)
    n_chunks = out_ref.shape[0]
    n_ctx, n_wsh = lax.axis_size("ctx"), lax.axis_size("wsh")
    zs = n_ctx // 2
    a, w = lax.axis_index("ctx"), lax.axis_index("wsh")
    z, x = a // 2, lax.rem(a, 2)
    y, c = w // 2, lax.rem(w, 2)
    core_peer = (a, y * 2 + (1 - c))
    y_peer = (a, (1 - y) * 2 + c)
    x_peer = (z * 2 + (1 - x), w)
    low, high = lax.rem(z, 2), z // 2
    pair_peer = ((z + 1 - 2 * low) * 2 + x, w)
    skip_peer = (lax.rem(z + 2, zs) * 2 + x, w)
    up_peer, down_peer = (a + 2, w), (a - 2, w)
    near = reach(n_ctx)
    hops = near // 2
    MESH = pl.DeviceIdType.MESH

    rows = out_ref.shape[1]
    half = out_ref.shape[2] // 2
    piece = rows // zs
    tall = own.shape[0]
    cut = from_x.shape[1]

    def z_peer(d):
        return (lax.rem(z + d, zs) * 2 + x, w)

    barrier = pltpu.get_barrier_semaphore()
    for dev in [core_peer, y_peer, x_peer] + [z_peer(d) for d in range(1, zs)]:
        pl.semaphore_signal(barrier, inc=1, device_id=dev, device_id_type=MESH)
    pl.semaphore_wait(barrier, zs + 2)

    def send(src, dst, sems, idx, dev):
        return pltpu.make_async_remote_copy(
            src_ref=src, dst_ref=dst, send_sem=sems.at[(0,) + idx], recv_sem=sems.at[(1,) + idx],
            device_id=dev, device_id_type=MESH)

    def wait_in(ref, sems, idx):
        send(ref, ref, sems, idx, core_peer).wait_recv()

    def wait_out(ref, sems, idx):
        send(ref, ref, sems, idx, core_peer).wait_send()

    def distance(i):
        return (hops - i // 4) * (1 - 2 * lax.rem(i // 2, 2))

    def position(i):
        dz = distance(i)
        mine_too = lax.rem(i, 2)
        run = 2 * (z + dz) + (1 - x) * (1 - mine_too) + x * mine_too
        return run, mine_too, (z + dz >= 0) & (z + dz < zs) & (jnp.abs(run - a) <= near)

    n_pos = 4 * hops + 2

    def load(i):
        run, _mine_too, there = position(i)
        return there, [
            pltpu.make_async_copy(src.at[run], loads.at[lax.rem(i, 2), j], sem_load.at[lax.rem(i, 2), j])
            for j, src in enumerate((dk_ref, dv_ref, tok_ref))
        ]

    def load_start(i):
        there, copies = load(i)

        @pl.when(there & (i < n_pos))
        def _():
            for copy in copies:
                copy.start()

    def share(k, owner):
        if k < n_ready:
            p, row0, col0 = sources[k]
            return parts[p].at[owner, pl.ds(row0, rows), pl.ds(col0, 2 * half)]
        return gbf.at[k - n_ready, owner]

    def share_load(k):
        for yy in range(2):
            pltpu.make_async_copy(share(k, yy * 2 + c), mine.at[k % 4, yy], sem_l.at[k]).start()

    def share_send(k):
        for yy in range(2):
            send(share(k, yy * 2 + (1 - c)), buf_a.at[k, yy], sem_a, (k,), core_peer).start()

    load_start(0)
    fetch = [pltpu.make_async_copy(w_ref, weights, sem_in.at[0]), pltpu.make_async_copy(dq_ref, dq, sem_in.at[1]),
             pltpu.make_async_copy(own_in_ref, own, sem_in.at[2])]
    for copy in fetch:
        copy.start()
    for k in range(n_ready):
        share_send(k)
        if k < 4:
            share_load(k)
    acc[...] = jnp.zeros_like(acc)
    bias[...] = jnp.zeros_like(bias)
    fetch[0].wait()

    near_rows, far_rows = pl.ds(0, cut), pl.ds(cut, tall - cut)

    def unit(i):
        run, mine_too, there = position(i)
        at = lax.rem(i, 2)
        load_start(i + 1)

        @pl.when(there)
        def _():
            for copy in load(i)[1]:
                copy.wait()

            def tokens_part(r, carry):
                rs = pl.ds(pl.multiple_of(r * 128, 128), 128)
                g = lax.dot_general(loads[at, 0, rs, :], weights[0], NT, preferred_element_type=F32)
                g = g + lax.dot_general(loads[at, 1, rs, :], weights[1], NT, preferred_element_type=F32)
                run_part[i, rs, :] = g.astype(BF)
                bias[0:8, :] += jnp.sum(loads[at, 1, rs, :].astype(F32).reshape(16, 8, 2 * half), axis=0)
                return carry

            lax.fori_loop(0, tall // 128, tokens_part, 0)

            @pl.when(mine_too == 0)
            def _():
                send(run_part.at[i, near_rows, :], from_x.at[i // 2], sem_x, (i // 2,), x_peer).start()

            @pl.when(i < 4)
            def _():
                far_send(i)

            def weights_part(r, carry):
                fs = pl.ds(pl.multiple_of(r * 256, 256), 256)
                flipped = loads[at, 2, :, fs].T
                for j in range(2):
                    acc[j, fs, :] += lax.dot_general(flipped, loads[at, j], NN, preferred_element_type=F32)
                return carry

            lax.fori_loop(0, 2 * half // 256, weights_part, 0)

    def from_below(i):
        dz = distance(i)
        step = 1 - 2 * lax.rem(i // 2, 2)
        sender, target = z - step, z - step + dz
        side = jnp.abs(2 * dz + (1 - 2 * x) * (1 - lax.rem(i, 2))) <= near
        return (sender >= 0) & (sender < zs) & (target >= 0) & (target < zs) & side

    def toward(i, copy_of):
        step = 1 - 2 * lax.rem(i // 2, 2)

        @pl.when(step == 1)
        def _():
            copy_of(up_peer).start()

        @pl.when(step == -1)
        def _():
            copy_of(down_peer).start()

    def far_send(i):
        toward(i, lambda dev: send(run_part.at[i, far_rows, :], far_z.at[i], sem_far, (i,), dev))

    def far_pass(i):
        _run, _mine_too, there = position(i)

        @pl.when(there)
        def _():
            @pl.when(from_below(i - 4))
            def _():
                wait_in(far_z.at[i - 4], sem_far, (i - 4,))
                run_part[i, far_rows, :] = (
                    run_part[i, far_rows, :].astype(F32) + far_z[i - 4].astype(F32)).astype(BF)

            far_send(i)

    def far_end():
        for col in range(2):
            total = n_pos - 2 + col
            for src in (4 + col, 6 + col):
                @pl.when(from_below(src))
                def _():
                    wait_in(far_z.at[src], sem_far, (src,))
                    run_part[total, far_rows, :] = (
                        run_part[total, far_rows, :].astype(F32) + far_z[src].astype(F32)).astype(BF)
            if col == 0:
                send(run_part.at[total, far_rows, :], last_x, sem_x, (n_pos // 2,), x_peer).start()
        own[far_rows, :] += run_part[n_pos - 1, far_rows, :].astype(F32)

    def near_pass(n):
        dz = distance(2 * n)
        i = 2 * n + 1

        @pl.when((z + dz >= 0) & (z + dz < zs))
        def _():
            @pl.when(jnp.abs(2 * dz + 2 * x - 1) <= near)
            def _():
                wait_in(from_x.at[n], sem_x, (n,))
                run_part[i, near_rows, :] = (
                    run_part[i, near_rows, :].astype(F32) + from_x[n].astype(F32)).astype(BF)

            @pl.when((n >= 2) & from_below(i - 4))
            def _():
                wait_in(from_z.at[n - 2], sem_z, (n - 2,))
                run_part[i, near_rows, :] = (
                    run_part[i, near_rows, :].astype(F32) + from_z[n - 2].astype(F32)).astype(BF)

            toward(i, lambda dev: send(run_part.at[i, near_rows, :], from_z.at[n], sem_z, (n,), dev))

    def near_own():
        n = n_pos // 2 - 1
        wait_in(from_x.at[n], sem_x, (n,))
        own[near_rows, :] += run_part[n_pos - 1, near_rows, :].astype(F32) + from_x[n].astype(F32)

    def near_end():
        for n in (2, 3):
            @pl.when(from_below(2 * n + 1))
            def _():
                wait_in(from_z.at[n], sem_z, (n,))
                own[near_rows, :] += from_z[n].astype(F32)

    def add(p, q):
        return (p.astype(F32) + q.astype(F32)).astype(BF)

    def column(side):
        return pl.ds(pl.multiple_of(side * half, 128), half)

    def band(start, size):
        return pl.ds(pl.multiple_of(start, 16), size)

    def stage_b(k):
        at = lax.rem(k, 4)
        pltpu.make_async_copy(mine.at[at], mine.at[at], sem_l.at[k]).wait()
        wait_in(buf_a.at[k], sem_a, (k,))
        buf_h[k] = add(mine[at, 1 - y], buf_a[k, 1 - y])
        send(buf_h.at[k], buf_b.at[k], sem_b, (k,), y_peer).start()
        buf_a[k, y] = add(mine[at, y], buf_a[k, y])

    def stage_c(k):
        wait_in(buf_b.at[k], sem_b, (k,))
        buf_s[k] = add(buf_a[k, y, :, column(1 - x)], buf_b[k, :, column(1 - x)])
        send(buf_s.at[k], buf_c.at[k], sem_c, (0, k), x_peer).start()

    my_two, other_two = band(low * 2 * piece, 2 * piece), band((1 - low) * 2 * piece, 2 * piece)
    my_one, other_one = band(high * piece, piece), band((1 - high) * piece, piece)
    my_rows = band(low * 2 * piece + high * piece, piece)

    def stage_d(k):
        wait_in(buf_c.at[k], sem_c, (0, k))
        cols = column(x)
        joined = buf_a[k, y, :, cols].astype(F32) + buf_b[k, :, cols].astype(F32) + buf_c[k].astype(F32)
        buf_c[k] = joined.astype(BF)
        send(buf_c.at[k, other_two, :], buf_d.at[k], sem_d, (0, k), pair_peer).start()

    def stage_d2(k):
        wait_in(buf_d.at[k], sem_d, (0, k))
        buf_d[k] = add(buf_d[k], buf_c[k, my_two, :])
        send(buf_d.at[k, other_one, :], buf_e.at[k], sem_d, (1, k), skip_peer).start()

    def stage_e(k):
        wait_in(buf_e.at[k], sem_d, (1, k))
        buf_e[k] = add(buf_e[k], buf_d[k, my_one, :])
        out_ref[k, my_rows, column(x)] = buf_e[k]
        send(buf_e.at[k], out_ref.at[k, my_rows, column(x)], sem_d, (2, k), skip_peer).start()

    def stage_e2(k):
        wait_in(buf_e.at[k], sem_d, (2, k))
        there = out_ref.at[k, my_two, column(x)]
        send(there, there, sem_d, (3, k), pair_peer).start()

    def stage_f(k):
        wait_in(buf_d.at[k], sem_d, (3, k))
        there = out_ref.at[k, :, column(x)]
        send(there, there, sem_c, (1, k), x_peer).start()

    def guarded(fn, k, first, last):
        @pl.when((k >= first) & (k < last))
        def _():
            fn(k)

    def chunk_step(m):
        for lag, stage in enumerate((stage_c, stage_d, stage_d2, stage_e, stage_e2, stage_f)):
            guarded(stage, m - (lag and lag + 5), 0, n_chunks)

    def first_step(t, carry):
        guarded(unit, t, 0, n_pos)
        for j in range(2):
            guarded(stage_b, 2 * t + j, 0, n_ready)
        for k in range(4, n_ready):
            @pl.when(t == (k - 4) // 2)
            def _():
                share_load(k)

        @pl.when(lax.rem(t, 2) == 1)
        def _():
            guarded(near_pass, t // 2 - 1, 0, 4)

        guarded(far_pass, t - 2, 4, 8)

        @pl.when((lax.rem(t, 2) == 0) & (t >= 2))
        def _():
            chunk_step(t // 2 - 1)

        return carry

    lax.fori_loop(0, n_pos, first_step, 0)
    done = n_pos // 2 - 1

    fetch[1].wait()
    fetch[2].wait()
    own_tok = pltpu.make_async_copy(mine_tok_ref, loads.at[0, 2], sem_load.at[0, 2])
    own_tok.start()

    def to_bf(j, target):
        for owner in range(n_wsh):
            gbf[target, owner] = acc[j, owner * rows : (owner + 1) * rows, :].astype(BF)
        share_load(n_ready + target)
        share_send(n_ready + target)

    to_bf(0, 0)
    to_bf(1, 1)
    own_tok.wait()

    def query_part(r, carry):
        fs = pl.ds(pl.multiple_of(r * 256, 256), 256)
        acc[0, fs, :] = lax.dot_general(loads[0, 2, :, fs].T, dq[...], NN, preferred_element_type=F32)
        return carry

    lax.fori_loop(0, 2 * half // 256, query_part, 0)
    to_bf(0, 2)

    def query_tokens(r, carry):
        rs = pl.ds(pl.multiple_of(r * 128, 128), 128)
        own[rs, :] += lax.dot_general(dq[rs, :], weights[2], NT, preferred_element_type=F32)
        bias[8:16, :] += jnp.sum(dq[rs, :].astype(F32).reshape(16, 8, 2 * half), axis=0)
        return carry

    lax.fori_loop(0, tall // 128, query_tokens, 0)

    sums[0] = vec_ref[...]
    sums[0, 0:1, :] = jnp.sum(bias[8:16, :], axis=0, keepdims=True)
    sums[0, 1:2, :] = jnp.sum(bias[0:8, :], axis=0, keepdims=True)
    pair = (core_peer, y_peer, x_peer)

    def vec_send(stage):
        send(sums.at[stage], heard.at[stage], sem_v, (stage,), pair[stage]).start()

    def vec_stage(stage):
        wait_in(heard.at[stage], sem_v, (stage,))
        total = sums[stage] + heard[stage]
        sums[stage + 1] = total
        if stage < 2:
            vec_send(stage + 1)
        else:
            line[z] = total
            for d in range(1, zs):
                send(sums.at[3], line.at[z], sem_v, (3,), z_peer(d)).start()

    def vec_last():
        wait_in(line.at[pl.ds(0, zs - 1)], sem_v, (3,))
        total = line[0]
        for d in range(1, zs):
            total = total + line[d]
        small, wide = total[0:8, 0:rows], total[8:9, :]
        for owner in range(1, n_wsh):
            small = jnp.where(w == owner, total[0:8, owner * rows : (owner + 1) * rows], small)
            wide = jnp.where(w == owner, total[8 + owner : 9 + owner, :], wide)
        vec_out[...] = small
        wide_out[...] = wide

    vec_send(0)

    def second_step(m, carry):
        guarded(stage_b, m - done + n_ready, n_ready, n_chunks)
        chunk_step(m)
        guarded(lambda k: near_own(), m - done, 0, 1)
        for stage in range(3):
            guarded(lambda k: vec_stage(stage), m - done - 1 - stage, 0, 1)
        guarded(lambda k: near_end(), m - done - 3, 0, 1)
        guarded(lambda k: far_end(), m - done - 4, 0, 1)
        guarded(lambda k: vec_last(), m - done - 5, 0, 1)
        return carry

    lax.fori_loop(done, n_chunks + 10, second_step, 0)
    wait_in(last_x, sem_x, (n_pos // 2,))
    own[far_rows, :] += last_x[...].astype(F32)
    grad_ref[...] = own[...].astype(BF)

    def drain(k, carry):
        wait_in(buf_s.at[k], sem_c, (1, k))
        wait_out(buf_a.at[k], sem_a, (k,))
        wait_out(buf_b.at[k], sem_b, (k,))
        wait_out(buf_s.at[k], sem_c, (0, k))
        wait_out(buf_s.at[k], sem_c, (1, k))
        wait_out(buf_d.at[k], sem_d, (0, k))
        wait_out(buf_e.at[k], sem_d, (1, k))
        wait_out(buf_e.at[k], sem_d, (2, k))
        wait_out(buf_d.at[k], sem_d, (3, k))
        return carry

    lax.fori_loop(0, n_chunks, drain, 0)
    for stage in range(3):
        wait_out(heard.at[stage], sem_v, (stage,))
    wait_out(line.at[pl.ds(0, zs - 1)], sem_v, (3,))
    wait_out(last_x, sem_x, (n_pos // 2,))

    def drain_runs(i, carry):
        _run, mine_too, there = position(i)

        @pl.when(there)
        def _():
            wait_out(far_z.at[i], sem_far, (i,))

            @pl.when(mine_too == 1)
            def _():
                wait_out(from_z.at[i // 2], sem_z, (i // 2,))

        return carry

    lax.fori_loop(0, n_pos - 2, drain_runs, 0)

    def drain_x(n, carry):
        _run, _mine_too, there = position(2 * n)

        @pl.when(there)
        def _():
            wait_out(from_x.at[n], sem_x, (n,))

        return carry

    lax.fori_loop(0, n_pos // 2, drain_x, 0)


def widen_kernel(spans, in_ref, *outs):
    for (first, down, across), out in zip(spans, outs):
        for r in range(down):
            for col in range(across):
                out[r, :, col * D : (col + 1) * D] = in_ref[first + r * across + col].astype(F32)


def widen(summed, spans):
    n, rows, _width = summed.shape
    part = rows // 4
    outs = pl.pallas_call(
        functools.partial(widen_kernel, spans),
        grid=(4,),
        out_shape=[jax.ShapeDtypeStruct((down, rows, across * D), F32) for _first, down, across in spans],
        in_specs=[pl.BlockSpec((n, part, D), lambda i: (0, i, 0))],
        out_specs=[pl.BlockSpec((down, part, across * D), lambda i: (0, i, 0)) for _first, down, across in spans],
        name="widen",
    )(summed)
    return [o.reshape(-1, o.shape[2]) for o in outs]


def finish(matrices, vec, grad_k, grad_v, all_tokens, grad_q, kvq_w, own_grad, inputs):
    n_ctx, n_wsh = lax.axis_size("ctx"), lax.axis_size("wsh")
    zs, hops = n_ctx // 2, reach(n_ctx) // 2
    rows = D // n_wsh
    parts, sources, spans = [], [], []
    for p, g in enumerate(matrices):
        down, across = g.shape[0] // D, g.shape[1] // D
        parts.append(g.astype(BF).reshape(n_wsh, down * rows, across * D))
        spans.append((len(sources), down, across))
        sources += [(p, r * rows, col * D) for r in range(down) for col in range(across)]
    n = len(sources) + 3
    spans += [(len(sources) + j, 1, 1) for j in range(3)]
    half, piece, tall = D // 2, rows // zs, inputs.shape[0]
    n_pos, cut = 4 * hops + 2, tall // 2
    vm, dma, shape = pltpu.VMEM, pltpu.SemaphoreType.DMA, jax.ShapeDtypeStruct
    any_spec = pl.BlockSpec(memory_space=pltpu.HBM)
    vm_spec = pl.BlockSpec(memory_space=pltpu.VMEM)
    summed, small, wide, grad_own = pl.pallas_call(
        functools.partial(finish_kernel, sources, len(parts)),
        out_shape=(shape((n, rows, D), BF), shape((8, rows), F32), shape((1, D), F32), shape((tall, D), BF)),
        in_specs=[any_spec] * len(parts) + [vm_spec] + [any_spec] * 7,
        out_specs=(vm_spec,) * 4,
        scratch_shapes=[
            vm((4, 2, rows, D), BF), vm((n, 2, rows, D), BF), vm((n, rows, D), BF), vm((n, rows, D), BF),
            vm((n, rows, half), BF), vm((n, rows, half), BF), vm((n, 2 * piece, half), BF), vm((n, piece, half), BF),
            vm((3, n_wsh, rows, D), BF),
            vm((4,) + vec.shape, F32), vm((3,) + vec.shape, F32), vm((zs,) + vec.shape, F32),
            vm((2, 3, tall, D), BF), vm((3, D, D), BF), vm((2, D, D), F32), vm((tall, D), BF), vm((tall, D), F32),
            vm((16, D), F32),
            vm((n_pos, tall, D), BF), vm((n_pos // 2, cut, D), BF), vm((4, cut, D), BF),
            vm((n_pos - 2, tall - cut, D), BF), vm((tall - cut, D), BF),
            dma((n,)), dma((2, n)), dma((2, n)), dma((2, 2, n)), dma((2, 4, n)), dma((2, 4)),
            dma((2, n_pos // 2 + 1)), dma((2, 4)), dma((2, n_pos - 2)), dma((2, 3)), dma((3,)),
        ],
        compiler_params=pltpu.CompilerParams(collective_id=2, has_side_effects=True, vmem_limit_bytes=63 * 2**20),
        name="finish",
    )(*parts, vec, grad_k, grad_v, all_tokens, grad_q, kvq_w, own_grad, inputs)
    return widen(summed, spans), small, wide, grad_own


def gather_kernel(cut, tok_ref, docs_ref, wk_ref, wv_ref, wq_ref, wu_ref, vec_ref,
                  tok_out, k_out, v_out, q_out, w_out, vec_out, wu_out, query_doc, key_doc,
                  tok, kbuf, vbuf, qbuf, wbuf, vecs, wu, kdoc,
                  sem_in, sem_out, sem_w, sem_l, sem_o):
    n_ctx = lax.axis_size("ctx")
    zs = n_ctx // 2
    a, w = lax.axis_index("ctx"), lax.axis_index("wsh")
    z, x = a // 2, lax.rem(a, 2)
    y, c = w // 2, lax.rem(w, 2)
    core_peer = (a, y * 2 + (1 - c))
    y_peer = (a, (1 - y) * 2 + c)
    x_peer = (z * 2 + (1 - x), w)
    up, down = (a + 2, w), (a - 2, w)
    near = reach(n_ctx)
    MESH = pl.DeviceIdType.MESH
    n_slices = sem_in.shape[1]
    tall = tok.shape[1] // n_slices
    own = wk_ref.shape[0]
    far = 4 * (near // 2 + 1)

    barrier = pltpu.get_barrier_semaphore()
    around = [(lax.rem(z + d, zs) * 2 + x, w) for d in (1, zs - 1)]
    for dev in [core_peer, y_peer, x_peer] + around:
        pl.semaphore_signal(barrier, inc=1, device_id=dev, device_id_type=MESH)
    pl.semaphore_wait(barrier, 5)

    def relative(u):
        dz = (u // 4) * (1 - 2 * lax.rem(u, 2))
        other = lax.rem(u // 2, 2)
        run = 2 * (z + dz) + (x + other - 2 * x * other)
        there = (z + dz >= 0) & (z + dz < zs) & (jnp.abs(run - a) <= near) & ((u >= 4) | (lax.rem(u, 2) == 0))
        return run, dz, other, there

    def rows(s):
        return pl.ds(pl.multiple_of(s * tall, tall), tall)

    def remote(src, dst, send_sem, recv_sem, dev):
        return pltpu.make_async_remote_copy(
            src_ref=src, dst_ref=dst, send_sem=send_sem, recv_sem=recv_sem, device_id=dev, device_id_type=MESH)

    def routes(u, s):
        run, dz, other, there = relative(u)
        z_first = s < cut
        to_x = there & (z_first | (dz == 0)) & (other == 0) & (jnp.abs(run - x_peer[0]) <= near)
        along = there & ((other == 0) | jnp.logical_not(z_first))
        to_up = along & (dz <= 0) & (z + 1 < zs) & (jnp.abs(run - (a + 2)) <= near)
        to_down = along & (dz >= 0) & (z > 0) & (jnp.abs(run - (a - 2)) <= near)
        return run, ((0, x_peer, to_x), (1, up, to_up), (2, down, to_down))

    def pass_on(u, s):
        run, where = routes(u, s)
        for d, dev, ok in where:
            @pl.when(ok)
            def _():
                source = tok_ref if isinstance(u, int) and u == 0 else tok.at[run]
                remote(source.at[rows(s), :], tok.at[run, rows(s), :], sem_out.at[d, u, s], sem_in.at[run, s], dev).start()

    def await_slice(u, s):
        run, _dz, _other, there = relative(u)

        @pl.when(there)
        def _():
            remote(tok.at[run, rows(s), :], tok.at[run, rows(s), :], sem_out.at[0, 0, 0], sem_in.at[run, s], x_peer).wait_recv()

    def start_own(s, carry):
        pass_on(0, s)
        return carry

    def weight_rows(owner):
        return pl.ds(pl.multiple_of(owner * own, 16), own)

    def shard(m, owner):
        if m == 3:
            return vecs.at[owner]
        return (wbuf.at[0], wbuf.at[1], wbuf.at[2], None, wu)[m].at[weight_rows(owner), :]

    vecs[w, 0 : vec_ref.shape[0], :] = vec_ref[...]
    shards = (wk_ref, wv_ref, wq_ref, vecs.at[w], wu_ref)
    for m in (3, 0, 1, 2, 4):
        remote(shards[m], shard(m, w), sem_w.at[0, 1, m], sem_w.at[1, 1, m], y_peer).start()
        remote(shards[m], shard(m, w), sem_w.at[0, 0, m], sem_w.at[1, 0, m], core_peer).start()
        if m != 3:
            pltpu.make_async_copy(shards[m], shard(m, w), sem_w.at[0, 3, m]).start()
    lax.fori_loop(0, n_slices, start_own, 0)
    pltpu.make_async_copy(tok_ref, tok.at[a], sem_l.at[4]).start()

    for j in range(n_ctx):
        @pl.when(jnp.abs(j - a) > near)
        def _():
            tok[j] = jnp.zeros_like(tok[j])

    n_rows = tok.shape[1]

    def is_own_lane(first):
        pos = first + lax.broadcasted_iota(jnp.int32, (n_rows, 128), 0)
        doc = jnp.full((n_rows, 128), -1, jnp.int32)
        for d in range(docs_ref.shape[1]):
            doc = doc + jnp.where(pos >= docs_ref[0, d], 1, 0)
        return lax.broadcasted_iota(jnp.int32, (n_rows, 128), 1) == doc

    def key_lanes(j, carry):
        kdoc[pl.ds(pl.multiple_of(j * n_rows, n_rows), n_rows), :] = jnp.where(
            is_own_lane(j * n_rows), 0.0, -1e30).astype(BF)
        return carry

    lax.fori_loop(0, n_ctx, key_lanes, 0)
    pltpu.make_async_copy(kdoc, key_doc, sem_l.at[3]).start()
    query_doc[...] = jnp.where(is_own_lane(a * n_rows), 1.0, 0.0).astype(BF)

    def weight_arrival(m, kind):
        part = shard(m, w)
        return remote(part, part, sem_w.at[0, kind, m], sem_w.at[1, kind, m], core_peer)

    across = (1 - y) * 2 + c

    def weight_forward(m):
        weight_arrival(m, 1).wait_recv()
        remote(shard(m, across), shard(m, across), sem_w.at[0, 2, m], sem_w.at[1, 2, m], core_peer).start()

    def weight_end(m):
        weight_arrival(m, 0).wait_recv()
        weight_arrival(m, 2).wait_recv()
        if m != 3:
            pltpu.make_async_copy(shard(m, w), shard(m, w), sem_w.at[0, 3, m]).wait()

    def relay(first, last):
        def one(i, carry):
            s = i // (last - first)
            u = first + lax.rem(i, last - first)
            await_slice(u, s)
            pass_on(u, s)
            return carry

        lax.fori_loop(0, n_slices * (last - first), one, 0)

    relay(2, 6)
    weight_forward(3)
    weight_forward(0)
    weight_forward(1)
    weight_end(3)
    vec_out[0:8, :] = jnp.concatenate([vecs[o, 0:8, :] for o in range(4)], axis=1)
    for o in range(4):
        vec_out[8 + o : 9 + o, :] = jnp.concatenate([vecs[o, 8 + i : 9 + i, :] for i in range(4)], axis=1)
    pltpu.make_async_copy(tok_ref, tok.at[a], sem_l.at[4]).wait()
    weight_end(0)
    weight_end(1)

    step_rows = 128
    steps = tok.shape[1] // step_rows

    def query_part(i, carry):
        r = pl.ds(pl.multiple_of(i * step_rows, step_rows), step_rows)
        q = (jnp.dot(tok[a, r, :], wbuf[2], preferred_element_type=F32) + vec_out[0:1, :]).astype(BF)
        qbuf[r, :] = q * jnp.asarray(SCALE, BF)
        return carry

    def project(u, carry):
        run, _dz, _other, there = relative(u)

        @pl.when(u == 6)
        def _():
            weight_forward(2)
            weight_end(2)
            lax.fori_loop(0, steps, query_part, 0)
            pltpu.make_async_copy(qbuf, q_out, sem_l.at[5]).start()
            relay(6, 10)

        @pl.when(there)
        def _():
            @pl.when(u >= 10)
            def _():
                def one(s, carry):
                    await_slice(u, s)
                    return carry

                lax.fori_loop(0, n_slices, one, 0)

            def part(i, carry):
                r = pl.ds(pl.multiple_of(i * step_rows, step_rows), step_rows)
                t = tok[run, r, :]
                kbuf[run, r, :] = jnp.dot(t, wbuf[0], preferred_element_type=F32).astype(BF)
                vbuf[run, r, :] = (jnp.dot(t, wbuf[1], preferred_element_type=F32) + vec_out[1:2, :]).astype(BF)
                return carry

            lax.fori_loop(0, steps, part, 0)
            for i, (src, dst) in enumerate(((kbuf, k_out), (vbuf, v_out), (tok, tok_out))):
                pltpu.make_async_copy(src.at[run], dst.at[run], sem_o.at[i, run]).start()

        return carry

    for j in range(n_ctx):
        @pl.when(jnp.abs(j - a) > near)
        def _():
            kbuf[j] = jnp.zeros_like(kbuf[j])
            vbuf[j] = jnp.zeros_like(vbuf[j])
            for i, (src, dst) in enumerate(((kbuf, k_out), (vbuf, v_out), (tok, tok_out))):
                pltpu.make_async_copy(src.at[j], dst.at[j], sem_o.at[i, j]).start()

    lax.fori_loop(0, far, project, 0)

    pltpu.make_async_copy(wbuf, w_out, sem_l.at[6]).start()

    weight_forward(4)
    weight_end(4)
    pltpu.make_async_copy(wu, wu_out, sem_l.at[1]).start()
    for m in range(5):
        for kind in range(3):
            weight_arrival(m, kind).wait_send()

    def drain(i, carry):
        s = i // far
        u = lax.rem(i, far)
        run, where = routes(u, s)
        for d, dev, ok in where:
            @pl.when(ok & (u < 10))
            def _():
                remote(tok.at[run, rows(s), :], tok.at[run, rows(s), :], sem_out.at[d, u, s], sem_in.at[run, s], dev).wait_send()
        return carry

    lax.fori_loop(0, n_slices * far, drain, 0)
    for j in range(n_ctx):
        for i, (src, dst) in enumerate(((kbuf, k_out), (vbuf, v_out), (tok, tok_out))):
            pltpu.make_async_copy(src.at[j], dst.at[j], sem_o.at[i, j]).wait()
    pltpu.make_async_copy(qbuf, q_out, sem_l.at[5]).wait()
    pltpu.make_async_copy(wbuf, w_out, sem_l.at[6]).wait()
    pltpu.make_async_copy(wu, wu_out, sem_l.at[1]).wait()
    pltpu.make_async_copy(kdoc, key_doc, sem_l.at[3]).wait()


def gather_project(inputs, doc_starts, vectors, key_weight, value_weight, query_weight, up_weight):
    n_ctx, n_wsh = lax.axis_size("ctx"), lax.axis_size("wsh")
    tall = inputs.shape[0]
    n_slices = 8
    far = 4 * (reach(n_ctx) // 2 + 1)
    vm, dma = pltpu.VMEM, pltpu.SemaphoreType.DMA
    any_spec = pl.BlockSpec(memory_space=pltpu.HBM)
    vm_spec = pl.BlockSpec(memory_space=pltpu.VMEM)
    runs = (n_ctx, tall, D)
    shape = jax.ShapeDtypeStruct
    return pl.pallas_call(
        functools.partial(gather_kernel, 5),
        out_shape=(shape(runs, BF), shape(runs, BF), shape(runs, BF), shape((tall, D), BF), shape((3, D, D), BF),
                   shape((16, D), F32), shape((D, up_weight.shape[1]), BF), shape((tall, 128), BF),
                   shape((n_ctx * tall, 128), BF)),
        in_specs=[any_spec, pl.BlockSpec(memory_space=pltpu.SMEM)] + [any_spec] * 4 + [vm_spec],
        out_specs=(any_spec,) * 5 + (vm_spec,) + (any_spec,) + (vm_spec, any_spec),
        scratch_shapes=[
            vm(runs, BF), vm(runs, BF), vm(runs, BF), vm((tall, D), BF), vm((3, D, D), BF), vm((n_wsh, 16, D // n_wsh), F32),
            vm((D, up_weight.shape[1]), BF), vm((n_ctx * tall, 128), BF),
            dma((n_ctx, n_slices)), dma((3, far, n_slices)), dma((2, 4, 5)), dma((7,)), dma((3, n_ctx)),
        ],
        compiler_params=pltpu.CompilerParams(collective_id=1, has_side_effects=True, vmem_limit_bytes=63 * 2**20),
        name="gather_project",
    )(inputs, doc_starts, key_weight, value_weight, query_weight, up_weight, vectors)


def local(
    tokens,
    cotangent,
    doc_starts,
    query_weight,
    key_weight,
    value_weight,
    out_weight,
    up_weight,
    down_weight,
    query_bias,
    value_bias,
    out_bias,
    attn_gain,
    attn_shift,
    up_bias,
    down_bias,
    final_gain,
    final_shift,
):
    inputs = tokens[0]
    doc_start = doc_starts[0]
    tok_rows = inputs.shape[0]
    stream_rows = tok_rows * lax.axis_size("ctx")
    tile = min(tok_rows, 256)
    n_ctx, n_wsh = lax.axis_size("ctx"), lax.axis_size("wsh")
    own = D // n_wsh

    def gather(x):
        return lax.all_gather(x, "wsh", axis=0, tiled=True)

    fast = n_wsh == 4 and n_ctx == 8 and own % (n_ctx // 2 * 16) == 0 and tok_rows % 512 == 0
    if fast:
        small = (query_bias, value_bias, out_bias, attn_gain, attn_shift, down_bias, final_gain, final_shift)
        vectors, place = jnp.zeros(((8 + n_wsh) * own,), F32), 0
        for v in small + (up_bias,):
            ends = (place, vectors.shape[0] - place - v.shape[0], 0)
            vectors = vectors + lax.pad(v.astype(F32), jnp.zeros((), F32), (ends,))
            place += v.shape[0]
        vectors = vectors.reshape(8 + n_wsh, own)
        all_tokens, keys, values, queries, kvq_w, vec, up_w, query_doc, key_doc = gather_project(
            inputs, doc_starts, vectors, key_weight, value_weight, query_weight, up_weight
        )
        out_own, down_own, _unused = lax.optimization_barrier((out_weight, down_weight, vec))
        across = [(i, i ^ 2) for i in range(n_wsh)]
        out_far = lax.ppermute(out_own, "wsh", across)
        down_far = lax.ppermute(down_own, "wsh", across)
        all_tokens, keys, values = [r.reshape(stream_rows, D) for r in (all_tokens, keys, values)]
    else:
        first_row = lax.axis_index("ctx") * tok_rows
        query_doc, key_doc = document_lanes(doc_start, first_row, tok_rows, stream_rows)
        small = jnp.stack(
            [query_bias, value_bias, out_bias, attn_gain, attn_shift, down_bias, final_gain, final_shift]
        )
        all_tokens = lax.all_gather(inputs, "ctx", axis=0, tiled=True)
        query_w, key_w, value_w = gather(query_weight), gather(key_weight), gather(value_weight)
        small = gather(small.T).astype(F32)
        query_b, value_b, out_b, attn_g, attn_s, down_b, final_g, final_s = [small[:, i] for i in range(8)]
        up_b = gather(up_bias).astype(F32)
        queries = jnp.dot(inputs, query_w, preferred_element_type=F32) + query_b
        queries = queries.astype(BF) * jnp.asarray(SCALE, BF)
        keys = jnp.dot(all_tokens, key_w, preferred_element_type=F32).astype(BF)
        values = (jnp.dot(all_tokens, value_w, preferred_element_type=F32) + value_b).astype(BF)
    mixed_t, log_rows = attn_fwd(doc_start, queries, query_doc, keys, key_doc, values, tq=tile)
    if fast:
        layer_out, grad_sum1, grad_attn, vec_grads, grad_up_w, grad_down_w, grad_out_w = middle(
            mixed_t, inputs, cotangent[0], vec, out_own, out_far, up_w, down_own, down_far
        )
        grad_q, grad_k, grad_v = attn_bwd(
            doc_start, queries, query_doc, grad_attn, log_rows, mixed_t, keys, key_doc, values, tq=tile
        )
        mats, small, wide, grad_inputs = finish(
            (grad_up_w, grad_out_w, grad_down_w), vec_grads, grad_k.reshape(n_ctx, tok_rows, D),
            grad_v.reshape(n_ctx, tok_rows, D), all_tokens.reshape(n_ctx, tok_rows, D), grad_q, kvq_w, grad_sum1, inputs,
        )
        up_sum, out_sum, down_sum, key_sum, value_sum, query_sum = mats
        return (
            layer_out.reshape(1, tok_rows, D), grad_inputs.reshape(1, tok_rows, D), query_sum, key_sum, value_sum,
            out_sum, up_sum, down_sum, small[0], small[1], small[2], small[3], small[4], wide[0],
            small[5], small[6], small[7],
        )

    out_w = gather(out_weight)
    up_w = gather(up_weight)
    down_w = gather(down_weight)
    attn_t = mixed_t.astype(BF)
    inputs_f = inputs.astype(F32)
    branch = lax.dot_general(attn_t, out_w, TN, preferred_element_type=F32) + out_b
    first_norm, first_pull = jax.vjp(layer_norm, inputs_f + branch, attn_g, attn_s)
    first_b = first_norm.astype(BF)
    up_f = jnp.dot(first_b, up_w, preferred_element_type=F32) + up_b
    act_f, act_pull = jax.vjp(gelu_act, up_f)
    act_b = act_f.astype(BF)
    down_f = jnp.dot(act_b, down_w, preferred_element_type=F32) + down_b
    final_f, final_pull = jax.vjp(layer_norm, first_norm + down_f, final_g, final_s)
    layer_out = final_f.astype(BF)

    grad_sum2, grad_final_g, grad_final_s = final_pull(cotangent[0].astype(F32))
    grad_down = grad_sum2.astype(BF)
    grad_down_w = jnp.einsum("tf,td->fd", act_b, grad_down, preferred_element_type=F32)
    grad_down_b = jnp.sum(grad_down.astype(F32), axis=0)
    grad_act = jnp.einsum("td,fd->tf", grad_down, down_w, preferred_element_type=F32)
    (grad_up_f,) = act_pull(grad_act)
    grad_up = grad_up_f.astype(BF)
    grad_up_w = jnp.einsum("td,tf->df", first_b, grad_up, preferred_element_type=F32)
    grad_up_b = jnp.sum(grad_up.astype(F32), axis=0)
    grad_first = grad_sum2 + jnp.einsum("tf,df->td", grad_up, up_w, preferred_element_type=F32)
    grad_sum1, grad_attn_g, grad_attn_s = first_pull(grad_first)
    grad_branch = grad_sum1.astype(BF)
    grad_out_w = jnp.dot(attn_t, grad_branch, preferred_element_type=F32)
    grad_out_b = jnp.sum(grad_branch.astype(F32), axis=0)
    grad_attn = jnp.einsum("te,de->td", grad_branch, out_w, preferred_element_type=F32).astype(BF)
    grad_q, grad_k, grad_v = attn_bwd(
        doc_start, queries, query_doc, grad_attn, log_rows, mixed_t, keys, key_doc, values, tq=tile
    )
    def total(g):
        part = lax.psum_scatter(g.astype(BF), "wsh", scatter_dimension=0, tiled=True)
        return lax.psum(part, "ctx").astype(F32)

    grad_all = jnp.einsum("te,de->td", grad_k, key_w, preferred_element_type=F32)
    grad_all = grad_all + jnp.einsum("te,de->td", grad_v, value_w, preferred_element_type=F32)
    grad_own = lax.psum_scatter(grad_all.astype(BF), "ctx", scatter_dimension=0, tiled=True)
    grad_query_w = jnp.einsum("td,te->de", inputs, grad_q, preferred_element_type=F32)
    grad_key_w = jnp.einsum("td,te->de", all_tokens, grad_k, preferred_element_type=F32)
    grad_value_w = jnp.einsum("td,te->de", all_tokens, grad_v, preferred_element_type=F32)
    grad_query_b = jnp.sum(grad_q.astype(F32), axis=0)
    grad_value_b = jnp.sum(grad_v.astype(F32), axis=0)
    grad_inputs = grad_sum1 + jnp.einsum("te,de->td", grad_q, query_w, preferred_element_type=F32)
    grad_inputs = grad_inputs + grad_own.astype(F32)
    sums = [
        total(g)
        for g in (
            grad_query_w, grad_key_w, grad_value_w, grad_out_w, grad_up_w, grad_down_w,
            grad_query_b, grad_value_b, grad_out_b, grad_attn_g, grad_attn_s, grad_up_b,
            grad_down_b, grad_final_g, grad_final_s,
        )
    ]
    return (
        layer_out.reshape(1, tok_rows, D),
        grad_inputs.astype(BF).reshape(1, tok_rows, D),
        *sums,
    )


def solution(mesh):
    rows, mat, vec = P("wsh", "ctx", None), P("wsh", None), P("wsh")
    return jax.shard_map(
        local,
        mesh=mesh,
        in_specs=(rows, rows, mat) + (mat,) * 6 + (vec,) * 9,
        out_specs=(rows, rows) + (mat,) * 6 + (vec,) * 9,
        check_vma=False,
    )
```

```python
import functools

import jax
import jax.numpy as jnp
from jax import lax
from jax.experimental import pallas as pl
from jax.experimental.pallas import tpu as pltpu
from jax.sharding import PartitionSpec as P

D = 768
HEADS = 12
HD = 64
SCALE = 0.125
EPS = 1e-12
ROOT_HALF = 0.7071067811865476
BF = jnp.bfloat16
F32 = jnp.float32
NT = (((1,), (1,)), ((), ()))
NN = (((1,), (0,)), ((), ()))
TN = (((0,), (0,)), ((), ()))


def layer_norm(values, gain_vec, shift_vec):
    average = jnp.mean(values, axis=-1, keepdims=True)
    centred = values - average
    variance = jnp.mean(centred * centred, axis=-1, keepdims=True)
    return centred * lax.rsqrt(variance + EPS) * gain_vec + shift_vec


def gelu_act(values):
    return 0.5 * values * (1.0 + lax.erf(values * ROOT_HALF))


def key_range(docs, first_row, tile, stream_rows):
    last = first_row + tile - 1
    low, high = 0, stream_rows
    for d in range(1, docs.shape[0]):
        low = jnp.where(docs[d] <= first_row, docs[d], low)
    for d in range(docs.shape[0] - 1, 0, -1):
        high = jnp.where(docs[d] > last, docs[d], high)
    first = low // 128 * 128
    count = (high - first + 255) // 256
    return jnp.minimum(first, stream_rows - count * 256), count


def document_lanes(doc_start, first_row, rows, stream_rows):
    far = jnp.full((128 - doc_start.shape[0],), 2**30, jnp.int32)
    starts = jnp.concatenate([doc_start, far])
    ends = jnp.concatenate([doc_start[1:], jnp.full((1,), stream_rows, jnp.int32), far])
    query_pos = first_row + jnp.arange(rows, dtype=jnp.int32)[:, None]
    key_pos = jnp.arange(stream_rows, dtype=jnp.int32)[:, None]
    query_doc = ((query_pos >= starts) & (query_pos < ends)).astype(BF)
    key_doc = jnp.where((key_pos >= starts) & (key_pos < ends), 0.0, -1e30).astype(BF)
    return query_doc, key_doc


def stack_heads(x, extra=None):
    lane = lax.broadcasted_iota(jnp.int32, x.shape, 1)
    zero = jnp.zeros_like(x)
    lo = jnp.where(lane < 64, x, zero)
    hi = jnp.where(lane < 64, zero, x)
    if extra is not None:
        lo = jnp.concatenate([lo, extra], axis=1)
        hi = jnp.concatenate([hi, extra], axis=1)
    return jnp.concatenate([lo, hi], axis=0)

def pick_heads(x, tq):
    return jnp.concatenate([x[:64, :tq], x[64:, tq:]], axis=0)

def two_level(start, count, tk, body, init):
    done, carried = 0, init
    for n in (6, 3, 1):
        if n * 256 > tk:
            continue

        def step(t, c, n=n, done=done):
            at = done + t * n
            return body(pl.multiple_of(at * 256, 256), pl.multiple_of(start + at * 256, 128), n * 256, c)

        trips = (count - done) // n
        carried = lax.fori_loop(0, trips, step, carried)
        done = done + trips * n
    return carried


def fwd_kernel(tq, tk, docs, q_ref, qaug_ref, k_ref, kaug_ref, v_ref, ot_ref, lse_ref, s_scr, acc):
    def part(i, carry):
        rows = pl.ds(pl.multiple_of(i * tq, tq), tq)
        start, count = key_range(docs, lax.axis_index("ctx") * q_ref.shape[0] + i * tq, tq, k_ref.shape[0])
        rhs = stack_heads(q_ref[rows, :], qaug_ref[rows, :])

        def scores(loc, off, size, m):
            lhs = jnp.concatenate([k_ref[pl.ds(off, size), :], kaug_ref[pl.ds(off, size), :]], axis=1)
            s = lax.dot_general(lhs, rhs, NT, preferred_element_type=F32)
            s_scr[pl.ds(loc, size), :] = s
            return jnp.maximum(m, jnp.max(s.reshape(size // 8, 8, 2 * tq), axis=0))

        m8 = two_level(start, count, tk, scores, jnp.full((8, 2 * tq), -3e38, F32))
        m = jnp.max(m8, axis=0, keepdims=True)
        acc[...] = jnp.zeros_like(acc)

        def mix(loc, off, size, l8):
            p = jnp.exp(s_scr[pl.ds(loc, size), :] - m)
            acc[...] += lax.dot_general(v_ref[pl.ds(off, size), :], p.astype(BF), TN, preferred_element_type=F32)
            return l8 + jnp.sum(p.reshape(size // 8, 8, 2 * tq), axis=0)

        l8 = two_level(start, count, tk, mix, jnp.zeros((8, 2 * tq), F32))
        l = jnp.sum(l8, axis=0, keepdims=True)
        ot_ref[:, rows] = pick_heads(acc[...] / l, tq)
        lse = m + jnp.log(l)
        lse_ref[0, :, rows] = jnp.concatenate([lse[:, :tq], lse[:, tq:]], axis=0)
        return carry

    lax.fori_loop(0, q_ref.shape[0] // tq, part, 0)


def attn_fwd(docs, q, qaug, k, kaug, v, *, tq=256, tk=1536):
    T, D = q.shape
    S = k.shape[0]
    pairs = D // 128
    return pl.pallas_call(
        functools.partial(fwd_kernel, tq, tk),
        out_shape=(jax.ShapeDtypeStruct((D, T), F32), jax.ShapeDtypeStruct((pairs, 2, T), F32)),
        grid_spec=pltpu.PrefetchScalarGridSpec(
            num_scalar_prefetch=1, grid=(pairs,),
            in_specs=[pl.BlockSpec((T, 128), lambda h, b: (0, h)),
                      pl.BlockSpec((T, 128), lambda h, b: (0, 0)),
                      pl.BlockSpec((S, 128), lambda h, b: (0, h)),
                      pl.BlockSpec((S, 128), lambda h, b: (0, 0)),
                      pl.BlockSpec((S, 128), lambda h, b: (0, h))],
            out_specs=(pl.BlockSpec((128, T), lambda h, b: (h, 0)),
                       pl.BlockSpec((1, 2, T), lambda h, b: (h, 0, 0))),
            scratch_shapes=[pltpu.VMEM((S, 2 * tq), F32), pltpu.VMEM((128, 2 * tq), F32)]),
        name="attend",
    )(docs, q, qaug, k, kaug, v)


def bwd_kernel(tq, tk, docs, q_ref, qaug_ref, do_ref, lse_ref, ot_ref, k_ref, kaug_ref, v_ref,
               dq_ref, dk_ref, dv_ref, dk_acc, dv_acc, dq_acc, delta_scr):
    n_rows, n_keys = q_ref.shape[0], k_ref.shape[0]
    first_row = lax.axis_index("ctx") * n_rows
    low, high = n_keys, 0
    for i in range(n_rows // tq):
        start, count = key_range(docs, first_row + i * tq, tq, n_keys)
        low, high = jnp.minimum(low, start), jnp.maximum(high, start + count * 256)

    def over_seen(fn):
        def one(t, carry):
            fn(pl.ds(pl.multiple_of(low + t * 128, 128), 128))
            return carry

        lax.fori_loop(0, (high - low) // 128, one, 0)

    def clear(rows):
        dk_acc[rows, :] = jnp.zeros((128, 128), F32)
        dv_acc[rows, :] = jnp.zeros((128, 128), F32)

    over_seen(clear)
    mixed = ot_ref[...] * do_ref[...].astype(F32).T
    deltas = [jnp.sum(mixed[:64], axis=0, keepdims=True), jnp.sum(mixed[64:], axis=0, keepdims=True)]
    delta_scr[...] = jnp.concatenate(deltas, axis=0)

    def part(i, carry):
        part_rows = pl.ds(pl.multiple_of(i * tq, tq), tq)
        start, count = key_range(docs, first_row + i * tq, tq, n_keys)
        q, do = q_ref[part_rows, :], do_ref[part_rows, :]
        qs = stack_heads(q)
        qrhs = stack_heads(q, qaug_ref[part_rows, :])
        dos = stack_heads(do)
        lse = jnp.concatenate([lse_ref[0, 0:1, part_rows], lse_ref[0, 1:2, part_rows]], axis=1)
        delta = jnp.concatenate([delta_scr[0:1, part_rows], delta_scr[1:2, part_rows]], axis=1)
        dq_acc[...] = jnp.zeros_like(dq_acc)

        def step(loc, off, size, carry):
            rows = pl.ds(off, size)
            lhs = jnp.concatenate([k_ref[rows, :], kaug_ref[rows, :]], axis=1)
            x = lax.dot_general(lhs, qrhs, NT, preferred_element_type=F32)
            y = lax.dot_general(v_ref[rows, :], dos, NT, preferred_element_type=F32)
            p = jnp.exp(x - lse)
            ds = (p * (y - delta)).astype(BF)
            pb = p.astype(BF)
            dv_acc[rows, :] += lax.dot_general(pb, dos, NN, preferred_element_type=F32)
            dk_acc[rows, :] += lax.dot_general(ds, qs, NN, preferred_element_type=F32)
            dq_acc[...] += lax.dot_general(k_ref[rows, :], ds, TN, preferred_element_type=F32)
            return carry

        two_level(start, count, tk, step, 0)
        dq_ref[part_rows, :] = (pick_heads(dq_acc[...], tq) * SCALE).T.astype(BF)
        return carry

    lax.fori_loop(0, n_rows // tq, part, 0)
    dk_ref[...] = jnp.zeros_like(dk_ref)
    dv_ref[...] = jnp.zeros_like(dv_ref)

    def give(rows):
        dk_ref[rows, :] = dk_acc[rows, :].astype(BF)
        dv_ref[rows, :] = dv_acc[rows, :].astype(BF)

    over_seen(give)


def attn_bwd(docs, q, qaug, do, lse, ot, k, kaug, v, *, tq=256, tk=1536):
    T, D = q.shape
    S = k.shape[0]
    pairs = D // 128
    return pl.pallas_call(
        functools.partial(bwd_kernel, tq, tk),
        out_shape=(jax.ShapeDtypeStruct((T, D), BF), jax.ShapeDtypeStruct((S, D), BF), jax.ShapeDtypeStruct((S, D), BF)),
        grid_spec=pltpu.PrefetchScalarGridSpec(
            num_scalar_prefetch=1, grid=(pairs,),
            in_specs=[pl.BlockSpec((T, 128), lambda h, b: (0, h)),
                      pl.BlockSpec((T, 128), lambda h, b: (0, 0)),
                      pl.BlockSpec((T, 128), lambda h, b: (0, h)),
                      pl.BlockSpec((1, 2, T), lambda h, b: (h, 0, 0)),
                      pl.BlockSpec((128, T), lambda h, b: (h, 0)),
                      pl.BlockSpec((S, 128), lambda h, b: (0, h)),
                      pl.BlockSpec((S, 128), lambda h, b: (0, 0)),
                      pl.BlockSpec((S, 128), lambda h, b: (0, h))],
            out_specs=(pl.BlockSpec((T, 128), lambda h, b: (0, h)),
                       pl.BlockSpec((S, 128), lambda h, b: (0, h)),
                       pl.BlockSpec((S, 128), lambda h, b: (0, h))),
            scratch_shapes=[pltpu.VMEM((S, 128), F32), pltpu.VMEM((S, 128), F32), pltpu.VMEM((128, 2 * tq), F32),
                            pltpu.VMEM((2, T), F32)]),
        name="attend_back",
    )(docs, q, qaug, do, lse, ot, k, kaug, v)


def middle_kernel(attn_ref, in_ref, cot_ref, vec_ref, out_own, out_far, wu_ref, down_own, down_far,
                  out_ref, sum1_ref, do_ref, grads_ref, up_out, down_out, attn_out,
                  wo, wu, wd, attn_b, first, hat1, scale1, first_b, act, slope, sum2, down_b, up_b, first_b2, first_t,
                  g_up, g_down, g_out, sem_w, sem_d, sem_o):
    rows, wide = in_ref.shape[0], wu.shape[1]
    a, w = lax.axis_index("ctx"), lax.axis_index("wsh")
    y, c = w // 2, lax.rem(w, 2)
    core_peer = (a, y * 2 + (1 - c))
    MESH = pl.DeviceIdType.MESH
    owners = (w, (1 - y) * 2 + c)
    barrier = pltpu.get_barrier_semaphore()
    pl.semaphore_signal(barrier, inc=1, device_id=core_peer, device_id_type=MESH)
    pl.semaphore_wait(barrier, 1)

    def share(j, s, full, ref):
        tall = ref.shape[0]
        there = full.at[pl.ds(pl.multiple_of(owners[s] * tall, 16), tall), :]
        return (
            pltpu.make_async_copy(ref, there, sem_w.at[j, s]),
            pltpu.make_async_remote_copy(
                src_ref=ref, dst_ref=there, send_sem=sem_d.at[0, j, s], recv_sem=sem_d.at[1, j, s],
                device_id=core_peer, device_id_type=MESH),
        )

    shares = [[share(j, s, full, ref) for s, ref in enumerate(pair)]
              for j, (full, pair) in enumerate(((wo, (out_own, out_far)), (wd, (down_own, down_far))))]
    up_load = pltpu.make_async_copy(wu_ref, wu, sem_w.at[2, 0])
    for pair in shares:
        for kept, passed in pair:
            passed.start()
            kept.start()
    up_load.start()

    def arrived(j):
        if j == 1:
            up_load.wait()
        else:
            for kept, passed in shares[j // 2]:
                kept.wait()
                passed.wait_recv()

    grads_ref[...] = jnp.zeros_like(grads_ref)
    attn_b[...] = attn_ref[...].astype(BF)
    out_b, attn_g, attn_s, down_bias, final_g, final_s = [vec_ref[i : i + 1, :] for i in range(2, 8)]
    arrived(0)
    block = 256

    def over_rows(fn):
        def one(i, carry):
            fn(pl.ds(pl.multiple_of(i * block, block), block))
            return carry

        lax.fori_loop(0, rows // block, one, 0)

    def norm(values):
        average = jnp.mean(values, axis=-1, keepdims=True)
        centred = values - average
        scale = lax.rsqrt(jnp.mean(centred * centred, axis=-1, keepdims=True) + EPS)
        return centred * scale, scale

    def norm_back(grad, hat, scale, gain):
        g = grad * gain
        return scale * (g - jnp.mean(g, axis=-1, keepdims=True) - hat * jnp.mean(g * hat, axis=-1, keepdims=True))

    def note(row, values):
        grads_ref[row : row + 1, :] += jnp.sum(values, axis=0, keepdims=True)

    def branch_part(r):
        a = attn_b[:, r].T
        v = lax.dot_general(a, wo[...], NN, preferred_element_type=F32) + out_b + in_ref[r, :].astype(F32)
        hat, scale = norm(v)
        hat1[r, :] = hat
        scale1[r, :] = scale
        f = hat * attn_g + attn_s
        first[r, :] = f
        first_b[r, :] = f.astype(BF)

    over_rows(branch_part)
    arrived(1)
    cols = vec_ref.shape[1]

    def over_wide(fn):
        def one(i, carry):
            fn(pl.ds(pl.multiple_of(i * cols, cols), cols), i)
            return carry

        lax.fori_loop(0, wide // cols, one, 0)

    def up_part(n, i):
        u = lax.dot_general(first_b[...], wu[:, n], NN, preferred_element_type=F32) + vec_ref[pl.ds(8 + i, 1), :]
        half = 0.5 * (1.0 + lax.erf(u * ROOT_HALF))
        act[:, n] = (u * half).astype(BF)
        slope[:, n] = half + u * (0.3989422804014327 * jnp.exp(-0.5 * u * u))

    over_wide(up_part)
    arrived(2)

    def down_part(r):
        v = lax.dot_general(act[r, :], wd[...], NN, preferred_element_type=F32) + down_bias + first[r, :]
        hat, scale = norm(v)
        out_ref[r, :] = (hat * final_g + final_s).astype(BF)
        cot = cot_ref[r, :].astype(F32)
        note(6, cot * hat)
        note(7, cot)
        g = norm_back(cot, hat, scale, final_g)
        sum2[r, :] = g
        rounded = g.astype(BF)
        down_b[r, :] = rounded
        note(5, rounded.astype(F32))

    over_rows(down_part)

    def up_back(n, i):
        g = lax.dot_general(down_b[...], wd[n, :], NT, preferred_element_type=F32) * slope[:, n]
        rounded = g.astype(BF)
        up_b[:, n] = rounded
        grads_ref[pl.ds(8 + i, 1), :] = jnp.sum(rounded.astype(F32), axis=0, keepdims=True)

    over_wide(up_back)

    def first_part(r):
        g = sum2[r, :] + lax.dot_general(up_b[r, :], wu[...], NT, preferred_element_type=F32)
        hat = hat1[r, :]
        note(3, g * hat)
        note(4, g)
        s1 = norm_back(g, hat, scale1[r, :], attn_g)
        sum1_ref[r, :] = s1
        rounded = s1.astype(BF)
        note(2, rounded.astype(F32))
        first_b2[r, :] = rounded

    over_rows(first_part)

    def do_part(r):
        do_ref[r, :] = lax.dot_general(first_b2[r, :], wo[...], NT, preferred_element_type=F32).astype(BF)

    over_rows(do_part)

    def wide_grads(n, i):
        g_down[n, :] = lax.dot_general(act[:, n].T, down_b[...], NN, preferred_element_type=F32).astype(BF)
        pltpu.make_async_copy(g_down.at[n, :], down_out.at[n, :], sem_o.at[0, i]).start()
        g_up[:, n] = lax.dot_general(first_t[...], up_b[:, n], NN, preferred_element_type=F32).astype(BF)
        pltpu.make_async_copy(g_up.at[:, n], up_out.at[:, n], sem_o.at[1, i]).start()

    first_t[...] = first_b[...].T
    over_wide(wide_grads)
    g_out[...] = lax.dot_general(attn_b[...], first_b2[...], NN, preferred_element_type=F32).astype(BF)
    pltpu.make_async_copy(g_out, attn_out, sem_o.at[2, 0]).start()

    def wide_end(n, i):
        pltpu.make_async_copy(g_down.at[n, :], down_out.at[n, :], sem_o.at[0, i]).wait()
        pltpu.make_async_copy(g_up.at[:, n], up_out.at[:, n], sem_o.at[1, i]).wait()

    over_wide(wide_end)
    pltpu.make_async_copy(g_out, attn_out, sem_o.at[2, 0]).wait()
    for pair in shares:
        for _kept, passed in pair:
            passed.wait_send()


def middle(attn_t, inputs, cotangent, vec, out_own, out_far, up_w, down_own, down_far):
    rows = inputs.shape[0]
    wide = up_w.shape[1]
    vm, dma, shape = pltpu.VMEM, pltpu.SemaphoreType.DMA, jax.ShapeDtypeStruct
    any_spec = pl.BlockSpec(memory_space=pltpu.HBM)
    vm_spec = pl.BlockSpec(memory_space=pltpu.VMEM)
    return pl.pallas_call(
        middle_kernel,
        out_shape=(shape((rows, D), BF), shape((rows, D), F32), shape((rows, D), BF), shape((16, D), F32),
                   shape((D, wide), BF), shape((wide, D), BF), shape((D, D), BF)),
        in_specs=[vm_spec] * 4 + [any_spec] * 5,
        out_specs=(vm_spec,) * 4 + (any_spec,) * 3,
        scratch_shapes=[
            vm((D, D), BF), vm((D, wide), BF), vm((wide, D), BF), vm((D, rows), BF), vm((rows, D), F32),
            vm((rows, D), F32), vm((rows, 1), F32), vm((rows, D), BF), vm((rows, wide), BF), vm((rows, wide), F32),
            vm((rows, D), F32), vm((rows, D), BF), vm((rows, wide), BF), vm((rows, D), BF), vm((D, rows), BF),
            vm((D, wide), BF), vm((wide, D), BF), vm((D, D), BF), dma((3, 2)), dma((2, 2, 2)), dma((3, wide // D)),
        ],
        compiler_params=pltpu.CompilerParams(collective_id=3, has_side_effects=True, vmem_limit_bytes=63 * 2**20),
        name="middle",
    )(attn_t, inputs, cotangent, vec, out_own, out_far, up_w, down_own, down_far)


def reach(n_ctx):
    return n_ctx // 2


def finish_kernel(sources, n_parts, *refs):
    parts = refs[:n_parts]
    (vec_ref, dk_ref, dv_ref, tok_ref, dq_ref, w_ref, own_in_ref, mine_tok_ref,
     out_ref, vec_out, wide_out, grad_ref,
     mine, buf_a, buf_h, buf_b, buf_s, buf_c, buf_d, buf_e, gbf,
     sums, heard, line,
     loads, weights, acc, dq, own, bias,
     run_part, from_x, from_z, far_z, last_x,
     sem_l, sem_a, sem_b, sem_c, sem_d, sem_v, sem_x, sem_z, sem_far, sem_load, sem_in) = refs[n_parts:]
    n_ready = len(sources)
    n_chunks = out_ref.shape[0]
    n_ctx, n_wsh = lax.axis_size("ctx"), lax.axis_size("wsh")
    zs = n_ctx // 2
    a, w = lax.axis_index("ctx"), lax.axis_index("wsh")
    z, x = a // 2, lax.rem(a, 2)
    y, c = w // 2, lax.rem(w, 2)
    core_peer = (a, y * 2 + (1 - c))
    y_peer = (a, (1 - y) * 2 + c)
    x_peer = (z * 2 + (1 - x), w)
    low, high = lax.rem(z, 2), z // 2
    pair_peer = ((z + 1 - 2 * low) * 2 + x, w)
    skip_peer = (lax.rem(z + 2, zs) * 2 + x, w)
    up_peer, down_peer = (a + 2, w), (a - 2, w)
    near = reach(n_ctx)
    hops = near // 2
    MESH = pl.DeviceIdType.MESH

    rows = out_ref.shape[1]
    half = out_ref.shape[2] // 2
    piece = rows // zs
    tall = own.shape[0]
    cut = from_x.shape[1]

    def z_peer(d):
        return (lax.rem(z + d, zs) * 2 + x, w)

    barrier = pltpu.get_barrier_semaphore()
    for dev in [core_peer, y_peer, x_peer] + [z_peer(d) for d in range(1, zs)]:
        pl.semaphore_signal(barrier, inc=1, device_id=dev, device_id_type=MESH)
    def send(src, dst, sems, idx, dev):
        return pltpu.make_async_remote_copy(
            src_ref=src, dst_ref=dst, send_sem=sems.at[(0,) + idx], recv_sem=sems.at[(1,) + idx],
            device_id=dev, device_id_type=MESH)

    def wait_in(ref, sems, idx):
        send(ref, ref, sems, idx, core_peer).wait_recv()

    def wait_out(ref, sems, idx):
        send(ref, ref, sems, idx, core_peer).wait_send()

    def distance(i):
        return (hops - i // 4) * (1 - 2 * lax.rem(i // 2, 2))

    def position(i):
        dz = distance(i)
        mine_too = lax.rem(i, 2)
        run = 2 * (z + dz) + (1 - x) * (1 - mine_too) + x * mine_too
        return run, mine_too, (z + dz >= 0) & (z + dz < zs) & (jnp.abs(run - a) <= near)

    n_pos = 4 * hops + 2

    def load(i):
        run, _mine_too, there = position(i)
        return there, [
            pltpu.make_async_copy(src.at[run], loads.at[lax.rem(i, 2), j], sem_load.at[lax.rem(i, 2), j])
            for j, src in enumerate((dk_ref, dv_ref, tok_ref))
        ]

    def load_start(i):
        there, copies = load(i)

        @pl.when(there & (i < n_pos))
        def _():
            for copy in copies:
                copy.start()

    def share(k, owner):
        if k < n_ready:
            p, row0, col0 = sources[k]
            return parts[p].at[owner, pl.ds(row0, rows), pl.ds(col0, 2 * half)]
        return gbf.at[k - n_ready, owner]

    def share_load(k):
        for yy in range(2):
            pltpu.make_async_copy(share(k, yy * 2 + c), mine.at[k % 4, yy], sem_l.at[k]).start()

    def share_send(k):
        for yy in range(2):
            send(share(k, yy * 2 + (1 - c)), buf_a.at[k, yy], sem_a, (k,), core_peer).start()

    load_start(0)
    fetch = [pltpu.make_async_copy(w_ref, weights, sem_in.at[0]), pltpu.make_async_copy(dq_ref, dq, sem_in.at[1]),
             pltpu.make_async_copy(own_in_ref, own, sem_in.at[2])]
    for copy in fetch:
        copy.start()
    for k in range(4):
        share_load(k)
    acc[...] = jnp.zeros_like(acc)
    bias[...] = jnp.zeros_like(bias)
    pl.semaphore_wait(barrier, zs + 2)
    for k in range(n_ready):
        share_send(k)
    fetch[0].wait()

    near_rows, far_rows = pl.ds(0, cut), pl.ds(cut, tall - cut)

    def unit(i):
        run, mine_too, there = position(i)
        at = lax.rem(i, 2)
        load_start(i + 1)

        @pl.when(there)
        def _():
            for copy in load(i)[1]:
                copy.wait()

            def tokens_part(r, carry):
                rs = pl.ds(pl.multiple_of(r * 256, 256), 256)
                g = lax.dot_general(loads[at, 0, rs, :], weights[0], NT, preferred_element_type=F32)
                g = g + lax.dot_general(loads[at, 1, rs, :], weights[1], NT, preferred_element_type=F32)
                run_part[i, rs, :] = g.astype(BF)
                bias[0:8, :] += jnp.sum(loads[at, 1, rs, :].astype(F32).reshape(32, 8, 2 * half), axis=0)
                return carry

            lax.fori_loop(0, tall // 256, tokens_part, 0)

            @pl.when(mine_too == 0)
            def _():
                send(run_part.at[i, near_rows, :], from_x.at[i // 2], sem_x, (i // 2,), x_peer).start()

            @pl.when(i < 4)
            def _():
                far_send(i)

            def weights_part(r, carry):
                fs = pl.ds(pl.multiple_of(r * 256, 256), 256)
                flipped = loads[at, 2, :, fs].T
                for j in range(2):
                    acc[j, fs, :] += lax.dot_general(flipped, loads[at, j], NN, preferred_element_type=F32)
                return carry

            lax.fori_loop(0, 2 * half // 256, weights_part, 0)

    def from_below(i):
        dz = distance(i)
        step = 1 - 2 * lax.rem(i // 2, 2)
        sender, target = z - step, z - step + dz
        side = jnp.abs(2 * dz + (1 - 2 * x) * (1 - lax.rem(i, 2))) <= near
        return (sender >= 0) & (sender < zs) & (target >= 0) & (target < zs) & side

    def toward(i, copy_of):
        step = 1 - 2 * lax.rem(i // 2, 2)

        @pl.when(step == 1)
        def _():
            copy_of(up_peer).start()

        @pl.when(step == -1)
        def _():
            copy_of(down_peer).start()

    def far_send(i):
        toward(i, lambda dev: send(run_part.at[i, far_rows, :], far_z.at[i], sem_far, (i,), dev))

    def far_pass(i):
        _run, _mine_too, there = position(i)

        @pl.when(there)
        def _():
            @pl.when(from_below(i - 4))
            def _():
                wait_in(far_z.at[i - 4], sem_far, (i - 4,))
                run_part[i, far_rows, :] = (
                    run_part[i, far_rows, :].astype(F32) + far_z[i - 4].astype(F32)).astype(BF)

            far_send(i)

    def far_end():
        for col in range(2):
            total = n_pos - 2 + col
            for src in (4 + col, 6 + col):
                @pl.when(from_below(src))
                def _():
                    wait_in(far_z.at[src], sem_far, (src,))
                    run_part[total, far_rows, :] = (
                        run_part[total, far_rows, :].astype(F32) + far_z[src].astype(F32)).astype(BF)
            if col == 0:
                send(run_part.at[total, far_rows, :], last_x, sem_x, (n_pos // 2,), x_peer).start()
        own[far_rows, :] += run_part[n_pos - 1, far_rows, :].astype(F32)

    def near_pass(n):
        dz = distance(2 * n)
        i = 2 * n + 1

        @pl.when((z + dz >= 0) & (z + dz < zs))
        def _():
            @pl.when(jnp.abs(2 * dz + 2 * x - 1) <= near)
            def _():
                wait_in(from_x.at[n], sem_x, (n,))
                run_part[i, near_rows, :] = (
                    run_part[i, near_rows, :].astype(F32) + from_x[n].astype(F32)).astype(BF)

            @pl.when((n >= 2) & from_below(i - 4))
            def _():
                wait_in(from_z.at[n - 2], sem_z, (n - 2,))
                run_part[i, near_rows, :] = (
                    run_part[i, near_rows, :].astype(F32) + from_z[n - 2].astype(F32)).astype(BF)

            toward(i, lambda dev: send(run_part.at[i, near_rows, :], from_z.at[n], sem_z, (n,), dev))

    def near_own():
        n = n_pos // 2 - 1
        wait_in(from_x.at[n], sem_x, (n,))
        own[near_rows, :] += run_part[n_pos - 1, near_rows, :].astype(F32) + from_x[n].astype(F32)

    def near_end():
        for n in (2, 3):
            @pl.when(from_below(2 * n + 1))
            def _():
                wait_in(from_z.at[n], sem_z, (n,))
                own[near_rows, :] += from_z[n].astype(F32)

    def add(p, q):
        return (p.astype(F32) + q.astype(F32)).astype(BF)

    def column(side):
        return pl.ds(pl.multiple_of(side * half, 128), half)

    def band(start, size):
        return pl.ds(pl.multiple_of(start, 16), size)

    def stage_b(k):
        at = lax.rem(k, 4)
        pltpu.make_async_copy(mine.at[at], mine.at[at], sem_l.at[k]).wait()
        wait_in(buf_a.at[k], sem_a, (k,))
        buf_h[k] = add(mine[at, 1 - y], buf_a[k, 1 - y])
        send(buf_h.at[k], buf_b.at[k], sem_b, (k,), y_peer).start()
        buf_a[k, y] = add(mine[at, y], buf_a[k, y])

    def stage_c(k):
        wait_in(buf_b.at[k], sem_b, (k,))
        buf_s[k] = add(buf_a[k, y, :, column(1 - x)], buf_b[k, :, column(1 - x)])
        send(buf_s.at[k], buf_c.at[k], sem_c, (0, k), x_peer).start()

    my_two, other_two = band(low * 2 * piece, 2 * piece), band((1 - low) * 2 * piece, 2 * piece)
    my_one, other_one = band(high * piece, piece), band((1 - high) * piece, piece)
    my_rows = band(low * 2 * piece + high * piece, piece)

    def stage_d(k):
        wait_in(buf_c.at[k], sem_c, (0, k))
        cols = column(x)
        joined = buf_a[k, y, :, cols].astype(F32) + buf_b[k, :, cols].astype(F32) + buf_c[k].astype(F32)
        buf_c[k] = joined.astype(BF)
        send(buf_c.at[k, other_two, :], buf_d.at[k], sem_d, (0, k), pair_peer).start()

    def stage_d2(k):
        wait_in(buf_d.at[k], sem_d, (0, k))
        buf_d[k] = add(buf_d[k], buf_c[k, my_two, :])
        send(buf_d.at[k, other_one, :], buf_e.at[k], sem_d, (1, k), skip_peer).start()

    def stage_e(k):
        wait_in(buf_e.at[k], sem_d, (1, k))
        buf_e[k] = add(buf_e[k], buf_d[k, my_one, :])
        out_ref[k, my_rows, column(x)] = buf_e[k]
        send(buf_e.at[k], out_ref.at[k, my_rows, column(x)], sem_d, (2, k), skip_peer).start()

    def stage_e2(k):
        wait_in(buf_e.at[k], sem_d, (2, k))
        there = out_ref.at[k, my_two, column(x)]
        send(there, there, sem_d, (3, k), pair_peer).start()

    def stage_f(k):
        wait_in(buf_d.at[k], sem_d, (3, k))
        there = out_ref.at[k, :, column(x)]
        send(there, there, sem_c, (1, k), x_peer).start()

    def guarded(fn, k, first, last):
        @pl.when((k >= first) & (k < last))
        def _():
            fn(k)

    def chunk_step(m):
        for lag, stage in enumerate((stage_c, stage_d, stage_d2, stage_e, stage_e2, stage_f)):
            guarded(stage, m - (lag and lag + 1), 0, n_chunks)

    def first_step(t, carry):
        guarded(unit, t, 0, n_pos)
        for j in range(2):
            guarded(stage_b, 2 * t + j, 0, n_ready)
        for k in range(4, n_ready):
            @pl.when(t == (k - 4) // 2)
            def _():
                share_load(k)

        @pl.when(lax.rem(t, 2) == 1)
        def _():
            guarded(near_pass, t // 2 - 1, 0, 4)

        guarded(far_pass, t - 2, 4, 8)

        @pl.when((lax.rem(t, 2) == 0) & (t >= 2))
        def _():
            chunk_step(t // 2 - 1)

        return carry

    lax.fori_loop(0, n_pos, first_step, 0)
    done = n_pos // 2 - 1

    fetch[1].wait()
    fetch[2].wait()
    own_tok = pltpu.make_async_copy(mine_tok_ref, loads.at[0, 2], sem_load.at[0, 2])
    own_tok.start()

    def to_bf(j, target):
        for owner in range(n_wsh):
            gbf[target, owner] = acc[j, owner * rows : (owner + 1) * rows, :].astype(BF)
        share_load(n_ready + target)
        share_send(n_ready + target)

    to_bf(0, 0)
    to_bf(1, 1)
    own_tok.wait()

    def query_part(r, carry):
        fs = pl.ds(pl.multiple_of(r * 256, 256), 256)
        acc[0, fs, :] = lax.dot_general(loads[0, 2, :, fs].T, dq[...], NN, preferred_element_type=F32)
        return carry

    lax.fori_loop(0, 2 * half // 256, query_part, 0)
    to_bf(0, 2)

    def query_tokens(r, carry):
        rs = pl.ds(pl.multiple_of(r * 256, 256), 256)
        own[rs, :] += lax.dot_general(dq[rs, :], weights[2], NT, preferred_element_type=F32)
        bias[8:16, :] += jnp.sum(dq[rs, :].astype(F32).reshape(32, 8, 2 * half), axis=0)
        return carry

    lax.fori_loop(0, tall // 256, query_tokens, 0)

    sums[0] = vec_ref[...]
    sums[0, 0:1, :] = jnp.sum(bias[8:16, :], axis=0, keepdims=True)
    sums[0, 1:2, :] = jnp.sum(bias[0:8, :], axis=0, keepdims=True)
    pair = (core_peer, y_peer, x_peer)

    def vec_send(stage):
        send(sums.at[stage], heard.at[stage], sem_v, (stage,), pair[stage]).start()

    def vec_stage(stage):
        wait_in(heard.at[stage], sem_v, (stage,))
        total = sums[stage] + heard[stage]
        sums[stage + 1] = total
        if stage < 2:
            vec_send(stage + 1)
        else:
            line[z] = total
            for d in range(1, zs):
                send(sums.at[3], line.at[z], sem_v, (3,), z_peer(d)).start()

    def vec_last():
        wait_in(line.at[pl.ds(0, zs - 1)], sem_v, (3,))
        total = line[0]
        for d in range(1, zs):
            total = total + line[d]
        small, wide = total[0:8, 0:rows], total[8:9, :]
        for owner in range(1, n_wsh):
            small = jnp.where(w == owner, total[0:8, owner * rows : (owner + 1) * rows], small)
            wide = jnp.where(w == owner, total[8 + owner : 9 + owner, :], wide)
        vec_out[...] = small
        wide_out[...] = wide

    vec_send(0)

    def second_step(m, carry):
        guarded(stage_b, m - done + n_ready, n_ready, n_chunks)
        chunk_step(m)
        guarded(lambda k: near_own(), m - done, 0, 1)
        for stage in range(3):
            guarded(lambda k: vec_stage(stage), m - done - 1 - stage, 0, 1)
        guarded(lambda k: near_end(), m - done - 3, 0, 1)
        guarded(lambda k: far_end(), m - done - 4, 0, 1)
        guarded(lambda k: vec_last(), m - done - 5, 0, 1)
        return carry

    lax.fori_loop(done, n_chunks + 6, second_step, 0)
    wait_in(last_x, sem_x, (n_pos // 2,))
    own[far_rows, :] += last_x[...].astype(F32)
    grad_ref[...] = own[...].astype(BF)

    def drain(k, carry):
        wait_in(buf_s.at[k], sem_c, (1, k))
        wait_out(buf_a.at[k], sem_a, (k,))
        wait_out(buf_b.at[k], sem_b, (k,))
        wait_out(buf_s.at[k], sem_c, (0, k))
        wait_out(buf_s.at[k], sem_c, (1, k))
        wait_out(buf_d.at[k], sem_d, (0, k))
        wait_out(buf_e.at[k], sem_d, (1, k))
        wait_out(buf_e.at[k], sem_d, (2, k))
        wait_out(buf_d.at[k], sem_d, (3, k))
        return carry

    lax.fori_loop(0, n_chunks, drain, 0)
    for stage in range(3):
        wait_out(heard.at[stage], sem_v, (stage,))
    wait_out(line.at[pl.ds(0, zs - 1)], sem_v, (3,))
    wait_out(last_x, sem_x, (n_pos // 2,))

    def drain_runs(i, carry):
        _run, mine_too, there = position(i)

        @pl.when(there)
        def _():
            wait_out(far_z.at[i], sem_far, (i,))

            @pl.when(mine_too == 1)
            def _():
                wait_out(from_z.at[i // 2], sem_z, (i // 2,))

        return carry

    lax.fori_loop(0, n_pos - 2, drain_runs, 0)

    def drain_x(n, carry):
        _run, _mine_too, there = position(2 * n)

        @pl.when(there)
        def _():
            wait_out(from_x.at[n], sem_x, (n,))

        return carry

    lax.fori_loop(0, n_pos // 2, drain_x, 0)


def widen_kernel(spans, in_ref, *outs):
    for (first, down, across), out in zip(spans, outs):
        for r in range(down):
            for col in range(across):
                out[r, :, col * D : (col + 1) * D] = in_ref[first + r * across + col].astype(F32)


def widen(summed, spans):
    n, rows, _width = summed.shape
    part = rows // 4
    outs = pl.pallas_call(
        functools.partial(widen_kernel, spans),
        grid=(4,),
        out_shape=[jax.ShapeDtypeStruct((down, rows, across * D), F32) for _first, down, across in spans],
        in_specs=[pl.BlockSpec((n, part, D), lambda i: (0, i, 0))],
        out_specs=[pl.BlockSpec((down, part, across * D), lambda i: (0, i, 0)) for _first, down, across in spans],
        name="widen",
    )(summed)
    return [o.reshape(-1, o.shape[2]) for o in outs]


def finish(matrices, vec, grad_k, grad_v, all_tokens, grad_q, kvq_w, own_grad, inputs):
    n_ctx, n_wsh = lax.axis_size("ctx"), lax.axis_size("wsh")
    zs, hops = n_ctx // 2, reach(n_ctx) // 2
    rows = D // n_wsh
    parts, sources, spans = [], [], []
    for p, g in enumerate(matrices):
        down, across = g.shape[0] // D, g.shape[1] // D
        parts.append(g.astype(BF).reshape(n_wsh, down * rows, across * D))
        spans.append((len(sources), down, across))
        sources += [(p, r * rows, col * D) for r in range(down) for col in range(across)]
    n = len(sources) + 3
    spans += [(len(sources) + j, 1, 1) for j in range(3)]
    half, piece, tall = D // 2, rows // zs, inputs.shape[0]
    n_pos, cut = 4 * hops + 2, tall * 5 // 8
    vm, dma, shape = pltpu.VMEM, pltpu.SemaphoreType.DMA, jax.ShapeDtypeStruct
    any_spec = pl.BlockSpec(memory_space=pltpu.HBM)
    vm_spec = pl.BlockSpec(memory_space=pltpu.VMEM)
    summed, small, wide, grad_own = pl.pallas_call(
        functools.partial(finish_kernel, sources, len(parts)),
        out_shape=(shape((n, rows, D), BF), shape((8, rows), F32), shape((1, D), F32), shape((tall, D), BF)),
        in_specs=[any_spec] * len(parts) + [vm_spec] + [any_spec] * 7,
        out_specs=(vm_spec,) * 4,
        scratch_shapes=[
            vm((4, 2, rows, D), BF), vm((n, 2, rows, D), BF), vm((n, rows, D), BF), vm((n, rows, D), BF),
            vm((n, rows, half), BF), vm((n, rows, half), BF), vm((n, 2 * piece, half), BF), vm((n, piece, half), BF),
            vm((3, n_wsh, rows, D), BF),
            vm((4,) + vec.shape, F32), vm((3,) + vec.shape, F32), vm((zs,) + vec.shape, F32),
            vm((2, 3, tall, D), BF), vm((3, D, D), BF), vm((2, D, D), F32), vm((tall, D), BF), vm((tall, D), F32),
            vm((16, D), F32),
            vm((n_pos, tall, D), BF), vm((n_pos // 2, cut, D), BF), vm((4, cut, D), BF),
            vm((n_pos - 2, tall - cut, D), BF), vm((tall - cut, D), BF),
            dma((n,)), dma((2, n)), dma((2, n)), dma((2, 2, n)), dma((2, 4, n)), dma((2, 4)),
            dma((2, n_pos // 2 + 1)), dma((2, 4)), dma((2, n_pos - 2)), dma((2, 3)), dma((3,)),
        ],
        compiler_params=pltpu.CompilerParams(collective_id=2, has_side_effects=True, vmem_limit_bytes=63 * 2**20),
        name="finish",
    )(*parts, vec, grad_k, grad_v, all_tokens, grad_q, kvq_w, own_grad, inputs)
    return widen(summed, spans), small, wide, grad_own


def gather_kernel(cut, tok_ref, docs_ref, wk_ref, wv_ref, wq_ref, wu_ref, vec_ref,
                  tok_out, k_out, v_out, q_out, w_out, vec_out, wu_out, query_doc, key_doc,
                  tok, kbuf, vbuf, qbuf, wbuf, vecs, wu, kdoc,
                  sem_in, sem_out, sem_w, sem_l, sem_o):
    n_ctx = lax.axis_size("ctx")
    zs = n_ctx // 2
    a, w = lax.axis_index("ctx"), lax.axis_index("wsh")
    z, x = a // 2, lax.rem(a, 2)
    y, c = w // 2, lax.rem(w, 2)
    core_peer = (a, y * 2 + (1 - c))
    y_peer = (a, (1 - y) * 2 + c)
    x_peer = (z * 2 + (1 - x), w)
    up, down = (a + 2, w), (a - 2, w)
    near = reach(n_ctx)
    MESH = pl.DeviceIdType.MESH
    n_slices = sem_in.shape[1]
    tall = tok.shape[1] // n_slices
    own = wk_ref.shape[0]
    far = 4 * (near // 2 + 1)

    barrier = pltpu.get_barrier_semaphore()
    around = [(lax.rem(z + d, zs) * 2 + x, w) for d in (1, zs - 1)]
    for dev in [core_peer, y_peer, x_peer] + around:
        pl.semaphore_signal(barrier, inc=1, device_id=dev, device_id_type=MESH)
    pl.semaphore_wait(barrier, 5)

    def relative(u):
        dz = (u // 4) * (1 - 2 * lax.rem(u, 2))
        other = lax.rem(u // 2, 2)
        run = 2 * (z + dz) + (x + other - 2 * x * other)
        there = (z + dz >= 0) & (z + dz < zs) & (jnp.abs(run - a) <= near) & ((u >= 4) | (lax.rem(u, 2) == 0))
        return run, dz, other, there

    def rows(s):
        return pl.ds(pl.multiple_of(s * tall, tall), tall)

    def remote(src, dst, send_sem, recv_sem, dev):
        return pltpu.make_async_remote_copy(
            src_ref=src, dst_ref=dst, send_sem=send_sem, recv_sem=recv_sem, device_id=dev, device_id_type=MESH)

    def routes(u, s):
        run, dz, other, there = relative(u)
        z_first = s < cut
        to_x = there & (z_first | (dz == 0)) & (other == 0) & (jnp.abs(run - x_peer[0]) <= near)
        along = there & ((other == 0) | jnp.logical_not(z_first))
        to_up = along & (dz <= 0) & (z + 1 < zs) & (jnp.abs(run - (a + 2)) <= near)
        to_down = along & (dz >= 0) & (z > 0) & (jnp.abs(run - (a - 2)) <= near)
        return run, ((0, x_peer, to_x), (1, up, to_up), (2, down, to_down))

    def pass_on(u, s):
        run, where = routes(u, s)
        for d, dev, ok in where:
            @pl.when(ok)
            def _():
                source = tok_ref if isinstance(u, int) and u == 0 else tok.at[run]
                remote(source.at[rows(s), :], tok.at[run, rows(s), :], sem_out.at[d, u, s], sem_in.at[run, s], dev).start()

    def await_slice(u, s):
        run, _dz, _other, there = relative(u)

        @pl.when(there)
        def _():
            remote(tok.at[run, rows(s), :], tok.at[run, rows(s), :], sem_out.at[0, 0, 0], sem_in.at[run, s], x_peer).wait_recv()

    def start_own(s, carry):
        pass_on(0, s)
        return carry

    def weight_rows(owner):
        return pl.ds(pl.multiple_of(owner * own, 16), own)

    def shard(m, owner):
        if m == 3:
            return vecs.at[owner]
        return (wbuf.at[0], wbuf.at[1], wbuf.at[2], None, wu)[m].at[weight_rows(owner), :]

    vecs[w, 0 : vec_ref.shape[0], :] = vec_ref[...]
    shards = (wk_ref, wv_ref, wq_ref, vecs.at[w], wu_ref)
    for m in (3, 0, 1, 2, 4):
        remote(shards[m], shard(m, w), sem_w.at[0, 1, m], sem_w.at[1, 1, m], y_peer).start()
        remote(shards[m], shard(m, w), sem_w.at[0, 0, m], sem_w.at[1, 0, m], core_peer).start()
        if m != 3:
            pltpu.make_async_copy(shards[m], shard(m, w), sem_w.at[0, 3, m]).start()
    lax.fori_loop(0, n_slices, start_own, 0)
    pltpu.make_async_copy(tok_ref, tok.at[a], sem_l.at[4]).start()

    for j in range(n_ctx):
        @pl.when(jnp.abs(j - a) > near)
        def _():
            tok[j] = jnp.zeros_like(tok[j])

    n_rows = tok.shape[1]

    def is_own_lane(first):
        pos = first + lax.broadcasted_iota(jnp.int32, (n_rows, 128), 0)
        doc = jnp.full((n_rows, 128), -1, jnp.int32)
        for d in range(docs_ref.shape[1]):
            doc = doc + jnp.where(pos >= docs_ref[0, d], 1, 0)
        return lax.broadcasted_iota(jnp.int32, (n_rows, 128), 1) == doc

    def key_lanes(j, carry):
        kdoc[pl.ds(pl.multiple_of(j * n_rows, n_rows), n_rows), :] = jnp.where(
            is_own_lane(j * n_rows), 0.0, -1e30).astype(BF)
        return carry

    lax.fori_loop(0, n_ctx, key_lanes, 0)
    pltpu.make_async_copy(kdoc, key_doc, sem_l.at[3]).start()
    query_doc[...] = jnp.where(is_own_lane(a * n_rows), 1.0, 0.0).astype(BF)

    def weight_arrival(m, kind):
        part = shard(m, w)
        return remote(part, part, sem_w.at[0, kind, m], sem_w.at[1, kind, m], core_peer)

    across = (1 - y) * 2 + c

    def weight_forward(m):
        weight_arrival(m, 1).wait_recv()
        remote(shard(m, across), shard(m, across), sem_w.at[0, 2, m], sem_w.at[1, 2, m], core_peer).start()

    def weight_end(m):
        weight_arrival(m, 0).wait_recv()
        weight_arrival(m, 2).wait_recv()
        if m != 3:
            pltpu.make_async_copy(shard(m, w), shard(m, w), sem_w.at[0, 3, m]).wait()

    def relay(first, last):
        def one(i, carry):
            s = i // (last - first)
            u = first + lax.rem(i, last - first)
            await_slice(u, s)
            pass_on(u, s)
            return carry

        lax.fori_loop(0, n_slices * (last - first), one, 0)

    relay(2, 6)
    weight_forward(3)
    weight_forward(0)
    weight_forward(1)
    weight_end(3)
    vec_out[0:8, :] = jnp.concatenate([vecs[o, 0:8, :] for o in range(4)], axis=1)
    for o in range(4):
        vec_out[8 + o : 9 + o, :] = jnp.concatenate([vecs[o, 8 + i : 9 + i, :] for i in range(4)], axis=1)
    pltpu.make_async_copy(tok_ref, tok.at[a], sem_l.at[4]).wait()
    weight_end(0)
    weight_end(1)

    step_rows = 256
    steps = tok.shape[1] // step_rows

    def query_part(i, carry):
        r = pl.ds(pl.multiple_of(i * step_rows, step_rows), step_rows)
        q = (jnp.dot(tok[a, r, :], wbuf[2], preferred_element_type=F32) + vec_out[0:1, :]).astype(BF)
        qbuf[r, :] = q * jnp.asarray(SCALE, BF)
        return carry

    def project(u, carry):
        run, _dz, _other, there = relative(u)

        @pl.when(u == 6)
        def _():
            weight_forward(2)
            weight_end(2)
            lax.fori_loop(0, steps, query_part, 0)
            pltpu.make_async_copy(qbuf, q_out, sem_l.at[5]).start()
            relay(6, 10)

        @pl.when(there)
        def _():
            @pl.when(u >= 10)
            def _():
                def one(s, carry):
                    await_slice(u, s)
                    return carry

                lax.fori_loop(0, n_slices, one, 0)

            def part(i, carry):
                r = pl.ds(pl.multiple_of(i * step_rows, step_rows), step_rows)
                t = tok[run, r, :]
                kbuf[run, r, :] = jnp.dot(t, wbuf[0], preferred_element_type=F32).astype(BF)
                vbuf[run, r, :] = (jnp.dot(t, wbuf[1], preferred_element_type=F32) + vec_out[1:2, :]).astype(BF)
                return carry

            lax.fori_loop(0, steps, part, 0)
            for i, (src, dst) in enumerate(((kbuf, k_out), (vbuf, v_out), (tok, tok_out))):
                pltpu.make_async_copy(src.at[run], dst.at[run], sem_o.at[i, run]).start()

        return carry

    for j in range(n_ctx):
        @pl.when(jnp.abs(j - a) > near)
        def _():
            kbuf[j] = jnp.zeros_like(kbuf[j])
            vbuf[j] = jnp.zeros_like(vbuf[j])
            for i, (src, dst) in enumerate(((kbuf, k_out), (vbuf, v_out), (tok, tok_out))):
                pltpu.make_async_copy(src.at[j], dst.at[j], sem_o.at[i, j]).start()

    lax.fori_loop(0, far, project, 0)

    pltpu.make_async_copy(wbuf, w_out, sem_l.at[6]).start()

    weight_forward(4)
    weight_end(4)
    pltpu.make_async_copy(wu, wu_out, sem_l.at[1]).start()
    for m in range(5):
        for kind in range(3):
            weight_arrival(m, kind).wait_send()

    def drain(i, carry):
        s = i // far
        u = lax.rem(i, far)
        run, where = routes(u, s)
        for d, dev, ok in where:
            @pl.when(ok & (u < 10))
            def _():
                remote(tok.at[run, rows(s), :], tok.at[run, rows(s), :], sem_out.at[d, u, s], sem_in.at[run, s], dev).wait_send()
        return carry

    lax.fori_loop(0, n_slices * far, drain, 0)
    for j in range(n_ctx):
        for i, (src, dst) in enumerate(((kbuf, k_out), (vbuf, v_out), (tok, tok_out))):
            pltpu.make_async_copy(src.at[j], dst.at[j], sem_o.at[i, j]).wait()
    pltpu.make_async_copy(qbuf, q_out, sem_l.at[5]).wait()
    pltpu.make_async_copy(wbuf, w_out, sem_l.at[6]).wait()
    pltpu.make_async_copy(wu, wu_out, sem_l.at[1]).wait()
    pltpu.make_async_copy(kdoc, key_doc, sem_l.at[3]).wait()


def gather_project(inputs, doc_starts, vectors, key_weight, value_weight, query_weight, up_weight):
    n_ctx, n_wsh = lax.axis_size("ctx"), lax.axis_size("wsh")
    tall = inputs.shape[0]
    n_slices = 8
    far = 4 * (reach(n_ctx) // 2 + 1)
    vm, dma = pltpu.VMEM, pltpu.SemaphoreType.DMA
    any_spec = pl.BlockSpec(memory_space=pltpu.HBM)
    vm_spec = pl.BlockSpec(memory_space=pltpu.VMEM)
    runs = (n_ctx, tall, D)
    shape = jax.ShapeDtypeStruct
    return pl.pallas_call(
        functools.partial(gather_kernel, 5),
        out_shape=(shape(runs, BF), shape(runs, BF), shape(runs, BF), shape((tall, D), BF), shape((3, D, D), BF),
                   shape((16, D), F32), shape((D, up_weight.shape[1]), BF), shape((tall, 128), BF),
                   shape((n_ctx * tall, 128), BF)),
        in_specs=[any_spec, pl.BlockSpec(memory_space=pltpu.SMEM)] + [any_spec] * 4 + [vm_spec],
        out_specs=(any_spec,) * 5 + (vm_spec,) + (any_spec,) + (vm_spec, any_spec),
        scratch_shapes=[
            vm(runs, BF), vm(runs, BF), vm(runs, BF), vm((tall, D), BF), vm((3, D, D), BF), vm((n_wsh, 16, D // n_wsh), F32),
            vm((D, up_weight.shape[1]), BF), vm((n_ctx * tall, 128), BF),
            dma((n_ctx, n_slices)), dma((3, far, n_slices)), dma((2, 4, 5)), dma((7,)), dma((3, n_ctx)),
        ],
        compiler_params=pltpu.CompilerParams(collective_id=1, has_side_effects=True, vmem_limit_bytes=63 * 2**20),
        name="gather_project",
    )(inputs, doc_starts, key_weight, value_weight, query_weight, up_weight, vectors)


def local(
    tokens,
    cotangent,
    doc_starts,
    query_weight,
    key_weight,
    value_weight,
    out_weight,
    up_weight,
    down_weight,
    query_bias,
    value_bias,
    out_bias,
    attn_gain,
    attn_shift,
    up_bias,
    down_bias,
    final_gain,
    final_shift,
):
    inputs = tokens[0]
    doc_start = doc_starts[0]
    tok_rows = inputs.shape[0]
    stream_rows = tok_rows * lax.axis_size("ctx")
    tile = min(tok_rows, 256)
    n_ctx, n_wsh = lax.axis_size("ctx"), lax.axis_size("wsh")
    own = D // n_wsh

    def gather(x):
        return lax.all_gather(x, "wsh", axis=0, tiled=True)

    fast = n_wsh == 4 and n_ctx == 8 and own % (n_ctx // 2 * 16) == 0 and tok_rows % 512 == 0
    if fast:
        small = (query_bias, value_bias, out_bias, attn_gain, attn_shift, down_bias, final_gain, final_shift)
        vectors, place = jnp.zeros(((8 + n_wsh) * own,), F32), 0
        for v in small + (up_bias,):
            ends = (place, vectors.shape[0] - place - v.shape[0], 0)
            vectors = vectors + lax.pad(v.astype(F32), jnp.zeros((), F32), (ends,))
            place += v.shape[0]
        vectors = vectors.reshape(8 + n_wsh, own)
        all_tokens, keys, values, queries, kvq_w, vec, up_w, query_doc, key_doc = gather_project(
            inputs, doc_starts, vectors, key_weight, value_weight, query_weight, up_weight
        )
        out_own, down_own, _unused = lax.optimization_barrier((out_weight, down_weight, vec))
        across = [(i, i ^ 2) for i in range(n_wsh)]
        out_far = lax.ppermute(out_own, "wsh", across)
        down_far = lax.ppermute(down_own, "wsh", across)
        all_tokens, keys, values = [r.reshape(stream_rows, D) for r in (all_tokens, keys, values)]
    else:
        first_row = lax.axis_index("ctx") * tok_rows
        query_doc, key_doc = document_lanes(doc_start, first_row, tok_rows, stream_rows)
        small = jnp.stack(
            [query_bias, value_bias, out_bias, attn_gain, attn_shift, down_bias, final_gain, final_shift]
        )
        all_tokens = lax.all_gather(inputs, "ctx", axis=0, tiled=True)
        query_w, key_w, value_w = gather(query_weight), gather(key_weight), gather(value_weight)
        small = gather(small.T).astype(F32)
        query_b, value_b, out_b, attn_g, attn_s, down_b, final_g, final_s = [small[:, i] for i in range(8)]
        up_b = gather(up_bias).astype(F32)
        queries = jnp.dot(inputs, query_w, preferred_element_type=F32) + query_b
        queries = queries.astype(BF) * jnp.asarray(SCALE, BF)
        keys = jnp.dot(all_tokens, key_w, preferred_element_type=F32).astype(BF)
        values = (jnp.dot(all_tokens, value_w, preferred_element_type=F32) + value_b).astype(BF)
    mixed_t, log_rows = attn_fwd(doc_start, queries, query_doc, keys, key_doc, values, tq=tile)
    if fast:
        layer_out, grad_sum1, grad_attn, vec_grads, grad_up_w, grad_down_w, grad_out_w = middle(
            mixed_t, inputs, cotangent[0], vec, out_own, out_far, up_w, down_own, down_far
        )
        grad_q, grad_k, grad_v = attn_bwd(
            doc_start, queries, query_doc, grad_attn, log_rows, mixed_t, keys, key_doc, values, tq=tile
        )
        mats, small, wide, grad_inputs = finish(
            (grad_up_w, grad_out_w, grad_down_w), vec_grads, grad_k.reshape(n_ctx, tok_rows, D),
            grad_v.reshape(n_ctx, tok_rows, D), all_tokens.reshape(n_ctx, tok_rows, D), grad_q, kvq_w, grad_sum1, inputs,
        )
        up_sum, out_sum, down_sum, key_sum, value_sum, query_sum = mats
        return (
            layer_out.reshape(1, tok_rows, D), grad_inputs.reshape(1, tok_rows, D), query_sum, key_sum, value_sum,
            out_sum, up_sum, down_sum, small[0], small[1], small[2], small[3], small[4], wide[0],
            small[5], small[6], small[7],
        )

    out_w = gather(out_weight)
    up_w = gather(up_weight)
    down_w = gather(down_weight)
    attn_t = mixed_t.astype(BF)
    inputs_f = inputs.astype(F32)
    branch = lax.dot_general(attn_t, out_w, TN, preferred_element_type=F32) + out_b
    first_norm, first_pull = jax.vjp(layer_norm, inputs_f + branch, attn_g, attn_s)
    first_b = first_norm.astype(BF)
    up_f = jnp.dot(first_b, up_w, preferred_element_type=F32) + up_b
    act_f, act_pull = jax.vjp(gelu_act, up_f)
    act_b = act_f.astype(BF)
    down_f = jnp.dot(act_b, down_w, preferred_element_type=F32) + down_b
    final_f, final_pull = jax.vjp(layer_norm, first_norm + down_f, final_g, final_s)
    layer_out = final_f.astype(BF)

    grad_sum2, grad_final_g, grad_final_s = final_pull(cotangent[0].astype(F32))
    grad_down = grad_sum2.astype(BF)
    grad_down_w = jnp.einsum("tf,td->fd", act_b, grad_down, preferred_element_type=F32)
    grad_down_b = jnp.sum(grad_down.astype(F32), axis=0)
    grad_act = jnp.einsum("td,fd->tf", grad_down, down_w, preferred_element_type=F32)
    (grad_up_f,) = act_pull(grad_act)
    grad_up = grad_up_f.astype(BF)
    grad_up_w = jnp.einsum("td,tf->df", first_b, grad_up, preferred_element_type=F32)
    grad_up_b = jnp.sum(grad_up.astype(F32), axis=0)
    grad_first = grad_sum2 + jnp.einsum("tf,df->td", grad_up, up_w, preferred_element_type=F32)
    grad_sum1, grad_attn_g, grad_attn_s = first_pull(grad_first)
    grad_branch = grad_sum1.astype(BF)
    grad_out_w = jnp.dot(attn_t, grad_branch, preferred_element_type=F32)
    grad_out_b = jnp.sum(grad_branch.astype(F32), axis=0)
    grad_attn = jnp.einsum("te,de->td", grad_branch, out_w, preferred_element_type=F32).astype(BF)
    grad_q, grad_k, grad_v = attn_bwd(
        doc_start, queries, query_doc, grad_attn, log_rows, mixed_t, keys, key_doc, values, tq=tile
    )
    def total(g):
        part = lax.psum_scatter(g.astype(BF), "wsh", scatter_dimension=0, tiled=True)
        return lax.psum(part, "ctx").astype(F32)

    grad_all = jnp.einsum("te,de->td", grad_k, key_w, preferred_element_type=F32)
    grad_all = grad_all + jnp.einsum("te,de->td", grad_v, value_w, preferred_element_type=F32)
    grad_own = lax.psum_scatter(grad_all.astype(BF), "ctx", scatter_dimension=0, tiled=True)
    grad_query_w = jnp.einsum("td,te->de", inputs, grad_q, preferred_element_type=F32)
    grad_key_w = jnp.einsum("td,te->de", all_tokens, grad_k, preferred_element_type=F32)
    grad_value_w = jnp.einsum("td,te->de", all_tokens, grad_v, preferred_element_type=F32)
    grad_query_b = jnp.sum(grad_q.astype(F32), axis=0)
    grad_value_b = jnp.sum(grad_v.astype(F32), axis=0)
    grad_inputs = grad_sum1 + jnp.einsum("te,de->td", grad_q, query_w, preferred_element_type=F32)
    grad_inputs = grad_inputs + grad_own.astype(F32)
    sums = [
        total(g)
        for g in (
            grad_query_w, grad_key_w, grad_value_w, grad_out_w, grad_up_w, grad_down_w,
            grad_query_b, grad_value_b, grad_out_b, grad_attn_g, grad_attn_s, grad_up_b,
            grad_down_b, grad_final_g, grad_final_s,
        )
    ]
    return (
        layer_out.reshape(1, tok_rows, D),
        grad_inputs.astype(BF).reshape(1, tok_rows, D),
        *sums,
    )


def solution(mesh):
    rows, mat, vec = P("wsh", "ctx", None), P("wsh", None), P("wsh")
    return jax.shard_map(
        local,
        mesh=mesh,
        in_specs=(rows, rows, mat) + (mat,) * 6 + (vec,) * 9,
        out_specs=(rows, rows) + (mat,) * 6 + (vec,) * 9,
        check_vma=False,
    )
```

```python
import functools

import jax
import jax.numpy as jnp
from jax import lax
from jax.experimental import pallas as pl
from jax.experimental.pallas import tpu as pltpu
from jax.sharding import PartitionSpec as P

D = 768
HEADS = 12
HD = 64
SCALE = 0.125
EPS = 1e-12
ROOT_HALF = 0.7071067811865476
BF = jnp.bfloat16
F32 = jnp.float32
NT = (((1,), (1,)), ((), ()))
NN = (((1,), (0,)), ((), ()))
TN = (((0,), (0,)), ((), ()))


def layer_norm(values, gain_vec, shift_vec):
    average = jnp.mean(values, axis=-1, keepdims=True)
    centred = values - average
    variance = jnp.mean(centred * centred, axis=-1, keepdims=True)
    return centred * lax.rsqrt(variance + EPS) * gain_vec + shift_vec


def gelu_act(values):
    return 0.5 * values * (1.0 + lax.erf(values * ROOT_HALF))


def key_range(docs, first_row, tile, stream_rows):
    last = first_row + tile - 1
    low, high = 0, stream_rows
    for d in range(1, docs.shape[0]):
        low = jnp.where(docs[d] <= first_row, docs[d], low)
    for d in range(docs.shape[0] - 1, 0, -1):
        high = jnp.where(docs[d] > last, docs[d], high)
    first = low // 128 * 128
    count = (high - first + 255) // 256
    return jnp.minimum(first, stream_rows - count * 256), count


def document_lanes(doc_start, first_row, rows, stream_rows):
    far = jnp.full((128 - doc_start.shape[0],), 2**30, jnp.int32)
    starts = jnp.concatenate([doc_start, far])
    ends = jnp.concatenate([doc_start[1:], jnp.full((1,), stream_rows, jnp.int32), far])
    query_pos = first_row + jnp.arange(rows, dtype=jnp.int32)[:, None]
    key_pos = jnp.arange(stream_rows, dtype=jnp.int32)[:, None]
    query_doc = ((query_pos >= starts) & (query_pos < ends)).astype(BF)
    key_doc = jnp.where((key_pos >= starts) & (key_pos < ends), 0.0, -1e30).astype(BF)
    return query_doc, key_doc


def stack_heads(x, extra=None):
    lane = lax.broadcasted_iota(jnp.int32, x.shape, 1)
    zero = jnp.zeros_like(x)
    lo = jnp.where(lane < 64, x, zero)
    hi = jnp.where(lane < 64, zero, x)
    if extra is not None:
        lo = jnp.concatenate([lo, extra], axis=1)
        hi = jnp.concatenate([hi, extra], axis=1)
    return jnp.concatenate([lo, hi], axis=0)

def pick_heads(x, tq):
    return jnp.concatenate([x[:64, :tq], x[64:, tq:]], axis=0)

def two_level(start, count, tk, body, init):
    done, carried = 0, init
    for n in (6, 3, 1):
        if n * 256 > tk:
            continue

        def step(t, c, n=n, done=done):
            at = done + t * n
            return body(pl.multiple_of(at * 256, 256), pl.multiple_of(start + at * 256, 128), n * 256, c)

        trips = (count - done) // n
        carried = lax.fori_loop(0, trips, step, carried)
        done = done + trips * n
    return carried


def fwd_kernel(tq, tk, docs, q_ref, qaug_ref, k_ref, kaug_ref, v_ref, ot_ref, lse_ref, s_scr, acc):
    def part(i, carry):
        rows = pl.ds(pl.multiple_of(i * tq, tq), tq)
        start, count = key_range(docs, lax.axis_index("ctx") * q_ref.shape[0] + i * tq, tq, k_ref.shape[0])
        rhs = stack_heads(q_ref[rows, :], qaug_ref[rows, :])

        def scores(loc, off, size, m):
            lhs = jnp.concatenate([k_ref[pl.ds(off, size), :], kaug_ref[pl.ds(off, size), :]], axis=1)
            s = lax.dot_general(lhs, rhs, NT, preferred_element_type=F32)
            s_scr[pl.ds(loc, size), :] = s
            return jnp.maximum(m, jnp.max(s.reshape(size // 8, 8, 2 * tq), axis=0))

        m8 = two_level(start, count, tk, scores, jnp.full((8, 2 * tq), -3e38, F32))
        m = jnp.max(m8, axis=0, keepdims=True)
        acc[...] = jnp.zeros_like(acc)

        def mix(loc, off, size, l8):
            p = jnp.exp(s_scr[pl.ds(loc, size), :] - m)
            acc[...] += lax.dot_general(v_ref[pl.ds(off, size), :], p.astype(BF), TN, preferred_element_type=F32)
            return l8 + jnp.sum(p.reshape(size // 8, 8, 2 * tq), axis=0)

        l8 = two_level(start, count, tk, mix, jnp.zeros((8, 2 * tq), F32))
        l = jnp.sum(l8, axis=0, keepdims=True)
        ot_ref[:, rows] = pick_heads(acc[...] / l, tq)
        lse = m + jnp.log(l)
        lse_ref[0, :, rows] = jnp.concatenate([lse[:, :tq], lse[:, tq:]], axis=0)
        return carry

    lax.fori_loop(0, q_ref.shape[0] // tq, part, 0)


def attn_fwd(docs, q, qaug, k, kaug, v, *, tq=256, tk=1536):
    T, D = q.shape
    S = k.shape[0]
    pairs = D // 128
    return pl.pallas_call(
        functools.partial(fwd_kernel, tq, tk),
        out_shape=(jax.ShapeDtypeStruct((D, T), F32), jax.ShapeDtypeStruct((pairs, 2, T), F32)),
        grid_spec=pltpu.PrefetchScalarGridSpec(
            num_scalar_prefetch=1, grid=(pairs,),
            in_specs=[pl.BlockSpec((T, 128), lambda h, b: (0, h)),
                      pl.BlockSpec((T, 128), lambda h, b: (0, 0)),
                      pl.BlockSpec((S, 128), lambda h, b: (0, h)),
                      pl.BlockSpec((S, 128), lambda h, b: (0, 0)),
                      pl.BlockSpec((S, 128), lambda h, b: (0, h))],
            out_specs=(pl.BlockSpec((128, T), lambda h, b: (h, 0)),
                       pl.BlockSpec((1, 2, T), lambda h, b: (h, 0, 0))),
            scratch_shapes=[pltpu.VMEM((S, 2 * tq), F32), pltpu.VMEM((128, 2 * tq), F32)]),
        name="attend",
    )(docs, q, qaug, k, kaug, v)


def bwd_kernel(tq, tk, docs, q_ref, qaug_ref, do_ref, lse_ref, ot_ref, k_ref, kaug_ref, v_ref,
               dq_ref, dk_ref, dv_ref, dk_acc, dv_acc, dq_acc, delta_scr):
    n_rows, n_keys = q_ref.shape[0], k_ref.shape[0]
    first_row = lax.axis_index("ctx") * n_rows
    low, high = n_keys, 0
    for i in range(n_rows // tq):
        start, count = key_range(docs, first_row + i * tq, tq, n_keys)
        low, high = jnp.minimum(low, start), jnp.maximum(high, start + count * 256)

    def over_seen(fn):
        def one(t, carry):
            fn(pl.ds(pl.multiple_of(low + t * 128, 128), 128))
            return carry

        lax.fori_loop(0, (high - low) // 128, one, 0)

    def clear(rows):
        dk_acc[rows, :] = jnp.zeros((128, 128), F32)
        dv_acc[rows, :] = jnp.zeros((128, 128), F32)

    over_seen(clear)
    mixed = ot_ref[...] * do_ref[...].astype(F32).T
    deltas = [jnp.sum(mixed[:64], axis=0, keepdims=True), jnp.sum(mixed[64:], axis=0, keepdims=True)]
    delta_scr[...] = jnp.concatenate(deltas, axis=0)

    def part(i, carry):
        part_rows = pl.ds(pl.multiple_of(i * tq, tq), tq)
        start, count = key_range(docs, first_row + i * tq, tq, n_keys)
        q, do = q_ref[part_rows, :], do_ref[part_rows, :]
        qs = stack_heads(q)
        qrhs = stack_heads(q, qaug_ref[part_rows, :])
        dos = stack_heads(do)
        lse = jnp.concatenate([lse_ref[0, 0:1, part_rows], lse_ref[0, 1:2, part_rows]], axis=1)
        delta = jnp.concatenate([delta_scr[0:1, part_rows], delta_scr[1:2, part_rows]], axis=1)
        dq_acc[...] = jnp.zeros_like(dq_acc)

        def step(loc, off, size, carry):
            rows = pl.ds(off, size)
            lhs = jnp.concatenate([k_ref[rows, :], kaug_ref[rows, :]], axis=1)
            x = lax.dot_general(lhs, qrhs, NT, preferred_element_type=F32)
            y = lax.dot_general(v_ref[rows, :], dos, NT, preferred_element_type=F32)
            p = jnp.exp(x - lse)
            ds = (p * (y - delta)).astype(BF)
            pb = p.astype(BF)
            dv_acc[rows, :] += lax.dot_general(pb, dos, NN, preferred_element_type=F32)
            dk_acc[rows, :] += lax.dot_general(ds, qs, NN, preferred_element_type=F32)
            dq_acc[...] += lax.dot_general(k_ref[rows, :], ds, TN, preferred_element_type=F32)
            return carry

        two_level(start, count, tk, step, 0)
        dq_ref[part_rows, :] = (pick_heads(dq_acc[...], tq) * SCALE).T.astype(BF)
        return carry

    lax.fori_loop(0, n_rows // tq, part, 0)
    dk_ref[...] = jnp.zeros_like(dk_ref)
    dv_ref[...] = jnp.zeros_like(dv_ref)

    def give(rows):
        dk_ref[rows, :] = dk_acc[rows, :].astype(BF)
        dv_ref[rows, :] = dv_acc[rows, :].astype(BF)

    over_seen(give)


def attn_bwd(docs, q, qaug, do, lse, ot, k, kaug, v, *, tq=256, tk=1536):
    T, D = q.shape
    S = k.shape[0]
    pairs = D // 128
    return pl.pallas_call(
        functools.partial(bwd_kernel, tq, tk),
        out_shape=(jax.ShapeDtypeStruct((T, D), BF), jax.ShapeDtypeStruct((S, D), BF), jax.ShapeDtypeStruct((S, D), BF)),
        grid_spec=pltpu.PrefetchScalarGridSpec(
            num_scalar_prefetch=1, grid=(pairs,),
            in_specs=[pl.BlockSpec((T, 128), lambda h, b: (0, h)),
                      pl.BlockSpec((T, 128), lambda h, b: (0, 0)),
                      pl.BlockSpec((T, 128), lambda h, b: (0, h)),
                      pl.BlockSpec((1, 2, T), lambda h, b: (h, 0, 0)),
                      pl.BlockSpec((128, T), lambda h, b: (h, 0)),
                      pl.BlockSpec((S, 128), lambda h, b: (0, h)),
                      pl.BlockSpec((S, 128), lambda h, b: (0, 0)),
                      pl.BlockSpec((S, 128), lambda h, b: (0, h))],
            out_specs=(pl.BlockSpec((T, 128), lambda h, b: (0, h)),
                       pl.BlockSpec((S, 128), lambda h, b: (0, h)),
                       pl.BlockSpec((S, 128), lambda h, b: (0, h))),
            scratch_shapes=[pltpu.VMEM((S, 128), F32), pltpu.VMEM((S, 128), F32), pltpu.VMEM((128, 2 * tq), F32),
                            pltpu.VMEM((2, T), F32)]),
        name="attend_back",
    )(docs, q, qaug, do, lse, ot, k, kaug, v)


def middle_kernel(attn_ref, in_ref, cot_ref, vec_ref, wo_ref, wu_ref, down_own, down_far,
                  out_ref, sum1_ref, do_ref, grads_ref, up_out, down_out, attn_out,
                  wo, wu, wd, attn_b, first, hat1, scale1, first_b, act, slope, sum2, down_b, up_b, first_b2, first_t,
                  g_up, g_down, g_out, sem_w, sem_d, sem_o):
    rows, wide = in_ref.shape[0], wu.shape[1]
    a, w = lax.axis_index("ctx"), lax.axis_index("wsh")
    y, c = w // 2, lax.rem(w, 2)
    core_peer = (a, y * 2 + (1 - c))
    tall = down_own.shape[0]
    MESH = pl.DeviceIdType.MESH
    barrier = pltpu.get_barrier_semaphore()
    pl.semaphore_signal(barrier, inc=1, device_id=core_peer, device_id_type=MESH)
    pl.semaphore_wait(barrier, 1)
    passed = []
    for s, (ref, owner) in enumerate(((down_own, w), (down_far, (1 - y) * 2 + c))):
        there = wd.at[pl.ds(pl.multiple_of(owner * tall, 16), tall), :]
        passed.append(pltpu.make_async_remote_copy(
            src_ref=ref, dst_ref=there, send_sem=sem_d.at[0, s], recv_sem=sem_d.at[1, s],
            device_id=core_peer, device_id_type=MESH))
        passed[-1].start()
        pltpu.make_async_copy(ref, there, sem_w.at[2 + s]).start()
    loading = [pltpu.make_async_copy(wo_ref, wo, sem_w.at[0]), pltpu.make_async_copy(wu_ref, wu, sem_w.at[1])]
    for copy in loading:
        copy.start()

    def arrived(j):
        if j < 2:
            loading[j].wait()
        else:
            for s, owner in enumerate((w, (1 - y) * 2 + c)):
                there = wd.at[pl.ds(pl.multiple_of(owner * tall, 16), tall), :]
                pltpu.make_async_copy(there, there, sem_w.at[2 + s]).wait()
                passed[s].wait_recv()

    grads_ref[...] = jnp.zeros_like(grads_ref)
    attn_b[...] = attn_ref[...].astype(BF)
    out_b, attn_g, attn_s, down_bias, final_g, final_s = [vec_ref[i : i + 1, :] for i in range(2, 8)]
    arrived(0)
    block = 256

    def over_rows(fn):
        def one(i, carry):
            fn(pl.ds(pl.multiple_of(i * block, block), block))
            return carry

        lax.fori_loop(0, rows // block, one, 0)

    def norm(values):
        average = jnp.mean(values, axis=-1, keepdims=True)
        centred = values - average
        scale = lax.rsqrt(jnp.mean(centred * centred, axis=-1, keepdims=True) + EPS)
        return centred * scale, scale

    def norm_back(grad, hat, scale, gain):
        g = grad * gain
        return scale * (g - jnp.mean(g, axis=-1, keepdims=True) - hat * jnp.mean(g * hat, axis=-1, keepdims=True))

    def note(row, values):
        grads_ref[row : row + 1, :] += jnp.sum(values, axis=0, keepdims=True)

    def branch_part(r):
        a = attn_b[:, r].T
        v = lax.dot_general(a, wo[...], NN, preferred_element_type=F32) + out_b + in_ref[r, :].astype(F32)
        hat, scale = norm(v)
        hat1[r, :] = hat
        scale1[r, :] = scale
        f = hat * attn_g + attn_s
        first[r, :] = f
        first_b[r, :] = f.astype(BF)

    over_rows(branch_part)
    arrived(1)
    cols = vec_ref.shape[1]

    def over_wide(fn):
        def one(i, carry):
            fn(pl.ds(pl.multiple_of(i * cols, cols), cols), i)
            return carry

        lax.fori_loop(0, wide // cols, one, 0)

    def up_part(n, i):
        u = lax.dot_general(first_b[...], wu[:, n], NN, preferred_element_type=F32) + vec_ref[pl.ds(8 + i, 1), :]
        half = 0.5 * (1.0 + lax.erf(u * ROOT_HALF))
        act[:, n] = (u * half).astype(BF)
        slope[:, n] = half + u * (0.3989422804014327 * jnp.exp(-0.5 * u * u))

    over_wide(up_part)
    arrived(2)

    def down_part(r):
        v = lax.dot_general(act[r, :], wd[...], NN, preferred_element_type=F32) + down_bias + first[r, :]
        hat, scale = norm(v)
        out_ref[r, :] = (hat * final_g + final_s).astype(BF)
        cot = cot_ref[r, :].astype(F32)
        note(6, cot * hat)
        note(7, cot)
        g = norm_back(cot, hat, scale, final_g)
        sum2[r, :] = g
        rounded = g.astype(BF)
        down_b[r, :] = rounded
        note(5, rounded.astype(F32))

    over_rows(down_part)

    def up_back(n, i):
        g = lax.dot_general(down_b[...], wd[n, :], NT, preferred_element_type=F32) * slope[:, n]
        rounded = g.astype(BF)
        up_b[:, n] = rounded
        grads_ref[pl.ds(8 + i, 1), :] = jnp.sum(rounded.astype(F32), axis=0, keepdims=True)

    over_wide(up_back)

    def first_part(r):
        g = sum2[r, :] + lax.dot_general(up_b[r, :], wu[...], NT, preferred_element_type=F32)
        hat = hat1[r, :]
        note(3, g * hat)
        note(4, g)
        s1 = norm_back(g, hat, scale1[r, :], attn_g)
        sum1_ref[r, :] = s1
        rounded = s1.astype(BF)
        note(2, rounded.astype(F32))
        first_b2[r, :] = rounded

    over_rows(first_part)

    def do_part(r):
        do_ref[r, :] = lax.dot_general(first_b2[r, :], wo[...], NT, preferred_element_type=F32).astype(BF)

    over_rows(do_part)

    def wide_grads(n, i):
        g_down[n, :] = lax.dot_general(act[:, n].T, down_b[...], NN, preferred_element_type=F32).astype(BF)
        pltpu.make_async_copy(g_down.at[n, :], down_out.at[n, :], sem_o.at[0, i]).start()
        g_up[:, n] = lax.dot_general(first_t[...], up_b[:, n], NN, preferred_element_type=F32).astype(BF)
        pltpu.make_async_copy(g_up.at[:, n], up_out.at[:, n], sem_o.at[1, i]).start()

    first_t[...] = first_b[...].T
    over_wide(wide_grads)
    g_out[...] = lax.dot_general(attn_b[...], first_b2[...], NN, preferred_element_type=F32).astype(BF)
    pltpu.make_async_copy(g_out, attn_out, sem_o.at[2, 0]).start()

    def wide_end(n, i):
        pltpu.make_async_copy(g_down.at[n, :], down_out.at[n, :], sem_o.at[0, i]).wait()
        pltpu.make_async_copy(g_up.at[:, n], up_out.at[:, n], sem_o.at[1, i]).wait()

    over_wide(wide_end)
    pltpu.make_async_copy(g_out, attn_out, sem_o.at[2, 0]).wait()
    for copy in passed:
        copy.wait_send()


def middle(attn_t, inputs, cotangent, vec, out_w, up_w, down_own, down_far):
    rows = inputs.shape[0]
    wide = up_w.shape[1]
    vm, dma, shape = pltpu.VMEM, pltpu.SemaphoreType.DMA, jax.ShapeDtypeStruct
    any_spec = pl.BlockSpec(memory_space=pltpu.HBM)
    vm_spec = pl.BlockSpec(memory_space=pltpu.VMEM)
    return pl.pallas_call(
        middle_kernel,
        out_shape=(shape((rows, D), BF), shape((rows, D), F32), shape((rows, D), BF), shape((16, D), F32),
                   shape((D, wide), BF), shape((wide, D), BF), shape((D, D), BF)),
        in_specs=[vm_spec] * 4 + [any_spec] * 4,
        out_specs=(vm_spec,) * 4 + (any_spec,) * 3,
        scratch_shapes=[
            vm((D, D), BF), vm((D, wide), BF), vm((wide, D), BF), vm((D, rows), BF), vm((rows, D), F32),
            vm((rows, D), F32), vm((rows, 1), F32), vm((rows, D), BF), vm((rows, wide), BF), vm((rows, wide), F32),
            vm((rows, D), F32), vm((rows, D), BF), vm((rows, wide), BF), vm((rows, D), BF), vm((D, rows), BF),
            vm((D, wide), BF), vm((wide, D), BF), vm((D, D), BF), dma((4,)), dma((2, 2)), dma((3, wide // D)),
        ],
        compiler_params=pltpu.CompilerParams(collective_id=3, has_side_effects=True, vmem_limit_bytes=63 * 2**20),
        name="middle",
    )(attn_t, inputs, cotangent, vec, out_w, up_w, down_own, down_far)


def reach(n_ctx):
    return n_ctx // 2


def finish_kernel(sources, n_parts, *refs):
    parts = refs[:n_parts]
    (vec_ref, dk_ref, dv_ref, tok_ref, dq_ref, w_ref, own_in_ref, mine_tok_ref,
     out_ref, vec_out, wide_out, grad_ref,
     mine, buf_a, buf_h, buf_b, buf_s, buf_c, buf_d, buf_e, gbf,
     sums, heard, line,
     loads, weights, acc, dq, own, bias,
     run_part, from_x, from_z, far_z, last_x,
     sem_l, sem_a, sem_b, sem_c, sem_d, sem_v, sem_x, sem_z, sem_far, sem_load, sem_in) = refs[n_parts:]
    n_ready = len(sources)
    n_chunks = out_ref.shape[0]
    n_ctx, n_wsh = lax.axis_size("ctx"), lax.axis_size("wsh")
    zs = n_ctx // 2
    a, w = lax.axis_index("ctx"), lax.axis_index("wsh")
    z, x = a // 2, lax.rem(a, 2)
    y, c = w // 2, lax.rem(w, 2)
    core_peer = (a, y * 2 + (1 - c))
    y_peer = (a, (1 - y) * 2 + c)
    x_peer = (z * 2 + (1 - x), w)
    low, high = lax.rem(z, 2), z // 2
    pair_peer = ((z + 1 - 2 * low) * 2 + x, w)
    skip_peer = (lax.rem(z + 2, zs) * 2 + x, w)
    up_peer, down_peer = (a + 2, w), (a - 2, w)
    near = reach(n_ctx)
    hops = near // 2
    MESH = pl.DeviceIdType.MESH

    rows = out_ref.shape[1]
    half = out_ref.shape[2] // 2
    piece = rows // zs
    tall = own.shape[0]
    cut = from_x.shape[1]

    def z_peer(d):
        return (lax.rem(z + d, zs) * 2 + x, w)

    barrier = pltpu.get_barrier_semaphore()
    for dev in [core_peer, y_peer, x_peer] + [z_peer(d) for d in range(1, zs)]:
        pl.semaphore_signal(barrier, inc=1, device_id=dev, device_id_type=MESH)
    def send(src, dst, sems, idx, dev):
        return pltpu.make_async_remote_copy(
            src_ref=src, dst_ref=dst, send_sem=sems.at[(0,) + idx], recv_sem=sems.at[(1,) + idx],
            device_id=dev, device_id_type=MESH)

    def wait_in(ref, sems, idx):
        send(ref, ref, sems, idx, core_peer).wait_recv()

    def wait_out(ref, sems, idx):
        send(ref, ref, sems, idx, core_peer).wait_send()

    def distance(i):
        return (hops - i // 4) * (1 - 2 * lax.rem(i // 2, 2))

    def position(i):
        dz = distance(i)
        mine_too = lax.rem(i, 2)
        run = 2 * (z + dz) + (1 - x) * (1 - mine_too) + x * mine_too
        return run, mine_too, (z + dz >= 0) & (z + dz < zs) & (jnp.abs(run - a) <= near)

    n_pos = 4 * hops + 2

    def load(i):
        run, _mine_too, there = position(i)
        return there, [
            pltpu.make_async_copy(src.at[run], loads.at[lax.rem(i, 2), j], sem_load.at[lax.rem(i, 2), j])
            for j, src in enumerate((dk_ref, dv_ref, tok_ref))
        ]

    def load_start(i):
        there, copies = load(i)

        @pl.when(there & (i < n_pos))
        def _():
            for copy in copies:
                copy.start()

    def share(k, owner):
        if k < n_ready:
            p, row0, col0 = sources[k]
            return parts[p].at[owner, pl.ds(row0, rows), pl.ds(col0, 2 * half)]
        return gbf.at[k - n_ready, owner]

    def share_load(k):
        for yy in range(2):
            pltpu.make_async_copy(share(k, yy * 2 + c), mine.at[k % 4, yy], sem_l.at[k]).start()

    def share_send(k):
        for yy in range(2):
            send(share(k, yy * 2 + (1 - c)), buf_a.at[k, yy], sem_a, (k,), core_peer).start()

    load_start(0)
    fetch = [pltpu.make_async_copy(w_ref, weights, sem_in.at[0]), pltpu.make_async_copy(dq_ref, dq, sem_in.at[1]),
             pltpu.make_async_copy(own_in_ref, own, sem_in.at[2])]
    for copy in fetch:
        copy.start()
    for k in range(4):
        share_load(k)
    acc[...] = jnp.zeros_like(acc)
    bias[...] = jnp.zeros_like(bias)
    pl.semaphore_wait(barrier, zs + 2)
    for k in range(n_ready):
        share_send(k)
    fetch[0].wait()

    near_rows, far_rows = pl.ds(0, cut), pl.ds(cut, tall - cut)

    def unit(i):
        run, mine_too, there = position(i)
        at = lax.rem(i, 2)
        load_start(i + 1)

        @pl.when(there)
        def _():
            for copy in load(i)[1]:
                copy.wait()

            def tokens_part(r, carry):
                rs = pl.ds(pl.multiple_of(r * 256, 256), 256)
                g = lax.dot_general(loads[at, 0, rs, :], weights[0], NT, preferred_element_type=F32)
                g = g + lax.dot_general(loads[at, 1, rs, :], weights[1], NT, preferred_element_type=F32)
                run_part[i, rs, :] = g.astype(BF)
                bias[0:8, :] += jnp.sum(loads[at, 1, rs, :].astype(F32).reshape(32, 8, 2 * half), axis=0)
                return carry

            lax.fori_loop(0, tall // 256, tokens_part, 0)

            @pl.when(mine_too == 0)
            def _():
                send(run_part.at[i, near_rows, :], from_x.at[i // 2], sem_x, (i // 2,), x_peer).start()

            @pl.when(i < 4)
            def _():
                far_send(i)

            def weights_part(r, carry):
                fs = pl.ds(pl.multiple_of(r * 256, 256), 256)
                flipped = loads[at, 2, :, fs].T
                for j in range(2):
                    acc[j, fs, :] += lax.dot_general(flipped, loads[at, j], NN, preferred_element_type=F32)
                return carry

            lax.fori_loop(0, 2 * half // 256, weights_part, 0)

    def from_below(i):
        dz = distance(i)
        step = 1 - 2 * lax.rem(i // 2, 2)
        sender, target = z - step, z - step + dz
        side = jnp.abs(2 * dz + (1 - 2 * x) * (1 - lax.rem(i, 2))) <= near
        return (sender >= 0) & (sender < zs) & (target >= 0) & (target < zs) & side

    def toward(i, copy_of):
        step = 1 - 2 * lax.rem(i // 2, 2)

        @pl.when(step == 1)
        def _():
            copy_of(up_peer).start()

        @pl.when(step == -1)
        def _():
            copy_of(down_peer).start()

    def far_send(i):
        toward(i, lambda dev: send(run_part.at[i, far_rows, :], far_z.at[i], sem_far, (i,), dev))

    def far_pass(i):
        _run, _mine_too, there = position(i)

        @pl.when(there)
        def _():
            @pl.when(from_below(i - 4))
            def _():
                wait_in(far_z.at[i - 4], sem_far, (i - 4,))
                run_part[i, far_rows, :] = (
                    run_part[i, far_rows, :].astype(F32) + far_z[i - 4].astype(F32)).astype(BF)

            far_send(i)

    def far_end():
        for col in range(2):
            total = n_pos - 2 + col
            for src in (4 + col, 6 + col):
                @pl.when(from_below(src))
                def _():
                    wait_in(far_z.at[src], sem_far, (src,))
                    run_part[total, far_rows, :] = (
                        run_part[total, far_rows, :].astype(F32) + far_z[src].astype(F32)).astype(BF)
            if col == 0:
                send(run_part.at[total, far_rows, :], last_x, sem_x, (n_pos // 2,), x_peer).start()
        own[far_rows, :] += run_part[n_pos - 1, far_rows, :].astype(F32)

    def near_pass(n):
        dz = distance(2 * n)
        i = 2 * n + 1

        @pl.when((z + dz >= 0) & (z + dz < zs))
        def _():
            @pl.when(jnp.abs(2 * dz + 2 * x - 1) <= near)
            def _():
                wait_in(from_x.at[n], sem_x, (n,))
                run_part[i, near_rows, :] = (
                    run_part[i, near_rows, :].astype(F32) + from_x[n].astype(F32)).astype(BF)

            @pl.when((n >= 2) & from_below(i - 4))
            def _():
                wait_in(from_z.at[n - 2], sem_z, (n - 2,))
                run_part[i, near_rows, :] = (
                    run_part[i, near_rows, :].astype(F32) + from_z[n - 2].astype(F32)).astype(BF)

            toward(i, lambda dev: send(run_part.at[i, near_rows, :], from_z.at[n], sem_z, (n,), dev))

    def near_own():
        n = n_pos // 2 - 1
        wait_in(from_x.at[n], sem_x, (n,))
        own[near_rows, :] += run_part[n_pos - 1, near_rows, :].astype(F32) + from_x[n].astype(F32)

    def near_end():
        for n in (2, 3):
            @pl.when(from_below(2 * n + 1))
            def _():
                wait_in(from_z.at[n], sem_z, (n,))
                own[near_rows, :] += from_z[n].astype(F32)

    def add(p, q):
        return (p.astype(F32) + q.astype(F32)).astype(BF)

    def column(side):
        return pl.ds(pl.multiple_of(side * half, 128), half)

    def band(start, size):
        return pl.ds(pl.multiple_of(start, 16), size)

    def stage_b(k):
        at = lax.rem(k, 4)
        pltpu.make_async_copy(mine.at[at], mine.at[at], sem_l.at[k]).wait()
        wait_in(buf_a.at[k], sem_a, (k,))
        buf_h[k] = add(mine[at, 1 - y], buf_a[k, 1 - y])
        send(buf_h.at[k], buf_b.at[k], sem_b, (k,), y_peer).start()
        buf_a[k, y] = add(mine[at, y], buf_a[k, y])

    def stage_c(k):
        wait_in(buf_b.at[k], sem_b, (k,))
        buf_s[k] = add(buf_a[k, y, :, column(1 - x)], buf_b[k, :, column(1 - x)])
        send(buf_s.at[k], buf_c.at[k], sem_c, (0, k), x_peer).start()

    my_two, other_two = band(low * 2 * piece, 2 * piece), band((1 - low) * 2 * piece, 2 * piece)
    my_one, other_one = band(high * piece, piece), band((1 - high) * piece, piece)
    my_rows = band(low * 2 * piece + high * piece, piece)

    def stage_d(k):
        wait_in(buf_c.at[k], sem_c, (0, k))
        cols = column(x)
        joined = buf_a[k, y, :, cols].astype(F32) + buf_b[k, :, cols].astype(F32) + buf_c[k].astype(F32)
        buf_c[k] = joined.astype(BF)
        send(buf_c.at[k, other_two, :], buf_d.at[k], sem_d, (0, k), pair_peer).start()

    def stage_d2(k):
        wait_in(buf_d.at[k], sem_d, (0, k))
        buf_d[k] = add(buf_d[k], buf_c[k, my_two, :])
        send(buf_d.at[k, other_one, :], buf_e.at[k], sem_d, (1, k), skip_peer).start()

    def stage_e(k):
        wait_in(buf_e.at[k], sem_d, (1, k))
        buf_e[k] = add(buf_e[k], buf_d[k, my_one, :])
        out_ref[k, my_rows, column(x)] = buf_e[k]
        send(buf_e.at[k], out_ref.at[k, my_rows, column(x)], sem_d, (2, k), skip_peer).start()

    def stage_e2(k):
        wait_in(buf_e.at[k], sem_d, (2, k))
        there = out_ref.at[k, my_two, column(x)]
        send(there, there, sem_d, (3, k), pair_peer).start()

    def stage_f(k):
        wait_in(buf_d.at[k], sem_d, (3, k))
        there = out_ref.at[k, :, column(x)]
        send(there, there, sem_c, (1, k), x_peer).start()

    def guarded(fn, k, first, last):
        @pl.when((k >= first) & (k < last))
        def _():
            fn(k)

    def chunk_step(m):
        for lag, stage in enumerate((stage_c, stage_d, stage_d2, stage_e, stage_e2, stage_f)):
            guarded(stage, m - (lag and lag + 1), 0, n_chunks)

    def first_step(t, carry):
        guarded(unit, t, 0, n_pos)
        for j in range(2):
            guarded(stage_b, 2 * t + j, 0, n_ready)
        for k in range(4, n_ready):
            @pl.when(t == (k - 4) // 2)
            def _():
                share_load(k)

        @pl.when(lax.rem(t, 2) == 1)
        def _():
            guarded(near_pass, t // 2 - 1, 0, 4)

        guarded(far_pass, t - 2, 4, 8)

        @pl.when((lax.rem(t, 2) == 0) & (t >= 2))
        def _():
            chunk_step(t // 2 - 1)

        return carry

    lax.fori_loop(0, n_pos, first_step, 0)
    done = n_pos // 2 - 1

    fetch[1].wait()
    fetch[2].wait()
    own_tok = pltpu.make_async_copy(mine_tok_ref, loads.at[0, 2], sem_load.at[0, 2])
    own_tok.start()

    def to_bf(j, target):
        for owner in range(n_wsh):
            gbf[target, owner] = acc[j, owner * rows : (owner + 1) * rows, :].astype(BF)
        share_load(n_ready + target)
        share_send(n_ready + target)

    to_bf(0, 0)
    to_bf(1, 1)
    own_tok.wait()

    def query_part(r, carry):
        fs = pl.ds(pl.multiple_of(r * 256, 256), 256)
        acc[0, fs, :] = lax.dot_general(loads[0, 2, :, fs].T, dq[...], NN, preferred_element_type=F32)
        return carry

    lax.fori_loop(0, 2 * half // 256, query_part, 0)
    to_bf(0, 2)

    def query_tokens(r, carry):
        rs = pl.ds(pl.multiple_of(r * 256, 256), 256)
        own[rs, :] += lax.dot_general(dq[rs, :], weights[2], NT, preferred_element_type=F32)
        bias[8:16, :] += jnp.sum(dq[rs, :].astype(F32).reshape(32, 8, 2 * half), axis=0)
        return carry

    lax.fori_loop(0, tall // 256, query_tokens, 0)

    sums[0] = vec_ref[...]
    sums[0, 0:1, :] = jnp.sum(bias[8:16, :], axis=0, keepdims=True)
    sums[0, 1:2, :] = jnp.sum(bias[0:8, :], axis=0, keepdims=True)
    pair = (core_peer, y_peer, x_peer)

    def vec_send(stage):
        send(sums.at[stage], heard.at[stage], sem_v, (stage,), pair[stage]).start()

    def vec_stage(stage):
        wait_in(heard.at[stage], sem_v, (stage,))
        total = sums[stage] + heard[stage]
        sums[stage + 1] = total
        if stage < 2:
            vec_send(stage + 1)
        else:
            line[z] = total
            for d in range(1, zs):
                send(sums.at[3], line.at[z], sem_v, (3,), z_peer(d)).start()

    def vec_last():
        wait_in(line.at[pl.ds(0, zs - 1)], sem_v, (3,))
        total = line[0]
        for d in range(1, zs):
            total = total + line[d]
        small, wide = total[0:8, 0:rows], total[8:9, :]
        for owner in range(1, n_wsh):
            small = jnp.where(w == owner, total[0:8, owner * rows : (owner + 1) * rows], small)
            wide = jnp.where(w == owner, total[8 + owner : 9 + owner, :], wide)
        vec_out[...] = small
        wide_out[...] = wide

    vec_send(0)

    def second_step(m, carry):
        guarded(stage_b, m - done + n_ready, n_ready, n_chunks)
        chunk_step(m)
        guarded(lambda k: near_own(), m - done, 0, 1)
        for stage in range(3):
            guarded(lambda k: vec_stage(stage), m - done - 1 - stage, 0, 1)
        guarded(lambda k: near_end(), m - done - 3, 0, 1)
        guarded(lambda k: far_end(), m - done - 4, 0, 1)
        guarded(lambda k: vec_last(), m - done - 5, 0, 1)
        return carry

    lax.fori_loop(done, n_chunks + 6, second_step, 0)
    wait_in(last_x, sem_x, (n_pos // 2,))
    own[far_rows, :] += last_x[...].astype(F32)
    grad_ref[...] = own[...].astype(BF)

    def drain(k, carry):
        wait_in(buf_s.at[k], sem_c, (1, k))
        wait_out(buf_a.at[k], sem_a, (k,))
        wait_out(buf_b.at[k], sem_b, (k,))
        wait_out(buf_s.at[k], sem_c, (0, k))
        wait_out(buf_s.at[k], sem_c, (1, k))
        wait_out(buf_d.at[k], sem_d, (0, k))
        wait_out(buf_e.at[k], sem_d, (1, k))
        wait_out(buf_e.at[k], sem_d, (2, k))
        wait_out(buf_d.at[k], sem_d, (3, k))
        return carry

    lax.fori_loop(0, n_chunks, drain, 0)
    for stage in range(3):
        wait_out(heard.at[stage], sem_v, (stage,))
    wait_out(line.at[pl.ds(0, zs - 1)], sem_v, (3,))
    wait_out(last_x, sem_x, (n_pos // 2,))

    def drain_runs(i, carry):
        _run, mine_too, there = position(i)

        @pl.when(there)
        def _():
            wait_out(far_z.at[i], sem_far, (i,))

            @pl.when(mine_too == 1)
            def _():
                wait_out(from_z.at[i // 2], sem_z, (i // 2,))

        return carry

    lax.fori_loop(0, n_pos - 2, drain_runs, 0)

    def drain_x(n, carry):
        _run, _mine_too, there = position(2 * n)

        @pl.when(there)
        def _():
            wait_out(from_x.at[n], sem_x, (n,))

        return carry

    lax.fori_loop(0, n_pos // 2, drain_x, 0)


def widen_kernel(spans, in_ref, *outs):
    for (first, down, across), out in zip(spans, outs):
        for r in range(down):
            for col in range(across):
                out[r, :, col * D : (col + 1) * D] = in_ref[first + r * across + col].astype(F32)


def widen(summed, spans):
    n, rows, _width = summed.shape
    part = rows // 2
    outs = pl.pallas_call(
        functools.partial(widen_kernel, spans),
        grid=(2,),
        out_shape=[jax.ShapeDtypeStruct((down, rows, across * D), F32) for _first, down, across in spans],
        in_specs=[pl.BlockSpec((n, part, D), lambda i: (0, i, 0))],
        out_specs=[pl.BlockSpec((down, part, across * D), lambda i: (0, i, 0)) for _first, down, across in spans],
        name="widen",
    )(summed)
    return [o.reshape(-1, o.shape[2]) for o in outs]


def finish(matrices, vec, grad_k, grad_v, all_tokens, grad_q, kvq_w, own_grad, inputs):
    n_ctx, n_wsh = lax.axis_size("ctx"), lax.axis_size("wsh")
    zs, hops = n_ctx // 2, reach(n_ctx) // 2
    rows = D // n_wsh
    parts, sources, spans = [], [], []
    for p, g in enumerate(matrices):
        down, across = g.shape[0] // D, g.shape[1] // D
        parts.append(g.astype(BF).reshape(n_wsh, down * rows, across * D))
        spans.append((len(sources), down, across))
        sources += [(p, r * rows, col * D) for r in range(down) for col in range(across)]
    n = len(sources) + 3
    spans += [(len(sources) + j, 1, 1) for j in range(3)]
    half, piece, tall = D // 2, rows // zs, inputs.shape[0]
    n_pos, cut = 4 * hops + 2, tall * 5 // 8
    vm, dma, shape = pltpu.VMEM, pltpu.SemaphoreType.DMA, jax.ShapeDtypeStruct
    any_spec = pl.BlockSpec(memory_space=pltpu.HBM)
    vm_spec = pl.BlockSpec(memory_space=pltpu.VMEM)
    summed, small, wide, grad_own = pl.pallas_call(
        functools.partial(finish_kernel, sources, len(parts)),
        out_shape=(shape((n, rows, D), BF), shape((8, rows), F32), shape((1, D), F32), shape((tall, D), BF)),
        in_specs=[any_spec] * len(parts) + [vm_spec] + [any_spec] * 7,
        out_specs=(vm_spec,) * 4,
        scratch_shapes=[
            vm((4, 2, rows, D), BF), vm((n, 2, rows, D), BF), vm((n, rows, D), BF), vm((n, rows, D), BF),
            vm((n, rows, half), BF), vm((n, rows, half), BF), vm((n, 2 * piece, half), BF), vm((n, piece, half), BF),
            vm((3, n_wsh, rows, D), BF),
            vm((4,) + vec.shape, F32), vm((3,) + vec.shape, F32), vm((zs,) + vec.shape, F32),
            vm((2, 3, tall, D), BF), vm((3, D, D), BF), vm((2, D, D), F32), vm((tall, D), BF), vm((tall, D), F32),
            vm((16, D), F32),
            vm((n_pos, tall, D), BF), vm((n_pos // 2, cut, D), BF), vm((4, cut, D), BF),
            vm((n_pos - 2, tall - cut, D), BF), vm((tall - cut, D), BF),
            dma((n,)), dma((2, n)), dma((2, n)), dma((2, 2, n)), dma((2, 4, n)), dma((2, 4)),
            dma((2, n_pos // 2 + 1)), dma((2, 4)), dma((2, n_pos - 2)), dma((2, 3)), dma((3,)),
        ],
        compiler_params=pltpu.CompilerParams(collective_id=2, has_side_effects=True, vmem_limit_bytes=63 * 2**20),
        name="finish",
    )(*parts, vec, grad_k, grad_v, all_tokens, grad_q, kvq_w, own_grad, inputs)
    return widen(summed, spans), small, wide, grad_own


def gather_kernel(cut, tok_ref, docs_ref, wk_ref, wv_ref, wq_ref, wo_ref, wu_ref, vec_ref,
                  tok_out, k_out, v_out, q_out, w_out, vec_out, wo_out, wu_out, query_doc, key_doc,
                  tok, kbuf, vbuf, qbuf, wbuf, vecs, wo, wu, kdoc,
                  sem_in, sem_out, sem_w, sem_l, sem_o):
    n_ctx = lax.axis_size("ctx")
    zs = n_ctx // 2
    a, w = lax.axis_index("ctx"), lax.axis_index("wsh")
    z, x = a // 2, lax.rem(a, 2)
    y, c = w // 2, lax.rem(w, 2)
    core_peer = (a, y * 2 + (1 - c))
    y_peer = (a, (1 - y) * 2 + c)
    x_peer = (z * 2 + (1 - x), w)
    up, down = (a + 2, w), (a - 2, w)
    near = reach(n_ctx)
    MESH = pl.DeviceIdType.MESH
    n_slices = sem_in.shape[1]
    tall = tok.shape[1] // n_slices
    own = wk_ref.shape[0]
    far = 4 * (near // 2 + 1)

    barrier = pltpu.get_barrier_semaphore()
    around = [(lax.rem(z + d, zs) * 2 + x, w) for d in (1, zs - 1)]
    for dev in [core_peer, y_peer, x_peer] + around:
        pl.semaphore_signal(barrier, inc=1, device_id=dev, device_id_type=MESH)
    pl.semaphore_wait(barrier, 5)

    def relative(u):
        dz = (u // 4) * (1 - 2 * lax.rem(u, 2))
        other = lax.rem(u // 2, 2)
        run = 2 * (z + dz) + (x + other - 2 * x * other)
        there = (z + dz >= 0) & (z + dz < zs) & (jnp.abs(run - a) <= near) & ((u >= 4) | (lax.rem(u, 2) == 0))
        return run, dz, other, there

    def rows(s):
        return pl.ds(pl.multiple_of(s * tall, tall), tall)

    def remote(src, dst, send_sem, recv_sem, dev):
        return pltpu.make_async_remote_copy(
            src_ref=src, dst_ref=dst, send_sem=send_sem, recv_sem=recv_sem, device_id=dev, device_id_type=MESH)

    def routes(u, s):
        run, dz, other, there = relative(u)
        z_first = s < cut
        to_x = there & (z_first | (dz == 0)) & (other == 0) & (jnp.abs(run - x_peer[0]) <= near)
        along = there & ((other == 0) | jnp.logical_not(z_first))
        to_up = along & (dz <= 0) & (z + 1 < zs) & (jnp.abs(run - (a + 2)) <= near)
        to_down = along & (dz >= 0) & (z > 0) & (jnp.abs(run - (a - 2)) <= near)
        return run, ((0, x_peer, to_x), (1, up, to_up), (2, down, to_down))

    def pass_on(u, s):
        run, where = routes(u, s)
        for d, dev, ok in where:
            @pl.when(ok)
            def _():
                source = tok_ref if isinstance(u, int) and u == 0 else tok.at[run]
                remote(source.at[rows(s), :], tok.at[run, rows(s), :], sem_out.at[d, u, s], sem_in.at[run, s], dev).start()

    def await_slice(u, s):
        run, _dz, _other, there = relative(u)

        @pl.when(there)
        def _():
            remote(tok.at[run, rows(s), :], tok.at[run, rows(s), :], sem_out.at[0, 0, 0], sem_in.at[run, s], x_peer).wait_recv()

    def start_own(s, carry):
        pass_on(0, s)
        return carry

    def weight_rows(owner):
        return pl.ds(pl.multiple_of(owner * own, 16), own)

    def shard(m, owner):
        if m == 3:
            return vecs.at[owner]
        return (wbuf.at[0], wbuf.at[1], wbuf.at[2], None, wo, wu)[m].at[weight_rows(owner), :]

    vecs[w, 0 : vec_ref.shape[0], :] = vec_ref[...]
    shards = (wk_ref, wv_ref, wq_ref, vecs.at[w], wo_ref, wu_ref)
    for m in (3, 0, 1, 2, 4, 5):
        remote(shards[m], shard(m, w), sem_w.at[0, 1, m], sem_w.at[1, 1, m], y_peer).start()
        remote(shards[m], shard(m, w), sem_w.at[0, 0, m], sem_w.at[1, 0, m], core_peer).start()
        if m != 3:
            pltpu.make_async_copy(shards[m], shard(m, w), sem_w.at[0, 3, m]).start()
    lax.fori_loop(0, n_slices, start_own, 0)
    pltpu.make_async_copy(tok_ref, tok.at[a], sem_l.at[4]).start()

    for j in range(n_ctx):
        @pl.when(jnp.abs(j - a) > near)
        def _():
            tok[j] = jnp.zeros_like(tok[j])

    n_rows = tok.shape[1]

    def is_own_lane(first):
        pos = first + lax.broadcasted_iota(jnp.int32, (n_rows, 128), 0)
        doc = jnp.full((n_rows, 128), -1, jnp.int32)
        for d in range(docs_ref.shape[1]):
            doc = doc + jnp.where(pos >= docs_ref[0, d], 1, 0)
        return lax.broadcasted_iota(jnp.int32, (n_rows, 128), 1) == doc

    def key_lanes(j, carry):
        kdoc[pl.ds(pl.multiple_of(j * n_rows, n_rows), n_rows), :] = jnp.where(
            is_own_lane(j * n_rows), 0.0, -1e30).astype(BF)
        return carry

    lax.fori_loop(0, n_ctx, key_lanes, 0)
    pltpu.make_async_copy(kdoc, key_doc, sem_l.at[3]).start()
    query_doc[...] = jnp.where(is_own_lane(a * n_rows), 1.0, 0.0).astype(BF)

    def weight_arrival(m, kind):
        part = shard(m, w)
        return remote(part, part, sem_w.at[0, kind, m], sem_w.at[1, kind, m], core_peer)

    across = (1 - y) * 2 + c

    def weight_forward(m):
        weight_arrival(m, 1).wait_recv()
        remote(shard(m, across), shard(m, across), sem_w.at[0, 2, m], sem_w.at[1, 2, m], core_peer).start()

    def weight_end(m):
        weight_arrival(m, 0).wait_recv()
        weight_arrival(m, 2).wait_recv()
        if m != 3:
            pltpu.make_async_copy(shard(m, w), shard(m, w), sem_w.at[0, 3, m]).wait()

    def relay(first, last):
        def one(i, carry):
            s = i // (last - first)
            u = first + lax.rem(i, last - first)
            await_slice(u, s)
            pass_on(u, s)
            return carry

        lax.fori_loop(0, n_slices * (last - first), one, 0)

    relay(2, 6)
    weight_forward(3)
    weight_forward(0)
    weight_forward(1)
    weight_end(3)
    vec_out[0:8, :] = jnp.concatenate([vecs[o, 0:8, :] for o in range(4)], axis=1)
    for o in range(4):
        vec_out[8 + o : 9 + o, :] = jnp.concatenate([vecs[o, 8 + i : 9 + i, :] for i in range(4)], axis=1)
    pltpu.make_async_copy(tok_ref, tok.at[a], sem_l.at[4]).wait()
    weight_end(0)
    weight_end(1)

    step_rows = 256
    steps = tok.shape[1] // step_rows

    def query_part(i, carry):
        r = pl.ds(pl.multiple_of(i * step_rows, step_rows), step_rows)
        q = (jnp.dot(tok[a, r, :], wbuf[2], preferred_element_type=F32) + vec_out[0:1, :]).astype(BF)
        qbuf[r, :] = q * jnp.asarray(SCALE, BF)
        return carry

    def project(u, carry):
        run, _dz, _other, there = relative(u)

        @pl.when(u == 6)
        def _():
            weight_forward(2)
            weight_end(2)
            lax.fori_loop(0, steps, query_part, 0)
            pltpu.make_async_copy(qbuf, q_out, sem_l.at[5]).start()
            relay(6, 10)

        @pl.when(there)
        def _():
            @pl.when(u >= 10)
            def _():
                def one(s, carry):
                    await_slice(u, s)
                    return carry

                lax.fori_loop(0, n_slices, one, 0)

            def part(i, carry):
                r = pl.ds(pl.multiple_of(i * step_rows, step_rows), step_rows)
                t = tok[run, r, :]
                kbuf[run, r, :] = jnp.dot(t, wbuf[0], preferred_element_type=F32).astype(BF)
                vbuf[run, r, :] = (jnp.dot(t, wbuf[1], preferred_element_type=F32) + vec_out[1:2, :]).astype(BF)
                return carry

            lax.fori_loop(0, steps, part, 0)
            for i, (src, dst) in enumerate(((kbuf, k_out), (vbuf, v_out), (tok, tok_out))):
                pltpu.make_async_copy(src.at[run], dst.at[run], sem_o.at[i, run]).start()

        return carry

    for j in range(n_ctx):
        @pl.when(jnp.abs(j - a) > near)
        def _():
            kbuf[j] = jnp.zeros_like(kbuf[j])
            vbuf[j] = jnp.zeros_like(vbuf[j])
            for i, (src, dst) in enumerate(((kbuf, k_out), (vbuf, v_out), (tok, tok_out))):
                pltpu.make_async_copy(src.at[j], dst.at[j], sem_o.at[i, j]).start()

    lax.fori_loop(0, far, project, 0)

    pltpu.make_async_copy(wbuf, w_out, sem_l.at[6]).start()

    for m in (4, 5):
        weight_forward(m)
    for m, full, target in ((4, wo, wo_out), (5, wu, wu_out)):
        weight_end(m)
        pltpu.make_async_copy(full, target, sem_l.at[m - 4]).start()
    for m in range(6):
        for kind in range(3):
            weight_arrival(m, kind).wait_send()

    def drain(i, carry):
        s = i // far
        u = lax.rem(i, far)
        run, where = routes(u, s)
        for d, dev, ok in where:
            @pl.when(ok & (u < 10))
            def _():
                remote(tok.at[run, rows(s), :], tok.at[run, rows(s), :], sem_out.at[d, u, s], sem_in.at[run, s], dev).wait_send()
        return carry

    lax.fori_loop(0, n_slices * far, drain, 0)
    for j in range(n_ctx):
        for i, (src, dst) in enumerate(((kbuf, k_out), (vbuf, v_out), (tok, tok_out))):
            pltpu.make_async_copy(src.at[j], dst.at[j], sem_o.at[i, j]).wait()
    pltpu.make_async_copy(qbuf, q_out, sem_l.at[5]).wait()
    pltpu.make_async_copy(wbuf, w_out, sem_l.at[6]).wait()
    pltpu.make_async_copy(wo, wo_out, sem_l.at[0]).wait()
    pltpu.make_async_copy(wu, wu_out, sem_l.at[1]).wait()
    pltpu.make_async_copy(kdoc, key_doc, sem_l.at[3]).wait()


def gather_project(inputs, doc_starts, vectors, key_weight, value_weight, query_weight, out_weight, up_weight):
    n_ctx, n_wsh = lax.axis_size("ctx"), lax.axis_size("wsh")
    tall = inputs.shape[0]
    n_slices = 8
    far = 4 * (reach(n_ctx) // 2 + 1)
    vm, dma = pltpu.VMEM, pltpu.SemaphoreType.DMA
    any_spec = pl.BlockSpec(memory_space=pltpu.HBM)
    vm_spec = pl.BlockSpec(memory_space=pltpu.VMEM)
    runs = (n_ctx, tall, D)
    shape = jax.ShapeDtypeStruct
    return pl.pallas_call(
        functools.partial(gather_kernel, 5),
        out_shape=(shape(runs, BF), shape(runs, BF), shape(runs, BF), shape((tall, D), BF), shape((3, D, D), BF),
                   shape((16, D), F32), shape((D, D), BF), shape((D, up_weight.shape[1]), BF), shape((tall, 128), BF),
                   shape((n_ctx * tall, 128), BF)),
        in_specs=[any_spec, pl.BlockSpec(memory_space=pltpu.SMEM)] + [any_spec] * 5 + [vm_spec],
        out_specs=(any_spec,) * 5 + (vm_spec,) + (any_spec,) * 2 + (vm_spec, any_spec),
        scratch_shapes=[
            vm(runs, BF), vm(runs, BF), vm(runs, BF), vm((tall, D), BF), vm((3, D, D), BF), vm((n_wsh, 16, D // n_wsh), F32),
            vm((D, D), BF), vm((D, up_weight.shape[1]), BF), vm((n_ctx * tall, 128), BF),
            dma((n_ctx, n_slices)), dma((3, far, n_slices)), dma((2, 4, 6)), dma((7,)), dma((3, n_ctx)),
        ],
        compiler_params=pltpu.CompilerParams(collective_id=1, has_side_effects=True, vmem_limit_bytes=63 * 2**20),
        name="gather_project",
    )(inputs, doc_starts, key_weight, value_weight, query_weight, out_weight, up_weight, vectors)


def local(
    tokens,
    cotangent,
    doc_starts,
    query_weight,
    key_weight,
    value_weight,
    out_weight,
    up_weight,
    down_weight,
    query_bias,
    value_bias,
    out_bias,
    attn_gain,
    attn_shift,
    up_bias,
    down_bias,
    final_gain,
    final_shift,
):
    inputs = tokens[0]
    doc_start = doc_starts[0]
    tok_rows = inputs.shape[0]
    stream_rows = tok_rows * lax.axis_size("ctx")
    tile = min(tok_rows, 256)
    n_ctx, n_wsh = lax.axis_size("ctx"), lax.axis_size("wsh")
    own = D // n_wsh

    def gather(x):
        return lax.all_gather(x, "wsh", axis=0, tiled=True)

    fast = n_wsh == 4 and n_ctx == 8 and own % (n_ctx // 2 * 16) == 0 and tok_rows % 512 == 0
    if fast:
        small = (query_bias, value_bias, out_bias, attn_gain, attn_shift, down_bias, final_gain, final_shift)
        vectors, place = jnp.zeros(((8 + n_wsh) * own,), F32), 0
        for v in small + (up_bias,):
            ends = (place, vectors.shape[0] - place - v.shape[0], 0)
            vectors = vectors + lax.pad(v.astype(F32), jnp.zeros((), F32), (ends,))
            place += v.shape[0]
        vectors = vectors.reshape(8 + n_wsh, own)
        all_tokens, keys, values, queries, kvq_w, vec, out_w, up_w, query_doc, key_doc = gather_project(
            inputs, doc_starts, vectors, key_weight, value_weight, query_weight, out_weight, up_weight
        )
        down_own, _unused = lax.optimization_barrier((down_weight, vec))
        down_far = lax.ppermute(down_own, "wsh", [(i, i ^ 2) for i in range(n_wsh)])
        all_tokens, keys, values = [r.reshape(stream_rows, D) for r in (all_tokens, keys, values)]
    else:
        first_row = lax.axis_index("ctx") * tok_rows
        query_doc, key_doc = document_lanes(doc_start, first_row, tok_rows, stream_rows)
        small = jnp.stack(
            [query_bias, value_bias, out_bias, attn_gain, attn_shift, down_bias, final_gain, final_shift]
        )
        all_tokens = lax.all_gather(inputs, "ctx", axis=0, tiled=True)
        query_w, key_w, value_w = gather(query_weight), gather(key_weight), gather(value_weight)
        small = gather(small.T).astype(F32)
        query_b, value_b, out_b, attn_g, attn_s, down_b, final_g, final_s = [small[:, i] for i in range(8)]
        up_b = gather(up_bias).astype(F32)
        queries = jnp.dot(inputs, query_w, preferred_element_type=F32) + query_b
        queries = queries.astype(BF) * jnp.asarray(SCALE, BF)
        keys = jnp.dot(all_tokens, key_w, preferred_element_type=F32).astype(BF)
        values = (jnp.dot(all_tokens, value_w, preferred_element_type=F32) + value_b).astype(BF)
    mixed_t, log_rows = attn_fwd(doc_start, queries, query_doc, keys, key_doc, values, tq=tile)
    if fast:
        layer_out, grad_sum1, grad_attn, vec_grads, grad_up_w, grad_down_w, grad_out_w = middle(
            mixed_t, inputs, cotangent[0], vec, out_w, up_w, down_own, down_far
        )
        grad_q, grad_k, grad_v = attn_bwd(
            doc_start, queries, query_doc, grad_attn, log_rows, mixed_t, keys, key_doc, values, tq=tile
        )
        mats, small, wide, grad_inputs = finish(
            (grad_up_w, grad_out_w, grad_down_w), vec_grads, grad_k.reshape(n_ctx, tok_rows, D),
            grad_v.reshape(n_ctx, tok_rows, D), all_tokens.reshape(n_ctx, tok_rows, D), grad_q, kvq_w, grad_sum1, inputs,
        )
        up_sum, out_sum, down_sum, key_sum, value_sum, query_sum = mats
        return (
            layer_out.reshape(1, tok_rows, D), grad_inputs.reshape(1, tok_rows, D), query_sum, key_sum, value_sum,
            out_sum, up_sum, down_sum, small[0], small[1], small[2], small[3], small[4], wide[0],
            small[5], small[6], small[7],
        )

    out_w = gather(out_weight)
    up_w = gather(up_weight)
    down_w = gather(down_weight)
    attn_t = mixed_t.astype(BF)
    inputs_f = inputs.astype(F32)
    branch = lax.dot_general(attn_t, out_w, TN, preferred_element_type=F32) + out_b
    first_norm, first_pull = jax.vjp(layer_norm, inputs_f + branch, attn_g, attn_s)
    first_b = first_norm.astype(BF)
    up_f = jnp.dot(first_b, up_w, preferred_element_type=F32) + up_b
    act_f, act_pull = jax.vjp(gelu_act, up_f)
    act_b = act_f.astype(BF)
    down_f = jnp.dot(act_b, down_w, preferred_element_type=F32) + down_b
    final_f, final_pull = jax.vjp(layer_norm, first_norm + down_f, final_g, final_s)
    layer_out = final_f.astype(BF)

    grad_sum2, grad_final_g, grad_final_s = final_pull(cotangent[0].astype(F32))
    grad_down = grad_sum2.astype(BF)
    grad_down_w = jnp.einsum("tf,td->fd", act_b, grad_down, preferred_element_type=F32)
    grad_down_b = jnp.sum(grad_down.astype(F32), axis=0)
    grad_act = jnp.einsum("td,fd->tf", grad_down, down_w, preferred_element_type=F32)
    (grad_up_f,) = act_pull(grad_act)
    grad_up = grad_up_f.astype(BF)
    grad_up_w = jnp.einsum("td,tf->df", first_b, grad_up, preferred_element_type=F32)
    grad_up_b = jnp.sum(grad_up.astype(F32), axis=0)
    grad_first = grad_sum2 + jnp.einsum("tf,df->td", grad_up, up_w, preferred_element_type=F32)
    grad_sum1, grad_attn_g, grad_attn_s = first_pull(grad_first)
    grad_branch = grad_sum1.astype(BF)
    grad_out_w = jnp.dot(attn_t, grad_branch, preferred_element_type=F32)
    grad_out_b = jnp.sum(grad_branch.astype(F32), axis=0)
    grad_attn = jnp.einsum("te,de->td", grad_branch, out_w, preferred_element_type=F32).astype(BF)
    grad_q, grad_k, grad_v = attn_bwd(
        doc_start, queries, query_doc, grad_attn, log_rows, mixed_t, keys, key_doc, values, tq=tile
    )
    def total(g):
        part = lax.psum_scatter(g.astype(BF), "wsh", scatter_dimension=0, tiled=True)
        return lax.psum(part, "ctx").astype(F32)

    grad_all = jnp.einsum("te,de->td", grad_k, key_w, preferred_element_type=F32)
    grad_all = grad_all + jnp.einsum("te,de->td", grad_v, value_w, preferred_element_type=F32)
    grad_own = lax.psum_scatter(grad_all.astype(BF), "ctx", scatter_dimension=0, tiled=True)
    grad_query_w = jnp.einsum("td,te->de", inputs, grad_q, preferred_element_type=F32)
    grad_key_w = jnp.einsum("td,te->de", all_tokens, grad_k, preferred_element_type=F32)
    grad_value_w = jnp.einsum("td,te->de", all_tokens, grad_v, preferred_element_type=F32)
    grad_query_b = jnp.sum(grad_q.astype(F32), axis=0)
    grad_value_b = jnp.sum(grad_v.astype(F32), axis=0)
    grad_inputs = grad_sum1 + jnp.einsum("te,de->td", grad_q, query_w, preferred_element_type=F32)
    grad_inputs = grad_inputs + grad_own.astype(F32)
    sums = [
        total(g)
        for g in (
            grad_query_w, grad_key_w, grad_value_w, grad_out_w, grad_up_w, grad_down_w,
            grad_query_b, grad_value_b, grad_out_b, grad_attn_g, grad_attn_s, grad_up_b,
            grad_down_b, grad_final_g, grad_final_s,
        )
    ]
    return (
        layer_out.reshape(1, tok_rows, D),
        grad_inputs.astype(BF).reshape(1, tok_rows, D),
        *sums,
    )


def solution(mesh):
    rows, mat, vec = P("wsh", "ctx", None), P("wsh", None), P("wsh")
    return jax.shard_map(
        local,
        mesh=mesh,
        in_specs=(rows, rows, mat) + (mat,) * 6 + (vec,) * 9,
        out_specs=(rows, rows) + (mat,) * 6 + (vec,) * 9,
        check_vma=False,
    )
```

```python
import functools

import jax
import jax.numpy as jnp
from jax import lax
from jax.experimental import pallas as pl
from jax.experimental.pallas import tpu as pltpu
from jax.sharding import PartitionSpec as P

D = 768
HEADS = 12
HD = 64
SCALE = 0.125
EPS = 1e-12
ROOT_HALF = 0.7071067811865476
BF = jnp.bfloat16
F32 = jnp.float32
NT = (((1,), (1,)), ((), ()))
NN = (((1,), (0,)), ((), ()))
TN = (((0,), (0,)), ((), ()))


def layer_norm(values, gain_vec, shift_vec):
    average = jnp.mean(values, axis=-1, keepdims=True)
    centred = values - average
    variance = jnp.mean(centred * centred, axis=-1, keepdims=True)
    return centred * lax.rsqrt(variance + EPS) * gain_vec + shift_vec


def gelu_act(values):
    return 0.5 * values * (1.0 + lax.erf(values * ROOT_HALF))


def key_range(docs, first_row, tile, stream_rows):
    last = first_row + tile - 1
    low, high = 0, stream_rows
    for d in range(1, docs.shape[0]):
        low = jnp.where(docs[d] <= first_row, docs[d], low)
    for d in range(docs.shape[0] - 1, 0, -1):
        high = jnp.where(docs[d] > last, docs[d], high)
    first = low // 128 * 128
    count = (high - first + 255) // 256
    return jnp.minimum(first, stream_rows - count * 256), count


def document_lanes(doc_start, first_row, rows, stream_rows):
    far = jnp.full((128 - doc_start.shape[0],), 2**30, jnp.int32)
    starts = jnp.concatenate([doc_start, far])
    ends = jnp.concatenate([doc_start[1:], jnp.full((1,), stream_rows, jnp.int32), far])
    query_pos = first_row + jnp.arange(rows, dtype=jnp.int32)[:, None]
    key_pos = jnp.arange(stream_rows, dtype=jnp.int32)[:, None]
    query_doc = ((query_pos >= starts) & (query_pos < ends)).astype(BF)
    key_doc = jnp.where((key_pos >= starts) & (key_pos < ends), 0.0, -1e30).astype(BF)
    return query_doc, key_doc


def stack_heads(x, extra=None):
    lane = lax.broadcasted_iota(jnp.int32, x.shape, 1)
    zero = jnp.zeros_like(x)
    lo = jnp.where(lane < 64, x, zero)
    hi = jnp.where(lane < 64, zero, x)
    if extra is not None:
        lo = jnp.concatenate([lo, extra], axis=1)
        hi = jnp.concatenate([hi, extra], axis=1)
    return jnp.concatenate([lo, hi], axis=0)

def pick_heads(x, tq):
    return jnp.concatenate([x[:64, :tq], x[64:, tq:]], axis=0)

def two_level(start, count, tk, body, init):
    done, carried = 0, init
    for n in (6, 3, 1):
        if n * 256 > tk:
            continue

        def step(t, c, n=n, done=done):
            at = done + t * n
            return body(pl.multiple_of(at * 256, 256), pl.multiple_of(start + at * 256, 128), n * 256, c)

        trips = (count - done) // n
        carried = lax.fori_loop(0, trips, step, carried)
        done = done + trips * n
    return carried


def fwd_kernel(tq, tk, docs, q_ref, qaug_ref, k_ref, kaug_ref, v_ref, ot_ref, lse_ref, s_scr, acc):
    def part(i, carry):
        rows = pl.ds(pl.multiple_of(i * tq, tq), tq)
        start, count = key_range(docs, lax.axis_index("ctx") * q_ref.shape[0] + i * tq, tq, k_ref.shape[0])
        rhs = stack_heads(q_ref[rows, :], qaug_ref[rows, :])

        def scores(loc, off, size, m):
            lhs = jnp.concatenate([k_ref[pl.ds(off, size), :], kaug_ref[pl.ds(off, size), :]], axis=1)
            s = lax.dot_general(lhs, rhs, NT, preferred_element_type=F32)
            s_scr[pl.ds(loc, size), :] = s
            return jnp.maximum(m, jnp.max(s.reshape(size // 8, 8, 2 * tq), axis=0))

        m8 = two_level(start, count, tk, scores, jnp.full((8, 2 * tq), -3e38, F32))
        m = jnp.max(m8, axis=0, keepdims=True)
        acc[...] = jnp.zeros_like(acc)

        def mix(loc, off, size, l8):
            p = jnp.exp(s_scr[pl.ds(loc, size), :] - m)
            acc[...] += lax.dot_general(v_ref[pl.ds(off, size), :], p.astype(BF), TN, preferred_element_type=F32)
            return l8 + jnp.sum(p.reshape(size // 8, 8, 2 * tq), axis=0)

        l8 = two_level(start, count, tk, mix, jnp.zeros((8, 2 * tq), F32))
        l = jnp.sum(l8, axis=0, keepdims=True)
        ot_ref[:, rows] = pick_heads(acc[...] / l, tq)
        lse = m + jnp.log(l)
        lse_ref[0, :, rows] = jnp.concatenate([lse[:, :tq], lse[:, tq:]], axis=0)
        return carry

    lax.fori_loop(0, q_ref.shape[0] // tq, part, 0)


def attn_fwd(docs, q, qaug, k, kaug, v, *, tq=256, tk=1536):
    T, D = q.shape
    S = k.shape[0]
    pairs = D // 128
    return pl.pallas_call(
        functools.partial(fwd_kernel, tq, tk),
        out_shape=(jax.ShapeDtypeStruct((D, T), F32), jax.ShapeDtypeStruct((pairs, 2, T), F32)),
        grid_spec=pltpu.PrefetchScalarGridSpec(
            num_scalar_prefetch=1, grid=(pairs,),
            in_specs=[pl.BlockSpec((T, 128), lambda h, b: (0, h)),
                      pl.BlockSpec((T, 128), lambda h, b: (0, 0)),
                      pl.BlockSpec((S, 128), lambda h, b: (0, h)),
                      pl.BlockSpec((S, 128), lambda h, b: (0, 0)),
                      pl.BlockSpec((S, 128), lambda h, b: (0, h))],
            out_specs=(pl.BlockSpec((128, T), lambda h, b: (h, 0)),
                       pl.BlockSpec((1, 2, T), lambda h, b: (h, 0, 0))),
            scratch_shapes=[pltpu.VMEM((S, 2 * tq), F32), pltpu.VMEM((128, 2 * tq), F32)]),
        name="attend",
    )(docs, q, qaug, k, kaug, v)


def bwd_kernel(tq, tk, docs, q_ref, qaug_ref, do_ref, lse_ref, ot_ref, k_ref, kaug_ref, v_ref,
               dq_ref, dk_ref, dv_ref, dk_acc, dv_acc, dq_acc, delta_scr):
    n_rows, n_keys = q_ref.shape[0], k_ref.shape[0]
    first_row = lax.axis_index("ctx") * n_rows
    low, high = n_keys, 0
    for i in range(n_rows // tq):
        start, count = key_range(docs, first_row + i * tq, tq, n_keys)
        low, high = jnp.minimum(low, start), jnp.maximum(high, start + count * 256)

    def over_seen(fn):
        def one(t, carry):
            fn(pl.ds(pl.multiple_of(low + t * 128, 128), 128))
            return carry

        lax.fori_loop(0, (high - low) // 128, one, 0)

    def clear(rows):
        dk_acc[rows, :] = jnp.zeros((128, 128), F32)
        dv_acc[rows, :] = jnp.zeros((128, 128), F32)

    over_seen(clear)
    mixed = ot_ref[...] * do_ref[...].astype(F32).T
    deltas = [jnp.sum(mixed[:64], axis=0, keepdims=True), jnp.sum(mixed[64:], axis=0, keepdims=True)]
    delta_scr[...] = jnp.concatenate(deltas, axis=0)

    def part(i, carry):
        part_rows = pl.ds(pl.multiple_of(i * tq, tq), tq)
        start, count = key_range(docs, first_row + i * tq, tq, n_keys)
        q, do = q_ref[part_rows, :], do_ref[part_rows, :]
        qs = stack_heads(q)
        qrhs = stack_heads(q, qaug_ref[part_rows, :])
        dos = stack_heads(do)
        lse = jnp.concatenate([lse_ref[0, 0:1, part_rows], lse_ref[0, 1:2, part_rows]], axis=1)
        delta = jnp.concatenate([delta_scr[0:1, part_rows], delta_scr[1:2, part_rows]], axis=1)
        dq_acc[...] = jnp.zeros_like(dq_acc)

        def step(loc, off, size, carry):
            rows = pl.ds(off, size)
            lhs = jnp.concatenate([k_ref[rows, :], kaug_ref[rows, :]], axis=1)
            x = lax.dot_general(lhs, qrhs, NT, preferred_element_type=F32)
            y = lax.dot_general(v_ref[rows, :], dos, NT, preferred_element_type=F32)
            p = jnp.exp(x - lse)
            ds = (p * (y - delta)).astype(BF)
            pb = p.astype(BF)
            dv_acc[rows, :] += lax.dot_general(pb, dos, NN, preferred_element_type=F32)
            dk_acc[rows, :] += lax.dot_general(ds, qs, NN, preferred_element_type=F32)
            dq_acc[...] += lax.dot_general(k_ref[rows, :], ds, TN, preferred_element_type=F32)
            return carry

        two_level(start, count, tk, step, 0)
        dq_ref[part_rows, :] = (pick_heads(dq_acc[...], tq) * SCALE).T.astype(BF)
        return carry

    lax.fori_loop(0, n_rows // tq, part, 0)
    dk_ref[...] = jnp.zeros_like(dk_ref)
    dv_ref[...] = jnp.zeros_like(dv_ref)

    def give(rows):
        dk_ref[rows, :] = dk_acc[rows, :].astype(BF)
        dv_ref[rows, :] = dv_acc[rows, :].astype(BF)

    over_seen(give)


def attn_bwd(docs, q, qaug, do, lse, ot, k, kaug, v, *, tq=256, tk=1536):
    T, D = q.shape
    S = k.shape[0]
    pairs = D // 128
    return pl.pallas_call(
        functools.partial(bwd_kernel, tq, tk),
        out_shape=(jax.ShapeDtypeStruct((T, D), BF), jax.ShapeDtypeStruct((S, D), BF), jax.ShapeDtypeStruct((S, D), BF)),
        grid_spec=pltpu.PrefetchScalarGridSpec(
            num_scalar_prefetch=1, grid=(pairs,),
            in_specs=[pl.BlockSpec((T, 128), lambda h, b: (0, h)),
                      pl.BlockSpec((T, 128), lambda h, b: (0, 0)),
                      pl.BlockSpec((T, 128), lambda h, b: (0, h)),
                      pl.BlockSpec((1, 2, T), lambda h, b: (h, 0, 0)),
                      pl.BlockSpec((128, T), lambda h, b: (h, 0)),
                      pl.BlockSpec((S, 128), lambda h, b: (0, h)),
                      pl.BlockSpec((S, 128), lambda h, b: (0, 0)),
                      pl.BlockSpec((S, 128), lambda h, b: (0, h))],
            out_specs=(pl.BlockSpec((T, 128), lambda h, b: (0, h)),
                       pl.BlockSpec((S, 128), lambda h, b: (0, h)),
                       pl.BlockSpec((S, 128), lambda h, b: (0, h))),
            scratch_shapes=[pltpu.VMEM((S, 128), F32), pltpu.VMEM((S, 128), F32), pltpu.VMEM((128, 2 * tq), F32),
                            pltpu.VMEM((2, T), F32)]),
        name="attend_back",
    )(docs, q, qaug, do, lse, ot, k, kaug, v)


def middle_kernel(attn_ref, in_ref, cot_ref, vec_ref, wo_ref, wu_ref, down_own, down_far,
                  out_ref, sum1_ref, do_ref, grads_ref, up_out, down_out, attn_out,
                  wo, wu, wd, attn_b, first, hat1, scale1, first_b, act, slope, sum2, down_b, up_b, first_b2, first_t,
                  g_up, g_down, g_out, sem_w, sem_d, sem_o):
    rows, wide = in_ref.shape[0], wu.shape[1]
    a, w = lax.axis_index("ctx"), lax.axis_index("wsh")
    y, c = w // 2, lax.rem(w, 2)
    core_peer = (a, y * 2 + (1 - c))
    tall = down_own.shape[0]
    MESH = pl.DeviceIdType.MESH
    barrier = pltpu.get_barrier_semaphore()
    pl.semaphore_signal(barrier, inc=1, device_id=core_peer, device_id_type=MESH)
    pl.semaphore_wait(barrier, 1)
    passed = []
    for s, (ref, owner) in enumerate(((down_own, w), (down_far, (1 - y) * 2 + c))):
        there = wd.at[pl.ds(pl.multiple_of(owner * tall, 16), tall), :]
        passed.append(pltpu.make_async_remote_copy(
            src_ref=ref, dst_ref=there, send_sem=sem_d.at[0, s], recv_sem=sem_d.at[1, s],
            device_id=core_peer, device_id_type=MESH))
        passed[-1].start()
        pltpu.make_async_copy(ref, there, sem_w.at[2 + s]).start()
    loading = [pltpu.make_async_copy(wo_ref, wo, sem_w.at[0]), pltpu.make_async_copy(wu_ref, wu, sem_w.at[1])]
    for copy in loading:
        copy.start()

    def arrived(j):
        if j < 2:
            loading[j].wait()
        else:
            for s, owner in enumerate((w, (1 - y) * 2 + c)):
                there = wd.at[pl.ds(pl.multiple_of(owner * tall, 16), tall), :]
                pltpu.make_async_copy(there, there, sem_w.at[2 + s]).wait()
                passed[s].wait_recv()

    grads_ref[...] = jnp.zeros_like(grads_ref)
    attn_b[...] = attn_ref[...].astype(BF)
    out_b, attn_g, attn_s, down_bias, final_g, final_s = [vec_ref[i : i + 1, :] for i in range(2, 8)]
    arrived(0)
    block = 256

    def over_rows(fn):
        def one(i, carry):
            fn(pl.ds(pl.multiple_of(i * block, block), block))
            return carry

        lax.fori_loop(0, rows // block, one, 0)

    def norm(values):
        average = jnp.mean(values, axis=-1, keepdims=True)
        centred = values - average
        scale = lax.rsqrt(jnp.mean(centred * centred, axis=-1, keepdims=True) + EPS)
        return centred * scale, scale

    def norm_back(grad, hat, scale, gain):
        g = grad * gain
        return scale * (g - jnp.mean(g, axis=-1, keepdims=True) - hat * jnp.mean(g * hat, axis=-1, keepdims=True))

    def note(row, values):
        grads_ref[row : row + 1, :] += jnp.sum(values, axis=0, keepdims=True)

    def branch_part(r):
        a = attn_b[:, r].T
        v = lax.dot_general(a, wo[...], NN, preferred_element_type=F32) + out_b + in_ref[r, :].astype(F32)
        hat, scale = norm(v)
        hat1[r, :] = hat
        scale1[r, :] = scale
        f = hat * attn_g + attn_s
        first[r, :] = f
        first_b[r, :] = f.astype(BF)

    over_rows(branch_part)
    arrived(1)
    cols = vec_ref.shape[1]

    def over_wide(fn):
        def one(i, carry):
            fn(pl.ds(pl.multiple_of(i * cols, cols), cols), i)
            return carry

        lax.fori_loop(0, wide // cols, one, 0)

    def up_part(n, i):
        u = lax.dot_general(first_b[...], wu[:, n], NN, preferred_element_type=F32) + vec_ref[pl.ds(8 + i, 1), :]
        half = 0.5 * (1.0 + lax.erf(u * ROOT_HALF))
        act[:, n] = (u * half).astype(BF)
        slope[:, n] = half + u * (0.3989422804014327 * jnp.exp(-0.5 * u * u))

    over_wide(up_part)
    arrived(2)

    def down_part(r):
        v = lax.dot_general(act[r, :], wd[...], NN, preferred_element_type=F32) + down_bias + first[r, :]
        hat, scale = norm(v)
        out_ref[r, :] = (hat * final_g + final_s).astype(BF)
        cot = cot_ref[r, :].astype(F32)
        note(6, cot * hat)
        note(7, cot)
        g = norm_back(cot, hat, scale, final_g)
        sum2[r, :] = g
        rounded = g.astype(BF)
        down_b[r, :] = rounded
        note(5, rounded.astype(F32))

    over_rows(down_part)

    def up_back(n, i):
        g = lax.dot_general(down_b[...], wd[n, :], NT, preferred_element_type=F32) * slope[:, n]
        rounded = g.astype(BF)
        up_b[:, n] = rounded
        grads_ref[pl.ds(8 + i, 1), :] = jnp.sum(rounded.astype(F32), axis=0, keepdims=True)

    over_wide(up_back)

    def first_part(r):
        g = sum2[r, :] + lax.dot_general(up_b[r, :], wu[...], NT, preferred_element_type=F32)
        hat = hat1[r, :]
        note(3, g * hat)
        note(4, g)
        s1 = norm_back(g, hat, scale1[r, :], attn_g)
        sum1_ref[r, :] = s1
        rounded = s1.astype(BF)
        note(2, rounded.astype(F32))
        first_b2[r, :] = rounded

    over_rows(first_part)

    def do_part(r):
        do_ref[r, :] = lax.dot_general(first_b2[r, :], wo[...], NT, preferred_element_type=F32).astype(BF)

    over_rows(do_part)

    def wide_grads(n, i):
        g_down[n, :] = lax.dot_general(act[:, n].T, down_b[...], NN, preferred_element_type=F32).astype(BF)
        pltpu.make_async_copy(g_down.at[n, :], down_out.at[n, :], sem_o.at[0, i]).start()
        g_up[:, n] = lax.dot_general(first_t[...], up_b[:, n], NN, preferred_element_type=F32).astype(BF)
        pltpu.make_async_copy(g_up.at[:, n], up_out.at[:, n], sem_o.at[1, i]).start()

    first_t[...] = first_b[...].T
    over_wide(wide_grads)
    g_out[...] = lax.dot_general(attn_b[...], first_b2[...], NN, preferred_element_type=F32).astype(BF)
    pltpu.make_async_copy(g_out, attn_out, sem_o.at[2, 0]).start()

    def wide_end(n, i):
        pltpu.make_async_copy(g_down.at[n, :], down_out.at[n, :], sem_o.at[0, i]).wait()
        pltpu.make_async_copy(g_up.at[:, n], up_out.at[:, n], sem_o.at[1, i]).wait()

    over_wide(wide_end)
    pltpu.make_async_copy(g_out, attn_out, sem_o.at[2, 0]).wait()
    for copy in passed:
        copy.wait_send()


def middle(attn_t, inputs, cotangent, vec, out_w, up_w, down_own, down_far):
    rows = inputs.shape[0]
    wide = up_w.shape[1]
    vm, dma, shape = pltpu.VMEM, pltpu.SemaphoreType.DMA, jax.ShapeDtypeStruct
    any_spec = pl.BlockSpec(memory_space=pltpu.HBM)
    vm_spec = pl.BlockSpec(memory_space=pltpu.VMEM)
    return pl.pallas_call(
        middle_kernel,
        out_shape=(shape((rows, D), BF), shape((rows, D), F32), shape((rows, D), BF), shape((16, D), F32),
                   shape((D, wide), BF), shape((wide, D), BF), shape((D, D), BF)),
        in_specs=[vm_spec] * 4 + [any_spec] * 4,
        out_specs=(vm_spec,) * 4 + (any_spec,) * 3,
        scratch_shapes=[
            vm((D, D), BF), vm((D, wide), BF), vm((wide, D), BF), vm((D, rows), BF), vm((rows, D), F32),
            vm((rows, D), F32), vm((rows, 1), F32), vm((rows, D), BF), vm((rows, wide), BF), vm((rows, wide), F32),
            vm((rows, D), F32), vm((rows, D), BF), vm((rows, wide), BF), vm((rows, D), BF), vm((D, rows), BF),
            vm((D, wide), BF), vm((wide, D), BF), vm((D, D), BF), dma((4,)), dma((2, 2)), dma((3, wide // D)),
        ],
        compiler_params=pltpu.CompilerParams(collective_id=3, has_side_effects=True, vmem_limit_bytes=63 * 2**20),
        name="middle",
    )(attn_t, inputs, cotangent, vec, out_w, up_w, down_own, down_far)


def reach(n_ctx):
    return n_ctx // 2


def finish_kernel(sources, n_parts, *refs):
    parts = refs[:n_parts]
    (vec_ref, dk_ref, dv_ref, tok_ref, dq_ref, w_ref, own_in_ref, mine_tok_ref,
     out_ref, vec_out, wide_out, grad_ref,
     mine, buf_a, buf_h, buf_b, buf_s, buf_c, buf_d, buf_e, gbf,
     sums, heard, line,
     loads, weights, acc, dq, own, bias,
     run_part, from_x, from_z, far_z, last_x,
     sem_l, sem_a, sem_b, sem_c, sem_d, sem_v, sem_x, sem_z, sem_far, sem_load, sem_in) = refs[n_parts:]
    n_ready = len(sources)
    n_chunks = out_ref.shape[0]
    n_ctx, n_wsh = lax.axis_size("ctx"), lax.axis_size("wsh")
    zs = n_ctx // 2
    a, w = lax.axis_index("ctx"), lax.axis_index("wsh")
    z, x = a // 2, lax.rem(a, 2)
    y, c = w // 2, lax.rem(w, 2)
    core_peer = (a, y * 2 + (1 - c))
    y_peer = (a, (1 - y) * 2 + c)
    x_peer = (z * 2 + (1 - x), w)
    low, high = lax.rem(z, 2), z // 2
    pair_peer = ((z + 1 - 2 * low) * 2 + x, w)
    skip_peer = (lax.rem(z + 2, zs) * 2 + x, w)
    up_peer, down_peer = (a + 2, w), (a - 2, w)
    near = reach(n_ctx)
    hops = near // 2
    MESH = pl.DeviceIdType.MESH

    rows = out_ref.shape[1]
    half = out_ref.shape[2] // 2
    piece = rows // zs
    tall = own.shape[0]
    cut = from_x.shape[1]

    def z_peer(d):
        return (lax.rem(z + d, zs) * 2 + x, w)

    barrier = pltpu.get_barrier_semaphore()
    for dev in [core_peer, y_peer, x_peer] + [z_peer(d) for d in range(1, zs)]:
        pl.semaphore_signal(barrier, inc=1, device_id=dev, device_id_type=MESH)
    def send(src, dst, sems, idx, dev):
        return pltpu.make_async_remote_copy(
            src_ref=src, dst_ref=dst, send_sem=sems.at[(0,) + idx], recv_sem=sems.at[(1,) + idx],
            device_id=dev, device_id_type=MESH)

    def wait_in(ref, sems, idx):
        send(ref, ref, sems, idx, core_peer).wait_recv()

    def wait_out(ref, sems, idx):
        send(ref, ref, sems, idx, core_peer).wait_send()

    def distance(i):
        return (hops - i // 4) * (1 - 2 * lax.rem(i // 2, 2))

    def position(i):
        dz = distance(i)
        mine_too = lax.rem(i, 2)
        run = 2 * (z + dz) + (1 - x) * (1 - mine_too) + x * mine_too
        return run, mine_too, (z + dz >= 0) & (z + dz < zs) & (jnp.abs(run - a) <= near)

    n_pos = 4 * hops + 2

    def load(i):
        run, _mine_too, there = position(i)
        return there, [
            pltpu.make_async_copy(src.at[run], loads.at[lax.rem(i, 2), j], sem_load.at[lax.rem(i, 2), j])
            for j, src in enumerate((dk_ref, dv_ref, tok_ref))
        ]

    def load_start(i):
        there, copies = load(i)

        @pl.when(there & (i < n_pos))
        def _():
            for copy in copies:
                copy.start()

    def share(k, owner):
        if k < n_ready:
            p, row0, col0 = sources[k]
            return parts[p].at[owner, pl.ds(row0, rows), pl.ds(col0, 2 * half)]
        return gbf.at[k - n_ready, owner]

    def share_load(k):
        for yy in range(2):
            pltpu.make_async_copy(share(k, yy * 2 + c), mine.at[k % 4, yy], sem_l.at[k]).start()

    def share_send(k):
        for yy in range(2):
            send(share(k, yy * 2 + (1 - c)), buf_a.at[k, yy], sem_a, (k,), core_peer).start()

    load_start(0)
    fetch = [pltpu.make_async_copy(w_ref, weights, sem_in.at[0]), pltpu.make_async_copy(dq_ref, dq, sem_in.at[1]),
             pltpu.make_async_copy(own_in_ref, own, sem_in.at[2])]
    for copy in fetch:
        copy.start()
    for k in range(4):
        share_load(k)
    acc[...] = jnp.zeros_like(acc)
    bias[...] = jnp.zeros_like(bias)
    pl.semaphore_wait(barrier, zs + 2)
    for k in range(n_ready):
        share_send(k)
    fetch[0].wait()

    near_rows, far_rows = pl.ds(0, cut), pl.ds(cut, tall - cut)

    def unit(i):
        run, mine_too, there = position(i)
        at = lax.rem(i, 2)
        load_start(i + 1)

        @pl.when(there)
        def _():
            for copy in load(i)[1]:
                copy.wait()

            def tokens_part(r, carry):
                rs = pl.ds(pl.multiple_of(r * 256, 256), 256)
                g = lax.dot_general(loads[at, 0, rs, :], weights[0], NT, preferred_element_type=F32)
                g = g + lax.dot_general(loads[at, 1, rs, :], weights[1], NT, preferred_element_type=F32)
                run_part[i, rs, :] = g.astype(BF)
                bias[0:8, :] += jnp.sum(loads[at, 1, rs, :].astype(F32).reshape(32, 8, 2 * half), axis=0)
                return carry

            lax.fori_loop(0, tall // 256, tokens_part, 0)

            @pl.when(mine_too == 0)
            def _():
                send(run_part.at[i, near_rows, :], from_x.at[i // 2], sem_x, (i // 2,), x_peer).start()

            @pl.when(i < 4)
            def _():
                far_send(i)

            def weights_part(r, carry):
                fs = pl.ds(pl.multiple_of(r * 256, 256), 256)
                flipped = loads[at, 2, :, fs].T
                for j in range(2):
                    acc[j, fs, :] += lax.dot_general(flipped, loads[at, j], NN, preferred_element_type=F32)
                return carry

            lax.fori_loop(0, 2 * half // 256, weights_part, 0)

    def from_below(i):
        dz = distance(i)
        step = 1 - 2 * lax.rem(i // 2, 2)
        sender, target = z - step, z - step + dz
        side = jnp.abs(2 * dz + (1 - 2 * x) * (1 - lax.rem(i, 2))) <= near
        return (sender >= 0) & (sender < zs) & (target >= 0) & (target < zs) & side

    def toward(i, copy_of):
        step = 1 - 2 * lax.rem(i // 2, 2)

        @pl.when(step == 1)
        def _():
            copy_of(up_peer).start()

        @pl.when(step == -1)
        def _():
            copy_of(down_peer).start()

    def far_send(i):
        toward(i, lambda dev: send(run_part.at[i, far_rows, :], far_z.at[i], sem_far, (i,), dev))

    def far_pass(i):
        _run, _mine_too, there = position(i)

        @pl.when(there)
        def _():
            @pl.when(from_below(i - 4))
            def _():
                wait_in(far_z.at[i - 4], sem_far, (i - 4,))
                run_part[i, far_rows, :] = (
                    run_part[i, far_rows, :].astype(F32) + far_z[i - 4].astype(F32)).astype(BF)

            far_send(i)

    def far_end():
        for col in range(2):
            total = n_pos - 2 + col
            for src in (4 + col, 6 + col):
                @pl.when(from_below(src))
                def _():
                    wait_in(far_z.at[src], sem_far, (src,))
                    run_part[total, far_rows, :] = (
                        run_part[total, far_rows, :].astype(F32) + far_z[src].astype(F32)).astype(BF)
            if col == 0:
                send(run_part.at[total, far_rows, :], last_x, sem_x, (n_pos // 2,), x_peer).start()
        own[far_rows, :] += run_part[n_pos - 1, far_rows, :].astype(F32)

    def near_pass(n):
        dz = distance(2 * n)
        i = 2 * n + 1

        @pl.when((z + dz >= 0) & (z + dz < zs))
        def _():
            @pl.when(jnp.abs(2 * dz + 2 * x - 1) <= near)
            def _():
                wait_in(from_x.at[n], sem_x, (n,))
                run_part[i, near_rows, :] = (
                    run_part[i, near_rows, :].astype(F32) + from_x[n].astype(F32)).astype(BF)

            @pl.when((n >= 2) & from_below(i - 4))
            def _():
                wait_in(from_z.at[n - 2], sem_z, (n - 2,))
                run_part[i, near_rows, :] = (
                    run_part[i, near_rows, :].astype(F32) + from_z[n - 2].astype(F32)).astype(BF)

            toward(i, lambda dev: send(run_part.at[i, near_rows, :], from_z.at[n], sem_z, (n,), dev))

    def near_own():
        n = n_pos // 2 - 1
        wait_in(from_x.at[n], sem_x, (n,))
        own[near_rows, :] += run_part[n_pos - 1, near_rows, :].astype(F32) + from_x[n].astype(F32)

    def near_end():
        for n in (2, 3):
            @pl.when(from_below(2 * n + 1))
            def _():
                wait_in(from_z.at[n], sem_z, (n,))
                own[near_rows, :] += from_z[n].astype(F32)

    def add(p, q):
        return (p.astype(F32) + q.astype(F32)).astype(BF)

    def column(side):
        return pl.ds(pl.multiple_of(side * half, 128), half)

    def band(start, size):
        return pl.ds(pl.multiple_of(start, 16), size)

    def stage_b(k):
        at = lax.rem(k, 4)
        pltpu.make_async_copy(mine.at[at], mine.at[at], sem_l.at[k]).wait()
        wait_in(buf_a.at[k], sem_a, (k,))
        buf_h[k] = add(mine[at, 1 - y], buf_a[k, 1 - y])
        send(buf_h.at[k], buf_b.at[k], sem_b, (k,), y_peer).start()
        buf_a[k, y] = add(mine[at, y], buf_a[k, y])

    def stage_c(k):
        wait_in(buf_b.at[k], sem_b, (k,))
        buf_s[k] = add(buf_a[k, y, :, column(1 - x)], buf_b[k, :, column(1 - x)])
        send(buf_s.at[k], buf_c.at[k], sem_c, (0, k), x_peer).start()

    my_two, other_two = band(low * 2 * piece, 2 * piece), band((1 - low) * 2 * piece, 2 * piece)
    my_one, other_one = band(high * piece, piece), band((1 - high) * piece, piece)
    my_rows = band(low * 2 * piece + high * piece, piece)

    def stage_d(k):
        wait_in(buf_c.at[k], sem_c, (0, k))
        cols = column(x)
        joined = buf_a[k, y, :, cols].astype(F32) + buf_b[k, :, cols].astype(F32) + buf_c[k].astype(F32)
        buf_c[k] = joined.astype(BF)
        send(buf_c.at[k, other_two, :], buf_d.at[k], sem_d, (0, k), pair_peer).start()

    def stage_d2(k):
        wait_in(buf_d.at[k], sem_d, (0, k))
        buf_d[k] = add(buf_d[k], buf_c[k, my_two, :])
        send(buf_d.at[k, other_one, :], buf_e.at[k], sem_d, (1, k), skip_peer).start()

    def stage_e(k):
        wait_in(buf_e.at[k], sem_d, (1, k))
        buf_e[k] = add(buf_e[k], buf_d[k, my_one, :])
        out_ref[k, my_rows, column(x)] = buf_e[k]
        send(buf_e.at[k], out_ref.at[k, my_rows, column(x)], sem_d, (2, k), skip_peer).start()

    def stage_e2(k):
        wait_in(buf_e.at[k], sem_d, (2, k))
        there = out_ref.at[k, my_two, column(x)]
        send(there, there, sem_d, (3, k), pair_peer).start()

    def stage_f(k):
        wait_in(buf_d.at[k], sem_d, (3, k))
        there = out_ref.at[k, :, column(x)]
        send(there, there, sem_c, (1, k), x_peer).start()

    def guarded(fn, k, first, last):
        @pl.when((k >= first) & (k < last))
        def _():
            fn(k)

    def chunk_step(m):
        for lag, stage in enumerate((stage_c, stage_d, stage_d2, stage_e, stage_e2, stage_f)):
            guarded(stage, m - (lag and lag + 1), 0, n_chunks)

    def first_step(t, carry):
        guarded(unit, t, 0, n_pos)
        for j in range(2):
            guarded(stage_b, 2 * t + j, 0, n_ready)
        for k in range(4, n_ready):
            @pl.when(t == (k - 4) // 2)
            def _():
                share_load(k)

        @pl.when(lax.rem(t, 2) == 1)
        def _():
            guarded(near_pass, t // 2 - 1, 0, 4)

        guarded(far_pass, t - 2, 4, 8)

        @pl.when((lax.rem(t, 2) == 0) & (t >= 2))
        def _():
            chunk_step(t // 2 - 1)

        return carry

    lax.fori_loop(0, n_pos, first_step, 0)
    done = n_pos // 2 - 1

    fetch[1].wait()
    fetch[2].wait()
    own_tok = pltpu.make_async_copy(mine_tok_ref, loads.at[0, 2], sem_load.at[0, 2])
    own_tok.start()

    def to_bf(j, target):
        for owner in range(n_wsh):
            gbf[target, owner] = acc[j, owner * rows : (owner + 1) * rows, :].astype(BF)
        share_load(n_ready + target)
        share_send(n_ready + target)

    to_bf(0, 0)
    to_bf(1, 1)
    own_tok.wait()

    def query_part(r, carry):
        fs = pl.ds(pl.multiple_of(r * 256, 256), 256)
        acc[0, fs, :] = lax.dot_general(loads[0, 2, :, fs].T, dq[...], NN, preferred_element_type=F32)
        return carry

    lax.fori_loop(0, 2 * half // 256, query_part, 0)
    to_bf(0, 2)

    def query_tokens(r, carry):
        rs = pl.ds(pl.multiple_of(r * 256, 256), 256)
        own[rs, :] += lax.dot_general(dq[rs, :], weights[2], NT, preferred_element_type=F32)
        bias[8:16, :] += jnp.sum(dq[rs, :].astype(F32).reshape(32, 8, 2 * half), axis=0)
        return carry

    lax.fori_loop(0, tall // 256, query_tokens, 0)

    sums[0] = vec_ref[...]
    sums[0, 0:1, :] = jnp.sum(bias[8:16, :], axis=0, keepdims=True)
    sums[0, 1:2, :] = jnp.sum(bias[0:8, :], axis=0, keepdims=True)
    pair = (core_peer, y_peer, x_peer)

    def vec_send(stage):
        send(sums.at[stage], heard.at[stage], sem_v, (stage,), pair[stage]).start()

    def vec_stage(stage):
        wait_in(heard.at[stage], sem_v, (stage,))
        total = sums[stage] + heard[stage]
        sums[stage + 1] = total
        if stage < 2:
            vec_send(stage + 1)
        else:
            line[z] = total
            for d in range(1, zs):
                send(sums.at[3], line.at[z], sem_v, (3,), z_peer(d)).start()

    def vec_last():
        wait_in(line.at[pl.ds(0, zs - 1)], sem_v, (3,))
        total = line[0]
        for d in range(1, zs):
            total = total + line[d]
        small, wide = total[0:8, 0:rows], total[8:9, :]
        for owner in range(1, n_wsh):
            small = jnp.where(w == owner, total[0:8, owner * rows : (owner + 1) * rows], small)
            wide = jnp.where(w == owner, total[8 + owner : 9 + owner, :], wide)
        vec_out[...] = small
        wide_out[...] = wide

    vec_send(0)

    def second_step(m, carry):
        guarded(stage_b, m - done + n_ready, n_ready, n_chunks)
        chunk_step(m)
        guarded(lambda k: near_own(), m - done, 0, 1)
        for stage in range(3):
            guarded(lambda k: vec_stage(stage), m - done - 1 - stage, 0, 1)
        guarded(lambda k: near_end(), m - done - 3, 0, 1)
        guarded(lambda k: far_end(), m - done - 4, 0, 1)
        guarded(lambda k: vec_last(), m - done - 5, 0, 1)
        return carry

    lax.fori_loop(done, n_chunks + 6, second_step, 0)
    wait_in(last_x, sem_x, (n_pos // 2,))
    own[far_rows, :] += last_x[...].astype(F32)
    grad_ref[...] = own[...].astype(BF)

    def drain(k, carry):
        wait_in(buf_s.at[k], sem_c, (1, k))
        wait_out(buf_a.at[k], sem_a, (k,))
        wait_out(buf_b.at[k], sem_b, (k,))
        wait_out(buf_s.at[k], sem_c, (0, k))
        wait_out(buf_s.at[k], sem_c, (1, k))
        wait_out(buf_d.at[k], sem_d, (0, k))
        wait_out(buf_e.at[k], sem_d, (1, k))
        wait_out(buf_e.at[k], sem_d, (2, k))
        wait_out(buf_d.at[k], sem_d, (3, k))
        return carry

    lax.fori_loop(0, n_chunks, drain, 0)
    for stage in range(3):
        wait_out(heard.at[stage], sem_v, (stage,))
    wait_out(line.at[pl.ds(0, zs - 1)], sem_v, (3,))
    wait_out(last_x, sem_x, (n_pos // 2,))

    def drain_runs(i, carry):
        _run, mine_too, there = position(i)

        @pl.when(there)
        def _():
            wait_out(far_z.at[i], sem_far, (i,))

            @pl.when(mine_too == 1)
            def _():
                wait_out(from_z.at[i // 2], sem_z, (i // 2,))

        return carry

    lax.fori_loop(0, n_pos - 2, drain_runs, 0)

    def drain_x(n, carry):
        _run, _mine_too, there = position(2 * n)

        @pl.when(there)
        def _():
            wait_out(from_x.at[n], sem_x, (n,))

        return carry

    lax.fori_loop(0, n_pos // 2, drain_x, 0)


def widen_kernel(spans, in_ref, small_ref, wide_ref, grad_ref, layer_ref, grad_out, layer_out, *outs):
    grad_out[...] = grad_ref[...]
    layer_out[...] = layer_ref[...]
    for (first, down, across), out in zip(spans, outs):
        for r in range(down):
            for col in range(across):
                out[r, :, col * D : (col + 1) * D] = in_ref[first + r * across + col].astype(F32)
    vectors = outs[len(spans) :]
    for i, out in enumerate(vectors[:-1]):
        out[...] = small_ref[i : i + 1, :]
    vectors[-1][...] = wide_ref[...]


def widen(summed, spans, small, wide, grad_inputs, layer_out):
    n, rows, _width = summed.shape
    part = rows // 2
    tokens = pl.BlockSpec((grad_inputs.shape[0] // 2, D), lambda i: (i, 0))
    shape = jax.ShapeDtypeStruct
    vectors = [(1, small.shape[1])] * small.shape[0] + [wide.shape]
    outs = pl.pallas_call(
        functools.partial(widen_kernel, spans),
        grid=(2,),
        out_shape=[shape(grad_inputs.shape, BF)] * 2
        + [shape((down, rows, across * D), F32) for _first, down, across in spans]
        + [shape(v, F32) for v in vectors],
        in_specs=[pl.BlockSpec((n, part, D), lambda i: (0, i, 0)), pl.BlockSpec(small.shape, lambda i: (0, 0)),
                  pl.BlockSpec(wide.shape, lambda i: (0, 0)), tokens, tokens],
        out_specs=[tokens] * 2 + [pl.BlockSpec((down, part, across * D), lambda i: (0, i, 0)) for _first, down, across in spans]
        + [pl.BlockSpec(v, lambda i: (0, 0)) for v in vectors],
        name="widen",
    )(summed, small, wide, grad_inputs, layer_out)
    grad_inputs, layer_out, mats, vectors = outs[0], outs[1], outs[2 : len(spans) + 2], outs[len(spans) + 2 :]
    return grad_inputs, layer_out, [o.reshape(-1, o.shape[2]) for o in mats], [v.reshape(-1) for v in vectors[:-1]], vectors[-1].reshape(-1)


def finish(matrices, vec, grad_k, grad_v, all_tokens, grad_q, kvq_w, own_grad, inputs, layer_out):
    n_ctx, n_wsh = lax.axis_size("ctx"), lax.axis_size("wsh")
    zs, hops = n_ctx // 2, reach(n_ctx) // 2
    rows = D // n_wsh
    parts, sources, spans = [], [], []
    for p, g in enumerate(matrices):
        down, across = g.shape[0] // D, g.shape[1] // D
        parts.append(g.astype(BF).reshape(n_wsh, down * rows, across * D))
        spans.append((len(sources), down, across))
        sources += [(p, r * rows, col * D) for r in range(down) for col in range(across)]
    n = len(sources) + 3
    spans += [(len(sources) + j, 1, 1) for j in range(3)]
    half, piece, tall = D // 2, rows // zs, inputs.shape[0]
    n_pos, cut = 4 * hops + 2, tall * 5 // 8
    vm, dma, shape = pltpu.VMEM, pltpu.SemaphoreType.DMA, jax.ShapeDtypeStruct
    any_spec = pl.BlockSpec(memory_space=pltpu.HBM)
    vm_spec = pl.BlockSpec(memory_space=pltpu.VMEM)
    summed, small, wide, grad_own = pl.pallas_call(
        functools.partial(finish_kernel, sources, len(parts)),
        out_shape=(shape((n, rows, D), BF), shape((8, rows), F32), shape((1, D), F32), shape((tall, D), BF)),
        in_specs=[any_spec] * len(parts) + [vm_spec] + [any_spec] * 7,
        out_specs=(vm_spec,) * 4,
        scratch_shapes=[
            vm((4, 2, rows, D), BF), vm((n, 2, rows, D), BF), vm((n, rows, D), BF), vm((n, rows, D), BF),
            vm((n, rows, half), BF), vm((n, rows, half), BF), vm((n, 2 * piece, half), BF), vm((n, piece, half), BF),
            vm((3, n_wsh, rows, D), BF),
            vm((4,) + vec.shape, F32), vm((3,) + vec.shape, F32), vm((zs,) + vec.shape, F32),
            vm((2, 3, tall, D), BF), vm((3, D, D), BF), vm((2, D, D), F32), vm((tall, D), BF), vm((tall, D), F32),
            vm((16, D), F32),
            vm((n_pos, tall, D), BF), vm((n_pos // 2, cut, D), BF), vm((4, cut, D), BF),
            vm((n_pos - 2, tall - cut, D), BF), vm((tall - cut, D), BF),
            dma((n,)), dma((2, n)), dma((2, n)), dma((2, 2, n)), dma((2, 4, n)), dma((2, 4)),
            dma((2, n_pos // 2 + 1)), dma((2, 4)), dma((2, n_pos - 2)), dma((2, 3)), dma((3,)),
        ],
        compiler_params=pltpu.CompilerParams(collective_id=2, has_side_effects=True, vmem_limit_bytes=63 * 2**20),
        name="finish",
    )(*parts, vec, grad_k, grad_v, all_tokens, grad_q, kvq_w, own_grad, inputs)
    return widen(summed, spans, small, wide, grad_own, layer_out)


def gather_kernel(cut, tok_ref, docs_ref, wk_ref, wv_ref, wq_ref, wo_ref, wu_ref, vec_ref,
                  tok_out, k_out, v_out, q_out, w_out, vec_out, wo_out, wu_out, query_doc, key_doc,
                  tok, kbuf, vbuf, qbuf, wbuf, vecs, wo, wu, kdoc,
                  sem_in, sem_out, sem_w, sem_l, sem_o):
    n_ctx = lax.axis_size("ctx")
    zs = n_ctx // 2
    a, w = lax.axis_index("ctx"), lax.axis_index("wsh")
    z, x = a // 2, lax.rem(a, 2)
    y, c = w // 2, lax.rem(w, 2)
    core_peer = (a, y * 2 + (1 - c))
    y_peer = (a, (1 - y) * 2 + c)
    x_peer = (z * 2 + (1 - x), w)
    up, down = (a + 2, w), (a - 2, w)
    near = reach(n_ctx)
    MESH = pl.DeviceIdType.MESH
    n_slices = sem_in.shape[1]
    tall = tok.shape[1] // n_slices
    own = wk_ref.shape[0]
    far = 4 * (near // 2 + 1)

    barrier = pltpu.get_barrier_semaphore()
    around = [(lax.rem(z + d, zs) * 2 + x, w) for d in (1, zs - 1)]
    for dev in [core_peer, y_peer, x_peer] + around:
        pl.semaphore_signal(barrier, inc=1, device_id=dev, device_id_type=MESH)
    pl.semaphore_wait(barrier, 5)

    def relative(u):
        dz = (u // 4) * (1 - 2 * lax.rem(u, 2))
        other = lax.rem(u // 2, 2)
        run = 2 * (z + dz) + (x + other - 2 * x * other)
        there = (z + dz >= 0) & (z + dz < zs) & (jnp.abs(run - a) <= near) & ((u >= 4) | (lax.rem(u, 2) == 0))
        return run, dz, other, there

    def rows(s):
        return pl.ds(pl.multiple_of(s * tall, tall), tall)

    def remote(src, dst, send_sem, recv_sem, dev):
        return pltpu.make_async_remote_copy(
            src_ref=src, dst_ref=dst, send_sem=send_sem, recv_sem=recv_sem, device_id=dev, device_id_type=MESH)

    def routes(u, s):
        run, dz, other, there = relative(u)
        z_first = s < cut
        to_x = there & (z_first | (dz == 0)) & (other == 0) & (jnp.abs(run - x_peer[0]) <= near)
        along = there & ((other == 0) | jnp.logical_not(z_first))
        to_up = along & (dz <= 0) & (z + 1 < zs) & (jnp.abs(run - (a + 2)) <= near)
        to_down = along & (dz >= 0) & (z > 0) & (jnp.abs(run - (a - 2)) <= near)
        return run, ((0, x_peer, to_x), (1, up, to_up), (2, down, to_down))

    def pass_on(u, s):
        run, where = routes(u, s)
        for d, dev, ok in where:
            @pl.when(ok)
            def _():
                source = tok_ref if isinstance(u, int) and u == 0 else tok.at[run]
                remote(source.at[rows(s), :], tok.at[run, rows(s), :], sem_out.at[d, u, s], sem_in.at[run, s], dev).start()

    def await_slice(u, s):
        run, _dz, _other, there = relative(u)

        @pl.when(there)
        def _():
            remote(tok.at[run, rows(s), :], tok.at[run, rows(s), :], sem_out.at[0, 0, 0], sem_in.at[run, s], x_peer).wait_recv()

    def start_own(s, carry):
        pass_on(0, s)
        return carry

    def weight_rows(owner):
        return pl.ds(pl.multiple_of(owner * own, 16), own)

    def shard(m, owner):
        if m == 3:
            return vecs.at[owner]
        return (wbuf.at[0], wbuf.at[1], wbuf.at[2], None, wo, wu)[m].at[weight_rows(owner), :]

    vecs[w, 0 : vec_ref.shape[0], :] = vec_ref[...]
    shards = (wk_ref, wv_ref, wq_ref, vecs.at[w], wo_ref, wu_ref)
    for m in (3, 0, 1, 2, 4, 5):
        remote(shards[m], shard(m, w), sem_w.at[0, 1, m], sem_w.at[1, 1, m], y_peer).start()
        remote(shards[m], shard(m, w), sem_w.at[0, 0, m], sem_w.at[1, 0, m], core_peer).start()
        if m != 3:
            pltpu.make_async_copy(shards[m], shard(m, w), sem_w.at[0, 3, m]).start()
    lax.fori_loop(0, n_slices, start_own, 0)
    pltpu.make_async_copy(tok_ref, tok.at[a], sem_l.at[4]).start()

    for j in range(n_ctx):
        @pl.when(jnp.abs(j - a) > near)
        def _():
            tok[j] = jnp.zeros_like(tok[j])

    n_rows = tok.shape[1]

    def is_own_lane(first):
        pos = first + lax.broadcasted_iota(jnp.int32, (n_rows, 128), 0)
        doc = jnp.full((n_rows, 128), -1, jnp.int32)
        for d in range(docs_ref.shape[1]):
            doc = doc + jnp.where(pos >= docs_ref[0, d], 1, 0)
        return lax.broadcasted_iota(jnp.int32, (n_rows, 128), 1) == doc

    def key_lanes(j, carry):
        kdoc[pl.ds(pl.multiple_of(j * n_rows, n_rows), n_rows), :] = jnp.where(
            is_own_lane(j * n_rows), 0.0, -1e30).astype(BF)
        return carry

    lax.fori_loop(0, n_ctx, key_lanes, 0)
    pltpu.make_async_copy(kdoc, key_doc, sem_l.at[3]).start()
    query_doc[...] = jnp.where(is_own_lane(a * n_rows), 1.0, 0.0).astype(BF)

    def weight_arrival(m, kind):
        part = shard(m, w)
        return remote(part, part, sem_w.at[0, kind, m], sem_w.at[1, kind, m], core_peer)

    across = (1 - y) * 2 + c

    def weight_forward(m):
        weight_arrival(m, 1).wait_recv()
        remote(shard(m, across), shard(m, across), sem_w.at[0, 2, m], sem_w.at[1, 2, m], core_peer).start()

    def weight_end(m):
        weight_arrival(m, 0).wait_recv()
        weight_arrival(m, 2).wait_recv()
        if m != 3:
            pltpu.make_async_copy(shard(m, w), shard(m, w), sem_w.at[0, 3, m]).wait()

    def relay(first, last):
        def one(i, carry):
            s = i // (last - first)
            u = first + lax.rem(i, last - first)
            await_slice(u, s)
            pass_on(u, s)
            return carry

        lax.fori_loop(0, n_slices * (last - first), one, 0)

    relay(2, 6)
    weight_forward(3)
    weight_forward(0)
    weight_forward(1)
    weight_end(3)
    vec_out[0:8, :] = jnp.concatenate([vecs[o, 0:8, :] for o in range(4)], axis=1)
    for o in range(4):
        vec_out[8 + o : 9 + o, :] = jnp.concatenate([vecs[o, 8 + i : 9 + i, :] for i in range(4)], axis=1)
    pltpu.make_async_copy(tok_ref, tok.at[a], sem_l.at[4]).wait()
    weight_end(0)
    weight_end(1)

    step_rows = 256
    steps = tok.shape[1] // step_rows

    def query_part(i, carry):
        r = pl.ds(pl.multiple_of(i * step_rows, step_rows), step_rows)
        q = (jnp.dot(tok[a, r, :], wbuf[2], preferred_element_type=F32) + vec_out[0:1, :]).astype(BF)
        qbuf[r, :] = q * jnp.asarray(SCALE, BF)
        return carry

    def project(u, carry):
        run, _dz, _other, there = relative(u)

        @pl.when(u == 6)
        def _():
            weight_forward(2)
            weight_end(2)
            lax.fori_loop(0, steps, query_part, 0)
            pltpu.make_async_copy(qbuf, q_out, sem_l.at[5]).start()
            relay(6, 10)

        @pl.when(there)
        def _():
            @pl.when(u >= 10)
            def _():
                def one(s, carry):
                    await_slice(u, s)
                    return carry

                lax.fori_loop(0, n_slices, one, 0)

            def part(i, carry):
                r = pl.ds(pl.multiple_of(i * step_rows, step_rows), step_rows)
                t = tok[run, r, :]
                kbuf[run, r, :] = jnp.dot(t, wbuf[0], preferred_element_type=F32).astype(BF)
                vbuf[run, r, :] = (jnp.dot(t, wbuf[1], preferred_element_type=F32) + vec_out[1:2, :]).astype(BF)
                return carry

            lax.fori_loop(0, steps, part, 0)
            for i, (src, dst) in enumerate(((kbuf, k_out), (vbuf, v_out), (tok, tok_out))):
                pltpu.make_async_copy(src.at[run], dst.at[run], sem_o.at[i, run]).start()

        return carry

    for j in range(n_ctx):
        @pl.when(jnp.abs(j - a) > near)
        def _():
            kbuf[j] = jnp.zeros_like(kbuf[j])
            vbuf[j] = jnp.zeros_like(vbuf[j])
            for i, (src, dst) in enumerate(((kbuf, k_out), (vbuf, v_out), (tok, tok_out))):
                pltpu.make_async_copy(src.at[j], dst.at[j], sem_o.at[i, j]).start()

    lax.fori_loop(0, far, project, 0)

    pltpu.make_async_copy(wbuf, w_out, sem_l.at[6]).start()

    for m in (4, 5):
        weight_forward(m)
    for m, full, target in ((4, wo, wo_out), (5, wu, wu_out)):
        weight_end(m)
        pltpu.make_async_copy(full, target, sem_l.at[m - 4]).start()
    for m in range(6):
        for kind in range(3):
            weight_arrival(m, kind).wait_send()

    def drain(i, carry):
        s = i // far
        u = lax.rem(i, far)
        run, where = routes(u, s)
        for d, dev, ok in where:
            @pl.when(ok & (u < 10))
            def _():
                remote(tok.at[run, rows(s), :], tok.at[run, rows(s), :], sem_out.at[d, u, s], sem_in.at[run, s], dev).wait_send()
        return carry

    lax.fori_loop(0, n_slices * far, drain, 0)
    for j in range(n_ctx):
        for i, (src, dst) in enumerate(((kbuf, k_out), (vbuf, v_out), (tok, tok_out))):
            pltpu.make_async_copy(src.at[j], dst.at[j], sem_o.at[i, j]).wait()
    pltpu.make_async_copy(qbuf, q_out, sem_l.at[5]).wait()
    pltpu.make_async_copy(wbuf, w_out, sem_l.at[6]).wait()
    pltpu.make_async_copy(wo, wo_out, sem_l.at[0]).wait()
    pltpu.make_async_copy(wu, wu_out, sem_l.at[1]).wait()
    pltpu.make_async_copy(kdoc, key_doc, sem_l.at[3]).wait()


def gather_project(inputs, doc_starts, vectors, key_weight, value_weight, query_weight, out_weight, up_weight):
    n_ctx, n_wsh = lax.axis_size("ctx"), lax.axis_size("wsh")
    tall = inputs.shape[0]
    n_slices = 8
    far = 4 * (reach(n_ctx) // 2 + 1)
    vm, dma = pltpu.VMEM, pltpu.SemaphoreType.DMA
    any_spec = pl.BlockSpec(memory_space=pltpu.HBM)
    vm_spec = pl.BlockSpec(memory_space=pltpu.VMEM)
    runs = (n_ctx, tall, D)
    shape = jax.ShapeDtypeStruct
    return pl.pallas_call(
        functools.partial(gather_kernel, 5),
        out_shape=(shape(runs, BF), shape(runs, BF), shape(runs, BF), shape((tall, D), BF), shape((3, D, D), BF),
                   shape((16, D), F32), shape((D, D), BF), shape((D, up_weight.shape[1]), BF), shape((tall, 128), BF),
                   shape((n_ctx * tall, 128), BF)),
        in_specs=[any_spec, pl.BlockSpec(memory_space=pltpu.SMEM)] + [any_spec] * 5 + [vm_spec],
        out_specs=(any_spec,) * 5 + (vm_spec,) + (any_spec,) * 2 + (vm_spec, any_spec),
        scratch_shapes=[
            vm(runs, BF), vm(runs, BF), vm(runs, BF), vm((tall, D), BF), vm((3, D, D), BF), vm((n_wsh, 16, D // n_wsh), F32),
            vm((D, D), BF), vm((D, up_weight.shape[1]), BF), vm((n_ctx * tall, 128), BF),
            dma((n_ctx, n_slices)), dma((3, far, n_slices)), dma((2, 4, 6)), dma((7,)), dma((3, n_ctx)),
        ],
        compiler_params=pltpu.CompilerParams(collective_id=1, has_side_effects=True, vmem_limit_bytes=63 * 2**20),
        name="gather_project",
    )(inputs, doc_starts, key_weight, value_weight, query_weight, out_weight, up_weight, vectors)


def local(
    tokens,
    cotangent,
    doc_starts,
    query_weight,
    key_weight,
    value_weight,
    out_weight,
    up_weight,
    down_weight,
    query_bias,
    value_bias,
    out_bias,
    attn_gain,
    attn_shift,
    up_bias,
    down_bias,
    final_gain,
    final_shift,
):
    inputs = tokens[0]
    doc_start = doc_starts[0]
    tok_rows = inputs.shape[0]
    stream_rows = tok_rows * lax.axis_size("ctx")
    tile = min(tok_rows, 256)
    n_ctx, n_wsh = lax.axis_size("ctx"), lax.axis_size("wsh")
    own = D // n_wsh

    def gather(x):
        return lax.all_gather(x, "wsh", axis=0, tiled=True)

    fast = n_wsh == 4 and n_ctx == 8 and own % (n_ctx // 2 * 16) == 0 and tok_rows % 512 == 0
    if fast:
        small = (query_bias, value_bias, out_bias, attn_gain, attn_shift, down_bias, final_gain, final_shift)
        vectors, place = jnp.zeros(((8 + n_wsh) * own,), F32), 0
        for v in small + (up_bias,):
            ends = (place, vectors.shape[0] - place - v.shape[0], 0)
            vectors = vectors + lax.pad(v.astype(F32), jnp.zeros((), F32), (ends,))
            place += v.shape[0]
        vectors = vectors.reshape(8 + n_wsh, own)
        all_tokens, keys, values, queries, kvq_w, vec, out_w, up_w, query_doc, key_doc = gather_project(
            inputs, doc_starts, vectors, key_weight, value_weight, query_weight, out_weight, up_weight
        )
        down_own, _unused = lax.optimization_barrier((down_weight, vec))
        down_far = lax.ppermute(down_own, "wsh", [(i, i ^ 2) for i in range(n_wsh)])
        all_tokens, keys, values = [r.reshape(stream_rows, D) for r in (all_tokens, keys, values)]
    else:
        first_row = lax.axis_index("ctx") * tok_rows
        query_doc, key_doc = document_lanes(doc_start, first_row, tok_rows, stream_rows)
        small = jnp.stack(
            [query_bias, value_bias, out_bias, attn_gain, attn_shift, down_bias, final_gain, final_shift]
        )
        all_tokens = lax.all_gather(inputs, "ctx", axis=0, tiled=True)
        query_w, key_w, value_w = gather(query_weight), gather(key_weight), gather(value_weight)
        small = gather(small.T).astype(F32)
        query_b, value_b, out_b, attn_g, attn_s, down_b, final_g, final_s = [small[:, i] for i in range(8)]
        up_b = gather(up_bias).astype(F32)
        queries = jnp.dot(inputs, query_w, preferred_element_type=F32) + query_b
        queries = queries.astype(BF) * jnp.asarray(SCALE, BF)
        keys = jnp.dot(all_tokens, key_w, preferred_element_type=F32).astype(BF)
        values = (jnp.dot(all_tokens, value_w, preferred_element_type=F32) + value_b).astype(BF)
    mixed_t, log_rows = attn_fwd(doc_start, queries, query_doc, keys, key_doc, values, tq=tile)
    if fast:
        layer_out, grad_sum1, grad_attn, vec_grads, grad_up_w, grad_down_w, grad_out_w = middle(
            mixed_t, inputs, cotangent[0], vec, out_w, up_w, down_own, down_far
        )
        grad_q, grad_k, grad_v = attn_bwd(
            doc_start, queries, query_doc, grad_attn, log_rows, mixed_t, keys, key_doc, values, tq=tile
        )
        grad_inputs, layer_out, mats, small, wide = finish(
            (grad_up_w, grad_out_w, grad_down_w), vec_grads, grad_k.reshape(n_ctx, tok_rows, D),
            grad_v.reshape(n_ctx, tok_rows, D), all_tokens.reshape(n_ctx, tok_rows, D), grad_q, kvq_w, grad_sum1, inputs, layer_out,
        )
        up_sum, out_sum, down_sum, key_sum, value_sum, query_sum = mats
        return (
            layer_out.reshape(1, tok_rows, D), grad_inputs.reshape(1, tok_rows, D), query_sum, key_sum, value_sum,
            out_sum, up_sum, down_sum, small[0], small[1], small[2], small[3], small[4], wide,
            small[5], small[6], small[7],
        )

    out_w = gather(out_weight)
    up_w = gather(up_weight)
    down_w = gather(down_weight)
    attn_t = mixed_t.astype(BF)
    inputs_f = inputs.astype(F32)
    branch = lax.dot_general(attn_t, out_w, TN, preferred_element_type=F32) + out_b
    first_norm, first_pull = jax.vjp(layer_norm, inputs_f + branch, attn_g, attn_s)
    first_b = first_norm.astype(BF)
    up_f = jnp.dot(first_b, up_w, preferred_element_type=F32) + up_b
    act_f, act_pull = jax.vjp(gelu_act, up_f)
    act_b = act_f.astype(BF)
    down_f = jnp.dot(act_b, down_w, preferred_element_type=F32) + down_b
    final_f, final_pull = jax.vjp(layer_norm, first_norm + down_f, final_g, final_s)
    layer_out = final_f.astype(BF)

    grad_sum2, grad_final_g, grad_final_s = final_pull(cotangent[0].astype(F32))
    grad_down = grad_sum2.astype(BF)
    grad_down_w = jnp.einsum("tf,td->fd", act_b, grad_down, preferred_element_type=F32)
    grad_down_b = jnp.sum(grad_down.astype(F32), axis=0)
    grad_act = jnp.einsum("td,fd->tf", grad_down, down_w, preferred_element_type=F32)
    (grad_up_f,) = act_pull(grad_act)
    grad_up = grad_up_f.astype(BF)
    grad_up_w = jnp.einsum("td,tf->df", first_b, grad_up, preferred_element_type=F32)
    grad_up_b = jnp.sum(grad_up.astype(F32), axis=0)
    grad_first = grad_sum2 + jnp.einsum("tf,df->td", grad_up, up_w, preferred_element_type=F32)
    grad_sum1, grad_attn_g, grad_attn_s = first_pull(grad_first)
    grad_branch = grad_sum1.astype(BF)
    grad_out_w = jnp.dot(attn_t, grad_branch, preferred_element_type=F32)
    grad_out_b = jnp.sum(grad_branch.astype(F32), axis=0)
    grad_attn = jnp.einsum("te,de->td", grad_branch, out_w, preferred_element_type=F32).astype(BF)
    grad_q, grad_k, grad_v = attn_bwd(
        doc_start, queries, query_doc, grad_attn, log_rows, mixed_t, keys, key_doc, values, tq=tile
    )
    def total(g):
        part = lax.psum_scatter(g.astype(BF), "wsh", scatter_dimension=0, tiled=True)
        return lax.psum(part, "ctx").astype(F32)

    grad_all = jnp.einsum("te,de->td", grad_k, key_w, preferred_element_type=F32)
    grad_all = grad_all + jnp.einsum("te,de->td", grad_v, value_w, preferred_element_type=F32)
    grad_own = lax.psum_scatter(grad_all.astype(BF), "ctx", scatter_dimension=0, tiled=True)
    grad_query_w = jnp.einsum("td,te->de", inputs, grad_q, preferred_element_type=F32)
    grad_key_w = jnp.einsum("td,te->de", all_tokens, grad_k, preferred_element_type=F32)
    grad_value_w = jnp.einsum("td,te->de", all_tokens, grad_v, preferred_element_type=F32)
    grad_query_b = jnp.sum(grad_q.astype(F32), axis=0)
    grad_value_b = jnp.sum(grad_v.astype(F32), axis=0)
    grad_inputs = grad_sum1 + jnp.einsum("te,de->td", grad_q, query_w, preferred_element_type=F32)
    grad_inputs = grad_inputs + grad_own.astype(F32)
    sums = [
        total(g)
        for g in (
            grad_query_w, grad_key_w, grad_value_w, grad_out_w, grad_up_w, grad_down_w,
            grad_query_b, grad_value_b, grad_out_b, grad_attn_g, grad_attn_s, grad_up_b,
            grad_down_b, grad_final_g, grad_final_s,
        )
    ]
    return (
        layer_out.reshape(1, tok_rows, D),
        grad_inputs.astype(BF).reshape(1, tok_rows, D),
        *sums,
    )


def solution(mesh):
    rows, mat, vec = P("wsh", "ctx", None), P("wsh", None), P("wsh")
    return jax.shard_map(
        local,
        mesh=mesh,
        in_specs=(rows, rows, mat) + (mat,) * 6 + (vec,) * 9,
        out_specs=(rows, rows) + (mat,) * 6 + (vec,) * 9,
        check_vma=False,
    )
```

```python
import functools

import jax
import jax.numpy as jnp
from jax import lax
from jax.experimental import pallas as pl
from jax.experimental.pallas import tpu as pltpu
from jax.sharding import PartitionSpec as P

D = 768
HEADS = 12
HD = 64
SCALE = 0.125
EPS = 1e-12
ROOT_HALF = 0.7071067811865476
BF = jnp.bfloat16
F32 = jnp.float32
NT = (((1,), (1,)), ((), ()))
NN = (((1,), (0,)), ((), ()))
TN = (((0,), (0,)), ((), ()))


def layer_norm(values, gain_vec, shift_vec):
    average = jnp.mean(values, axis=-1, keepdims=True)
    centred = values - average
    variance = jnp.mean(centred * centred, axis=-1, keepdims=True)
    return centred * lax.rsqrt(variance + EPS) * gain_vec + shift_vec


def gelu_act(values):
    return 0.5 * values * (1.0 + lax.erf(values * ROOT_HALF))


def key_range(docs, first_row, tile, stream_rows):
    last = first_row + tile - 1
    low, high = 0, stream_rows
    for d in range(1, docs.shape[0]):
        low = jnp.where(docs[d] <= first_row, docs[d], low)
    for d in range(docs.shape[0] - 1, 0, -1):
        high = jnp.where(docs[d] > last, docs[d], high)
    first = low // 128 * 128
    count = (high - first + 255) // 256
    return jnp.minimum(first, stream_rows - count * 256), count


def document_lanes(doc_start, first_row, rows, stream_rows):
    far = jnp.full((128 - doc_start.shape[0],), 2**30, jnp.int32)
    starts = jnp.concatenate([doc_start, far])
    ends = jnp.concatenate([doc_start[1:], jnp.full((1,), stream_rows, jnp.int32), far])
    query_pos = first_row + jnp.arange(rows, dtype=jnp.int32)[:, None]
    key_pos = jnp.arange(stream_rows, dtype=jnp.int32)[:, None]
    query_doc = ((query_pos >= starts) & (query_pos < ends)).astype(BF)
    key_doc = jnp.where((key_pos >= starts) & (key_pos < ends), 0.0, -1e30).astype(BF)
    return query_doc, key_doc


def stack_heads(x, extra=None):
    lane = lax.broadcasted_iota(jnp.int32, x.shape, 1)
    zero = jnp.zeros_like(x)
    lo = jnp.where(lane < 64, x, zero)
    hi = jnp.where(lane < 64, zero, x)
    if extra is not None:
        lo = jnp.concatenate([lo, extra], axis=1)
        hi = jnp.concatenate([hi, extra], axis=1)
    return jnp.concatenate([lo, hi], axis=0)

def pick_heads(x, tq):
    return jnp.concatenate([x[:64, :tq], x[64:, tq:]], axis=0)

def two_level(start, count, tk, body, init):
    done, carried = 0, init
    for n in (6, 3, 2, 1):
        if n * 256 > tk:
            continue

        def step(t, c, n=n, done=done):
            at = done + t * n
            return body(pl.multiple_of(at * 256, 256), pl.multiple_of(start + at * 256, 128), n * 256, c)

        trips = (count - done) // n
        carried = lax.fori_loop(0, trips, step, carried)
        done = done + trips * n
    return carried


def fwd_kernel(tq, tk, docs, q_ref, qaug_ref, k_ref, kaug_ref, v_ref, ot_ref, lse_ref, s_scr, acc):
    def part(i, carry):
        rows = pl.ds(pl.multiple_of(i * tq, tq), tq)
        start, count = key_range(docs, lax.axis_index("ctx") * q_ref.shape[0] + i * tq, tq, k_ref.shape[0])
        rhs = stack_heads(q_ref[rows, :], qaug_ref[rows, :])

        def scores(loc, off, size, m):
            lhs = jnp.concatenate([k_ref[pl.ds(off, size), :], kaug_ref[pl.ds(off, size), :]], axis=1)
            s = lax.dot_general(lhs, rhs, NT, preferred_element_type=F32)
            s_scr[pl.ds(loc, size), :] = s
            return jnp.maximum(m, jnp.max(s.reshape(size // 8, 8, 2 * tq), axis=0))

        m8 = two_level(start, count, tk, scores, jnp.full((8, 2 * tq), -3e38, F32))
        m = jnp.max(m8, axis=0, keepdims=True)
        acc[...] = jnp.zeros_like(acc)

        def mix(loc, off, size, l8):
            p = jnp.exp(s_scr[pl.ds(loc, size), :] - m)
            acc[...] += lax.dot_general(v_ref[pl.ds(off, size), :], p.astype(BF), TN, preferred_element_type=F32)
            return l8 + jnp.sum(p.reshape(size // 8, 8, 2 * tq), axis=0)

        l8 = two_level(start, count, tk, mix, jnp.zeros((8, 2 * tq), F32))
        l = jnp.sum(l8, axis=0, keepdims=True)
        ot_ref[:, rows] = pick_heads(acc[...] / l, tq)
        lse = m + jnp.log(l)
        lse_ref[0, :, rows] = jnp.concatenate([lse[:, :tq], lse[:, tq:]], axis=0)
        return carry

    lax.fori_loop(0, q_ref.shape[0] // tq, part, 0)


def attn_fwd(docs, q, qaug, k, kaug, v, *, tq=256, tk=1536):
    T, D = q.shape
    S = k.shape[0]
    pairs = D // 128
    return pl.pallas_call(
        functools.partial(fwd_kernel, tq, tk),
        out_shape=(jax.ShapeDtypeStruct((D, T), F32), jax.ShapeDtypeStruct((pairs, 2, T), F32)),
        grid_spec=pltpu.PrefetchScalarGridSpec(
            num_scalar_prefetch=1, grid=(pairs,),
            in_specs=[pl.BlockSpec((T, 128), lambda h, b: (0, h)),
                      pl.BlockSpec((T, 128), lambda h, b: (0, 0)),
                      pl.BlockSpec((S, 128), lambda h, b: (0, h)),
                      pl.BlockSpec((S, 128), lambda h, b: (0, 0)),
                      pl.BlockSpec((S, 128), lambda h, b: (0, h))],
            out_specs=(pl.BlockSpec((128, T), lambda h, b: (h, 0)),
                       pl.BlockSpec((1, 2, T), lambda h, b: (h, 0, 0))),
            scratch_shapes=[pltpu.VMEM((S, 2 * tq), F32), pltpu.VMEM((128, 2 * tq), F32)]),
        name="attend",
    )(docs, q, qaug, k, kaug, v)


def bwd_kernel(tq, tk, docs, q_ref, qaug_ref, do_ref, lse_ref, ot_ref, k_ref, kaug_ref, v_ref,
               dq_ref, dk_ref, dv_ref, dk_acc, dv_acc, dq_acc, delta_scr):
    n_rows, n_keys = q_ref.shape[0], k_ref.shape[0]
    first_row = lax.axis_index("ctx") * n_rows
    low, high = n_keys, 0
    for i in range(n_rows // tq):
        start, count = key_range(docs, first_row + i * tq, tq, n_keys)
        low, high = jnp.minimum(low, start), jnp.maximum(high, start + count * 256)

    def over_seen(fn):
        def one(t, carry):
            fn(pl.ds(pl.multiple_of(low + t * 128, 128), 128))
            return carry

        lax.fori_loop(0, (high - low) // 128, one, 0)

    def clear(rows):
        dk_acc[rows, :] = jnp.zeros((128, 128), F32)
        dv_acc[rows, :] = jnp.zeros((128, 128), F32)

    over_seen(clear)
    mixed = ot_ref[...] * do_ref[...].astype(F32).T
    deltas = [jnp.sum(mixed[:64], axis=0, keepdims=True), jnp.sum(mixed[64:], axis=0, keepdims=True)]
    delta_scr[...] = jnp.concatenate(deltas, axis=0)

    def part(i, carry):
        part_rows = pl.ds(pl.multiple_of(i * tq, tq), tq)
        start, count = key_range(docs, first_row + i * tq, tq, n_keys)
        q, do = q_ref[part_rows, :], do_ref[part_rows, :]
        qs = stack_heads(q)
        qrhs = stack_heads(q, qaug_ref[part_rows, :])
        dos = stack_heads(do)
        lse = jnp.concatenate([lse_ref[0, 0:1, part_rows], lse_ref[0, 1:2, part_rows]], axis=1)
        delta = jnp.concatenate([delta_scr[0:1, part_rows], delta_scr[1:2, part_rows]], axis=1)
        dq_acc[...] = jnp.zeros_like(dq_acc)

        def step(loc, off, size, carry):
            rows = pl.ds(off, size)
            lhs = jnp.concatenate([k_ref[rows, :], kaug_ref[rows, :]], axis=1)
            x = lax.dot_general(lhs, qrhs, NT, preferred_element_type=F32)
            y = lax.dot_general(v_ref[rows, :], dos, NT, preferred_element_type=F32)
            p = jnp.exp(x - lse)
            ds = (p * (y - delta)).astype(BF)
            pb = p.astype(BF)
            dv_acc[rows, :] += lax.dot_general(pb, dos, NN, preferred_element_type=F32)
            dk_acc[rows, :] += lax.dot_general(ds, qs, NN, preferred_element_type=F32)
            dq_acc[...] += lax.dot_general(k_ref[rows, :], ds, TN, preferred_element_type=F32)
            return carry

        two_level(start, count, tk, step, 0)
        dq_ref[part_rows, :] = (pick_heads(dq_acc[...], tq) * SCALE).T.astype(BF)
        return carry

    lax.fori_loop(0, n_rows // tq, part, 0)
    dk_ref[...] = jnp.zeros_like(dk_ref)
    dv_ref[...] = jnp.zeros_like(dv_ref)

    def give(rows):
        dk_ref[rows, :] = dk_acc[rows, :].astype(BF)
        dv_ref[rows, :] = dv_acc[rows, :].astype(BF)

    over_seen(give)


def attn_bwd(docs, q, qaug, do, lse, ot, k, kaug, v, *, tq=256, tk=1536):
    T, D = q.shape
    S = k.shape[0]
    pairs = D // 128
    return pl.pallas_call(
        functools.partial(bwd_kernel, tq, tk),
        out_shape=(jax.ShapeDtypeStruct((T, D), BF), jax.ShapeDtypeStruct((S, D), BF), jax.ShapeDtypeStruct((S, D), BF)),
        grid_spec=pltpu.PrefetchScalarGridSpec(
            num_scalar_prefetch=1, grid=(pairs,),
            in_specs=[pl.BlockSpec((T, 128), lambda h, b: (0, h)),
                      pl.BlockSpec((T, 128), lambda h, b: (0, 0)),
                      pl.BlockSpec((T, 128), lambda h, b: (0, h)),
                      pl.BlockSpec((1, 2, T), lambda h, b: (h, 0, 0)),
                      pl.BlockSpec((128, T), lambda h, b: (h, 0)),
                      pl.BlockSpec((S, 128), lambda h, b: (0, h)),
                      pl.BlockSpec((S, 128), lambda h, b: (0, 0)),
                      pl.BlockSpec((S, 128), lambda h, b: (0, h))],
            out_specs=(pl.BlockSpec((T, 128), lambda h, b: (0, h)),
                       pl.BlockSpec((S, 128), lambda h, b: (0, h)),
                       pl.BlockSpec((S, 128), lambda h, b: (0, h))),
            scratch_shapes=[pltpu.VMEM((S, 128), F32), pltpu.VMEM((S, 128), F32), pltpu.VMEM((128, 2 * tq), F32),
                            pltpu.VMEM((2, T), F32)]),
        name="attend_back",
    )(docs, q, qaug, do, lse, ot, k, kaug, v)


def middle_kernel(attn_ref, in_ref, cot_ref, vec_ref, wo_ref, wu_ref, down_own, down_far,
                  out_ref, sum1_ref, do_ref, grads_ref, up_out, down_out, attn_out,
                  wo, wu, wd, attn_b, first, hat1, scale1, first_b, act, slope, sum2, down_b, up_b, first_b2, first_t,
                  g_up, g_down, g_out, sem_w, sem_d, sem_o):
    rows, wide = in_ref.shape[0], wu.shape[1]
    a, w = lax.axis_index("ctx"), lax.axis_index("wsh")
    y, c = w // 2, lax.rem(w, 2)
    core_peer = (a, y * 2 + (1 - c))
    tall = down_own.shape[0]
    MESH = pl.DeviceIdType.MESH
    barrier = pltpu.get_barrier_semaphore()
    pl.semaphore_signal(barrier, inc=1, device_id=core_peer, device_id_type=MESH)
    pl.semaphore_wait(barrier, 1)
    passed = []
    for s, (ref, owner) in enumerate(((down_own, w), (down_far, (1 - y) * 2 + c))):
        there = wd.at[pl.ds(pl.multiple_of(owner * tall, 16), tall), :]
        passed.append(pltpu.make_async_remote_copy(
            src_ref=ref, dst_ref=there, send_sem=sem_d.at[0, s], recv_sem=sem_d.at[1, s],
            device_id=core_peer, device_id_type=MESH))
        passed[-1].start()
        pltpu.make_async_copy(ref, there, sem_w.at[2 + s]).start()
    loading = [pltpu.make_async_copy(wo_ref, wo, sem_w.at[0]), pltpu.make_async_copy(wu_ref, wu, sem_w.at[1])]
    for copy in loading:
        copy.start()

    def arrived(j):
        if j < 2:
            loading[j].wait()
        else:
            for s, owner in enumerate((w, (1 - y) * 2 + c)):
                there = wd.at[pl.ds(pl.multiple_of(owner * tall, 16), tall), :]
                pltpu.make_async_copy(there, there, sem_w.at[2 + s]).wait()
                passed[s].wait_recv()

    grads_ref[...] = jnp.zeros_like(grads_ref)
    attn_b[...] = attn_ref[...].astype(BF)
    out_b, attn_g, attn_s, down_bias, final_g, final_s = [vec_ref[i : i + 1, :] for i in range(2, 8)]
    arrived(0)
    block = 256

    def over_rows(fn):
        def one(i, carry):
            fn(pl.ds(pl.multiple_of(i * block, block), block))
            return carry

        lax.fori_loop(0, rows // block, one, 0)

    def norm(values):
        average = jnp.mean(values, axis=-1, keepdims=True)
        centred = values - average
        scale = lax.rsqrt(jnp.mean(centred * centred, axis=-1, keepdims=True) + EPS)
        return centred * scale, scale

    def norm_back(grad, hat, scale, gain):
        g = grad * gain
        return scale * (g - jnp.mean(g, axis=-1, keepdims=True) - hat * jnp.mean(g * hat, axis=-1, keepdims=True))

    def note(row, values):
        grads_ref[row : row + 1, :] += jnp.sum(values, axis=0, keepdims=True)

    def branch_part(r):
        a = attn_b[:, r].T
        v = lax.dot_general(a, wo[...], NN, preferred_element_type=F32) + out_b + in_ref[r, :].astype(F32)
        hat, scale = norm(v)
        hat1[r, :] = hat
        scale1[r, :] = scale
        f = hat * attn_g + attn_s
        first[r, :] = f
        first_b[r, :] = f.astype(BF)

    over_rows(branch_part)
    arrived(1)
    cols = vec_ref.shape[1]

    def over_wide(fn):
        def one(i, carry):
            fn(pl.ds(pl.multiple_of(i * cols, cols), cols), i)
            return carry

        lax.fori_loop(0, wide // cols, one, 0)

    def up_part(n, i):
        u = lax.dot_general(first_b[...], wu[:, n], NN, preferred_element_type=F32) + vec_ref[pl.ds(8 + i, 1), :]
        half = 0.5 * (1.0 + lax.erf(u * ROOT_HALF))
        act[:, n] = (u * half).astype(BF)
        slope[:, n] = half + u * (0.3989422804014327 * jnp.exp(-0.5 * u * u))

    over_wide(up_part)
    arrived(2)

    def down_part(r):
        v = lax.dot_general(act[r, :], wd[...], NN, preferred_element_type=F32) + down_bias + first[r, :]
        hat, scale = norm(v)
        out_ref[r, :] = (hat * final_g + final_s).astype(BF)
        cot = cot_ref[r, :].astype(F32)
        note(6, cot * hat)
        note(7, cot)
        g = norm_back(cot, hat, scale, final_g)
        sum2[r, :] = g
        rounded = g.astype(BF)
        down_b[r, :] = rounded
        note(5, rounded.astype(F32))

    over_rows(down_part)

    def up_back(n, i):
        g = lax.dot_general(down_b[...], wd[n, :], NT, preferred_element_type=F32) * slope[:, n]
        rounded = g.astype(BF)
        up_b[:, n] = rounded
        grads_ref[pl.ds(8 + i, 1), :] = jnp.sum(rounded.astype(F32), axis=0, keepdims=True)

    over_wide(up_back)

    def first_part(r):
        g = sum2[r, :] + lax.dot_general(up_b[r, :], wu[...], NT, preferred_element_type=F32)
        hat = hat1[r, :]
        note(3, g * hat)
        note(4, g)
        s1 = norm_back(g, hat, scale1[r, :], attn_g)
        sum1_ref[r, :] = s1
        rounded = s1.astype(BF)
        note(2, rounded.astype(F32))
        first_b2[r, :] = rounded

    over_rows(first_part)

    def do_part(r):
        do_ref[r, :] = lax.dot_general(first_b2[r, :], wo[...], NT, preferred_element_type=F32).astype(BF)

    over_rows(do_part)

    def wide_grads(n, i):
        g_down[n, :] = lax.dot_general(act[:, n].T, down_b[...], NN, preferred_element_type=F32).astype(BF)
        pltpu.make_async_copy(g_down.at[n, :], down_out.at[n, :], sem_o.at[0, i]).start()
        g_up[:, n] = lax.dot_general(first_t[...], up_b[:, n], NN, preferred_element_type=F32).astype(BF)
        pltpu.make_async_copy(g_up.at[:, n], up_out.at[:, n], sem_o.at[1, i]).start()

    first_t[...] = first_b[...].T
    over_wide(wide_grads)
    g_out[...] = lax.dot_general(attn_b[...], first_b2[...], NN, preferred_element_type=F32).astype(BF)
    pltpu.make_async_copy(g_out, attn_out, sem_o.at[2, 0]).start()

    def wide_end(n, i):
        pltpu.make_async_copy(g_down.at[n, :], down_out.at[n, :], sem_o.at[0, i]).wait()
        pltpu.make_async_copy(g_up.at[:, n], up_out.at[:, n], sem_o.at[1, i]).wait()

    over_wide(wide_end)
    pltpu.make_async_copy(g_out, attn_out, sem_o.at[2, 0]).wait()
    for copy in passed:
        copy.wait_send()


def middle(attn_t, inputs, cotangent, vec, out_w, up_w, down_own, down_far):
    rows = inputs.shape[0]
    wide = up_w.shape[1]
    vm, dma, shape = pltpu.VMEM, pltpu.SemaphoreType.DMA, jax.ShapeDtypeStruct
    any_spec = pl.BlockSpec(memory_space=pltpu.HBM)
    vm_spec = pl.BlockSpec(memory_space=pltpu.VMEM)
    return pl.pallas_call(
        middle_kernel,
        out_shape=(shape((rows, D), BF), shape((rows, D), F32), shape((rows, D), BF), shape((16, D), F32),
                   shape((D, wide), BF), shape((wide, D), BF), shape((D, D), BF)),
        in_specs=[vm_spec] * 4 + [any_spec] * 4,
        out_specs=(vm_spec,) * 4 + (any_spec,) * 3,
        scratch_shapes=[
            vm((D, D), BF), vm((D, wide), BF), vm((wide, D), BF), vm((D, rows), BF), vm((rows, D), F32),
            vm((rows, D), F32), vm((rows, 1), F32), vm((rows, D), BF), vm((rows, wide), BF), vm((rows, wide), F32),
            vm((rows, D), F32), vm((rows, D), BF), vm((rows, wide), BF), vm((rows, D), BF), vm((D, rows), BF),
            vm((D, wide), BF), vm((wide, D), BF), vm((D, D), BF), dma((4,)), dma((2, 2)), dma((3, wide // D)),
        ],
        compiler_params=pltpu.CompilerParams(collective_id=3, has_side_effects=True, vmem_limit_bytes=63 * 2**20),
        name="middle",
    )(attn_t, inputs, cotangent, vec, out_w, up_w, down_own, down_far)


def reach(n_ctx):
    return n_ctx // 2


def finish_kernel(sources, n_parts, *refs):
    parts = refs[:n_parts]
    (vec_ref, dk_ref, dv_ref, tok_ref, dq_ref, w_ref, own_in_ref, mine_tok_ref,
     out_ref, vec_out, wide_out, grad_ref,
     mine, buf_a, buf_h, buf_b, buf_s, buf_c, buf_d, buf_e, gbf,
     sums, heard, line,
     loads, weights, acc, dq, own, bias,
     run_part, from_x, from_z, far_z, last_x,
     sem_l, sem_a, sem_b, sem_c, sem_d, sem_v, sem_x, sem_z, sem_far, sem_load, sem_in) = refs[n_parts:]
    n_ready = len(sources)
    n_chunks = out_ref.shape[0]
    n_ctx, n_wsh = lax.axis_size("ctx"), lax.axis_size("wsh")
    zs = n_ctx // 2
    a, w = lax.axis_index("ctx"), lax.axis_index("wsh")
    z, x = a // 2, lax.rem(a, 2)
    y, c = w // 2, lax.rem(w, 2)
    core_peer = (a, y * 2 + (1 - c))
    y_peer = (a, (1 - y) * 2 + c)
    x_peer = (z * 2 + (1 - x), w)
    low, high = lax.rem(z, 2), z // 2
    pair_peer = ((z + 1 - 2 * low) * 2 + x, w)
    skip_peer = (lax.rem(z + 2, zs) * 2 + x, w)
    up_peer, down_peer = (a + 2, w), (a - 2, w)
    near = reach(n_ctx)
    hops = near // 2
    MESH = pl.DeviceIdType.MESH

    rows = out_ref.shape[1]
    half = out_ref.shape[2] // 2
    piece = rows // zs
    tall = own.shape[0]
    cut = from_x.shape[1]

    def z_peer(d):
        return (lax.rem(z + d, zs) * 2 + x, w)

    barrier = pltpu.get_barrier_semaphore()
    for dev in [core_peer, y_peer, x_peer] + [z_peer(d) for d in range(1, zs)]:
        pl.semaphore_signal(barrier, inc=1, device_id=dev, device_id_type=MESH)
    def send(src, dst, sems, idx, dev):
        return pltpu.make_async_remote_copy(
            src_ref=src, dst_ref=dst, send_sem=sems.at[(0,) + idx], recv_sem=sems.at[(1,) + idx],
            device_id=dev, device_id_type=MESH)

    def wait_in(ref, sems, idx):
        send(ref, ref, sems, idx, core_peer).wait_recv()

    def wait_out(ref, sems, idx):
        send(ref, ref, sems, idx, core_peer).wait_send()

    def distance(i):
        return (hops - i // 4) * (1 - 2 * lax.rem(i // 2, 2))

    def position(i):
        dz = distance(i)
        mine_too = lax.rem(i, 2)
        run = 2 * (z + dz) + (1 - x) * (1 - mine_too) + x * mine_too
        return run, mine_too, (z + dz >= 0) & (z + dz < zs) & (jnp.abs(run - a) <= near)

    n_pos = 4 * hops + 2

    def load(i):
        run, _mine_too, there = position(i)
        return there, [
            pltpu.make_async_copy(src.at[run], loads.at[lax.rem(i, 2), j], sem_load.at[lax.rem(i, 2), j])
            for j, src in enumerate((dk_ref, dv_ref, tok_ref))
        ]

    def load_start(i):
        there, copies = load(i)

        @pl.when(there & (i < n_pos))
        def _():
            for copy in copies:
                copy.start()

    def share(k, owner):
        if k < n_ready:
            p, row0, col0 = sources[k]
            return parts[p].at[owner, pl.ds(row0, rows), pl.ds(col0, 2 * half)]
        return gbf.at[k - n_ready, owner]

    def share_load(k):
        for yy in range(2):
            pltpu.make_async_copy(share(k, yy * 2 + c), mine.at[k % 4, yy], sem_l.at[k]).start()

    def share_send(k):
        for yy in range(2):
            send(share(k, yy * 2 + (1 - c)), buf_a.at[k, yy], sem_a, (k,), core_peer).start()

    load_start(0)
    fetch = [pltpu.make_async_copy(w_ref, weights, sem_in.at[0]), pltpu.make_async_copy(dq_ref, dq, sem_in.at[1]),
             pltpu.make_async_copy(own_in_ref, own, sem_in.at[2])]
    for copy in fetch:
        copy.start()
    for k in range(4):
        share_load(k)
    acc[...] = jnp.zeros_like(acc)
    bias[...] = jnp.zeros_like(bias)
    pl.semaphore_wait(barrier, zs + 2)
    for k in range(n_ready):
        share_send(k)
    fetch[0].wait()

    near_rows, far_rows = pl.ds(0, cut), pl.ds(cut, tall - cut)

    def unit(i):
        run, mine_too, there = position(i)
        at = lax.rem(i, 2)
        load_start(i + 1)

        @pl.when(there)
        def _():
            for copy in load(i)[1]:
                copy.wait()

            def tokens_part(r, carry):
                rs = pl.ds(pl.multiple_of(r * 256, 256), 256)
                g = lax.dot_general(loads[at, 0, rs, :], weights[0], NT, preferred_element_type=F32)
                g = g + lax.dot_general(loads[at, 1, rs, :], weights[1], NT, preferred_element_type=F32)
                run_part[i, rs, :] = g.astype(BF)
                bias[0:8, :] += jnp.sum(loads[at, 1, rs, :].astype(F32).reshape(32, 8, 2 * half), axis=0)
                return carry

            lax.fori_loop(0, tall // 256, tokens_part, 0)

            @pl.when(mine_too == 0)
            def _():
                send(run_part.at[i, near_rows, :], from_x.at[i // 2], sem_x, (i // 2,), x_peer).start()

            @pl.when(i < 4)
            def _():
                far_send(i)

            def weights_part(r, carry):
                fs = pl.ds(pl.multiple_of(r * 256, 256), 256)
                flipped = loads[at, 2, :, fs].T
                for j in range(2):
                    acc[j, fs, :] += lax.dot_general(flipped, loads[at, j], NN, preferred_element_type=F32)
                return carry

            lax.fori_loop(0, 2 * half // 256, weights_part, 0)

    def from_below(i):
        dz = distance(i)
        step = 1 - 2 * lax.rem(i // 2, 2)
        sender, target = z - step, z - step + dz
        side = jnp.abs(2 * dz + (1 - 2 * x) * (1 - lax.rem(i, 2))) <= near
        return (sender >= 0) & (sender < zs) & (target >= 0) & (target < zs) & side

    def toward(i, copy_of):
        step = 1 - 2 * lax.rem(i // 2, 2)

        @pl.when(step == 1)
        def _():
            copy_of(up_peer).start()

        @pl.when(step == -1)
        def _():
            copy_of(down_peer).start()

    def far_send(i):
        toward(i, lambda dev: send(run_part.at[i, far_rows, :], far_z.at[i], sem_far, (i,), dev))

    def far_pass(i):
        _run, _mine_too, there = position(i)

        @pl.when(there)
        def _():
            @pl.when(from_below(i - 4))
            def _():
                wait_in(far_z.at[i - 4], sem_far, (i - 4,))
                run_part[i, far_rows, :] = (
                    run_part[i, far_rows, :].astype(F32) + far_z[i - 4].astype(F32)).astype(BF)

            far_send(i)

    def far_end():
        for col in range(2):
            total = n_pos - 2 + col
            for src in (4 + col, 6 + col):
                @pl.when(from_below(src))
                def _():
                    wait_in(far_z.at[src], sem_far, (src,))
                    run_part[total, far_rows, :] = (
                        run_part[total, far_rows, :].astype(F32) + far_z[src].astype(F32)).astype(BF)
            if col == 0:
                send(run_part.at[total, far_rows, :], last_x, sem_x, (n_pos // 2,), x_peer).start()
        own[far_rows, :] += run_part[n_pos - 1, far_rows, :].astype(F32)

    def near_pass(n):
        dz = distance(2 * n)
        i = 2 * n + 1

        @pl.when((z + dz >= 0) & (z + dz < zs))
        def _():
            @pl.when(jnp.abs(2 * dz + 2 * x - 1) <= near)
            def _():
                wait_in(from_x.at[n], sem_x, (n,))
                run_part[i, near_rows, :] = (
                    run_part[i, near_rows, :].astype(F32) + from_x[n].astype(F32)).astype(BF)

            @pl.when((n >= 2) & from_below(i - 4))
            def _():
                wait_in(from_z.at[n - 2], sem_z, (n - 2,))
                run_part[i, near_rows, :] = (
                    run_part[i, near_rows, :].astype(F32) + from_z[n - 2].astype(F32)).astype(BF)

            toward(i, lambda dev: send(run_part.at[i, near_rows, :], from_z.at[n], sem_z, (n,), dev))

    def near_own():
        n = n_pos // 2 - 1
        wait_in(from_x.at[n], sem_x, (n,))
        own[near_rows, :] += run_part[n_pos - 1, near_rows, :].astype(F32) + from_x[n].astype(F32)

    def near_end():
        for n in (2, 3):
            @pl.when(from_below(2 * n + 1))
            def _():
                wait_in(from_z.at[n], sem_z, (n,))
                own[near_rows, :] += from_z[n].astype(F32)

    def add(p, q):
        return (p.astype(F32) + q.astype(F32)).astype(BF)

    def column(side):
        return pl.ds(pl.multiple_of(side * half, 128), half)

    def band(start, size):
        return pl.ds(pl.multiple_of(start, 16), size)

    def stage_b(k):
        at = lax.rem(k, 4)
        pltpu.make_async_copy(mine.at[at], mine.at[at], sem_l.at[k]).wait()
        wait_in(buf_a.at[k], sem_a, (k,))
        buf_h[k] = add(mine[at, 1 - y], buf_a[k, 1 - y])
        send(buf_h.at[k], buf_b.at[k], sem_b, (k,), y_peer).start()
        buf_a[k, y] = add(mine[at, y], buf_a[k, y])

    def stage_c(k):
        wait_in(buf_b.at[k], sem_b, (k,))
        buf_s[k] = add(buf_a[k, y, :, column(1 - x)], buf_b[k, :, column(1 - x)])
        send(buf_s.at[k], buf_c.at[k], sem_c, (0, k), x_peer).start()

    my_two, other_two = band(low * 2 * piece, 2 * piece), band((1 - low) * 2 * piece, 2 * piece)
    my_one, other_one = band(high * piece, piece), band((1 - high) * piece, piece)
    my_rows = band(low * 2 * piece + high * piece, piece)

    def stage_d(k):
        wait_in(buf_c.at[k], sem_c, (0, k))
        cols = column(x)
        joined = buf_a[k, y, :, cols].astype(F32) + buf_b[k, :, cols].astype(F32) + buf_c[k].astype(F32)
        buf_c[k] = joined.astype(BF)
        send(buf_c.at[k, other_two, :], buf_d.at[k], sem_d, (0, k), pair_peer).start()

    def stage_d2(k):
        wait_in(buf_d.at[k], sem_d, (0, k))
        buf_d[k] = add(buf_d[k], buf_c[k, my_two, :])
        send(buf_d.at[k, other_one, :], buf_e.at[k], sem_d, (1, k), skip_peer).start()

    def stage_e(k):
        wait_in(buf_e.at[k], sem_d, (1, k))
        buf_e[k] = add(buf_e[k], buf_d[k, my_one, :])
        out_ref[k, my_rows, column(x)] = buf_e[k]
        send(buf_e.at[k], out_ref.at[k, my_rows, column(x)], sem_d, (2, k), skip_peer).start()

    def stage_e2(k):
        wait_in(buf_e.at[k], sem_d, (2, k))
        there = out_ref.at[k, my_two, column(x)]
        send(there, there, sem_d, (3, k), pair_peer).start()

    def stage_f(k):
        wait_in(buf_d.at[k], sem_d, (3, k))
        there = out_ref.at[k, :, column(x)]
        send(there, there, sem_c, (1, k), x_peer).start()

    def guarded(fn, k, first, last):
        @pl.when((k >= first) & (k < last))
        def _():
            fn(k)

    def chunk_step(m):
        for lag, stage in enumerate((stage_c, stage_d, stage_d2, stage_e, stage_e2, stage_f)):
            guarded(stage, m - (lag and lag + 1), 0, n_chunks)

    def first_step(t, carry):
        guarded(unit, t, 0, n_pos)
        for j in range(2):
            guarded(stage_b, 2 * t + j, 0, n_ready)
        for k in range(4, n_ready):
            @pl.when(t == (k - 4) // 2)
            def _():
                share_load(k)

        @pl.when(lax.rem(t, 2) == 1)
        def _():
            guarded(near_pass, t // 2 - 1, 0, 4)

        guarded(far_pass, t - 2, 4, 8)

        @pl.when((lax.rem(t, 2) == 0) & (t >= 2))
        def _():
            chunk_step(t // 2 - 1)

        return carry

    lax.fori_loop(0, n_pos, first_step, 0)
    done = n_pos // 2 - 1

    fetch[1].wait()
    fetch[2].wait()
    own_tok = pltpu.make_async_copy(mine_tok_ref, loads.at[0, 2], sem_load.at[0, 2])
    own_tok.start()

    def to_bf(j, target):
        for owner in range(n_wsh):
            gbf[target, owner] = acc[j, owner * rows : (owner + 1) * rows, :].astype(BF)
        share_load(n_ready + target)
        share_send(n_ready + target)

    to_bf(0, 0)
    to_bf(1, 1)
    own_tok.wait()

    def query_part(r, carry):
        fs = pl.ds(pl.multiple_of(r * 256, 256), 256)
        acc[0, fs, :] = lax.dot_general(loads[0, 2, :, fs].T, dq[...], NN, preferred_element_type=F32)
        return carry

    lax.fori_loop(0, 2 * half // 256, query_part, 0)
    to_bf(0, 2)

    def query_tokens(r, carry):
        rs = pl.ds(pl.multiple_of(r * 256, 256), 256)
        own[rs, :] += lax.dot_general(dq[rs, :], weights[2], NT, preferred_element_type=F32)
        bias[8:16, :] += jnp.sum(dq[rs, :].astype(F32).reshape(32, 8, 2 * half), axis=0)
        return carry

    lax.fori_loop(0, tall // 256, query_tokens, 0)

    sums[0] = vec_ref[...]
    sums[0, 0:1, :] = jnp.sum(bias[8:16, :], axis=0, keepdims=True)
    sums[0, 1:2, :] = jnp.sum(bias[0:8, :], axis=0, keepdims=True)
    pair = (core_peer, y_peer, x_peer)

    def vec_send(stage):
        send(sums.at[stage], heard.at[stage], sem_v, (stage,), pair[stage]).start()

    def vec_stage(stage):
        wait_in(heard.at[stage], sem_v, (stage,))
        total = sums[stage] + heard[stage]
        sums[stage + 1] = total
        if stage < 2:
            vec_send(stage + 1)
        else:
            line[z] = total
            for d in range(1, zs):
                send(sums.at[3], line.at[z], sem_v, (3,), z_peer(d)).start()

    def vec_last():
        wait_in(line.at[pl.ds(0, zs - 1)], sem_v, (3,))
        total = line[0]
        for d in range(1, zs):
            total = total + line[d]
        small, wide = total[0:8, 0:rows], total[8:9, :]
        for owner in range(1, n_wsh):
            small = jnp.where(w == owner, total[0:8, owner * rows : (owner + 1) * rows], small)
            wide = jnp.where(w == owner, total[8 + owner : 9 + owner, :], wide)
        vec_out[...] = small
        wide_out[...] = wide

    vec_send(0)

    def second_step(m, carry):
        guarded(stage_b, m - done + n_ready, n_ready, n_chunks)
        chunk_step(m)
        guarded(lambda k: near_own(), m - done, 0, 1)
        for stage in range(3):
            guarded(lambda k: vec_stage(stage), m - done - 1 - stage, 0, 1)
        guarded(lambda k: near_end(), m - done - 3, 0, 1)
        guarded(lambda k: far_end(), m - done - 4, 0, 1)
        guarded(lambda k: vec_last(), m - done - 5, 0, 1)
        return carry

    lax.fori_loop(done, n_chunks + 6, second_step, 0)
    wait_in(last_x, sem_x, (n_pos // 2,))
    own[far_rows, :] += last_x[...].astype(F32)
    grad_ref[...] = own[...].astype(BF)

    def drain(k, carry):
        wait_in(buf_s.at[k], sem_c, (1, k))
        wait_out(buf_a.at[k], sem_a, (k,))
        wait_out(buf_b.at[k], sem_b, (k,))
        wait_out(buf_s.at[k], sem_c, (0, k))
        wait_out(buf_s.at[k], sem_c, (1, k))
        wait_out(buf_d.at[k], sem_d, (0, k))
        wait_out(buf_e.at[k], sem_d, (1, k))
        wait_out(buf_e.at[k], sem_d, (2, k))
        wait_out(buf_d.at[k], sem_d, (3, k))
        return carry

    lax.fori_loop(0, n_chunks, drain, 0)
    for stage in range(3):
        wait_out(heard.at[stage], sem_v, (stage,))
    wait_out(line.at[pl.ds(0, zs - 1)], sem_v, (3,))
    wait_out(last_x, sem_x, (n_pos // 2,))

    def drain_runs(i, carry):
        _run, mine_too, there = position(i)

        @pl.when(there)
        def _():
            wait_out(far_z.at[i], sem_far, (i,))

            @pl.when(mine_too == 1)
            def _():
                wait_out(from_z.at[i // 2], sem_z, (i // 2,))

        return carry

    lax.fori_loop(0, n_pos - 2, drain_runs, 0)

    def drain_x(n, carry):
        _run, _mine_too, there = position(2 * n)

        @pl.when(there)
        def _():
            wait_out(from_x.at[n], sem_x, (n,))

        return carry

    lax.fori_loop(0, n_pos // 2, drain_x, 0)


def widen_kernel(spans, in_ref, small_ref, wide_ref, grad_ref, layer_ref, grad_out, layer_out, *outs):
    grad_out[...] = grad_ref[...]
    layer_out[...] = layer_ref[...]
    for (first, down, across), out in zip(spans, outs):
        for r in range(down):
            for col in range(across):
                out[r, :, col * D : (col + 1) * D] = in_ref[first + r * across + col].astype(F32)
    vectors = outs[len(spans) :]
    for i, out in enumerate(vectors[:-1]):
        out[...] = small_ref[i : i + 1, :]
    vectors[-1][...] = wide_ref[...]


def widen(summed, spans, small, wide, grad_inputs, layer_out):
    n, rows, _width = summed.shape
    part = rows // 2
    tokens = pl.BlockSpec((grad_inputs.shape[0] // 2, D), lambda i: (i, 0))
    shape = jax.ShapeDtypeStruct
    vectors = [(1, small.shape[1])] * small.shape[0] + [wide.shape]
    outs = pl.pallas_call(
        functools.partial(widen_kernel, spans),
        grid=(2,),
        out_shape=[shape(grad_inputs.shape, BF)] * 2
        + [shape((down, rows, across * D), F32) for _first, down, across in spans]
        + [shape(v, F32) for v in vectors],
        in_specs=[pl.BlockSpec((n, part, D), lambda i: (0, i, 0)), pl.BlockSpec(small.shape, lambda i: (0, 0)),
                  pl.BlockSpec(wide.shape, lambda i: (0, 0)), tokens, tokens],
        out_specs=[tokens] * 2 + [pl.BlockSpec((down, part, across * D), lambda i: (0, i, 0)) for _first, down, across in spans]
        + [pl.BlockSpec(v, lambda i: (0, 0)) for v in vectors],
        name="widen",
    )(summed, small, wide, grad_inputs, layer_out)
    grad_inputs, layer_out, mats, vectors = outs[0], outs[1], outs[2 : len(spans) + 2], outs[len(spans) + 2 :]
    return grad_inputs, layer_out, [o.reshape(-1, o.shape[2]) for o in mats], [v.reshape(-1) for v in vectors[:-1]], vectors[-1].reshape(-1)


def finish(matrices, vec, grad_k, grad_v, all_tokens, grad_q, kvq_w, own_grad, inputs, layer_out):
    n_ctx, n_wsh = lax.axis_size("ctx"), lax.axis_size("wsh")
    zs, hops = n_ctx // 2, reach(n_ctx) // 2
    rows = D // n_wsh
    parts, sources, spans = [], [], []
    for p, g in enumerate(matrices):
        down, across = g.shape[0] // D, g.shape[1] // D
        parts.append(g.astype(BF).reshape(n_wsh, down * rows, across * D))
        spans.append((len(sources), down, across))
        sources += [(p, r * rows, col * D) for r in range(down) for col in range(across)]
    n = len(sources) + 3
    spans += [(len(sources) + j, 1, 1) for j in range(3)]
    half, piece, tall = D // 2, rows // zs, inputs.shape[0]
    n_pos, cut = 4 * hops + 2, tall * 5 // 8
    vm, dma, shape = pltpu.VMEM, pltpu.SemaphoreType.DMA, jax.ShapeDtypeStruct
    any_spec = pl.BlockSpec(memory_space=pltpu.HBM)
    vm_spec = pl.BlockSpec(memory_space=pltpu.VMEM)
    summed, small, wide, grad_own = pl.pallas_call(
        functools.partial(finish_kernel, sources, len(parts)),
        out_shape=(shape((n, rows, D), BF), shape((8, rows), F32), shape((1, D), F32), shape((tall, D), BF)),
        in_specs=[any_spec] * len(parts) + [vm_spec] + [any_spec] * 7,
        out_specs=(vm_spec,) * 4,
        scratch_shapes=[
            vm((4, 2, rows, D), BF), vm((n, 2, rows, D), BF), vm((n, rows, D), BF), vm((n, rows, D), BF),
            vm((n, rows, half), BF), vm((n, rows, half), BF), vm((n, 2 * piece, half), BF), vm((n, piece, half), BF),
            vm((3, n_wsh, rows, D), BF),
            vm((4,) + vec.shape, F32), vm((3,) + vec.shape, F32), vm((zs,) + vec.shape, F32),
            vm((2, 3, tall, D), BF), vm((3, D, D), BF), vm((2, D, D), F32), vm((tall, D), BF), vm((tall, D), F32),
            vm((16, D), F32),
            vm((n_pos, tall, D), BF), vm((n_pos // 2, cut, D), BF), vm((4, cut, D), BF),
            vm((n_pos - 2, tall - cut, D), BF), vm((tall - cut, D), BF),
            dma((n,)), dma((2, n)), dma((2, n)), dma((2, 2, n)), dma((2, 4, n)), dma((2, 4)),
            dma((2, n_pos // 2 + 1)), dma((2, 4)), dma((2, n_pos - 2)), dma((2, 3)), dma((3,)),
        ],
        compiler_params=pltpu.CompilerParams(collective_id=2, has_side_effects=True, vmem_limit_bytes=63 * 2**20),
        name="finish",
    )(*parts, vec, grad_k, grad_v, all_tokens, grad_q, kvq_w, own_grad, inputs)
    return widen(summed, spans, small, wide, grad_own, layer_out)


def gather_kernel(cut, tok_ref, docs_ref, wk_ref, wv_ref, wq_ref, wo_ref, wu_ref, vec_ref,
                  tok_out, k_out, v_out, q_out, w_out, vec_out, wo_out, wu_out, query_doc, key_doc,
                  tok, kbuf, vbuf, qbuf, wbuf, vecs, wo, wu, kdoc,
                  sem_in, sem_out, sem_w, sem_l, sem_o):
    n_ctx = lax.axis_size("ctx")
    zs = n_ctx // 2
    a, w = lax.axis_index("ctx"), lax.axis_index("wsh")
    z, x = a // 2, lax.rem(a, 2)
    y, c = w // 2, lax.rem(w, 2)
    core_peer = (a, y * 2 + (1 - c))
    y_peer = (a, (1 - y) * 2 + c)
    x_peer = (z * 2 + (1 - x), w)
    up, down = (a + 2, w), (a - 2, w)
    near = reach(n_ctx)
    MESH = pl.DeviceIdType.MESH
    n_slices = sem_in.shape[1]
    tall = tok.shape[1] // n_slices
    own = wk_ref.shape[0]
    far = 4 * (near // 2 + 1)

    barrier = pltpu.get_barrier_semaphore()
    around = [(lax.rem(z + d, zs) * 2 + x, w) for d in (1, zs - 1)]
    for dev in [core_peer, y_peer, x_peer] + around:
        pl.semaphore_signal(barrier, inc=1, device_id=dev, device_id_type=MESH)
    pl.semaphore_wait(barrier, 5)

    def relative(u):
        dz = (u // 4) * (1 - 2 * lax.rem(u, 2))
        other = lax.rem(u // 2, 2)
        run = 2 * (z + dz) + (x + other - 2 * x * other)
        there = (z + dz >= 0) & (z + dz < zs) & (jnp.abs(run - a) <= near) & ((u >= 4) | (lax.rem(u, 2) == 0))
        return run, dz, other, there

    def rows(s):
        return pl.ds(pl.multiple_of(s * tall, tall), tall)

    def remote(src, dst, send_sem, recv_sem, dev):
        return pltpu.make_async_remote_copy(
            src_ref=src, dst_ref=dst, send_sem=send_sem, recv_sem=recv_sem, device_id=dev, device_id_type=MESH)

    def routes(u, s):
        run, dz, other, there = relative(u)
        z_first = s < cut
        to_x = there & (z_first | (dz == 0)) & (other == 0) & (jnp.abs(run - x_peer[0]) <= near)
        along = there & ((other == 0) | jnp.logical_not(z_first))
        to_up = along & (dz <= 0) & (z + 1 < zs) & (jnp.abs(run - (a + 2)) <= near)
        to_down = along & (dz >= 0) & (z > 0) & (jnp.abs(run - (a - 2)) <= near)
        return run, ((0, x_peer, to_x), (1, up, to_up), (2, down, to_down))

    def pass_on(u, s):
        run, where = routes(u, s)
        for d, dev, ok in where:
            @pl.when(ok)
            def _():
                source = tok_ref if isinstance(u, int) and u == 0 else tok.at[run]
                remote(source.at[rows(s), :], tok.at[run, rows(s), :], sem_out.at[d, u, s], sem_in.at[run, s], dev).start()

    def await_slice(u, s):
        run, _dz, _other, there = relative(u)

        @pl.when(there)
        def _():
            remote(tok.at[run, rows(s), :], tok.at[run, rows(s), :], sem_out.at[0, 0, 0], sem_in.at[run, s], x_peer).wait_recv()

    def start_own(s, carry):
        pass_on(0, s)
        return carry

    def weight_rows(owner):
        return pl.ds(pl.multiple_of(owner * own, 16), own)

    def shard(m, owner):
        if m == 3:
            return vecs.at[owner]
        return (wbuf.at[0], wbuf.at[1], wbuf.at[2], None, wo, wu)[m].at[weight_rows(owner), :]

    vecs[w, 0 : vec_ref.shape[0], :] = vec_ref[...]
    shards = (wk_ref, wv_ref, wq_ref, vecs.at[w], wo_ref, wu_ref)
    for m in (3, 0, 1, 2, 4, 5):
        remote(shards[m], shard(m, w), sem_w.at[0, 1, m], sem_w.at[1, 1, m], y_peer).start()
        remote(shards[m], shard(m, w), sem_w.at[0, 0, m], sem_w.at[1, 0, m], core_peer).start()
        if m != 3:
            pltpu.make_async_copy(shards[m], shard(m, w), sem_w.at[0, 3, m]).start()
    lax.fori_loop(0, n_slices, start_own, 0)
    pltpu.make_async_copy(tok_ref, tok.at[a], sem_l.at[4]).start()

    for j in range(n_ctx):
        @pl.when(jnp.abs(j - a) > near)
        def _():
            tok[j] = jnp.zeros_like(tok[j])

    n_rows = tok.shape[1]

    def is_own_lane(first):
        pos = first + lax.broadcasted_iota(jnp.int32, (n_rows, 128), 0)
        doc = jnp.full((n_rows, 128), -1, jnp.int32)
        for d in range(docs_ref.shape[1]):
            doc = doc + jnp.where(pos >= docs_ref[0, d], 1, 0)
        return lax.broadcasted_iota(jnp.int32, (n_rows, 128), 1) == doc

    def key_lanes(j, carry):
        kdoc[pl.ds(pl.multiple_of(j * n_rows, n_rows), n_rows), :] = jnp.where(
            is_own_lane(j * n_rows), 0.0, -1e30).astype(BF)
        return carry

    lax.fori_loop(0, n_ctx, key_lanes, 0)
    pltpu.make_async_copy(kdoc, key_doc, sem_l.at[3]).start()
    query_doc[...] = jnp.where(is_own_lane(a * n_rows), 1.0, 0.0).astype(BF)

    def weight_arrival(m, kind):
        part = shard(m, w)
        return remote(part, part, sem_w.at[0, kind, m], sem_w.at[1, kind, m], core_peer)

    across = (1 - y) * 2 + c

    def weight_forward(m):
        weight_arrival(m, 1).wait_recv()
        remote(shard(m, across), shard(m, across), sem_w.at[0, 2, m], sem_w.at[1, 2, m], core_peer).start()

    def weight_end(m):
        weight_arrival(m, 0).wait_recv()
        weight_arrival(m, 2).wait_recv()
        if m != 3:
            pltpu.make_async_copy(shard(m, w), shard(m, w), sem_w.at[0, 3, m]).wait()

    def relay(first, last):
        def one(i, carry):
            s = i // (last - first)
            u = first + lax.rem(i, last - first)
            await_slice(u, s)
            pass_on(u, s)
            return carry

        lax.fori_loop(0, n_slices * (last - first), one, 0)

    relay(2, 6)
    weight_forward(3)
    weight_forward(0)
    weight_forward(1)
    weight_end(3)
    vec_out[0:8, :] = jnp.concatenate([vecs[o, 0:8, :] for o in range(4)], axis=1)
    for o in range(4):
        vec_out[8 + o : 9 + o, :] = jnp.concatenate([vecs[o, 8 + i : 9 + i, :] for i in range(4)], axis=1)
    pltpu.make_async_copy(tok_ref, tok.at[a], sem_l.at[4]).wait()
    weight_end(0)
    weight_end(1)

    step_rows = 256
    steps = tok.shape[1] // step_rows

    def query_part(i, carry):
        r = pl.ds(pl.multiple_of(i * step_rows, step_rows), step_rows)
        q = (jnp.dot(tok[a, r, :], wbuf[2], preferred_element_type=F32) + vec_out[0:1, :]).astype(BF)
        qbuf[r, :] = q * jnp.asarray(SCALE, BF)
        return carry

    def project(u, carry):
        run, _dz, _other, there = relative(u)

        @pl.when(u == 6)
        def _():
            weight_forward(2)
            weight_end(2)
            lax.fori_loop(0, steps, query_part, 0)
            pltpu.make_async_copy(qbuf, q_out, sem_l.at[5]).start()
            relay(6, 10)

        @pl.when(there)
        def _():
            @pl.when(u >= 10)
            def _():
                def one(s, carry):
                    await_slice(u, s)
                    return carry

                lax.fori_loop(0, n_slices, one, 0)

            def part(i, carry):
                r = pl.ds(pl.multiple_of(i * step_rows, step_rows), step_rows)
                t = tok[run, r, :]
                kbuf[run, r, :] = jnp.dot(t, wbuf[0], preferred_element_type=F32).astype(BF)
                vbuf[run, r, :] = (jnp.dot(t, wbuf[1], preferred_element_type=F32) + vec_out[1:2, :]).astype(BF)
                return carry

            lax.fori_loop(0, steps, part, 0)
            for i, (src, dst) in enumerate(((kbuf, k_out), (vbuf, v_out), (tok, tok_out))):
                pltpu.make_async_copy(src.at[run], dst.at[run], sem_o.at[i, run]).start()

        return carry

    for j in range(n_ctx):
        @pl.when(jnp.abs(j - a) > near)
        def _():
            kbuf[j] = jnp.zeros_like(kbuf[j])
            vbuf[j] = jnp.zeros_like(vbuf[j])
            for i, (src, dst) in enumerate(((kbuf, k_out), (vbuf, v_out), (tok, tok_out))):
                pltpu.make_async_copy(src.at[j], dst.at[j], sem_o.at[i, j]).start()

    lax.fori_loop(0, far, project, 0)

    pltpu.make_async_copy(wbuf, w_out, sem_l.at[6]).start()

    for m in (4, 5):
        weight_forward(m)
    for m, full, target in ((4, wo, wo_out), (5, wu, wu_out)):
        weight_end(m)
        pltpu.make_async_copy(full, target, sem_l.at[m - 4]).start()
    for m in range(6):
        for kind in range(3):
            weight_arrival(m, kind).wait_send()

    def drain(i, carry):
        s = i // far
        u = lax.rem(i, far)
        run, where = routes(u, s)
        for d, dev, ok in where:
            @pl.when(ok & (u < 10))
            def _():
                remote(tok.at[run, rows(s), :], tok.at[run, rows(s), :], sem_out.at[d, u, s], sem_in.at[run, s], dev).wait_send()
        return carry

    lax.fori_loop(0, n_slices * far, drain, 0)
    for j in range(n_ctx):
        for i, (src, dst) in enumerate(((kbuf, k_out), (vbuf, v_out), (tok, tok_out))):
            pltpu.make_async_copy(src.at[j], dst.at[j], sem_o.at[i, j]).wait()
    pltpu.make_async_copy(qbuf, q_out, sem_l.at[5]).wait()
    pltpu.make_async_copy(wbuf, w_out, sem_l.at[6]).wait()
    pltpu.make_async_copy(wo, wo_out, sem_l.at[0]).wait()
    pltpu.make_async_copy(wu, wu_out, sem_l.at[1]).wait()
    pltpu.make_async_copy(kdoc, key_doc, sem_l.at[3]).wait()


def gather_project(inputs, doc_starts, vectors, key_weight, value_weight, query_weight, out_weight, up_weight):
    n_ctx, n_wsh = lax.axis_size("ctx"), lax.axis_size("wsh")
    tall = inputs.shape[0]
    n_slices = 8
    far = 4 * (reach(n_ctx) // 2 + 1)
    vm, dma = pltpu.VMEM, pltpu.SemaphoreType.DMA
    any_spec = pl.BlockSpec(memory_space=pltpu.HBM)
    vm_spec = pl.BlockSpec(memory_space=pltpu.VMEM)
    runs = (n_ctx, tall, D)
    shape = jax.ShapeDtypeStruct
    return pl.pallas_call(
        functools.partial(gather_kernel, 5),
        out_shape=(shape(runs, BF), shape(runs, BF), shape(runs, BF), shape((tall, D), BF), shape((3, D, D), BF),
                   shape((16, D), F32), shape((D, D), BF), shape((D, up_weight.shape[1]), BF), shape((tall, 128), BF),
                   shape((n_ctx * tall, 128), BF)),
        in_specs=[any_spec, pl.BlockSpec(memory_space=pltpu.SMEM)] + [any_spec] * 5 + [vm_spec],
        out_specs=(any_spec,) * 5 + (vm_spec,) + (any_spec,) * 2 + (vm_spec, any_spec),
        scratch_shapes=[
            vm(runs, BF), vm(runs, BF), vm(runs, BF), vm((tall, D), BF), vm((3, D, D), BF), vm((n_wsh, 16, D // n_wsh), F32),
            vm((D, D), BF), vm((D, up_weight.shape[1]), BF), vm((n_ctx * tall, 128), BF),
            dma((n_ctx, n_slices)), dma((3, far, n_slices)), dma((2, 4, 6)), dma((7,)), dma((3, n_ctx)),
        ],
        compiler_params=pltpu.CompilerParams(collective_id=1, has_side_effects=True, vmem_limit_bytes=63 * 2**20),
        name="gather_project",
    )(inputs, doc_starts, key_weight, value_weight, query_weight, out_weight, up_weight, vectors)


def local(
    tokens,
    cotangent,
    doc_starts,
    query_weight,
    key_weight,
    value_weight,
    out_weight,
    up_weight,
    down_weight,
    query_bias,
    value_bias,
    out_bias,
    attn_gain,
    attn_shift,
    up_bias,
    down_bias,
    final_gain,
    final_shift,
):
    inputs = tokens[0]
    doc_start = doc_starts[0]
    tok_rows = inputs.shape[0]
    stream_rows = tok_rows * lax.axis_size("ctx")
    tile = min(tok_rows, 256)
    n_ctx, n_wsh = lax.axis_size("ctx"), lax.axis_size("wsh")
    own = D // n_wsh

    def gather(x):
        return lax.all_gather(x, "wsh", axis=0, tiled=True)

    fast = n_wsh == 4 and n_ctx == 8 and own % (n_ctx // 2 * 16) == 0 and tok_rows % 512 == 0
    if fast:
        small = (query_bias, value_bias, out_bias, attn_gain, attn_shift, down_bias, final_gain, final_shift)
        vectors, place = jnp.zeros(((8 + n_wsh) * own,), F32), 0
        for v in small + (up_bias,):
            ends = (place, vectors.shape[0] - place - v.shape[0], 0)
            vectors = vectors + lax.pad(v.astype(F32), jnp.zeros((), F32), (ends,))
            place += v.shape[0]
        vectors = vectors.reshape(8 + n_wsh, own)
        all_tokens, keys, values, queries, kvq_w, vec, out_w, up_w, query_doc, key_doc = gather_project(
            inputs, doc_starts, vectors, key_weight, value_weight, query_weight, out_weight, up_weight
        )
        down_own, _unused = lax.optimization_barrier((down_weight, vec))
        down_far = lax.ppermute(down_own, "wsh", [(i, i ^ 2) for i in range(n_wsh)])
        all_tokens, keys, values = [r.reshape(stream_rows, D) for r in (all_tokens, keys, values)]
    else:
        first_row = lax.axis_index("ctx") * tok_rows
        query_doc, key_doc = document_lanes(doc_start, first_row, tok_rows, stream_rows)
        small = jnp.stack(
            [query_bias, value_bias, out_bias, attn_gain, attn_shift, down_bias, final_gain, final_shift]
        )
        all_tokens = lax.all_gather(inputs, "ctx", axis=0, tiled=True)
        query_w, key_w, value_w = gather(query_weight), gather(key_weight), gather(value_weight)
        small = gather(small.T).astype(F32)
        query_b, value_b, out_b, attn_g, attn_s, down_b, final_g, final_s = [small[:, i] for i in range(8)]
        up_b = gather(up_bias).astype(F32)
        queries = jnp.dot(inputs, query_w, preferred_element_type=F32) + query_b
        queries = queries.astype(BF) * jnp.asarray(SCALE, BF)
        keys = jnp.dot(all_tokens, key_w, preferred_element_type=F32).astype(BF)
        values = (jnp.dot(all_tokens, value_w, preferred_element_type=F32) + value_b).astype(BF)
    mixed_t, log_rows = attn_fwd(doc_start, queries, query_doc, keys, key_doc, values, tq=tile)
    if fast:
        layer_out, grad_sum1, grad_attn, vec_grads, grad_up_w, grad_down_w, grad_out_w = middle(
            mixed_t, inputs, cotangent[0], vec, out_w, up_w, down_own, down_far
        )
        grad_q, grad_k, grad_v = attn_bwd(
            doc_start, queries, query_doc, grad_attn, log_rows, mixed_t, keys, key_doc, values, tq=tile
        )
        grad_inputs, layer_out, mats, small, wide = finish(
            (grad_up_w, grad_out_w, grad_down_w), vec_grads, grad_k.reshape(n_ctx, tok_rows, D),
            grad_v.reshape(n_ctx, tok_rows, D), all_tokens.reshape(n_ctx, tok_rows, D), grad_q, kvq_w, grad_sum1, inputs, layer_out,
        )
        up_sum, out_sum, down_sum, key_sum, value_sum, query_sum = mats
        return (
            layer_out.reshape(1, tok_rows, D), grad_inputs.reshape(1, tok_rows, D), query_sum, key_sum, value_sum,
            out_sum, up_sum, down_sum, small[0], small[1], small[2], small[3], small[4], wide,
            small[5], small[6], small[7],
        )

    out_w = gather(out_weight)
    up_w = gather(up_weight)
    down_w = gather(down_weight)
    attn_t = mixed_t.astype(BF)
    inputs_f = inputs.astype(F32)
    branch = lax.dot_general(attn_t, out_w, TN, preferred_element_type=F32) + out_b
    first_norm, first_pull = jax.vjp(layer_norm, inputs_f + branch, attn_g, attn_s)
    first_b = first_norm.astype(BF)
    up_f = jnp.dot(first_b, up_w, preferred_element_type=F32) + up_b
    act_f, act_pull = jax.vjp(gelu_act, up_f)
    act_b = act_f.astype(BF)
    down_f = jnp.dot(act_b, down_w, preferred_element_type=F32) + down_b
    final_f, final_pull = jax.vjp(layer_norm, first_norm + down_f, final_g, final_s)
    layer_out = final_f.astype(BF)

    grad_sum2, grad_final_g, grad_final_s = final_pull(cotangent[0].astype(F32))
    grad_down = grad_sum2.astype(BF)
    grad_down_w = jnp.einsum("tf,td->fd", act_b, grad_down, preferred_element_type=F32)
    grad_down_b = jnp.sum(grad_down.astype(F32), axis=0)
    grad_act = jnp.einsum("td,fd->tf", grad_down, down_w, preferred_element_type=F32)
    (grad_up_f,) = act_pull(grad_act)
    grad_up = grad_up_f.astype(BF)
    grad_up_w = jnp.einsum("td,tf->df", first_b, grad_up, preferred_element_type=F32)
    grad_up_b = jnp.sum(grad_up.astype(F32), axis=0)
    grad_first = grad_sum2 + jnp.einsum("tf,df->td", grad_up, up_w, preferred_element_type=F32)
    grad_sum1, grad_attn_g, grad_attn_s = first_pull(grad_first)
    grad_branch = grad_sum1.astype(BF)
    grad_out_w = jnp.dot(attn_t, grad_branch, preferred_element_type=F32)
    grad_out_b = jnp.sum(grad_branch.astype(F32), axis=0)
    grad_attn = jnp.einsum("te,de->td", grad_branch, out_w, preferred_element_type=F32).astype(BF)
    grad_q, grad_k, grad_v = attn_bwd(
        doc_start, queries, query_doc, grad_attn, log_rows, mixed_t, keys, key_doc, values, tq=tile
    )
    def total(g):
        part = lax.psum_scatter(g.astype(BF), "wsh", scatter_dimension=0, tiled=True)
        return lax.psum(part, "ctx").astype(F32)

    grad_all = jnp.einsum("te,de->td", grad_k, key_w, preferred_element_type=F32)
    grad_all = grad_all + jnp.einsum("te,de->td", grad_v, value_w, preferred_element_type=F32)
    grad_own = lax.psum_scatter(grad_all.astype(BF), "ctx", scatter_dimension=0, tiled=True)
    grad_query_w = jnp.einsum("td,te->de", inputs, grad_q, preferred_element_type=F32)
    grad_key_w = jnp.einsum("td,te->de", all_tokens, grad_k, preferred_element_type=F32)
    grad_value_w = jnp.einsum("td,te->de", all_tokens, grad_v, preferred_element_type=F32)
    grad_query_b = jnp.sum(grad_q.astype(F32), axis=0)
    grad_value_b = jnp.sum(grad_v.astype(F32), axis=0)
    grad_inputs = grad_sum1 + jnp.einsum("te,de->td", grad_q, query_w, preferred_element_type=F32)
    grad_inputs = grad_inputs + grad_own.astype(F32)
    sums = [
        total(g)
        for g in (
            grad_query_w, grad_key_w, grad_value_w, grad_out_w, grad_up_w, grad_down_w,
            grad_query_b, grad_value_b, grad_out_b, grad_attn_g, grad_attn_s, grad_up_b,
            grad_down_b, grad_final_g, grad_final_s,
        )
    ]
    return (
        layer_out.reshape(1, tok_rows, D),
        grad_inputs.astype(BF).reshape(1, tok_rows, D),
        *sums,
    )


def solution(mesh):
    rows, mat, vec = P("wsh", "ctx", None), P("wsh", None), P("wsh")
    return jax.shard_map(
        local,
        mesh=mesh,
        in_specs=(rows, rows, mat) + (mat,) * 6 + (vec,) * 9,
        out_specs=(rows, rows) + (mat,) * 6 + (vec,) * 9,
        check_vma=False,
    )
```
